32 devices in a mesh: dp: 16 (over z, y, x), seq: 2 (over core).
Axes of the slice: x: 2, y: 2, z: 4, core: 2. Of those that a mesh axis runs over, the one named last changes fastest.
Arguments:
- hidden_in: bfloat16 [2, 16, 512, 768], P(None, 'dp', 'seq'), may hold values from -6 to 6
- cotangent: bfloat16 [2, 16, 512, 768], P(None, 'dp', 'seq'), may hold values from -6 to 6
- attention_keep: int32 [2, 16, 12, 512, 128], P(None, 'dp', None, 'seq'), may hold values from 0 to 4095
- output_keep: int32 [2, 16, 512, 192], P(None, 'dp', 'seq'), may hold values from 0 to 4095
- feed_keep: int32 [2, 16, 512, 192], P(None, 'dp', 'seq'), may hold values from 0 to 4095
- qkv_weight: bfloat16 [768, 2304], P(('dp', 'seq')), may hold values from -0.21875 to 0.21875
- qkv_bias: bfloat16 [1536], P(('dp', 'seq')), may hold values from -3 to 3
- out_weight: bfloat16 [768, 768], P(('dp', 'seq')), may hold values from -3 to 3
- out_bias: bfloat16 [768], P(('dp', 'seq')), may hold values from -3 to 3
- first_gain: bfloat16 [768], P(('dp', 'seq')), may hold values from 0.099609375 to 1.8984375
- first_shift: bfloat16 [768], P(('dp', 'seq')), may hold values from -3 to 3
- up_weight: bfloat16 [768, 3072], P(('dp', 'seq')), may hold values from -0.21875 to 0.21875
- up_bias: bfloat16 [3072], P(('dp', 'seq')), may hold values from -3 to 3
- down_weight: bfloat16 [3072, 768], P(('dp', 'seq')), may hold values from -0.109375 to 0.109375
- down_bias: bfloat16 [768], P(('dp', 'seq')), may hold values from -3 to 3
- second_gain: bfloat16 [768], P(('dp', 'seq')), may hold values from 0.099609375 to 1.8984375
- second_shift: bfloat16 [768], P(('dp', 'seq')), may hold values from -3 to 3
Outputs:
- layer_out: bfloat16 [2, 16, 512, 768], P(None, 'dp', 'seq')
- grad_input: bfloat16 [2, 16, 512, 768], P(None, 'dp', 'seq')
- grad_qkv_weight: float32 [768, 2304], P(('dp', 'seq'))
- grad_qkv_bias: float32 [1536], P(('dp', 'seq'))
- grad_out_weight: float32 [768, 768], P(('dp', 'seq'))
- grad_out_bias: float32 [768], P(('dp', 'seq'))
- grad_first_gain: float32 [768], P(('dp', 'seq'))
- grad_first_shift: float32 [768], P(('dp', 'seq'))
- grad_up_weight: float32 [768, 3072], P(('dp', 'seq'))
- grad_up_bias: float32 [3072], P(('dp', 'seq'))
- grad_down_weight: float32 [3072, 768], P(('dp', 'seq'))
- grad_down_bias: float32 [768], P(('dp', 'seq'))
- grad_second_gain: float32 [768], P(('dp', 'seq'))
- grad_second_shift: float32 [768], P(('dp', 'seq'))
The draws below stay inside these ranges and needn't reach their ends.
Inputs may be any that keep to these rules, and one draw needn't show every extreme that they name: `attention_keep`: each word packs four 3-bit values, lowest bits first. `output_keep`: each word packs four 3-bit values, lowest bits first. `feed_keep`: each word packs four 3-bit values, lowest bits first.
All inputs are finite; a program needn't handle non-finite values.
Results may differ from the reference program's by a relative error of at most 0.015.
Values may be sent and summed in bfloat16 or wider, within the bound.
No kernel may reach another device: no remote copies, remote signals or barrier semaphores. Data moves between devices by JAX's collectives and lax.ppermute only.
A program may use at most 192 MiB of HBM per device.

```python
import math
import jax
import jax.numpy as jnp
from jax import lax

D = 768
H = 12
DH = 64
FF = 3072
LEN = 512
MICRO = 2
SEQS = 16


def set_ends(drawn, key, least, high):
    dims = drawn.shape
    place = [jax.random.randint(jax.random.fold_in(key, axis), (), 0, dims[axis]) for axis in range(len(dims))]
    drawn = drawn.at[tuple(place)].set(least)
    longest = dims.index(max(dims))
    place[longest] = (place[longest] + 1) % dims[longest]
    return drawn.at[tuple(place)].set(high)


def levels(rng, dims, shards, least, top_value):
    gain, own = 1.0, jax.random.fold_in(rng, 6)
    for axis_at, blocks in shards:
        draws = jnp.exp(jax.random.uniform(jax.random.fold_in(own, axis_at), (blocks,), jnp.float32, least / len(shards), top_value / len(shards)))
        gain = gain * jnp.repeat(draws, dims[axis_at] // blocks).reshape([-1 if axis == axis_at else 1 for axis in range(len(dims))])
    return gain


def bell_draw(rng, shape, width, reach, shards=(), held_as=jnp.bfloat16):
    factor_of = levels(rng, shape, shards, -0.22, 0.18) if shards else 1.0
    drawn = jax.random.normal(rng, shape, jnp.float32) * width * factor_of
    return jnp.minimum(jnp.maximum(drawn, -reach), reach).astype(held_as)


def setup_inputs(seed: int = 0) -> dict:
    arg_keys = jax.random.split(jax.random.key(seed), 18)
    hidden_in = bell_draw(arg_keys[0], (MICRO, SEQS, LEN, D), 1.0, 6.0, ((1, 16), (2, 2)))
    cotangent = bell_draw(arg_keys[1], (MICRO, SEQS, LEN, D), 1.0, 6.0, ((1, 16), (2, 2)))
    attention_keep = set_ends(jax.random.randint(arg_keys[2], (MICRO, SEQS, H, LEN, LEN // 4), 0, 4096), jax.random.fold_in(arg_keys[2], 1), 0, 4095).astype(jnp.int32)
    output_keep = set_ends(jax.random.randint(arg_keys[3], (MICRO, SEQS, LEN, D // 4), 0, 4096), jax.random.fold_in(arg_keys[3], 1), 0, 4095).astype(jnp.int32)
    feed_keep = set_ends(jax.random.randint(arg_keys[4], (MICRO, SEQS, LEN, D // 4), 0, 4096), jax.random.fold_in(arg_keys[4], 1), 0, 4095).astype(jnp.int32)
    qkv_weight = bell_draw(arg_keys[5], (D, 3 * D), D ** -0.5, 0.21875, ((0, 32),))
    qkv_bias = bell_draw(arg_keys[6], (2 * D,), 0.5, 3.0, ((0, 32),))
    out_weight = bell_draw(arg_keys[7], (D, D), (3 * D // LEN) ** -0.5, 3.0, ((0, 32),))
    out_bias = bell_draw(arg_keys[8], (D,), 0.5, 3.0, ((0, 32),))
    first_gain = jnp.clip(1.0 + 0.18 * jax.random.normal(arg_keys[9], (D,), jnp.float32), 0.099609375, 1.8984375).astype(jnp.bfloat16)
    first_shift = bell_draw(arg_keys[10], (D,), 0.5, 3.0, ((0, 32),))
    up_weight = bell_draw(arg_keys[11], (D, FF), D ** -0.5, 0.21875, ((0, 32),))
    up_bias = bell_draw(arg_keys[12], (FF,), 0.5, 3.0, ((0, 32),))
    down_weight = bell_draw(arg_keys[13], (FF, D), FF ** -0.5, 0.109375, ((0, 32),))
    down_bias = bell_draw(arg_keys[14], (D,), 0.5, 3.0, ((0, 32),))
    second_gain = jnp.clip(1.0 + 0.18 * jax.random.normal(arg_keys[15], (D,), jnp.float32), 0.099609375, 1.8984375).astype(jnp.bfloat16)
    second_shift = bell_draw(arg_keys[16], (D,), 0.5, 3.0, ((0, 32),))
    return dict(hidden_in=hidden_in, cotangent=cotangent, attention_keep=attention_keep, output_keep=output_keep, feed_keep=feed_keep, qkv_weight=qkv_weight, qkv_bias=qkv_bias, out_weight=out_weight, out_bias=out_bias, first_gain=first_gain, first_shift=first_shift, up_weight=up_weight, up_bias=up_bias, down_weight=down_weight, down_bias=down_bias, second_gain=second_gain, second_shift=second_shift)


@jax.custom_vjp
def low(v):
    return lax.optimization_barrier(v.astype(jnp.bfloat16)).astype(jnp.float32)

@jax.custom_vjp
def low_back(v):
    return v

def low_keep(v):
    return (low(v), None)

def low_pass(kept, grad):
    return (grad,)

def back_keep(v):
    return (v, None)

def back_low(kept, grad):
    return (low(grad),)
low.defvjp(low_keep, low_pass)
low_back.defvjp(back_keep, back_low)
highest = lax.Precision.HIGHEST
epsilon = 1e-12
keep_scale = 8.0 / 7.0

def matmul(left_side, right_side):
    return jnp.dot(left_side, right_side, precision=highest)

def unpack_keep(packed_words):
    shifts = jnp.arange(4, dtype=jnp.int32) * 3
    nibble = jnp.right_shift(packed_words[..., None], shifts) & 7
    keep_value = (nibble >= 1).astype(jnp.float32) * keep_scale
    return keep_value.reshape(packed_words.shape[:-1] + (packed_words.shape[-1] * 4,))

def layer_norm(values, norm_gain, norm_shift):
    centred = values - lax.optimization_barrier(jnp.mean(values, axis=-1, keepdims=True))
    variance = lax.optimization_barrier(jnp.mean(centred * centred, axis=-1, keepdims=True))
    return centred * lax.rsqrt(variance + epsilon) * norm_gain + norm_shift

def forward_block(hidden, params, attention_words, output_words, feed_words):
    qkv_weight, qkv_bias, out_weight, out_bias, first_gain, first_shift, up_weight, up_bias, down_weight, down_bias, second_gain, second_shift = params
    group_size = hidden.shape[0]
    token_rows = hidden.reshape(group_size * LEN, D)
    bias_full = jnp.concatenate([qkv_bias[:D], jnp.zeros((D,), jnp.float32), qkv_bias[D:]])
    projected = low(low_back(matmul(token_rows, qkv_weight) + bias_full))
    heads_all = projected.reshape(group_size, LEN, 3, H, DH)
    queries = heads_all[:, :, 0]
    keys_all = heads_all[:, :, 1]
    values_all = heads_all[:, :, 2]
    scores = low_back(jnp.einsum('gqhd,gkhd->ghqk', queries, keys_all, precision=highest) * 0.125)
    softmax_weights = jax.nn.softmax(scores, axis=-1)
    dropped = low(softmax_weights * unpack_keep(attention_words))
    context = jnp.einsum('ghqk,gkhd->gqhd', dropped, values_all, precision=highest)
    context = low(low_back(context.reshape(group_size * LEN, D)))
    attended = low_back(matmul(context, out_weight) + out_bias)
    first_sum = token_rows + attended * unpack_keep(output_words).reshape(group_size * LEN, D)
    normed = layer_norm(first_sum, first_gain, first_shift)
    inner_sum = low_back(matmul(low(normed), up_weight) + up_bias)
    activated = low(jax.nn.gelu(inner_sum, approximate=False))
    outer_sum = low_back(matmul(activated, down_weight) + down_bias)
    second_sum = normed + outer_sum * unpack_keep(feed_words).reshape(group_size * LEN, D)
    return layer_norm(second_sum, second_gain, second_shift).reshape(group_size, LEN, D)

def reference(hidden_in, cotangent, attention_keep, output_keep, feed_keep, qkv_weight, qkv_bias, out_weight, out_bias, first_gain, first_shift, up_weight, up_bias, down_weight, down_bias, second_gain, second_shift):
    params = tuple((weight.astype(jnp.float32) for weight in (qkv_weight, qkv_bias, out_weight, out_bias, first_gain, first_shift, up_weight, up_bias, down_weight, down_bias, second_gain, second_shift)))
    group_size = math.gcd(SEQS, max(1, 4096 // LEN))
    block_count = MICRO * SEQS // group_size

    def blocked(array):
        return array.reshape((block_count, group_size) + array.shape[2:])

    def scan_step(totals, inputs):
        hidden, upstream, attention_words, output_words, feed_words = inputs

        def apply_layer(values, weights):
            return forward_block(values, weights, attention_words, output_words, feed_words)
        result, pullback = jax.vjp(apply_layer, hidden.astype(jnp.float32), params)
        grad_hidden, grad_params = pullback(upstream.astype(jnp.float32))
        totals = jax.tree.map(lambda before, added: before + added, totals, grad_params)
        return (totals, (result.astype(jnp.bfloat16), grad_hidden.astype(jnp.bfloat16)))
    zeros_start = tuple((jnp.zeros_like(weight) for weight in params))
    totals, (outputs, inputs_grad) = lax.scan(scan_step, zeros_start, (blocked(hidden_in), blocked(cotangent), blocked(attention_keep), blocked(output_keep), blocked(feed_keep)))
    return (outputs.reshape(hidden_in.shape), inputs_grad.reshape(hidden_in.shape), totals[0], totals[1], totals[2], totals[3], totals[4], totals[5], totals[6], totals[7], totals[8], totals[9], totals[10], totals[11])
```

```python
import functools

import jax
import jax.numpy as jnp
from jax import lax
from jax.experimental import pallas as pl
from jax.experimental.pallas import tpu as pltpu
from jax.sharding import Mesh
from jax.sharding import PartitionSpec as P

H = 12
MICRO = 2
epsilon = 1e-12
keep_scale = 8.0 / 7.0
root_half = 0.7071067811865476
inverse_root_tau = 0.3989422804014327
f32 = jnp.float32
bf16 = jnp.bfloat16
ANY = pl.BlockSpec(memory_space=pl.ANY)


def matmul(left_side, right_side):
    return jnp.dot(left_side, right_side, preferred_element_type=f32)


def matmul_t(left_side, right_side):
    return lax.dot_general(left_side, right_side, (((1,), (1,)), ((), ())), preferred_element_type=f32)


def t_matmul(left_side, right_side):
    return lax.dot_general(left_side, right_side, (((0,), (0,)), ((), ())), preferred_element_type=f32)


def pp(value, axis, step=1):
    size = lax.axis_size(axis)
    return lax.ppermute(value, axis, [(i, i ^ step) for i in range(size)])


def pick(value, axis, index):
    return lax.dynamic_index_in_dim(value, index, axis, keepdims=False)


def swap_if(flag, value, axis):
    low = lax.slice_in_dim(value, 0, 1, axis=axis)
    high = lax.slice_in_dim(value, 1, 2, axis=axis)
    return jnp.where(flag, lax.concatenate([high, low], axis), value)


def gather_z(shard):
    if lax.axis_size("z") != 4:
        return lax.all_gather(shard, "z", axis=0)
    z = lax.axis_index("z")
    parts = [shard] + [pp(shard, "z", k) for k in (1, 2, 3)]
    square = jnp.stack(parts).reshape((2, 2) + shard.shape)
    square = swap_if((z & 1) == 1, square, 1)
    square = swap_if((z & 2) == 2, square, 0)
    return square.reshape((4,) + shard.shape)


def gather_pieces(shard, order):
    own = gather_z(shard)
    across_x = pp(own, "x")
    across_y = pp(own, "y")
    if order == "xy":
        corner = pp(across_x, "y")
    else:
        corner = pp(across_y, "x")
    here = (own, across_x, across_y, corner)
    return here + tuple(pp(piece, "seq") for piece in here)


def assemble_body(plan, ids, *refs):
    pieces, outs, sem = refs[:8], refs[8:-1], refs[-1]
    copies = []
    for number, piece in enumerate(pieces):
        c = ids[0] ^ (number >> 2)
        y = ids[1] ^ ((number >> 1) & 1)
        x = ids[2] ^ (number & 1)
        for start, rows, out, column in plan:
            src = piece.at[:, pl.ds(start, rows), :]
            dst = outs[out].at[:, y, x, c, :, pl.ds(column, 768)]
            copies.append(pltpu.make_async_copy(src, dst, sem.at[len(copies)]))
    for copy in copies:
        copy.start()
    for copy in copies:
        copy.wait()


def assemble(pieces, plan, shapes):
    depth, height, width = pieces[0].shape
    if all(start % 8 == 0 and rows % 8 == 0 for start, rows, _, _ in plan):
        ids = jnp.stack([lax.axis_index("seq"), lax.axis_index("y"), lax.axis_index("x")]).astype(jnp.int32)
        return pl.pallas_call(
            functools.partial(assemble_body, plan),
            grid_spec=pltpu.PrefetchScalarGridSpec(
                num_scalar_prefetch=1,
                grid=(1,),
                in_specs=[ANY] * 8,
                out_specs=[pl.BlockSpec(memory_space=pltpu.VMEM)] * len(shapes),
                scratch_shapes=[pltpu.SemaphoreType.DMA((8 * len(plan),))],
            ),
            out_shape=[
                jax.ShapeDtypeStruct((depth, 2, 2, 2, rows, columns), bf16) for rows, columns in shapes
            ],
        )(ids, *pieces)
    whole = jnp.stack(pieces).reshape((2, 2, 2) + pieces[0].shape)
    whole = swap_if(lax.axis_index("seq") == 1, whole, 0)
    whole = swap_if(lax.axis_index("y") == 1, whole, 1)
    whole = swap_if(lax.axis_index("x") == 1, whole, 2)
    whole = whole.transpose(3, 1, 2, 0, 4, 5)
    outs = []
    for number in range(len(shapes)):
        chosen = [(column, start, rows) for start, rows, out, column in plan if out == number]
        outs.append(
            jnp.concatenate([whole[..., start : start + rows, :] for _, start, rows in sorted(chosen)], axis=-1)
        )
    return outs


def add_up(*terms):
    total = terms[0].astype(f32)
    for term in terms[1:]:
        total = total + term.astype(f32)
    return total


def reduce_core(partial):
    c = lax.axis_index("seq")
    received = pp(pick(partial, 3, 1 - c), "seq")
    return add_up(pick(partial, 3, c), received).astype(bf16)


def reduce_z(partial):
    if lax.axis_size("z") != 4:
        return lax.psum_scatter(partial, "z", scatter_dimension=0, tiled=False).astype(f32)
    z = lax.axis_index("z")
    received = [pp(pick(partial, 0, z ^ k), "z", k) for k in (1, 2, 3)]
    return add_up(pick(partial, 0, z), *received)


def reduce_scatter(partial, order):
    y, x = lax.axis_index("y"), lax.axis_index("x")
    partial = reduce_core(partial)
    if order == "xy":
        received = pp(pick(partial, 2, 1 - x), "x")
        partial = add_up(pick(partial, 2, x), received).astype(bf16)
        received = pp(pick(partial, 1, 1 - y), "y")
        partial = add_up(pick(partial, 1, y), received).astype(bf16)
    else:
        received = pp(pick(partial, 1, 1 - y), "y")
        partial = add_up(pick(partial, 1, y), received).astype(bf16)
        received = pp(pick(partial, 1, 1 - x), "x")
        partial = add_up(pick(partial, 1, x), received).astype(bf16)
    return reduce_z(partial)


def lane_half(shape):
    return lax.broadcasted_iota(jnp.int32, shape, len(shape) - 1) < 64


def join_keys(core, near, far, buffer):
    for i in range(4):
        buffer[pl.ds(pl.multiple_of(i * 128 + core * 64, 64), 64), :] = near[0, i * 64 : (i + 1) * 64, :]
        buffer[pl.ds(pl.multiple_of(i * 128 + (1 - core) * 64, 64), 64), :] = far[0, i * 64 : (i + 1) * 64, :]


def attention_body(ids, q, k_near, v_near, k_far, v_far, words, context, signed, keys, values):
    core = ids[0]
    join_keys(core, k_near, k_far, keys)
    join_keys(core, v_near, v_far, values)
    queries = q[0]
    left = lane_half(queries.shape)
    zero = jnp.zeros_like(queries)
    outs = []
    for h in range(2):
        masked = jnp.where(left if h == 0 else ~left, queries, zero) * 0.125
        scores = lax.dot_general(masked, keys[...], (((1,), (1,)), ((), ())), preferred_element_type=f32)
        blocks = [scores[:, i * 128 : (i + 1) * 128] for i in range(4)]
        peak = jnp.maximum(jnp.maximum(blocks[0], blocks[1]), jnp.maximum(blocks[2], blocks[3]))
        peak = jnp.max(peak, axis=1, keepdims=True)
        blocks = [jnp.exp(block - peak) for block in blocks]
        total = jnp.sum((blocks[0] + blocks[1]) + (blocks[2] + blocks[3]), axis=1, keepdims=True)
        scale = 1.0 / total
        word = words[0, 0, h]
        dropped = []
        for i in range(4):
            weight = blocks[i] * scale
            keep = (word & (7 << (3 * i))) != 0
            weight = jnp.where(keep, weight, -weight).astype(bf16)
            signed[0, 0, h, i] = weight
            dropped.append(jnp.maximum(weight, jnp.zeros_like(weight)))
        outs.append(
            jnp.dot(jnp.concatenate(dropped, axis=1), values[...], preferred_element_type=f32) * keep_scale
        )
    context[0] = jnp.where(left, outs[0], outs[1]).astype(bf16)


def attention(ids, queries, near, far, words):
    micro, tokens, width = queries.shape
    pairs = width // 128
    qkv = lambda offset: pl.BlockSpec((1, tokens, 128), lambda m, p, ids, offset=offset: (m, 0, p + offset))
    return pl.pallas_call(
        attention_body,
        grid_spec=pltpu.PrefetchScalarGridSpec(
            num_scalar_prefetch=1,
            grid=(micro, pairs),
            in_specs=[
                qkv(0),
                qkv(0),
                qkv(pairs),
                qkv(0),
                qkv(pairs),
                pl.BlockSpec((1, 1, 2, tokens, 128), lambda m, p, ids: (m, 0, p, 0, 0)),
            ],
            out_specs=[
                qkv(0),
                pl.BlockSpec((1, 1, 2, 4, tokens, 128), lambda m, p, ids: (m, p, 0, 0, 0, 0)),
            ],
            scratch_shapes=[pltpu.VMEM((512, 128), bf16), pltpu.VMEM((512, 128), bf16)],
        ),
        out_shape=[
            jax.ShapeDtypeStruct((micro, tokens, width), bf16),
            jax.ShapeDtypeStruct((micro, pairs, 2, 4, tokens, 128), bf16),
        ],
        cost_estimate=pl.CostEstimate(flops=4 * 10**9, bytes_accessed=12 * 10**6, transcendentals=3 * 10**6),
        name="attention",
    )(ids, queries, near, near, far, far, words)


def attention_back_body(
    ids, q, k_near, v_near, k_far, v_far, signed, upstream, g_q, g_near, g_far, keys, values, sums
):
    core = ids[0]
    join_keys(core, k_near, k_far, keys)
    join_keys(core, v_near, v_far, values)
    queries = q[0]
    above = upstream[0]
    left = lane_half(queries.shape)
    left_long = lane_half((512, 128))
    zero = jnp.zeros_like(queries)
    grads = []
    for h in range(2):
        masked = jnp.where(left if h == 0 else ~left, above, zero)
        g_dropped = lax.dot_general(masked, values[...], (((1,), (1,)), ((), ())), preferred_element_type=f32)
        weights, kept, g_weights = [], [], []
        delta = None
        for i in range(4):
            both = signed[0, 0, h, i].astype(f32)
            weight = jnp.abs(both)
            g_weight = jnp.where(both > 0.0, g_dropped[:, i * 128 : (i + 1) * 128], 0.0)
            term = g_weight * weight
            delta = term if delta is None else delta + term
            weights.append(weight)
            g_weights.append(g_weight)
            kept.append(jnp.maximum(both, 0.0).astype(bf16))
        delta = jnp.sum(delta, axis=1, keepdims=True)
        g_scores = jnp.concatenate(
            [(weights[i] * (g_weights[i] - delta)).astype(bf16) for i in range(4)], axis=1
        )
        dropped = jnp.concatenate(kept, axis=1)
        grads.append(
            (
                jnp.dot(g_scores, keys[...], preferred_element_type=f32),
                t_matmul(g_scores, queries),
                t_matmul(dropped, above),
            )
        )
    g_q[0] = (jnp.where(left, grads[0][0], grads[1][0]) * (0.125 * keep_scale)).astype(bf16)
    for kind, factor in ((0, 0.125 * keep_scale), (1, keep_scale)):
        sums[...] = jnp.where(left_long, grads[0][kind + 1], grads[1][kind + 1]) * factor
        for i in range(4):
            g_near[0, kind, i * 64 : (i + 1) * 64, :] = sums[
                pl.ds(pl.multiple_of(i * 128 + core * 64, 64), 64), :
            ]
            g_far[0, kind, i * 64 : (i + 1) * 64, :] = sums[
                pl.ds(pl.multiple_of(i * 128 + (1 - core) * 64, 64), 64), :
            ].astype(bf16)


def attention_back(ids, queries, near, far, signed, upstream):
    micro, tokens, width = queries.shape
    pairs = width // 128
    qkv = lambda offset: pl.BlockSpec((1, tokens, 128), lambda m, p, ids, offset=offset: (m, 0, p + offset))
    both = pl.BlockSpec((1, 2, tokens, 128), lambda m, p, ids: (m, 0, 0, p))
    return pl.pallas_call(
        attention_back_body,
        grid_spec=pltpu.PrefetchScalarGridSpec(
            num_scalar_prefetch=1,
            grid=(micro, pairs),
            in_specs=[
                qkv(0),
                qkv(0),
                qkv(pairs),
                qkv(0),
                qkv(pairs),
                pl.BlockSpec((1, 1, 2, 4, tokens, 128), lambda m, p, ids: (m, p, 0, 0, 0, 0)),
                qkv(0),
            ],
            out_specs=[qkv(0), both, both],
            scratch_shapes=[
                pltpu.VMEM((512, 128), bf16),
                pltpu.VMEM((512, 128), bf16),
                pltpu.VMEM((512, 128), f32),
            ],
        ),
        out_shape=[
            jax.ShapeDtypeStruct((micro, tokens, width), bf16),
            jax.ShapeDtypeStruct((micro, 2, tokens, width), f32),
            jax.ShapeDtypeStruct((micro, 2, tokens, width), bf16),
        ],
        cost_estimate=pl.CostEstimate(flops=8 * 10**9, bytes_accessed=20 * 10**6, transcendentals=0),
        name="attention_back",
    )(ids, queries, near, near, far, far, signed, upstream)


def unpack_keep(packed_words):
    shifts = jnp.arange(4, dtype=jnp.int32) * 3
    nibble = jnp.right_shift(packed_words[..., None], shifts) & 7
    keep_value = (nibble >= 1).astype(f32) * keep_scale
    return keep_value.reshape(packed_words.shape[:-1] + (packed_words.shape[-1] * 4,))


def normalize(values, norm_gain, norm_shift):
    centred = values - jnp.mean(values, axis=-1, keepdims=True)
    inverse = lax.rsqrt(jnp.mean(centred * centred, axis=-1, keepdims=True) + epsilon)
    scaled = centred * inverse
    return (scaled * norm_gain + norm_shift, scaled, inverse)


def norm_back(upstream, scaled, inverse, norm_gain):
    weighted = upstream * norm_gain
    centre_term = jnp.mean(weighted, axis=-1, keepdims=True)
    slope_term = jnp.mean(weighted * scaled, axis=-1, keepdims=True)
    return inverse * (weighted - centre_term - scaled * slope_term)


def gelu_slope(inner_sum):
    normal_cdf = 0.5 * (1.0 + lax.erf(inner_sum * root_half))
    density = jnp.exp(-0.5 * inner_sum * inner_sum) * inverse_root_tau
    return normal_cdf + inner_sum * density


def local(
    hidden_in,
    cotangent,
    attention_keep,
    output_keep,
    feed_keep,
    qkv_weight,
    qkv_bias,
    out_weight,
    out_bias,
    first_gain,
    first_shift,
    up_weight,
    up_bias,
    down_weight,
    down_bias,
    second_gain,
    second_shift,
):
    micro, _, tokens, width = hidden_in.shape
    rows = micro * tokens
    own = qkv_weight.shape[0]
    depth = lax.axis_size("z")
    devices = depth * 8
    wide = up_weight.shape[1] // width
    ids = lax.axis_index("seq").astype(jnp.int32).reshape(1)

    bias_parts = (
        qkv_bias, out_bias, first_gain, first_shift, up_bias, down_bias, second_gain, second_shift
    )
    bias_row = jnp.concatenate(bias_parts)
    bias_block = jnp.zeros((8, width), bf16).at[0, : bias_row.shape[0]].set(bias_row)
    qkv_shard = jnp.concatenate([qkv_weight[:, i * width : (i + 1) * width] for i in range(3)] + [bias_block])
    up_shard = jnp.concatenate(
        [out_weight] + [up_weight[:, i * width : (i + 1) * width] for i in range(wide)]
    )
    qkv_pieces = gather_pieces(qkv_shard, "xy")
    up_pieces = gather_pieces(up_shard, "yx")
    down_pieces = gather_pieces(down_weight, "xy")

    q_w, k_w, v_w, bias_all = assemble(
        qkv_pieces,
        [(i * own, own, i, 0) for i in range(3)] + [(3 * own, 8, 3, 0)],
        [(own, width)] * 3 + [(8, width)],
    )
    out_w, up_w = assemble(
        up_pieces,
        [(0, own, 0, 0)] + [((i + 1) * own, own, 1, i * width) for i in range(wide)],
        [(own, width), (own, wide * width)],
    )
    (down_w,) = assemble(
        down_pieces, [(0, down_weight.shape[0], 0, 0)], [(down_weight.shape[0], width)]
    )
    q_w, k_w, v_w, out_w = (w.reshape(width, width) for w in (q_w, k_w, v_w, out_w))
    up_w = up_w.reshape(width, wide * width)
    down_w = down_w.reshape(wide * width, width)
    bias_all = bias_all.reshape(devices, 8, width)[:, 0]
    vectors, start = [], 0
    for part in bias_parts:
        vectors.append(bias_all[:, start : start + part.shape[0]].reshape(-1).astype(f32))
        start += part.shape[0]
    qkv_b, out_b, gain_one, shift_one, up_b, down_b, gain_two, shift_two = vectors

    hidden = hidden_in.reshape(rows, width)
    turned = hidden_in.reshape(micro, tokens // 4, 4, width).transpose(0, 2, 1, 3).reshape(rows, width)
    queries = (matmul(hidden, q_w) + qkv_b[:width]).astype(bf16).reshape(micro, tokens, width)
    keys = matmul(turned, k_w).astype(bf16)
    values = (matmul(turned, v_w) + qkv_b[width:]).astype(bf16)
    near = jnp.concatenate([keys, values], axis=1).reshape(micro, tokens, 2 * width)
    far = pp(near, "seq")
    context, signed = attention(ids, queries, near, far, attention_keep.reshape(micro, 1, H, tokens, -1))
    context = context.reshape(rows, width)

    attended = matmul(context, out_w) + out_b
    keep_output = unpack_keep(output_keep).reshape(rows, width)
    first_sum = hidden.astype(f32) + attended * keep_output
    normed, scaled_one, inverse_one = normalize(first_sum, gain_one, shift_one)
    normed_low = normed.astype(bf16)
    inner_sum = matmul(normed_low, up_w) + up_b
    activated = jax.nn.gelu(inner_sum, approximate=False).astype(bf16)
    outer_sum = matmul(activated, down_w) + down_b
    keep_feed = unpack_keep(feed_keep).reshape(rows, width)
    second_sum = normed + outer_sum * keep_feed
    result, scaled_two, inverse_two = normalize(second_sum, gain_two, shift_two)
    layer_out = result.astype(bf16).reshape(hidden_in.shape)

    upstream = cotangent.reshape(rows, width).astype(f32)
    g_second = norm_back(upstream, scaled_two, inverse_two, gain_two)
    grad_gain_two = jnp.sum(upstream * scaled_two, axis=0)
    grad_shift_two = jnp.sum(upstream, axis=0)
    g_outer = (g_second * keep_feed).astype(bf16)
    grad_down_b = jnp.sum(g_outer.astype(f32), axis=0)
    block = (depth, 2, 2, 2)
    grad_down = t_matmul(activated, g_outer).astype(bf16).reshape(block + (-1, width))
    grad_down = reduce_scatter(grad_down, "xy")
    g_inner = (matmul_t(g_outer, down_w) * gelu_slope(inner_sum)).astype(bf16)
    grad_up_b = jnp.sum(g_inner.astype(f32), axis=0)
    grad_up = t_matmul(normed_low, g_inner).astype(bf16)
    g_normed = g_second + matmul_t(g_inner, up_w)
    g_first = norm_back(g_normed, scaled_one, inverse_one, gain_one)
    grad_gain_one = jnp.sum(g_normed * scaled_one, axis=0)
    grad_shift_one = jnp.sum(g_normed, axis=0)
    g_attended = (g_first * keep_output).astype(bf16)
    grad_out_b = jnp.sum(g_attended.astype(f32), axis=0)
    grad_out = t_matmul(context, g_attended).astype(bf16)
    mid = jnp.concatenate(
        [grad_out.reshape(block + (own, width))]
        + [grad_up[:, i * width : (i + 1) * width].reshape(block + (own, width)) for i in range(wide)],
        axis=4,
    )
    mid = reduce_scatter(mid, "yx")
    grad_out = mid[:own]
    grad_up = jnp.concatenate([mid[(i + 1) * own : (i + 2) * own] for i in range(wide)], axis=1)

    g_context = matmul_t(g_attended, out_w).astype(bf16).reshape(micro, tokens, width)
    g_q, g_near, g_far = attention_back(ids, queries, near, far, signed, g_context)
    g_kv = (g_near + pp(g_far, "seq").astype(f32)).astype(bf16)
    g_q = g_q.reshape(rows, width)
    g_k = g_kv[:, 0].reshape(rows, width)
    g_v = g_kv[:, 1].reshape(rows, width)
    grad_qkv_b = jnp.concatenate([jnp.sum(g_q.astype(f32), axis=0), jnp.sum(g_v.astype(f32), axis=0)])
    bias_grads = (
        grad_qkv_b, grad_out_b, grad_gain_one, grad_shift_one, grad_up_b, grad_down_b, grad_gain_two, grad_shift_two
    )
    bias_rows = jnp.concatenate([g.reshape(devices, -1) for g in bias_grads], axis=1)
    high = bias_rows.astype(bf16)
    pair = jnp.stack([high, (bias_rows - high.astype(f32)).astype(bf16)], axis=1)
    pair = jnp.pad(pair, ((0, 0), (0, 6), (0, width - pair.shape[2])))
    last = jnp.concatenate(
        [t_matmul(hidden, g_q).astype(bf16).reshape(block + (own, width))]
        + [t_matmul(turned, g).astype(bf16).reshape(block + (own, width)) for g in (g_k, g_v)]
        + [pair.reshape(block + (8, width))],
        axis=4,
    )
    last = reduce_scatter(last, "xy")
    grad_qkv = jnp.concatenate([last[i * own : (i + 1) * own] for i in range(3)], axis=1)
    bias_sums = last[3 * own] + last[3 * own + 1]
    vector_grads, start = [], 0
    for part in bias_parts:
        vector_grads.append(bias_sums[start : start + part.shape[0]])
        start += part.shape[0]

    back = g_kv.reshape(micro, 2, 4, tokens // 4, width).transpose(0, 3, 2, 1, 4).reshape(rows, 2, width)
    grad_in = (
        g_first + matmul_t(g_q, q_w) + matmul_t(back[:, 0], k_w) + matmul_t(back[:, 1], v_w)
    ).astype(bf16).reshape(hidden_in.shape)
    return (
        layer_out,
        grad_in,
        grad_qkv,
        vector_grads[0],
        grad_out,
        vector_grads[1],
        vector_grads[2],
        vector_grads[3],
        grad_up,
        vector_grads[4],
        grad_down,
        vector_grads[5],
        vector_grads[6],
        vector_grads[7],
    )


def solution(mesh):
    groups, cores = mesh.devices.shape
    split = Mesh(mesh.devices.reshape(groups // 4, 2, 2, cores), ("z", "y", "x", "seq"))
    dp = ("z", "y", "x")
    every = ("z", "y", "x", "seq")
    tokens = P(None, dp, "seq", None)
    matrix = P(every, None)
    vector = P(every)
    params = (matrix, vector, matrix, vector, vector, vector, matrix, vector, matrix, vector, vector, vector)
    return jax.shard_map(
        local,
        mesh=split,
        in_specs=(tokens, tokens, P(None, dp, None, "seq", None), tokens, tokens) + params,
        out_specs=(tokens, tokens) + params,
        check_vma=False,
    )
```

```python
import functools

import jax
import jax.numpy as jnp
from jax import lax
from jax.experimental import pallas as pl
from jax.experimental.pallas import tpu as pltpu
from jax.sharding import Mesh
from jax.sharding import PartitionSpec as P

H = 12
epsilon = 1e-12
keep_scale = 8.0 / 7.0
root_half = 0.7071067811865476
inverse_root_tau = 0.3989422804014327
every = ("z", "y", "x", "seq")
f32 = jnp.float32
bf16 = jnp.bfloat16


def unpack_keep(packed_words):
    shifts = jnp.arange(4, dtype=jnp.int32) * 3
    nibble = jnp.right_shift(packed_words[..., None], shifts) & 7
    keep_value = (nibble >= 1).astype(jnp.float32) * keep_scale
    return keep_value.reshape(packed_words.shape[:-1] + (packed_words.shape[-1] * 4,))


def normalize(values, norm_gain, norm_shift):
    centred = values - jnp.mean(values, axis=-1, keepdims=True)
    inverse = lax.rsqrt(jnp.mean(centred * centred, axis=-1, keepdims=True) + epsilon)
    scaled = centred * inverse
    return (scaled * norm_gain + norm_shift, scaled, inverse)


def norm_back(upstream, scaled, inverse, norm_gain):
    weighted = upstream * norm_gain
    centre_term = jnp.mean(weighted, axis=-1, keepdims=True)
    slope_term = jnp.mean(weighted * scaled, axis=-1, keepdims=True)
    return inverse * (weighted - centre_term - scaled * slope_term)


def gelu_slope(inner_sum):
    normal_cdf = 0.5 * (1.0 + lax.erf(inner_sum * root_half))
    density = jnp.exp(-0.5 * inner_sum * inner_sum) * inverse_root_tau
    return normal_cdf + inner_sum * density


def matmul(left_side, right_side):
    return jnp.dot(left_side, right_side, preferred_element_type=jnp.float32)


def plain_local(
    hidden_in,
    cotangent,
    attention_keep,
    output_keep,
    feed_keep,
    qkv_weight,
    qkv_bias,
    out_weight,
    out_bias,
    first_gain,
    first_shift,
    up_weight,
    up_bias,
    down_weight,
    down_bias,
    second_gain,
    second_shift,
):
    model_width = hidden_in.shape[-1]
    sequence_count = hidden_in.shape[1]
    local_tokens = hidden_in.shape[2]
    token_rows = sequence_count * local_tokens
    head_count = H
    head_size = model_width // head_count
    held_params = (
        lax.all_gather(qkv_weight, every, axis=0, tiled=True),
        lax.all_gather(qkv_bias, every, axis=0, tiled=True),
        lax.all_gather(out_weight, every, axis=0, tiled=True),
        lax.all_gather(out_bias, every, axis=0, tiled=True),
        lax.all_gather(first_gain, every, axis=0, tiled=True),
        lax.all_gather(first_shift, every, axis=0, tiled=True),
        lax.all_gather(up_weight, every, axis=0, tiled=True),
        lax.all_gather(up_bias, every, axis=0, tiled=True),
        lax.all_gather(down_weight, every, axis=0, tiled=True),
        lax.all_gather(down_bias, every, axis=0, tiled=True),
        lax.all_gather(second_gain, every, axis=0, tiled=True),
        lax.all_gather(second_shift, every, axis=0, tiled=True),
    )
    totals = None
    outputs = []
    inputs_grad = []
    for micro_step in range(hidden_in.shape[0]):
        (
            full_qkv_w,
            full_qkv_b,
            full_out_w,
            full_out_b,
            full_gain_one,
            full_shift_one,
            full_up_w,
            full_up_b,
            full_down_w,
            full_down_b,
            full_gain_two,
            full_shift_two,
        ) = held_params
        rows_in = hidden_in[micro_step].reshape(token_rows, model_width)
        qkv_float = full_qkv_b.astype(jnp.float32)
        bias_full = jnp.concatenate(
            [
                qkv_float[:model_width],
                jnp.zeros((model_width,), jnp.float32),
                qkv_float[model_width:],
            ]
        )
        projected = (matmul(rows_in, full_qkv_w) + bias_full).astype(jnp.bfloat16)
        queries = projected[:, :model_width].reshape(
            sequence_count, local_tokens, head_count, head_size
        )
        keys_local = projected[:, model_width : 2 * model_width].reshape(
            sequence_count, local_tokens, model_width
        )
        values_local = projected[:, 2 * model_width :].reshape(
            sequence_count, local_tokens, model_width
        )
        keys_all, values_all = (
            lax.all_gather(keys_local, "seq", axis=1, tiled=True),
            lax.all_gather(values_local, "seq", axis=1, tiled=True),
        )
        keys_heads = keys_all.reshape(sequence_count, -1, head_count, head_size)
        values_heads = values_all.reshape(sequence_count, -1, head_count, head_size)
        scores = (
            jnp.einsum("sqhd,skhd->shqk", queries, keys_heads, preferred_element_type=jnp.float32)
            * 0.125
        )
        row_peak = jnp.max(scores, axis=-1, keepdims=True)
        exponent = jnp.exp(scores - row_peak)
        row_total = jnp.sum(exponent, axis=-1, keepdims=True)
        log_total = row_peak + jnp.log(row_total)
        softmax_weights = exponent / row_total
        keep_attention = unpack_keep(attention_keep[micro_step])
        dropped = (softmax_weights * keep_attention).astype(jnp.bfloat16)
        context = jnp.einsum(
            "shqk,skhd->sqhd", dropped, values_heads, preferred_element_type=jnp.float32
        )
        context = context.reshape(token_rows, model_width).astype(jnp.bfloat16)
        attended = matmul(context, full_out_w) + full_out_b.astype(jnp.float32)
        keep_output = unpack_keep(output_keep[micro_step]).reshape(token_rows, model_width)
        first_sum = rows_in.astype(jnp.float32) + attended * keep_output
        gain_one = full_gain_one.astype(jnp.float32)
        normed, scaled_one, inverse_one = normalize(
            first_sum, gain_one, full_shift_one.astype(jnp.float32)
        )
        normed_low = normed.astype(jnp.bfloat16)
        inner_sum = matmul(normed_low, full_up_w) + full_up_b.astype(jnp.float32)
        activated = jax.nn.gelu(inner_sum, approximate=False).astype(jnp.bfloat16)
        outer_sum = matmul(activated, full_down_w) + full_down_b.astype(jnp.float32)
        keep_feed = unpack_keep(feed_keep[micro_step]).reshape(token_rows, model_width)
        second_sum = normed + outer_sum * keep_feed
        gain_two = full_gain_two.astype(jnp.float32)
        result, scaled_two, inverse_two = normalize(
            second_sum, gain_two, full_shift_two.astype(jnp.float32)
        )
        outputs.append(
            result.astype(jnp.bfloat16).reshape(sequence_count, local_tokens, model_width)
        )
        (
            back_qkv_w,
            back_qkv_b,
            back_out_w,
            back_out_b,
            back_gain_one,
            back_shift_one,
            back_up_w,
            back_up_b,
            back_down_w,
            back_down_b,
            back_gain_two,
            back_shift_two,
        ) = held_params
        upstream = cotangent[micro_step].reshape(token_rows, model_width).astype(jnp.float32)
        g_second = norm_back(upstream, scaled_two, inverse_two, back_gain_two.astype(jnp.float32))
        grad_gain_two = jnp.sum(upstream * scaled_two, axis=0)
        grad_shift_two = jnp.sum(upstream, axis=0)
        g_outer = (g_second * keep_feed).astype(jnp.bfloat16)
        grad_down_b = jnp.sum(g_outer.astype(jnp.float32), axis=0)
        grad_down_w = matmul(activated.T, g_outer)
        g_inner = (matmul(g_outer, back_down_w.T) * gelu_slope(inner_sum)).astype(jnp.bfloat16)
        grad_up_b = jnp.sum(g_inner.astype(jnp.float32), axis=0)
        grad_up_w = matmul(normed_low.T, g_inner)
        g_normed = g_second + matmul(g_inner, back_up_w.T)
        g_first = norm_back(g_normed, scaled_one, inverse_one, back_gain_one.astype(jnp.float32))
        grad_gain_one = jnp.sum(g_normed * scaled_one, axis=0)
        grad_shift_one = jnp.sum(g_normed, axis=0)
        g_attended = (g_first * keep_output).astype(jnp.bfloat16)
        grad_out_b = jnp.sum(g_attended.astype(jnp.float32), axis=0)
        grad_out_w = matmul(context.T, g_attended)
        g_context = matmul(g_attended, back_out_w.T).astype(jnp.bfloat16)
        g_context = g_context.reshape(sequence_count, local_tokens, head_count, head_size)
        keys_again, values_again = (
            lax.all_gather(keys_local, "seq", axis=1, tiled=True),
            lax.all_gather(values_local, "seq", axis=1, tiled=True),
        )
        keys_heads = keys_again.reshape(sequence_count, -1, head_count, head_size)
        values_heads = values_again.reshape(sequence_count, -1, head_count, head_size)
        scores_again = (
            jnp.einsum("sqhd,skhd->shqk", queries, keys_heads, preferred_element_type=jnp.float32)
            * 0.125
        )
        weights_again = jnp.exp(scores_again - log_total)
        dropped_again = (weights_again * keep_attention).astype(jnp.bfloat16)
        g_values_all = jnp.einsum(
            "shqk,sqhd->skhd", dropped_again, g_context, preferred_element_type=jnp.float32
        )
        g_dropped = jnp.einsum(
            "sqhd,skhd->shqk", g_context, values_heads, preferred_element_type=jnp.float32
        )
        g_weights = g_dropped * keep_attention
        row_delta = jnp.sum(g_weights * weights_again, axis=-1, keepdims=True)
        g_scores = (weights_again * (g_weights - row_delta)).astype(jnp.bfloat16)
        g_queries = (
            jnp.einsum("shqk,skhd->sqhd", g_scores, keys_heads, preferred_element_type=jnp.float32)
            * 0.125
        )
        g_keys_all = (
            jnp.einsum("shqk,sqhd->skhd", g_scores, queries, preferred_element_type=jnp.float32)
            * 0.125
        )
        g_keys, g_values = (
            lax.psum_scatter(
                g_keys_all.reshape(sequence_count, -1, model_width).astype(jnp.bfloat16),
                "seq",
                scatter_dimension=1,
                tiled=True,
            ).astype(jnp.float32),
            lax.psum_scatter(
                g_values_all.reshape(sequence_count, -1, model_width).astype(jnp.bfloat16),
                "seq",
                scatter_dimension=1,
                tiled=True,
            ).astype(jnp.float32),
        )
        g_projected = jnp.concatenate(
            [
                g_queries.reshape(token_rows, model_width),
                g_keys.reshape(token_rows, model_width),
                g_values.reshape(token_rows, model_width),
            ],
            axis=1,
        ).astype(jnp.bfloat16)
        g_projected_float = g_projected.astype(jnp.float32)
        grad_qkv_b = jnp.concatenate(
            [
                jnp.sum(g_projected_float[:, :model_width], axis=0),
                jnp.sum(g_projected_float[:, 2 * model_width :], axis=0),
            ]
        )
        grad_qkv_w = matmul(rows_in.T, g_projected)
        input_grad = g_first + matmul(g_projected, back_qkv_w.T)
        inputs_grad.append(
            input_grad.astype(jnp.bfloat16).reshape(sequence_count, local_tokens, model_width)
        )
        grads_now = (
            grad_qkv_w,
            grad_qkv_b,
            grad_out_w,
            grad_out_b,
            grad_gain_one,
            grad_shift_one,
            grad_up_w,
            grad_up_b,
            grad_down_w,
            grad_down_b,
            grad_gain_two,
            grad_shift_two,
        )
        if totals is None:
            totals = grads_now
        else:
            totals = tuple((before + added for before, added in zip(totals, grads_now)))
    summed = (
        lax.psum_scatter(totals[0], every, scatter_dimension=0, tiled=True),
        lax.psum_scatter(totals[1], every, scatter_dimension=0, tiled=True),
        lax.psum_scatter(totals[2], every, scatter_dimension=0, tiled=True),
        lax.psum_scatter(totals[3], every, scatter_dimension=0, tiled=True),
        lax.psum_scatter(totals[4], every, scatter_dimension=0, tiled=True),
        lax.psum_scatter(totals[5], every, scatter_dimension=0, tiled=True),
        lax.psum_scatter(totals[6], every, scatter_dimension=0, tiled=True),
        lax.psum_scatter(totals[7], every, scatter_dimension=0, tiled=True),
        lax.psum_scatter(totals[8], every, scatter_dimension=0, tiled=True),
        lax.psum_scatter(totals[9], every, scatter_dimension=0, tiled=True),
        lax.psum_scatter(totals[10], every, scatter_dimension=0, tiled=True),
        lax.psum_scatter(totals[11], every, scatter_dimension=0, tiled=True),
    )
    return (
        jnp.stack(outputs, axis=0),
        jnp.stack(inputs_grad, axis=0),
        summed[0],
        summed[1],
        summed[2],
        summed[3],
        summed[4],
        summed[5],
        summed[6],
        summed[7],
        summed[8],
        summed[9],
        summed[10],
        summed[11],
    )


ANY = pl.BlockSpec(memory_space=pl.ANY)
WHOLE = pl.BlockSpec(memory_space=pltpu.VMEM)
MIB = 2**20


def dot_t(left_side, right_side):
    return lax.dot_general(left_side, right_side, (((1,), (1,)), ((), ())), preferred_element_type=f32)


def t_dot(left_side, right_side):
    return lax.dot_general(left_side, right_side, (((0,), (0,)), ((), ())), preferred_element_type=f32)


def iota(shape, axis):
    return lax.broadcasted_iota(jnp.int32, shape, axis)


def pp(value, axis, step=1):
    size = lax.axis_size(axis)
    return lax.ppermute(value, axis, [(i, i ^ step) for i in range(size)])


def pick(value, axis, index):
    return lax.dynamic_index_in_dim(value, index, axis, keepdims=False)


def swap_if(flag, value, axis):
    low = lax.slice_in_dim(value, 0, 1, axis=axis)
    high = lax.slice_in_dim(value, 1, 2, axis=axis)
    return jnp.where(flag, lax.concatenate([high, low], axis), value)


def after(value, *earlier):
    return lax.optimization_barrier((value,) + earlier)[0]


def hold(values, *earlier):
    return lax.optimization_barrier(tuple(values) + earlier)[: len(values)]


def gather_z(own, other):
    return jnp.stack([own, other])


def order_z(pair, received):
    z = lax.axis_index("z")
    square = jnp.stack([pair, received], axis=1)
    square = swap_if((z & 1) == 1, square, 1)
    square = swap_if((z & 2) == 2, square, 0)
    return square.reshape((4,) + pair.shape[1:])


def select_z(shard, received):
    z = lax.axis_index("z")
    square = jnp.stack([shard, *received]).reshape((2, 2) + shard.shape)
    square = swap_if((z & 1) == 1, square, 1)
    square = swap_if((z & 2) == 2, square, 0)
    return square.reshape((4,) + shard.shape)


def add_up(terms):
    total = terms[0].astype(f32)
    for term in terms[1:]:
        total = total + term.astype(f32)
    return total


class Weights:
    def __init__(self, pieces, plan, shapes):
        self.spans = [(number, first, array.shape[1]) for number, first, array in pieces]
        self.operands = [pltpu.with_memory_space_constraint(array, pltpu.HBM) for _, _, array in pieces]
        self.plan, self.shapes = plan, shapes
        self.specs = [pl.BlockSpec(memory_space=pltpu.HBM)] * len(pieces)
        self.scratch = [pltpu.VMEM((4, 2, 2, 2, rows, columns), bf16) for rows, columns in shapes]
        self.scratch.append(pltpu.SemaphoreType.DMA((8 * len(plan),)))

    def copies(self, ids, sources, places, sems):
        found = [[] for _ in self.shapes]
        count = 0
        for start, rows, out, row, column in self.plan:
            for (number, first, held), source in zip(self.spans, sources):
                if first <= start and start + rows <= first + held:
                    c = ids[0] ^ (number >> 2)
                    y = ids[1] ^ ((number >> 1) & 1)
                    x = ids[2] ^ (number & 1)
                    src = source.at[:, pl.ds(start - first, rows), :]
                    dst = places[out].at[:, y, x, c, pl.ds(row, rows), pl.ds(column, source.shape[2])]
                    found[out].append(pltpu.make_async_copy(src, dst, sems.at[count]))
                    count += 1
        return found

    def matrix(self, places, out):
        rows, columns = self.shapes[out]
        return places[out].reshape(32 * rows, columns)


def begin(copies):
    for group in copies:
        for copy in group:
            copy.start()


def finish(group):
    for copy in group:
        copy.wait()


def spread(block, row, count, per):
    values = block[:, : -(-per // 128) * 128]
    lanes = values.shape[1]
    select = (iota((lanes, count), 1) % per == iota((lanes, count), 0)).astype(bf16)
    wide = jnp.dot(values, select, preferred_element_type=f32)
    own = (iota(wide.shape, 1) // per) * 8 + row == iota(wide.shape, 0)
    return jnp.sum(jnp.where(own, wide, 0.0), axis=0, keepdims=True)


def unspread(vectors, pers, width):
    total = jnp.zeros((256, width), f32)
    for row, (vector, per) in enumerate(zip(vectors, pers)):
        count = vector.shape[1]
        lanes = -(-per // 128) * 128
        own = (iota((256, count), 1) // per) * 8 + row == iota((256, count), 0)
        wide = jnp.where(own, vector, 0.0).astype(bf16)
        select = (iota((count, lanes), 0) % per == iota((count, lanes), 1)).astype(bf16)
        narrow = jnp.dot(wide, select, preferred_element_type=f32)
        total = total + jnp.concatenate([narrow, jnp.zeros((256, width - lanes), f32)], axis=1)
    return total


def layer_norm(values):
    centred = values - jnp.mean(values, axis=-1, keepdims=True)
    inverse = lax.rsqrt(jnp.mean(centred * centred, axis=-1, keepdims=True) + epsilon)
    return centred * inverse, inverse


def turn_matrix(tokens):
    place = iota((tokens, tokens), 0)
    quarter = tokens // 4
    return (iota((tokens, tokens), 1) == 4 * (place % quarter) + place // quarter).astype(bf16)


def call(body, name, grid, operands, specs, outs, out_specs, scratch, room, load, aliases=None):
    return pl.pallas_call(
        body,
        grid_spec=pltpu.PrefetchScalarGridSpec(
            num_scalar_prefetch=1, grid=grid, in_specs=specs, out_specs=out_specs, scratch_shapes=scratch
        ),
        out_shape=outs,
        compiler_params=pltpu.CompilerParams(vmem_limit_bytes=room * MIB),
        cost_estimate=pl.CostEstimate(flops=1024, bytes_accessed=load * MIB, transcendentals=0),
        input_output_aliases=aliases or {},
        name=name,
    )(*operands)


def shaped(shape, dtype):
    return jax.ShapeDtypeStruct(shape, dtype)


def rows_spec(rows, columns):
    return pl.BlockSpec((rows, columns), lambda i, ids: (i, 0))


def fixed_spec(shape):
    return pl.BlockSpec(shape, lambda i, ids: (0,) * len(shape))


def prepare_body(ids, hidden, output_words, feed_words, turned, keep_output, keep_feed):
    tokens, width = hidden.shape
    turned[...] = jnp.dot(turn_matrix(tokens), hidden[...], preferred_element_type=f32).astype(bf16)
    quarter = width // 4
    for words, keep in ((output_words, keep_output), (feed_words, keep_feed)):
        packed = words[...]
        total = jnp.zeros((tokens, width), f32)
        for i in range(4):
            bit = ((packed & (7 << (3 * i))) != 0).astype(f32).astype(bf16)
            place = (iota((quarter, width), 1) == 4 * iota((quarter, width), 0) + i).astype(bf16)
            total = total + jnp.dot(bit, place, preferred_element_type=f32)
        keep[...] = total.astype(bf16)


def prepare(ids, hidden, output_words, feed_words, tokens):
    rows, width = hidden.shape
    wide, narrow = rows_spec(tokens, width), rows_spec(tokens, width // 4)
    return call(
        prepare_body,
        "prepare",
        (rows // tokens,),
        (ids, hidden, output_words, feed_words),
        [wide, narrow, narrow],
        [shaped((rows, width), bf16)] * 3,
        [wide] * 3,
        [],
        12,
        6,
    )


def project_body(weights, per, ids, *refs):
    count = len(weights.operands)
    sources, (hidden, turned, queries), rest = refs[:count], refs[count : count + 3], refs[count + 3 :]
    micro, tokens, width = queries.shape
    near, rest = rest[: 2 * micro], rest[2 * micro :]
    places, sems = rest[:-1], rest[-1]
    copies = weights.copies(ids, sources, places, sems)
    begin(copies)
    finish(copies[3])
    bias = spread(weights.matrix(places, 3)[...], 0, 2 * width, per)
    for n in range(3):
        finish(copies[n])
    for m in range(micro):
        natural, other = hidden[m * tokens : (m + 1) * tokens, :], turned[m * tokens : (m + 1) * tokens, :]
        q = jnp.dot(natural, weights.matrix(places, 0)[...], preferred_element_type=f32) + bias[:, :width]
        queries[m] = q.astype(bf16)
        k = jnp.dot(other, weights.matrix(places, 1)[...], preferred_element_type=f32)
        near[2 * m][...] = k.astype(bf16)
        v = jnp.dot(other, weights.matrix(places, 2)[...], preferred_element_type=f32) + bias[:, width:]
        near[2 * m + 1][...] = v.astype(bf16)


def project(ids, weights, hidden, turned, micro, per):
    rows, width = hidden.shape
    return call(
        functools.partial(project_body, weights, per),
        "project",
        (1,),
        (ids, *weights.operands, hidden, turned),
        weights.specs + [WHOLE] * 2,
        [shaped((micro, rows // micro, width), bf16)] + [shaped((rows // micro, width), bf16)] * (2 * micro),
        [WHOLE] * (1 + 2 * micro),
        weights.scratch,
        16,
        10,
    )


def lane_half(shape):
    return iota(shape, len(shape) - 1) < 64


def join_keys(core, near, far, buffer):
    quarter = near.shape[0] // 4
    for i in range(4):
        here = pl.multiple_of((2 * i + core) * quarter, quarter)
        there = pl.multiple_of((2 * i + 1 - core) * quarter, quarter)
        buffer[pl.ds(here, quarter), :] = near[i * quarter : (i + 1) * quarter, :]
        buffer[pl.ds(there, quarter), :] = far[i * quarter : (i + 1) * quarter, :]


def attention_body(ids, q, k_near, v_near, k_far, v_far, words, *refs):
    context, signed, keys, values = refs[-4:]
    core = ids[0]
    join_keys(core, k_near, k_far, keys)
    join_keys(core, v_near, v_far, values)
    queries = q[0]
    left = lane_half(queries.shape)
    zero = jnp.zeros_like(queries)
    outs = []
    for h in range(2):
        masked = jnp.where(left if h == 0 else ~left, queries, zero) * 0.125
        scores = dot_t(masked, keys[...])
        blocks = [scores[:, i * 128 : (i + 1) * 128] for i in range(4)]
        peak = jnp.maximum(jnp.maximum(blocks[0], blocks[1]), jnp.maximum(blocks[2], blocks[3]))
        peak = jnp.max(peak, axis=1, keepdims=True)
        blocks = [jnp.exp(block - peak) for block in blocks]
        total = jnp.sum((blocks[0] + blocks[1]) + (blocks[2] + blocks[3]), axis=1, keepdims=True)
        scale = 1.0 / total
        word = words[0, h]
        dropped = []
        for i in range(4):
            weight = blocks[i] * scale
            keep = (word & (7 << (3 * i))) != 0
            weight = jnp.where(keep, weight, -weight).astype(bf16)
            signed[0, 0, h, i] = weight
            dropped.append(jnp.maximum(weight, jnp.zeros_like(weight)))
        outs.append(
            jnp.dot(jnp.concatenate(dropped, axis=1), values[...], preferred_element_type=f32) * keep_scale
        )
    context[0] = jnp.where(left, outs[0], outs[1]).astype(bf16)


def attention(ids, m, queries, near, far, words, earlier=()):
    micro, tokens, width = queries.shape
    pairs = width // 128
    part = pl.BlockSpec((1, tokens, 128), lambda p, ids: (m, 0, p))
    flat = pl.BlockSpec((tokens, 128), lambda p, ids: (0, p))
    operands = (ids, queries, *near[2 * m : 2 * m + 2], *far[2 * m : 2 * m + 2], words)
    return call(
        attention_body,
        "attention",
        (pairs,),
        operands + tuple(earlier),
        [part] + [flat] * 4
        + [pl.BlockSpec((1, 2, tokens, 128), lambda p, ids: (m, p, 0, 0))]
        + [ANY] * len(earlier),
        [shaped((micro, tokens, width), bf16), shaped((micro, pairs, 2, 4, tokens, 128), bf16)],
        [part, pl.BlockSpec((1, 1, 2, 4, tokens, 128), lambda p, ids: (m, p, 0, 0, 0, 0))],
        [pltpu.VMEM((2 * tokens, 128), bf16)] * 2,
        8,
        14,
        {len(operands) + i: i for i in range(len(earlier))},
    )


def attention_back_body(ids, q, k_near, v_near, k_far, v_far, signed, upstream, *refs):
    g_q, g_near, g_far, keys, values, sums = refs[-6:]
    core = ids[0]
    join_keys(core, k_near, k_far, keys)
    join_keys(core, v_near, v_far, values)
    queries = q[0]
    above = upstream[...]
    left = lane_half(queries.shape)
    left_long = lane_half(keys.shape)
    zero = jnp.zeros_like(queries)
    grads = []
    for h in range(2):
        masked = jnp.where(left if h == 0 else ~left, above, zero)
        g_dropped = dot_t(masked, values[...])
        weights, kept, g_weights = [], [], []
        delta = None
        for i in range(4):
            both = signed[0, 0, h, i].astype(f32)
            weight = jnp.abs(both)
            g_weight = jnp.where(both > 0.0, g_dropped[:, i * 128 : (i + 1) * 128], 0.0)
            term = g_weight * weight
            delta = term if delta is None else delta + term
            weights.append(weight)
            g_weights.append(g_weight)
            kept.append(jnp.maximum(both, 0.0).astype(bf16))
        delta = jnp.sum(delta, axis=1, keepdims=True)
        g_scores = jnp.concatenate(
            [(weights[i] * (g_weights[i] - delta)).astype(bf16) for i in range(4)], axis=1
        )
        dropped = jnp.concatenate(kept, axis=1)
        grads.append(
            (
                jnp.dot(g_scores, keys[...], preferred_element_type=f32),
                t_dot(g_scores, queries),
                t_dot(dropped, above),
            )
        )
    g_q[0] = (jnp.where(left, grads[0][0], grads[1][0]) * (0.125 * keep_scale)).astype(bf16)
    quarter = keys.shape[0] // 8
    for kind, factor in ((0, 0.125 * keep_scale), (1, keep_scale)):
        sums[...] = jnp.where(left_long, grads[0][kind + 1], grads[1][kind + 1]) * factor
        for i in range(4):
            here = pl.multiple_of((2 * i + core) * quarter, quarter)
            there = pl.multiple_of((2 * i + 1 - core) * quarter, quarter)
            g_near[kind, 0, i * quarter : (i + 1) * quarter, :] = sums[pl.ds(here, quarter), :]
            g_far[kind, 0, i * quarter : (i + 1) * quarter, :] = sums[pl.ds(there, quarter), :].astype(bf16)


def attention_back(ids, m, queries, near, far, signed, upstream, earlier=()):
    micro, tokens, width = queries.shape
    pairs = width // 128
    part = pl.BlockSpec((1, tokens, 128), lambda p, ids: (m, 0, p))
    flat = pl.BlockSpec((tokens, 128), lambda p, ids: (0, p))
    both = pl.BlockSpec((2, 1, tokens, 128), lambda p, ids: (0, m, 0, p))
    operands = (ids, queries, *near[2 * m : 2 * m + 2], *far[2 * m : 2 * m + 2], signed, upstream)
    return call(
        attention_back_body,
        "attention_back",
        (pairs,),
        operands + tuple(earlier),
        [part] + [flat] * 4
        + [pl.BlockSpec((1, 1, 2, 4, tokens, 128), lambda p, ids: (m, p, 0, 0, 0, 0))]
        + [pl.BlockSpec((tokens, 128), lambda p, ids: (m, p))]
        + [ANY] * len(earlier),
        [
            shaped((micro, tokens, width), bf16),
            shaped((2, micro, tokens, width), f32),
            shaped((2, micro, tokens, width), bf16),
        ],
        [part, both, both],
        [pltpu.VMEM((2 * tokens, 128), bf16)] * 2 + [pltpu.VMEM((2 * tokens, 128), f32)],
        12,
        20,
        {len(operands) + i: i for i in range(len(earlier))},
    )


def up_body(weights, pers, ids, *refs):
    count = len(weights.operands)
    sources = refs[:count]
    context, hidden, keep, vectors, scaled, inverse, activated, slope = refs[count : count + 8]
    places, sems = refs[count + 8 : -1], refs[-1]
    copies = weights.copies(ids, sources, places, sems)
    width, wide = scaled.shape[1], activated.shape[1]

    @pl.when(pl.program_id(0) == 0)
    def _():
        begin([copies[0], copies[2], copies[1]])
        finish(copies[2])
        block = weights.matrix(places, 2)[...]
        for row, per in enumerate(pers):
            vectors[row : row + 1, : 32 * per] = spread(block, row, 32 * per, per)
        finish(copies[0])

    attended = jnp.dot(context[...], weights.matrix(places, 0)[...], preferred_element_type=f32)
    attended = attended + vectors[0:1, :width]
    first_sum = hidden[...].astype(f32) + attended * (keep[...].astype(f32) * keep_scale)
    normal, scale = layer_norm(first_sum)
    scaled[...] = normal
    inverse[...] = jnp.broadcast_to(scale, inverse.shape)
    low = (normal * vectors[1:2, :width] + vectors[2:3, :width]).astype(bf16)

    @pl.when(pl.program_id(0) == 0)
    def _():
        finish(copies[1])

    up = weights.matrix(places, 1)
    step = 512

    def part(n, carry):
        at = pl.ds(pl.multiple_of(n * step, step), step)
        inner = jnp.dot(low, up[:, at], preferred_element_type=f32) + vectors[3:4, at]
        cdf = 0.5 * (1.0 + lax.erf(inner * root_half))
        density = jnp.exp(-0.5 * inner * inner) * inverse_root_tau
        activated[:, at] = (inner * cdf).astype(bf16)
        slope[:, at] = (cdf + inner * density).astype(bf16)
        return carry

    lax.fori_loop(0, wide // step, part, 0)


def feed_up(ids, weights, pers, context, hidden, keep, tokens, wide):
    rows, width = hidden.shape
    narrow, broad = rows_spec(tokens, width), rows_spec(tokens, wide)
    return call(
        functools.partial(up_body, weights, pers),
        "feed_up",
        (rows // tokens,),
        (ids, *weights.operands, context, hidden, keep),
        weights.specs + [narrow] * 3,
        [
            shaped((8, wide), f32),
            shaped((rows, width), f32),
            shaped((rows, 128), f32),
            shaped((rows, wide), bf16),
            shaped((rows, wide), bf16),
        ],
        [fixed_spec((8, wide)), narrow, rows_spec(tokens, 128), broad, broad],
        weights.scratch,
        28,
        24,
    )


def hand_out(core, total, rows, own, send, first, at):
    def one(n, carry):
        here = pl.multiple_of((2 * n + core) * rows, 8)
        there = pl.multiple_of((2 * n + 1 - core) * rows, 8)
        own[first + n, at : at + rows, :] = total[pl.ds(here, rows), :].astype(bf16)
        send[first + n, at : at + rows, :] = total[pl.ds(there, rows), :].astype(bf16)
        return carry

    lax.fori_loop(0, total.shape[0] // (2 * rows), one, 0)


def down_body(weights, ids, *refs):
    count = len(weights.operands)
    sources = refs[:count]
    activated, slope, scaled, keep, cotangent, vectors = refs[count : count + 6]
    layer_out, g_second_out, g_inner, own, send, sums = refs[count + 6 : count + 12]
    places, (sems, total, g_outers) = refs[count + 12 : -3], refs[-3:]
    copies = weights.copies(ids, sources, places, sems)
    tokens, width = scaled.shape
    wide = activated.shape[1]
    first = pl.program_id(0) == 0
    mine = pl.ds(pl.multiple_of(pl.program_id(0) * tokens, tokens), tokens)

    @pl.when(first)
    def _():
        begin(copies)
        sums[...] = jnp.zeros_like(sums)
        finish(copies[0])

    down = weights.matrix(places, 0)
    outer = jnp.dot(activated[mine, :], down[...], preferred_element_type=f32) + vectors[4:5, :width]
    factor = keep[...].astype(f32) * keep_scale
    normed = scaled[...] * vectors[1:2, :width] + vectors[2:3, :width]
    normal, scale = layer_norm(normed + outer * factor)
    gain = vectors[5:6, :width]
    layer_out[...] = (normal * gain + vectors[6:7, :width]).astype(bf16)
    above = cotangent[...].astype(f32)
    weighted = above * gain
    g_second = scale * (
        weighted
        - jnp.mean(weighted, axis=-1, keepdims=True)
        - normal * jnp.mean(weighted * normal, axis=-1, keepdims=True)
    )
    g_second_out[...] = g_second
    g_outer = (g_second * factor).astype(bf16)
    g_outers[mine, :] = g_outer
    sums[0:1, :width] += jnp.sum(g_outer.astype(f32), axis=0, keepdims=True)
    sums[1:2, :width] += jnp.sum(above * normal, axis=0, keepdims=True)
    sums[2:3, :width] += jnp.sum(above, axis=0, keepdims=True)
    step = 512

    def part(n, carry):
        at = pl.ds(pl.multiple_of(n * step, step), step)
        g_in = (dot_t(g_outer, down[at, :]) * slope[:, at].astype(f32)).astype(bf16)
        g_inner[:, at] = g_in
        sums[3:4, at] += jnp.sum(g_in.astype(f32), axis=0, keepdims=True)
        return carry

    lax.fori_loop(0, wide // step, part, 0)

    @pl.when(pl.program_id(0) == pl.num_programs(0) - 1)
    def _():
        def grads(n, carry):
            at = pl.ds(pl.multiple_of(n * width, width), width)
            total[...] = t_dot(activated[:, at], g_outers[...])
            hand_out(ids[0], total, wide // 32, own, send, n * (16 * width // wide), 0)
            return carry

        lax.fori_loop(0, wide // width, grads, 0)


def feed_down(ids, weights, activated, slope, scaled, keep, cotangent, vectors, tokens):
    rows, width = scaled.shape
    wide = activated.shape[1]
    narrow, broad = rows_spec(tokens, width), rows_spec(tokens, wide)
    halves = (16, wide // 32, width)
    return call(
        functools.partial(down_body, weights),
        "feed_down",
        (rows // tokens,),
        (ids, *weights.operands, activated, slope, scaled, keep, cotangent, vectors),
        weights.specs + [WHOLE, broad, narrow, narrow, narrow, WHOLE],
        [
            shaped((rows, width), bf16),
            shaped((rows, width), f32),
            shaped((rows, wide), bf16),
            shaped(halves, bf16),
            shaped(halves, bf16),
            shaped((8, wide), f32),
        ],
        [narrow, narrow, broad, WHOLE, WHOLE, WHOLE],
        weights.scratch + [pltpu.VMEM((width, width), f32), pltpu.VMEM((rows, width), bf16)],
        40,
        36,
    )


def middle_body(weights, ids, *refs):
    count = len(weights.operands)
    sources = refs[:count]
    g_inner, g_second, scaled, inverse, keep, vectors = refs[count : count + 6]
    g_first_out, g_attended_out, g_context, sums = refs[count + 6 : count + 10]
    places, sems = refs[count + 10 : -1], refs[-1]
    copies = weights.copies(ids, sources, places, sems)
    width = scaled.shape[1]

    @pl.when(pl.program_id(0) == 0)
    def _():
        begin([copies[1], copies[0]])
        sums[...] = jnp.zeros_like(sums)
        finish(copies[1])
        finish(copies[0])

    normal = scaled[...]
    g_normed = g_second[...] + dot_t(g_inner[...], weights.matrix(places, 1)[...])
    weighted = g_normed * vectors[1:2, :width]
    g_first = inverse[:, 0:1] * (
        weighted
        - jnp.mean(weighted, axis=-1, keepdims=True)
        - normal * jnp.mean(weighted * normal, axis=-1, keepdims=True)
    )
    g_first_out[...] = g_first
    g_attended = (g_first * (keep[...].astype(f32) * keep_scale)).astype(bf16)
    g_attended_out[...] = g_attended
    sums[0:1, :] += jnp.sum(g_attended.astype(f32), axis=0, keepdims=True)
    sums[1:2, :] += jnp.sum(g_normed * normal, axis=0, keepdims=True)
    sums[2:3, :] += jnp.sum(g_normed, axis=0, keepdims=True)
    g_context[...] = dot_t(g_attended, weights.matrix(places, 0)[...]).astype(bf16)


def middle(ids, weights, g_inner, g_second, scaled, inverse, keep, vectors, tokens):
    rows, width = scaled.shape
    wide = g_inner.shape[1]
    narrow, broad = rows_spec(tokens, width), rows_spec(tokens, wide)
    return call(
        functools.partial(middle_body, weights),
        "middle",
        (rows // tokens,),
        (ids, *weights.operands, g_inner, g_second, scaled, inverse, keep, vectors),
        weights.specs + [broad, narrow, narrow, rows_spec(tokens, 128), narrow, WHOLE],
        [
            shaped((rows, width), f32),
            shaped((rows, width), bf16),
            shaped((rows, width), bf16),
            shaped((8, width), f32),
        ],
        [narrow, narrow, narrow, WHOLE],
        weights.scratch,
        24,
        14,
    )


def grads_body(pers, ids, g_inner, scaled, context, g_attended, vectors, sums, more, own, send, total, low, bias):
    n = pl.program_id(0)
    width = scaled.shape[1]
    rows = width // 32

    @pl.when(n == 0)
    def _():
        low[...] = (scaled[...] * vectors[1:2, :width] + vectors[2:3, :width]).astype(bf16)
        vector_sums = [more[i : i + 1, :] for i in range(3)]
        vector_sums += [sums[3:4, :]] + [sums[i : i + 1, :width] for i in range(3)]
        bias[...] = unspread(vector_sums, pers, width)
        hand_out(ids[0], bias, 8, own, send, 0, (1 + sums.shape[1] // width) * rows)
        total[...] = t_dot(context[...], g_attended[...])
        hand_out(ids[0], total, rows, own, send, 0, 0)

    total[...] = t_dot(low[...], g_inner[...])
    for block in range(sums.shape[1] // width):

        @pl.when(n == block)
        def _():
            hand_out(ids[0], total, rows, own, send, 0, (block + 1) * rows)


def middle_grads(ids, pers, g_inner, scaled, context, g_attended, vectors, sums, more):
    rows, width = scaled.shape
    wide = g_inner.shape[1]
    halves = (16, (width + wide) // 32 + 8, width)
    return call(
        functools.partial(grads_body, pers),
        "middle_grads",
        (wide // width,),
        (ids, g_inner, scaled, context, g_attended, vectors, sums, more),
        [pl.BlockSpec((rows, width), lambda i, ids: (0, i))] + [WHOLE] * 6,
        [shaped(halves, bf16), shaped(halves, bf16)],
        [WHOLE] * 2,
        [pltpu.VMEM((width, width), f32), pltpu.VMEM((rows, width), bf16), pltpu.VMEM((256, width), f32)],
        24,
        20,
    )


def inputs_body(per, ids, hidden, turned, g_q, g_near, g_far, own, send, g_keys, g_values, total, bias):
    rows, width = hidden.shape
    sums = []
    for n in range(3):
        if n == 0:
            grad = g_q[...].reshape(rows, width)
        else:
            grad = (g_near[n - 1] + g_far[n - 1].astype(f32)).astype(bf16).reshape(rows, width)
            (g_keys, g_values)[n - 1][...] = grad
        if n != 1:
            sums.append(jnp.sum(grad.astype(f32), axis=0, keepdims=True))
        left = hidden if n == 0 else turned
        for start in range(0, width, 256):
            total[start : start + 256, :] = t_dot(left[:, start : start + 256], grad)
        hand_out(ids[0], total, width // 32, own, send, 0, n * (width // 32))
    bias[...] = unspread([jnp.concatenate(sums, axis=1)], [per], width)
    hand_out(ids[0], bias, 8, own, send, 0, 3 * (width // 32))


def input_grads(ids, hidden, turned, g_q, g_near, g_far, per):
    rows, width = hidden.shape
    halves = (16, 3 * width // 32 + 8, width)
    return call(
        functools.partial(inputs_body, per),
        "input_grads",
        (1,),
        (ids, hidden, turned, g_q, g_near, g_far),
        [WHOLE] * 5,
        [shaped(halves, bf16)] * 2 + [shaped((rows, width), bf16)] * 2,
        [WHOLE] * 4,
        [pltpu.VMEM((width, width), f32), pltpu.VMEM((256, width), f32)],
        28,
        12,
    )


def last_body(weights, ids, *refs):
    count = len(weights.operands)
    sources = refs[:count]
    g_first, g_q, g_keys, g_values, out = refs[count : count + 5]
    places, sems = refs[count + 5 : -1], refs[-1]
    copies = weights.copies(ids, sources, places, sems)

    @pl.when(pl.program_id(0) == 0)
    def _():
        begin(copies)
        for group in copies:
            finish(group)

    turn = turn_matrix(g_q.shape[0])
    total = g_first[...] + dot_t(g_q[...], weights.matrix(places, 0)[...])
    total = total + dot_t(t_dot(turn, g_keys[...]).astype(bf16), weights.matrix(places, 1)[...])
    total = total + dot_t(t_dot(turn, g_values[...]).astype(bf16), weights.matrix(places, 2)[...])
    out[...] = total.astype(bf16)


def last(ids, weights, g_first, g_q, g_keys, g_values, tokens):
    rows, width = g_first.shape
    narrow = rows_spec(tokens, width)
    return call(
        functools.partial(last_body, weights),
        "input_back",
        (rows // tokens,),
        (ids, *weights.operands, g_first, g_q, g_keys, g_values),
        weights.specs + [narrow] * 4,
        [shaped((rows, width), bf16)],
        [narrow],
        weights.scratch,
        16,
        10,
    )[0]


def beside(shape, y, x):
    return pl.BlockSpec((4, 1, 1) + shape[3:], lambda i, ids: (0, ids[1] ^ y, ids[2] ^ x, 0, 0))


def corner_body(ids, one, two, low, high):
    cut = low.shape[1]
    low[...] = (one[:, 0, 0, :cut].astype(f32) + two[:, 0, 0, :cut].astype(f32)).astype(bf16)
    high[...] = (one[:, 0, 0, cut:].astype(f32) + two[:, 0, 0, cut:].astype(f32)).astype(bf16)


def reduce_corner(ids, terms, cut):
    _, _, _, rows, width = terms[0].shape
    return call(
        corner_body,
        "reduce_corner",
        (1,),
        (ids, *terms),
        [beside(terms[0].shape, 1, 1)] * 2,
        [shaped((4, cut, width), bf16), shaped((4, rows - cut, width), bf16)],
        [WHOLE] * 2,
        [],
        8,
        2,
    )


def sides_body(ids, one_y, two_y, one_x, two_x, low, high, to_y, to_x):
    cut = low.shape[1]
    to_y[:, :cut] = (
        one_y[:, 0, 0, :cut].astype(f32) + two_y[:, 0, 0, :cut].astype(f32) + low[...].astype(f32)
    ).astype(bf16)
    to_y[:, cut:] = (one_y[:, 0, 0, cut:].astype(f32) + two_y[:, 0, 0, cut:].astype(f32)).astype(bf16)
    to_x[:, :cut] = (one_x[:, 0, 0, :cut].astype(f32) + two_x[:, 0, 0, :cut].astype(f32)).astype(bf16)
    to_x[:, cut:] = (
        one_x[:, 0, 0, cut:].astype(f32) + two_x[:, 0, 0, cut:].astype(f32) + high[...].astype(f32)
    ).astype(bf16)


def reduce_sides(ids, terms, low, high):
    shape = terms[0].shape
    return call(
        sides_body,
        "reduce_sides",
        (1,),
        (ids, *terms, *terms, low, high),
        [beside(shape, 1, 0)] * 2 + [beside(shape, 0, 1)] * 2 + [WHOLE] * 2,
        [shaped((4,) + shape[3:], bf16)] * 2,
        [WHOLE] * 2,
        [],
        10,
        3,
    )


def depth_body(ids, one, two, from_y, from_x, near, middle, far, mine):
    for k, out in enumerate((mine, near, middle, far)):
        z = ids[3] ^ k
        total = one[z, 0, 0].astype(f32) + two[z, 0, 0].astype(f32)
        total = total + from_y[z].astype(f32) + from_x[z].astype(f32)
        out[...] = total.astype(out.dtype)


def reduce_depth(ids, terms, from_y, from_x):
    shape = terms[0].shape
    return call(
        depth_body,
        "reduce_depth",
        (1,),
        (ids, *terms, from_y, from_x),
        [beside(shape, 0, 0)] * 2 + [WHOLE] * 2,
        [shaped(shape[3:], bf16)] * 3 + [shaped(shape[3:], f32)],
        [WHOLE] * 4,
        [],
        10,
        3,
    )


def exchange_z(sends):
    return [pp(send, "z", k) for send, k in zip(sends, (1, 2, 3))]


def local(
    hidden_in,
    cotangent,
    attention_keep,
    output_keep,
    feed_keep,
    qkv_weight,
    qkv_bias,
    out_weight,
    out_bias,
    first_gain,
    first_shift,
    up_weight,
    up_bias,
    down_weight,
    down_bias,
    second_gain,
    second_shift,
):
    micro, _, tokens, width = hidden_in.shape
    rows = micro * tokens
    own = qkv_weight.shape[0]
    wide = up_weight.shape[1]
    blocks = wide // width
    c, y, x = lax.axis_index("seq"), lax.axis_index("y"), lax.axis_index("x")
    ids = jnp.stack([c, y, x, lax.axis_index("z")]).astype(jnp.int32)
    bias_parts = (out_bias, first_gain, first_shift, up_bias, down_bias, second_gain, second_shift)
    pers = [part.shape[0] for part in bias_parts]
    per = qkv_bias.shape[0]

    column = lambda weight, i: weight[:, i * width : (i + 1) * width]
    bias_rows = lambda parts: jnp.concatenate(
        [jnp.pad(part.reshape(1, -1), ((0, 0), (0, width - part.shape[0]))) for part in parts]
        + [jnp.zeros((8 - len(parts), width), bf16)]
    )
    square = (own, width)
    hidden = hidden_in.reshape(rows, width)

    shard_a = jnp.concatenate([column(qkv_weight, i) for i in range(3)] + [bias_rows((qkv_bias,))])
    own_a = select_z(shard_a, [pp(shard_a, "z", k) for k in (1, 2, 3)])
    x_a, y_a = pp(own_a, "x"), pp(own_a, "y")
    shard_b = jnp.concatenate(
        [out_weight] + [column(up_weight, i) for i in range(blocks)] + [bias_rows(bias_parts)]
    )
    shard_b = after(shard_b, own_a)
    far_b = pp(shard_b, "z", 2)
    x_a, y_a, far_b = hold((x_a, y_a, far_b))
    cut_a = 2 * own
    low_a, high_a = pp(x_a[:, :cut_a], "y"), pp(y_a[:, cut_a:], "x")
    pieces = [(0, 0, own_a), (1, 0, x_a), (2, 0, y_a), (3, 0, low_a), (3, cut_a, high_a)]
    pieces += [(number + 4, first, pp(piece, "seq")) for number, first, piece in pieces]
    pair_b = gather_z(shard_b, far_b)
    near_b = pp(pair_b, "z", 1)
    turned, keep_output, keep_feed = prepare(
        ids, after(hidden, far_b), output_keep.reshape(rows, -1), feed_keep.reshape(rows, -1), tokens
    )
    plan = [(i * own, own, i, 0, 0) for i in range(3)]
    weights = Weights(pieces, plan + [(3 * own, 8, 3, 0, 0)], [square] * 3 + [(8, width)])
    weights_again = Weights(pieces, plan, [square] * 3)
    queries, *near = project(ids, weights, hidden, turned, micro, per)
    far = [pp(value, "seq") for value in near]
    own_b = order_z(pair_b, after(near_b, *near))
    x_b, y_b = pp(own_b, "x"), pp(own_b, "y")
    shard_c = after(down_weight, own_b)
    far_c = pp(shard_c, "z", 2)
    words = attention_keep.reshape(micro, H, tokens, -1)
    far[0], far[1], far_c = hold((far[0], far[1], far_c), own_b)
    pair_c = gather_z(shard_c, far_c)
    near_c = pp(pair_c, "z", 1)
    context, signed = attention(ids, 0, queries, near, far, words)
    far[2], far[3] = hold((far[2], far[3]), context)
    context, signed = attention(ids, 1, queries, near, far, words, (context, signed))
    own_b, x_b, y_b, near_c = hold((own_b, x_b, y_b, near_c), context)
    cut_b = 3 * own
    low_b, high_b = pp(x_b[:, :cut_b], "y"), pp(y_b[:, cut_b:], "x")
    pieces = [(0, 0, own_b), (1, 0, x_b), (2, 0, y_b)]
    pieces += [(number + 4, first, pp(piece, "seq")) for number, first, piece in pieces]
    pieces += [(3, 0, low_b), (3, cut_b, high_b), (7, 0, pp(low_b, "seq")), (7, cut_b, pp(high_b, "seq"))]
    plan = [(0, own, 0, 0, 0)] + [((i + 1) * own, own, 1, 0, i * width) for i in range(blocks)]
    weights = Weights(
        pieces, plan + [((blocks + 1) * own, 8, 2, 0, 0)], [square, (own, wide), (8, width)]
    )
    back_weights = Weights(pieces, plan, [square, (own, wide)])
    own_c = order_z(pair_c, hold((near_c,), low_b, high_b)[0])
    x_c, y_c = pp(own_c, "x"), pp(own_c, "y")
    context = context.reshape(rows, width)
    vectors, scaled, inverse, activated, slope = feed_up(
        ids, weights, pers, context, hidden, keep_output, tokens, wide
    )
    x_c, y_c = hold((x_c, y_c), activated)
    down_rows = down_weight.shape[0]
    cut_c = down_rows // 2
    low_c, high_c = pp(x_c[:, :cut_c], "y"), pp(y_c[:, cut_c:], "x")
    pieces = [(0, 0, own_c), (1, 0, x_c), (2, 0, y_c), (3, 0, low_c), (3, cut_c, high_c)]
    pieces += [(number + 4, first, pp(piece, "seq")) for number, first, piece in pieces]
    weights = Weights(
        pieces, [(0, cut_c, 0, 0, 0), (cut_c, cut_c, 0, cut_c, 0)], [(down_rows, width)]
    )
    layer_out, g_second, g_inner, down_own, down_send, sums = feed_down(
        ids, weights, activated, slope, scaled, keep_feed, cotangent.reshape(rows, width), vectors, tokens
    )

    unit = lambda value: value.reshape((4, 2, 2) + value.shape[1:])
    down_core = pp(down_send, "seq")
    g_first, g_attended, g_context, more = middle(
        ids, back_weights, g_inner, g_second, scaled, inverse, keep_output, vectors, tokens
    )
    down = [unit(down_own), unit(after(down_core, g_context))]
    corner = reduce_corner(ids, down, cut_c)
    low, high = pp(corner[0], "x"), pp(corner[1], "y")
    mid_own, mid_send = middle_grads(
        ids, pers, g_inner, scaled, context, after(g_attended, *corner), vectors, sums, more
    )
    low, high = hold((low, high), mid_send)
    to_y, to_x = reduce_sides(ids, down, low, high)
    down_y, down_x = pp(to_y, "y"), pp(to_x, "x")
    mid_core = pp(after(mid_send, low, high), "seq")
    grads = attention_back(ids, 0, queries, near, far, signed, after(g_context, to_y, to_x))
    mid = [unit(mid_own), unit(after(mid_core, *grads))]
    corner = reduce_corner(ids, mid, cut_b)
    low, high = pp(corner[0], "x"), pp(corner[1], "y")
    g_q, g_near, g_far = attention_back(
        ids, 1, queries, near, far, signed, after(g_context, *corner), tuple(grads)
    )
    low, high, down_y, down_x = hold((low, high, down_y, down_x), g_q)
    far_grads = pp(after(g_far, low, high, down_y, down_x), "seq")
    to_y, to_x = reduce_sides(ids, mid, low, high)
    mid_y, mid_x = pp(to_y, "y"), pp(to_x, "x")
    *sends, down_mine = reduce_depth(ids, down, down_y, down_x)
    down_z = exchange_z(sends)
    a_own, a_send, g_keys, g_values = input_grads(
        ids, hidden, turned, g_q, g_near, after(far_grads, to_y, to_x, *sends), per
    )
    grad_in = last(ids, weights_again, g_first, g_q.reshape(rows, width), g_keys, g_values, tokens)
    mid_y, mid_x = hold((mid_y, mid_x), grad_in)
    core_sums = pp(after(a_send, mid_y, mid_x), "seq")
    part = [unit(a_own), unit(core_sums)]
    corner = reduce_corner(ids, part, cut_a)
    low, high = pp(corner[0], "x"), pp(corner[1], "y")
    *sends, mid_mine = reduce_depth(ids, mid, after(mid_y, *corner), mid_x)
    mid_z = exchange_z(sends)
    grad_down = add_up([down_mine, *hold(down_z, *sends)])
    low, high = hold((low, high), grad_down)
    to_y, to_x = reduce_sides(ids, part, low, high)
    side_y, side_x = pp(to_y, "y"), pp(to_x, "x")
    mid = add_up([mid_mine, *hold(mid_z, to_y, to_x)])
    side_y, side_x = hold((side_y, side_x), mid)
    *sends, part_mine = reduce_depth(ids, part, side_y, side_x)
    part = add_up([part_mine, *exchange_z(sends)])

    stripe = lambda value, i: value[i * own : (i + 1) * own]
    grad_qkv = jnp.concatenate([stripe(part, i) for i in range(3)], axis=1)
    grad_up = jnp.concatenate([stripe(mid, i + 1) for i in range(blocks)], axis=1)
    vector_grads = [mid[(blocks + 1) * own + i, :length] for i, length in enumerate(pers)]
    return (
        layer_out.reshape(hidden_in.shape),
        grad_in.reshape(hidden_in.shape),
        grad_qkv,
        part[3 * own, :per],
        stripe(mid, 0),
        vector_grads[0],
        vector_grads[1],
        vector_grads[2],
        grad_up,
        vector_grads[3],
        grad_down,
        vector_grads[4],
        vector_grads[5],
        vector_grads[6],
    )


def solution(mesh):
    groups, cores = mesh.devices.shape
    split = Mesh(mesh.devices.reshape(groups // 4, 2, 2, cores), ("z", "y", "x", "seq"))
    dp = ("z", "y", "x")
    token_rows = P(None, dp, "seq", None)
    matrix = P(every, None)
    vector = P(every)
    params = (matrix, vector, matrix, vector, vector, vector, matrix, vector, matrix, vector, vector, vector)

    def layer(*arrays):
        tiled = groups == 16 and cores == 2 and arrays[5].shape[0] % 8 == 0
        return (local if tiled else plain_local)(*arrays)

    return jax.shard_map(
        layer,
        mesh=split,
        in_specs=(token_rows, token_rows, P(None, dp, None, "seq", None), token_rows, token_rows) + params,
        out_specs=(token_rows, token_rows) + params,
        check_vma=False,
    )
```

```python
import functools

import jax
import jax.numpy as jnp
from jax import lax
from jax.experimental import pallas as pl
from jax.experimental.pallas import tpu as pltpu
from jax.sharding import Mesh
from jax.sharding import PartitionSpec as P

H = 12
epsilon = 1e-12
keep_scale = 8.0 / 7.0
root_half = 0.7071067811865476
inverse_root_tau = 0.3989422804014327
every = ("z", "y", "x", "seq")
f32 = jnp.float32
bf16 = jnp.bfloat16


def unpack_keep(packed_words):
    shifts = jnp.arange(4, dtype=jnp.int32) * 3
    nibble = jnp.right_shift(packed_words[..., None], shifts) & 7
    keep_value = (nibble >= 1).astype(jnp.float32) * keep_scale
    return keep_value.reshape(packed_words.shape[:-1] + (packed_words.shape[-1] * 4,))


def normalize(values, norm_gain, norm_shift):
    centred = values - jnp.mean(values, axis=-1, keepdims=True)
    inverse = lax.rsqrt(jnp.mean(centred * centred, axis=-1, keepdims=True) + epsilon)
    scaled = centred * inverse
    return (scaled * norm_gain + norm_shift, scaled, inverse)


def norm_back(upstream, scaled, inverse, norm_gain):
    weighted = upstream * norm_gain
    centre_term = jnp.mean(weighted, axis=-1, keepdims=True)
    slope_term = jnp.mean(weighted * scaled, axis=-1, keepdims=True)
    return inverse * (weighted - centre_term - scaled * slope_term)


def gelu_slope(inner_sum):
    normal_cdf = 0.5 * (1.0 + lax.erf(inner_sum * root_half))
    density = jnp.exp(-0.5 * inner_sum * inner_sum) * inverse_root_tau
    return normal_cdf + inner_sum * density


def matmul(left_side, right_side):
    return jnp.dot(left_side, right_side, preferred_element_type=jnp.float32)


def plain_local(
    hidden_in,
    cotangent,
    attention_keep,
    output_keep,
    feed_keep,
    qkv_weight,
    qkv_bias,
    out_weight,
    out_bias,
    first_gain,
    first_shift,
    up_weight,
    up_bias,
    down_weight,
    down_bias,
    second_gain,
    second_shift,
):
    model_width = hidden_in.shape[-1]
    sequence_count = hidden_in.shape[1]
    local_tokens = hidden_in.shape[2]
    token_rows = sequence_count * local_tokens
    head_count = H
    head_size = model_width // head_count
    held_params = (
        lax.all_gather(qkv_weight, every, axis=0, tiled=True),
        lax.all_gather(qkv_bias, every, axis=0, tiled=True),
        lax.all_gather(out_weight, every, axis=0, tiled=True),
        lax.all_gather(out_bias, every, axis=0, tiled=True),
        lax.all_gather(first_gain, every, axis=0, tiled=True),
        lax.all_gather(first_shift, every, axis=0, tiled=True),
        lax.all_gather(up_weight, every, axis=0, tiled=True),
        lax.all_gather(up_bias, every, axis=0, tiled=True),
        lax.all_gather(down_weight, every, axis=0, tiled=True),
        lax.all_gather(down_bias, every, axis=0, tiled=True),
        lax.all_gather(second_gain, every, axis=0, tiled=True),
        lax.all_gather(second_shift, every, axis=0, tiled=True),
    )
    totals = None
    outputs = []
    inputs_grad = []
    for micro_step in range(hidden_in.shape[0]):
        (
            full_qkv_w,
            full_qkv_b,
            full_out_w,
            full_out_b,
            full_gain_one,
            full_shift_one,
            full_up_w,
            full_up_b,
            full_down_w,
            full_down_b,
            full_gain_two,
            full_shift_two,
        ) = held_params
        rows_in = hidden_in[micro_step].reshape(token_rows, model_width)
        qkv_float = full_qkv_b.astype(jnp.float32)
        bias_full = jnp.concatenate(
            [
                qkv_float[:model_width],
                jnp.zeros((model_width,), jnp.float32),
                qkv_float[model_width:],
            ]
        )
        projected = (matmul(rows_in, full_qkv_w) + bias_full).astype(jnp.bfloat16)
        queries = projected[:, :model_width].reshape(
            sequence_count, local_tokens, head_count, head_size
        )
        keys_local = projected[:, model_width : 2 * model_width].reshape(
            sequence_count, local_tokens, model_width
        )
        values_local = projected[:, 2 * model_width :].reshape(
            sequence_count, local_tokens, model_width
        )
        keys_all, values_all = (
            lax.all_gather(keys_local, "seq", axis=1, tiled=True),
            lax.all_gather(values_local, "seq", axis=1, tiled=True),
        )
        keys_heads = keys_all.reshape(sequence_count, -1, head_count, head_size)
        values_heads = values_all.reshape(sequence_count, -1, head_count, head_size)
        scores = (
            jnp.einsum("sqhd,skhd->shqk", queries, keys_heads, preferred_element_type=jnp.float32)
            * 0.125
        )
        row_peak = jnp.max(scores, axis=-1, keepdims=True)
        exponent = jnp.exp(scores - row_peak)
        row_total = jnp.sum(exponent, axis=-1, keepdims=True)
        log_total = row_peak + jnp.log(row_total)
        softmax_weights = exponent / row_total
        keep_attention = unpack_keep(attention_keep[micro_step])
        dropped = (softmax_weights * keep_attention).astype(jnp.bfloat16)
        context = jnp.einsum(
            "shqk,skhd->sqhd", dropped, values_heads, preferred_element_type=jnp.float32
        )
        context = context.reshape(token_rows, model_width).astype(jnp.bfloat16)
        attended = matmul(context, full_out_w) + full_out_b.astype(jnp.float32)
        keep_output = unpack_keep(output_keep[micro_step]).reshape(token_rows, model_width)
        first_sum = rows_in.astype(jnp.float32) + attended * keep_output
        gain_one = full_gain_one.astype(jnp.float32)
        normed, scaled_one, inverse_one = normalize(
            first_sum, gain_one, full_shift_one.astype(jnp.float32)
        )
        normed_low = normed.astype(jnp.bfloat16)
        inner_sum = matmul(normed_low, full_up_w) + full_up_b.astype(jnp.float32)
        activated = jax.nn.gelu(inner_sum, approximate=False).astype(jnp.bfloat16)
        outer_sum = matmul(activated, full_down_w) + full_down_b.astype(jnp.float32)
        keep_feed = unpack_keep(feed_keep[micro_step]).reshape(token_rows, model_width)
        second_sum = normed + outer_sum * keep_feed
        gain_two = full_gain_two.astype(jnp.float32)
        result, scaled_two, inverse_two = normalize(
            second_sum, gain_two, full_shift_two.astype(jnp.float32)
        )
        outputs.append(
            result.astype(jnp.bfloat16).reshape(sequence_count, local_tokens, model_width)
        )
        (
            back_qkv_w,
            back_qkv_b,
            back_out_w,
            back_out_b,
            back_gain_one,
            back_shift_one,
            back_up_w,
            back_up_b,
            back_down_w,
            back_down_b,
            back_gain_two,
            back_shift_two,
        ) = held_params
        upstream = cotangent[micro_step].reshape(token_rows, model_width).astype(jnp.float32)
        g_second = norm_back(upstream, scaled_two, inverse_two, back_gain_two.astype(jnp.float32))
        grad_gain_two = jnp.sum(upstream * scaled_two, axis=0)
        grad_shift_two = jnp.sum(upstream, axis=0)
        g_outer = (g_second * keep_feed).astype(jnp.bfloat16)
        grad_down_b = jnp.sum(g_outer.astype(jnp.float32), axis=0)
        grad_down_w = matmul(activated.T, g_outer)
        g_inner = (matmul(g_outer, back_down_w.T) * gelu_slope(inner_sum)).astype(jnp.bfloat16)
        grad_up_b = jnp.sum(g_inner.astype(jnp.float32), axis=0)
        grad_up_w = matmul(normed_low.T, g_inner)
        g_normed = g_second + matmul(g_inner, back_up_w.T)
        g_first = norm_back(g_normed, scaled_one, inverse_one, back_gain_one.astype(jnp.float32))
        grad_gain_one = jnp.sum(g_normed * scaled_one, axis=0)
        grad_shift_one = jnp.sum(g_normed, axis=0)
        g_attended = (g_first * keep_output).astype(jnp.bfloat16)
        grad_out_b = jnp.sum(g_attended.astype(jnp.float32), axis=0)
        grad_out_w = matmul(context.T, g_attended)
        g_context = matmul(g_attended, back_out_w.T).astype(jnp.bfloat16)
        g_context = g_context.reshape(sequence_count, local_tokens, head_count, head_size)
        keys_again, values_again = (
            lax.all_gather(keys_local, "seq", axis=1, tiled=True),
            lax.all_gather(values_local, "seq", axis=1, tiled=True),
        )
        keys_heads = keys_again.reshape(sequence_count, -1, head_count, head_size)
        values_heads = values_again.reshape(sequence_count, -1, head_count, head_size)
        scores_again = (
            jnp.einsum("sqhd,skhd->shqk", queries, keys_heads, preferred_element_type=jnp.float32)
            * 0.125
        )
        weights_again = jnp.exp(scores_again - log_total)
        dropped_again = (weights_again * keep_attention).astype(jnp.bfloat16)
        g_values_all = jnp.einsum(
            "shqk,sqhd->skhd", dropped_again, g_context, preferred_element_type=jnp.float32
        )
        g_dropped = jnp.einsum(
            "sqhd,skhd->shqk", g_context, values_heads, preferred_element_type=jnp.float32
        )
        g_weights = g_dropped * keep_attention
        row_delta = jnp.sum(g_weights * weights_again, axis=-1, keepdims=True)
        g_scores = (weights_again * (g_weights - row_delta)).astype(jnp.bfloat16)
        g_queries = (
            jnp.einsum("shqk,skhd->sqhd", g_scores, keys_heads, preferred_element_type=jnp.float32)
            * 0.125
        )
        g_keys_all = (
            jnp.einsum("shqk,sqhd->skhd", g_scores, queries, preferred_element_type=jnp.float32)
            * 0.125
        )
        g_keys, g_values = (
            lax.psum_scatter(
                g_keys_all.reshape(sequence_count, -1, model_width).astype(jnp.bfloat16),
                "seq",
                scatter_dimension=1,
                tiled=True,
            ).astype(jnp.float32),
            lax.psum_scatter(
                g_values_all.reshape(sequence_count, -1, model_width).astype(jnp.bfloat16),
                "seq",
                scatter_dimension=1,
                tiled=True,
            ).astype(jnp.float32),
        )
        g_projected = jnp.concatenate(
            [
                g_queries.reshape(token_rows, model_width),
                g_keys.reshape(token_rows, model_width),
                g_values.reshape(token_rows, model_width),
            ],
            axis=1,
        ).astype(jnp.bfloat16)
        g_projected_float = g_projected.astype(jnp.float32)
        grad_qkv_b = jnp.concatenate(
            [
                jnp.sum(g_projected_float[:, :model_width], axis=0),
                jnp.sum(g_projected_float[:, 2 * model_width :], axis=0),
            ]
        )
        grad_qkv_w = matmul(rows_in.T, g_projected)
        input_grad = g_first + matmul(g_projected, back_qkv_w.T)
        inputs_grad.append(
            input_grad.astype(jnp.bfloat16).reshape(sequence_count, local_tokens, model_width)
        )
        grads_now = (
            grad_qkv_w,
            grad_qkv_b,
            grad_out_w,
            grad_out_b,
            grad_gain_one,
            grad_shift_one,
            grad_up_w,
            grad_up_b,
            grad_down_w,
            grad_down_b,
            grad_gain_two,
            grad_shift_two,
        )
        if totals is None:
            totals = grads_now
        else:
            totals = tuple((before + added for before, added in zip(totals, grads_now)))
    summed = (
        lax.psum_scatter(totals[0], every, scatter_dimension=0, tiled=True),
        lax.psum_scatter(totals[1], every, scatter_dimension=0, tiled=True),
        lax.psum_scatter(totals[2], every, scatter_dimension=0, tiled=True),
        lax.psum_scatter(totals[3], every, scatter_dimension=0, tiled=True),
        lax.psum_scatter(totals[4], every, scatter_dimension=0, tiled=True),
        lax.psum_scatter(totals[5], every, scatter_dimension=0, tiled=True),
        lax.psum_scatter(totals[6], every, scatter_dimension=0, tiled=True),
        lax.psum_scatter(totals[7], every, scatter_dimension=0, tiled=True),
        lax.psum_scatter(totals[8], every, scatter_dimension=0, tiled=True),
        lax.psum_scatter(totals[9], every, scatter_dimension=0, tiled=True),
        lax.psum_scatter(totals[10], every, scatter_dimension=0, tiled=True),
        lax.psum_scatter(totals[11], every, scatter_dimension=0, tiled=True),
    )
    return (
        jnp.stack(outputs, axis=0),
        jnp.stack(inputs_grad, axis=0),
        summed[0],
        summed[1],
        summed[2],
        summed[3],
        summed[4],
        summed[5],
        summed[6],
        summed[7],
        summed[8],
        summed[9],
        summed[10],
        summed[11],
    )


ANY = pl.BlockSpec(memory_space=pl.ANY)
WHOLE = pl.BlockSpec(memory_space=pltpu.VMEM)
MIB = 2**20
PARTS = (2, 1)


def dot_t(left_side, right_side):
    return lax.dot_general(left_side, right_side, (((1,), (1,)), ((), ())), preferred_element_type=f32)


def t_dot(left_side, right_side):
    return lax.dot_general(left_side, right_side, (((0,), (0,)), ((), ())), preferred_element_type=f32)


def iota(shape, axis):
    return lax.broadcasted_iota(jnp.int32, shape, axis)


def pp(value, axis, step=1):
    size = lax.axis_size(axis)
    return lax.ppermute(value, axis, [(i, i ^ step) for i in range(size)])


def pick(value, axis, index):
    return lax.dynamic_index_in_dim(value, index, axis, keepdims=False)


def swap_if(flag, value, axis):
    low = lax.slice_in_dim(value, 0, 1, axis=axis)
    high = lax.slice_in_dim(value, 1, 2, axis=axis)
    return jnp.where(flag, lax.concatenate([high, low], axis), value)


def after(value, *earlier):
    return lax.optimization_barrier((value,) + earlier)[0]


def hold(values, *earlier):
    return lax.optimization_barrier(tuple(values) + earlier)[: len(values)]


def select_z(shard, received):
    z = lax.axis_index("z")
    square = jnp.stack([shard, *received]).reshape((2, 2) + shard.shape)
    square = swap_if((z & 1) == 1, square, 1)
    square = swap_if((z & 2) == 2, square, 0)
    return square.reshape((4,) + shard.shape)


def add_up(terms):
    total = terms[0].astype(f32)
    for term in terms[1:]:
        total = total + term.astype(f32)
    return total


def divide(plan, cut):
    parts = []
    for start, rows, out, row, column in plan:
        ends = [start, cut, start + rows] if start < cut < start + rows else [start, start + rows]
        for first, last in zip(ends, ends[1:]):
            parts.append((first, last - first, out, row + first - start, column))
    return parts


class Weights:
    def __init__(self, pieces, plan, shapes):
        self.spans = [(number, first, array.shape[1]) for number, first, array in pieces]
        self.operands = [pltpu.with_memory_space_constraint(array, pltpu.HBM) for _, _, array in pieces]
        self.plan, self.shapes = plan, shapes
        self.specs = [pl.BlockSpec(memory_space=pltpu.HBM)] * len(pieces)
        self.scratch = [pltpu.VMEM((4, 2, 2, 2, rows, columns), bf16) for rows, columns in shapes]
        self.scratch.append(pltpu.SemaphoreType.DMA((8 * len(plan),)))

    def copies(self, ids, sources, places, sems):
        found = [[] for _ in self.shapes]
        count = 0
        for start, rows, out, row, column in self.plan:
            for (number, first, held), source in zip(self.spans, sources):
                if first <= start and start + rows <= first + held:
                    c = ids[0] ^ (number >> 2)
                    y = ids[1] ^ ((number >> 1) & 1)
                    x = ids[2] ^ (number & 1)
                    src = source.at[:, pl.ds(start - first, rows), :]
                    dst = places[out].at[:, y, x, c, pl.ds(row, rows), pl.ds(column, source.shape[2])]
                    found[out].append(pltpu.make_async_copy(src, dst, sems.at[count]))
                    count += 1
        return found

    def matrix(self, places, out):
        rows, columns = self.shapes[out]
        return places[out].reshape(32 * rows, columns)


def begin(copies):
    for group in copies:
        for copy in group:
            copy.start()


def finish(group):
    for copy in group:
        copy.wait()


def spread(block, row, count, per):
    values = block[:, : -(-per // 128) * 128]
    lanes = values.shape[1]
    select = (iota((lanes, count), 1) % per == iota((lanes, count), 0)).astype(bf16)
    wide = jnp.dot(values, select, preferred_element_type=f32)
    own = (iota(wide.shape, 1) // per) * 8 + row == iota(wide.shape, 0)
    return jnp.sum(jnp.where(own, wide, 0.0), axis=0, keepdims=True)


def unspread(vectors, pers, width):
    total = jnp.zeros((256, width), f32)
    for row, (vector, per) in enumerate(zip(vectors, pers)):
        count = vector.shape[1]
        lanes = -(-per // 128) * 128
        own = (iota((256, count), 1) // per) * 8 + row == iota((256, count), 0)
        wide = jnp.where(own, vector, 0.0).astype(bf16)
        select = (iota((count, lanes), 0) % per == iota((count, lanes), 1)).astype(bf16)
        narrow = jnp.dot(wide, select, preferred_element_type=f32)
        total = total + jnp.concatenate([narrow, jnp.zeros((256, width - lanes), f32)], axis=1)
    return total


def layer_norm(values):
    centred = values - jnp.mean(values, axis=-1, keepdims=True)
    inverse = lax.rsqrt(jnp.mean(centred * centred, axis=-1, keepdims=True) + epsilon)
    return centred * inverse, inverse


def turn_matrix(tokens):
    place = iota((tokens, tokens), 0)
    quarter = tokens // 4
    return (iota((tokens, tokens), 1) == 4 * (place % quarter) + place // quarter).astype(bf16)


def call(body, name, grid, operands, specs, outs, out_specs, scratch, room, load, aliases=None):
    return pl.pallas_call(
        body,
        grid_spec=pltpu.PrefetchScalarGridSpec(
            num_scalar_prefetch=1, grid=grid, in_specs=specs, out_specs=out_specs, scratch_shapes=scratch
        ),
        out_shape=outs,
        compiler_params=pltpu.CompilerParams(vmem_limit_bytes=room * MIB),
        cost_estimate=pl.CostEstimate(flops=1024, bytes_accessed=load * MIB, transcendentals=0),
        input_output_aliases=aliases or {},
        name=name,
    )(*operands)


def shaped(shape, dtype):
    return jax.ShapeDtypeStruct(shape, dtype)


def rows_spec(rows, columns):
    return pl.BlockSpec((rows, columns), lambda i, ids: (i, 0))


def fixed_spec(shape):
    return pl.BlockSpec(shape, lambda i, ids: (0,) * len(shape))


def prepare_body(ids, hidden, output_words, feed_words, turned, keep_output, keep_feed):
    tokens, width = hidden.shape
    turned[...] = jnp.dot(turn_matrix(tokens), hidden[...], preferred_element_type=f32).astype(bf16)
    quarter = width // 4
    for words, keep in ((output_words, keep_output), (feed_words, keep_feed)):
        packed = words[0, 0]
        total = jnp.zeros((tokens, width), f32)
        for i in range(4):
            bit = ((packed & (7 << (3 * i))) != 0).astype(f32).astype(bf16)
            place = (iota((quarter, width), 1) == 4 * iota((quarter, width), 0) + i).astype(bf16)
            total = total + t_dot(bit, place)
        keep[...] = total.astype(bf16)


def prepare(ids, hidden, output_words, feed_words, tokens):
    rows, width = hidden.shape
    wide = rows_spec(tokens, width)
    narrow = pl.BlockSpec((1, 1, width // 4, tokens), lambda i, ids: (i, 0, 0, 0))
    return call(
        prepare_body,
        "prepare",
        (rows // tokens,),
        (ids, hidden, output_words, feed_words),
        [wide, narrow, narrow],
        [shaped((rows, width), bf16)] * 3,
        [wide] * 3,
        [],
        12,
        6,
    )


def project_body(weights, per, ids, *refs):
    count = len(weights.operands)
    sources, (hidden, turned, queries), rest = refs[:count], refs[count : count + 3], refs[count + 3 :]
    micro, tokens, width = queries.shape
    places, sems = rest[len(rest) - 1 - len(weights.shapes) : -1], rest[-1]
    near = iter(rest[: len(rest) - 1 - len(weights.shapes)])
    copies = weights.copies(ids, sources, places, sems)
    begin(copies)
    finish(copies[3])
    bias = spread(weights.matrix(places, 3)[...], 0, 2 * width, per)
    for n in range(3):
        finish(copies[n])
    for m in range(micro):
        natural, other = hidden[m * tokens : (m + 1) * tokens, :], turned[m * tokens : (m + 1) * tokens, :]
        q = jnp.dot(natural, weights.matrix(places, 0)[...], preferred_element_type=f32) + bias[:, :width]
        queries[m] = q.astype(bf16)
        k = jnp.dot(other, weights.matrix(places, 1)[...], preferred_element_type=f32).astype(bf16)
        v = jnp.dot(other, weights.matrix(places, 2)[...], preferred_element_type=f32) + bias[:, width:]
        for value in (k, v.astype(bf16)):
            rows = tokens // PARTS[m]
            for part in range(PARTS[m]):
                next(near)[...] = value[part * rows : (part + 1) * rows]


def project(ids, weights, hidden, turned, micro, per):
    rows, width = hidden.shape
    return call(
        functools.partial(project_body, weights, per),
        "project",
        (1,),
        (ids, *weights.operands, hidden, turned),
        weights.specs + [WHOLE] * 2,
        [shaped((micro, rows // micro, width), bf16)]
        + [shaped((rows // micro // PARTS[m], width), bf16) for m in range(micro) for _ in range(2 * PARTS[m])],
        [WHOLE] * (1 + 2 * sum(PARTS)),
        weights.scratch,
        16,
        10,
    )


def lane_half(shape):
    return iota(shape, len(shape) - 1) < 64


def join_keys(core, near, far, buffer):
    quarter = buffer.shape[0] // 8
    parts = len(near)
    for i in range(4):
        here = pl.multiple_of((2 * i + core) * quarter, quarter)
        there = pl.multiple_of((2 * i + 1 - core) * quarter, quarter)
        at = (i * parts % 4) // parts * quarter
        buffer[pl.ds(here, quarter), :] = near[i * parts // 4][at : at + quarter, :]
        buffer[pl.ds(there, quarter), :] = far[i * parts // 4][at : at + quarter, :]


def attention_body(parts, ids, q, *refs):
    ours, words = refs[: 4 * parts], refs[4 * parts]
    context, signed, keys, values = refs[-4:]
    core = ids[0]
    join_keys(core, ours[:parts], ours[2 * parts : 3 * parts], keys)
    join_keys(core, ours[parts : 2 * parts], ours[3 * parts :], values)
    queries = q[0]
    left = lane_half(queries.shape)
    zero = jnp.zeros_like(queries)
    outs = []
    for h in range(2):
        masked = jnp.where(left if h == 0 else ~left, queries, zero) * 0.125
        scores = dot_t(masked, keys[...])
        blocks = [scores[:, i * 128 : (i + 1) * 128] for i in range(4)]
        peak = jnp.maximum(jnp.maximum(blocks[0], blocks[1]), jnp.maximum(blocks[2], blocks[3]))
        peak = jnp.max(peak, axis=1, keepdims=True)
        blocks = [jnp.exp(block - peak) for block in blocks]
        total = jnp.sum((blocks[0] + blocks[1]) + (blocks[2] + blocks[3]), axis=1, keepdims=True)
        scale = 1.0 / total
        word = words[0, h]
        dropped = []
        for i in range(4):
            weight = blocks[i] * scale
            keep = (word & (7 << (3 * i))) != 0
            weight = jnp.where(keep, weight, -weight).astype(bf16)
            signed[0, 0, h, i] = weight
            dropped.append(jnp.maximum(weight, jnp.zeros_like(weight)))
        outs.append(
            jnp.dot(jnp.concatenate(dropped, axis=1), values[...], preferred_element_type=f32) * keep_scale
        )
    context[0] = jnp.where(left, outs[0], outs[1]).astype(bf16)


def attention(ids, m, queries, near, far, words, earlier=()):
    micro, tokens, width = queries.shape
    pairs = width // 128
    part = pl.BlockSpec((1, tokens, 128), lambda p, ids: (m, 0, p))
    flat = pl.BlockSpec((tokens // PARTS[m], 128), lambda p, ids: (0, p))
    operands = (ids, queries, *near[m], *far[m], words)
    return call(
        functools.partial(attention_body, PARTS[m]),
        "attention",
        (pairs,),
        operands + tuple(earlier),
        [part] + [flat] * (4 * PARTS[m])
        + [pl.BlockSpec((1, 2, tokens, 128), lambda p, ids: (m, p, 0, 0))]
        + [ANY] * len(earlier),
        [shaped((micro, tokens, width), bf16), shaped((micro, pairs, 2, 4, tokens, 128), bf16)],
        [part, pl.BlockSpec((1, 1, 2, 4, tokens, 128), lambda p, ids: (m, p, 0, 0, 0, 0))],
        [pltpu.VMEM((2 * tokens, 128), bf16)] * 2,
        8,
        14,
        {len(operands) + i: i for i in range(len(earlier))},
    )


def attention_back_body(parts, ids, q, *refs):
    ours, signed, upstream = refs[: 4 * parts], refs[4 * parts], refs[4 * parts + 1]
    g_q, g_near, g_far, keys, values, sums = refs[-6:]
    core = ids[0]
    join_keys(core, ours[:parts], ours[2 * parts : 3 * parts], keys)
    join_keys(core, ours[parts : 2 * parts], ours[3 * parts :], values)
    queries = q[0]
    above = upstream[...]
    left = lane_half(queries.shape)
    left_long = lane_half(keys.shape)
    zero = jnp.zeros_like(queries)
    grads = []
    for h in range(2):
        masked = jnp.where(left if h == 0 else ~left, above, zero)
        g_dropped = dot_t(masked, values[...])
        weights, kept, g_weights = [], [], []
        delta = None
        for i in range(4):
            both = signed[0, 0, h, i].astype(f32)
            weight = jnp.abs(both)
            g_weight = jnp.where(both > 0.0, g_dropped[:, i * 128 : (i + 1) * 128], 0.0)
            term = g_weight * weight
            delta = term if delta is None else delta + term
            weights.append(weight)
            g_weights.append(g_weight)
            kept.append(jnp.maximum(both, 0.0).astype(bf16))
        delta = jnp.sum(delta, axis=1, keepdims=True)
        g_scores = jnp.concatenate(
            [(weights[i] * (g_weights[i] - delta)).astype(bf16) for i in range(4)], axis=1
        )
        dropped = jnp.concatenate(kept, axis=1)
        grads.append(
            (
                jnp.dot(g_scores, keys[...], preferred_element_type=f32),
                t_dot(g_scores, queries),
                t_dot(dropped, above),
            )
        )
    g_q[0] = (jnp.where(left, grads[0][0], grads[1][0]) * (0.125 * keep_scale)).astype(bf16)
    quarter = keys.shape[0] // 8
    for kind, factor in ((0, 0.125 * keep_scale), (1, keep_scale)):
        sums[...] = jnp.where(left_long, grads[0][kind + 1], grads[1][kind + 1]) * factor
        for i in range(4):
            here = pl.multiple_of((2 * i + core) * quarter, quarter)
            there = pl.multiple_of((2 * i + 1 - core) * quarter, quarter)
            g_near[kind, 0, i * quarter : (i + 1) * quarter, :] = sums[pl.ds(here, quarter), :]
            g_far[kind, 0, i * quarter : (i + 1) * quarter, :] = sums[pl.ds(there, quarter), :].astype(bf16)


def attention_back(ids, m, queries, near, far, signed, upstream, earlier=()):
    micro, tokens, width = queries.shape
    pairs = width // 128
    part = pl.BlockSpec((1, tokens, 128), lambda p, ids: (m, 0, p))
    flat = pl.BlockSpec((tokens // PARTS[m], 128), lambda p, ids: (0, p))
    both = pl.BlockSpec((2, 1, tokens, 128), lambda p, ids: (0, m, 0, p))
    operands = (ids, queries, *near[m], *far[m], signed, upstream)
    return call(
        functools.partial(attention_back_body, PARTS[m]),
        "attention_back",
        (pairs,),
        operands + tuple(earlier),
        [part] + [flat] * (4 * PARTS[m])
        + [pl.BlockSpec((1, 1, 2, 4, tokens, 128), lambda p, ids: (m, p, 0, 0, 0, 0))]
        + [pl.BlockSpec((tokens, 128), lambda p, ids: (m, p))]
        + [ANY] * len(earlier),
        [
            shaped((micro, tokens, width), bf16),
            shaped((2, micro, tokens, width), f32),
            shaped((2, micro, tokens, width), bf16),
        ],
        [part, both, both],
        [pltpu.VMEM((2 * tokens, 128), bf16)] * 2 + [pltpu.VMEM((2 * tokens, 128), f32)],
        12,
        20,
        {len(operands) + i: i for i in range(len(earlier))},
    )


def up_body(weights, pers, ids, *refs):
    count = len(weights.operands)
    sources = refs[:count]
    context, hidden, keep, vectors, scaled, inverse, activated, slope = refs[count : count + 8]
    places, sems = refs[count + 8 : -1], refs[-1]
    copies = weights.copies(ids, sources, places, sems)
    width, wide = scaled.shape[1], activated.shape[1]

    @pl.when(pl.program_id(0) == 0)
    def _():
        begin([copies[0], copies[2], copies[1]])
        finish(copies[2])
        block = weights.matrix(places, 2)[...]
        for row, per in enumerate(pers):
            vectors[row : row + 1, : 32 * per] = spread(block, row, 32 * per, per)
        finish(copies[0])

    attended = jnp.dot(context[...], weights.matrix(places, 0)[...], preferred_element_type=f32)
    attended = attended + vectors[0:1, :width]
    first_sum = hidden[...].astype(f32) + attended * (keep[...].astype(f32) * keep_scale)
    normal, scale = layer_norm(first_sum)
    scaled[...] = normal
    inverse[...] = jnp.broadcast_to(scale, inverse.shape)
    low = (normal * vectors[1:2, :width] + vectors[2:3, :width]).astype(bf16)

    @pl.when(pl.program_id(0) == 0)
    def _():
        finish(copies[1])

    up = weights.matrix(places, 1)
    step = 512

    def part(n, carry):
        at = pl.ds(pl.multiple_of(n * step, step), step)
        inner = jnp.dot(low, up[:, at], preferred_element_type=f32) + vectors[3:4, at]
        cdf = 0.5 * (1.0 + lax.erf(inner * root_half))
        density = jnp.exp(-0.5 * inner * inner) * inverse_root_tau
        activated[:, at] = (inner * cdf).astype(bf16)
        slope[:, at] = (cdf + inner * density).astype(bf16)
        return carry

    lax.fori_loop(0, wide // step, part, 0)


def feed_up(ids, weights, pers, context, hidden, keep, tokens, wide):
    rows, width = hidden.shape
    narrow, broad = rows_spec(tokens, width), rows_spec(tokens, wide)
    return call(
        functools.partial(up_body, weights, pers),
        "feed_up",
        (rows // tokens,),
        (ids, *weights.operands, context, hidden, keep),
        weights.specs + [narrow] * 3,
        [
            shaped((8, wide), f32),
            shaped((rows, width), f32),
            shaped((rows, 128), f32),
            shaped((rows, wide), bf16),
            shaped((rows, wide), bf16),
        ],
        [fixed_spec((8, wide)), narrow, rows_spec(tokens, 128), broad, broad],
        weights.scratch,
        28,
        24,
    )


def hand_out(core, total, rows, own, send, first, at):
    def one(n, carry):
        here = pl.multiple_of((2 * n + core) * rows, 8)
        there = pl.multiple_of((2 * n + 1 - core) * rows, 8)
        own[first + n, at : at + rows, :] = total[pl.ds(here, rows), :].astype(bf16)
        send[first + n, at : at + rows, :] = total[pl.ds(there, rows), :].astype(bf16)
        return carry

    lax.fori_loop(0, total.shape[0] // (2 * rows), one, 0)


def down_body(weights, ids, *refs):
    count = len(weights.operands)
    sources = refs[:count]
    activated, slope, scaled, keep, cotangent, vectors = refs[count : count + 6]
    layer_out, g_second_out, g_inner, own, send, sums = refs[count + 6 : count + 12]
    places, (sems, total, g_outers) = refs[count + 12 : -3], refs[-3:]
    copies = weights.copies(ids, sources, places, sems)
    tokens, width = scaled.shape
    wide = activated.shape[1]
    first = pl.program_id(0) == 0
    mine = pl.ds(pl.multiple_of(pl.program_id(0) * tokens, tokens), tokens)

    @pl.when(first)
    def _():
        begin(copies)
        sums[...] = jnp.zeros_like(sums)
        finish(copies[0])

    down = weights.matrix(places, 0)
    outer = jnp.dot(activated[mine, :], down[...], preferred_element_type=f32) + vectors[4:5, :width]
    factor = keep[...].astype(f32) * keep_scale
    normed = scaled[...] * vectors[1:2, :width] + vectors[2:3, :width]
    normal, scale = layer_norm(normed + outer * factor)
    gain = vectors[5:6, :width]
    layer_out[...] = (normal * gain + vectors[6:7, :width]).astype(bf16)
    above = cotangent[...].astype(f32)
    weighted = above * gain
    g_second = scale * (
        weighted
        - jnp.mean(weighted, axis=-1, keepdims=True)
        - normal * jnp.mean(weighted * normal, axis=-1, keepdims=True)
    )
    g_second_out[...] = g_second
    g_outer = (g_second * factor).astype(bf16)
    g_outers[mine, :] = g_outer
    sums[0:1, :width] += jnp.sum(g_outer.astype(f32), axis=0, keepdims=True)
    sums[1:2, :width] += jnp.sum(above * normal, axis=0, keepdims=True)
    sums[2:3, :width] += jnp.sum(above, axis=0, keepdims=True)
    step = 512

    def part(n, carry):
        at = pl.ds(pl.multiple_of(n * step, step), step)
        g_in = (dot_t(g_outer, down[at, :]) * slope[:, at].astype(f32)).astype(bf16)
        g_inner[:, at] = g_in
        sums[3:4, at] += jnp.sum(g_in.astype(f32), axis=0, keepdims=True)
        return carry

    lax.fori_loop(0, wide // step, part, 0)

    @pl.when(pl.program_id(0) == pl.num_programs(0) - 1)
    def _():
        def grads(n, carry):
            at = pl.ds(pl.multiple_of(n * width, width), width)
            total[...] = t_dot(activated[:, at], g_outers[...])
            hand_out(ids[0], total, wide // 32, own, send, n * (16 * width // wide), 0)
            return carry

        lax.fori_loop(0, wide // width, grads, 0)


def feed_down(ids, weights, activated, slope, scaled, keep, cotangent, vectors, tokens):
    rows, width = scaled.shape
    wide = activated.shape[1]
    narrow, broad = rows_spec(tokens, width), rows_spec(tokens, wide)
    halves = (16, wide // 32, width)
    return call(
        functools.partial(down_body, weights),
        "feed_down",
        (rows // tokens,),
        (ids, *weights.operands, activated, slope, scaled, keep, cotangent, vectors),
        weights.specs + [WHOLE, broad, narrow, narrow, narrow, WHOLE],
        [
            shaped((rows, width), bf16),
            shaped((rows, width), f32),
            shaped((rows, wide), bf16),
            shaped(halves, bf16),
            shaped(halves, bf16),
            shaped((8, wide), f32),
        ],
        [narrow, narrow, broad, WHOLE, WHOLE, WHOLE],
        weights.scratch + [pltpu.VMEM((width, width), f32), pltpu.VMEM((rows, width), bf16)],
        30,
        36,
    )


def middle_body(weights, ids, *refs):
    count = len(weights.operands)
    sources = refs[:count]
    g_inner, g_second, scaled, inverse, keep, vectors = refs[count : count + 6]
    g_first_out, g_attended_out, g_context, sums = refs[count + 6 : count + 10]
    places, sems = refs[count + 10 : -1], refs[-1]
    copies = weights.copies(ids, sources, places, sems)
    width = scaled.shape[1]

    @pl.when(pl.program_id(0) == 0)
    def _():
        begin([copies[1], copies[0]])
        sums[...] = jnp.zeros_like(sums)
        finish(copies[1])
        finish(copies[0])

    normal = scaled[...]
    g_normed = g_second[...] + dot_t(g_inner[...], weights.matrix(places, 1)[...])
    weighted = g_normed * vectors[1:2, :width]
    g_first = inverse[:, 0:1] * (
        weighted
        - jnp.mean(weighted, axis=-1, keepdims=True)
        - normal * jnp.mean(weighted * normal, axis=-1, keepdims=True)
    )
    g_first_out[...] = g_first
    g_attended = (g_first * (keep[...].astype(f32) * keep_scale)).astype(bf16)
    g_attended_out[...] = g_attended
    sums[0:1, :] += jnp.sum(g_attended.astype(f32), axis=0, keepdims=True)
    sums[1:2, :] += jnp.sum(g_normed * normal, axis=0, keepdims=True)
    sums[2:3, :] += jnp.sum(g_normed, axis=0, keepdims=True)
    g_context[...] = dot_t(g_attended, weights.matrix(places, 0)[...]).astype(bf16)


def middle(ids, weights, g_inner, g_second, scaled, inverse, keep, vectors, tokens):
    rows, width = scaled.shape
    wide = g_inner.shape[1]
    narrow, broad = rows_spec(tokens, width), rows_spec(tokens, wide)
    return call(
        functools.partial(middle_body, weights),
        "middle",
        (rows // tokens,),
        (ids, *weights.operands, g_inner, g_second, scaled, inverse, keep, vectors),
        weights.specs + [broad, narrow, narrow, rows_spec(tokens, 128), narrow, WHOLE],
        [
            shaped((rows, width), f32),
            shaped((rows, width), bf16),
            shaped((rows, width), bf16),
            shaped((8, width), f32),
        ],
        [narrow, narrow, narrow, WHOLE],
        weights.scratch,
        24,
        14,
    )


def grads_body(pers, ids, g_inner, scaled, context, g_attended, vectors, sums, more, own, send, total, low, bias):
    n = pl.program_id(0)
    width = scaled.shape[1]
    rows = width // 32

    @pl.when(n == 0)
    def _():
        low[...] = (scaled[...] * vectors[1:2, :width] + vectors[2:3, :width]).astype(bf16)
        vector_sums = [more[i : i + 1, :] for i in range(3)]
        vector_sums += [sums[3:4, :]] + [sums[i : i + 1, :width] for i in range(3)]
        bias[...] = unspread(vector_sums, pers, width)
        hand_out(ids[0], bias, 8, own, send, 0, (1 + sums.shape[1] // width) * rows)
        total[...] = t_dot(context[...], g_attended[...])
        hand_out(ids[0], total, rows, own, send, 0, 0)

    total[...] = t_dot(low[...], g_inner[...])
    for block in range(sums.shape[1] // width):

        @pl.when(n == block)
        def _():
            hand_out(ids[0], total, rows, own, send, 0, (block + 1) * rows)


def middle_grads(ids, pers, g_inner, scaled, context, g_attended, vectors, sums, more):
    rows, width = scaled.shape
    wide = g_inner.shape[1]
    halves = (16, (width + wide) // 32 + 8, width)
    return call(
        functools.partial(grads_body, pers),
        "middle_grads",
        (wide // width,),
        (ids, g_inner, scaled, context, g_attended, vectors, sums, more),
        [pl.BlockSpec((rows, width), lambda i, ids: (0, i))] + [WHOLE] * 6,
        [shaped(halves, bf16), shaped(halves, bf16)],
        [WHOLE] * 2,
        [pltpu.VMEM((width, width), f32), pltpu.VMEM((rows, width), bf16), pltpu.VMEM((256, width), f32)],
        24,
        20,
    )


def inputs_body(per, ids, hidden, turned, g_q, g_near, g_far, own, send, g_keys, g_values, total, bias):
    rows, width = hidden.shape
    sums = []
    for n in range(3):
        if n == 0:
            grad = g_q[...].reshape(rows, width)
        else:
            grad = (g_near[n - 1] + g_far[n - 1].astype(f32)).astype(bf16).reshape(rows, width)
            (g_keys, g_values)[n - 1][...] = grad
        if n != 1:
            sums.append(jnp.sum(grad.astype(f32), axis=0, keepdims=True))
        left = hidden if n == 0 else turned
        for start in range(0, width, 256):
            total[start : start + 256, :] = t_dot(left[:, start : start + 256], grad)
        hand_out(ids[0], total, width // 32, own, send, 0, n * (width // 32))
    bias[...] = unspread([jnp.concatenate(sums, axis=1)], [per], width)
    hand_out(ids[0], bias, 8, own, send, 0, 3 * (width // 32))


def input_grads(ids, hidden, turned, g_q, g_near, g_far, per):
    rows, width = hidden.shape
    halves = (16, 3 * width // 32 + 8, width)
    return call(
        functools.partial(inputs_body, per),
        "input_grads",
        (1,),
        (ids, hidden, turned, g_q, g_near, g_far),
        [WHOLE] * 5,
        [shaped(halves, bf16)] * 2 + [shaped((rows, width), bf16)] * 2,
        [WHOLE] * 4,
        [pltpu.VMEM((width, width), f32), pltpu.VMEM((256, width), f32)],
        28,
        12,
    )


def last_body(weights, ids, *refs):
    count = len(weights.operands)
    sources = refs[:count]
    g_first, g_q, g_keys, g_values, out = refs[count : count + 5]
    places, sems = refs[count + 5 : -1], refs[-1]
    copies = weights.copies(ids, sources, places, sems)

    @pl.when(pl.program_id(0) == 0)
    def _():
        begin(copies)
        for group in copies:
            finish(group)

    turn = turn_matrix(g_q.shape[0])
    total = g_first[...] + dot_t(g_q[...], weights.matrix(places, 0)[...])
    total = total + dot_t(t_dot(turn, g_keys[...]).astype(bf16), weights.matrix(places, 1)[...])
    total = total + dot_t(t_dot(turn, g_values[...]).astype(bf16), weights.matrix(places, 2)[...])
    out[...] = total.astype(bf16)


def last(ids, weights, g_first, g_q, g_keys, g_values, tokens):
    rows, width = g_first.shape
    narrow = rows_spec(tokens, width)
    return call(
        functools.partial(last_body, weights),
        "input_back",
        (rows // tokens,),
        (ids, *weights.operands, g_first, g_q, g_keys, g_values),
        weights.specs + [narrow] * 4,
        [shaped((rows, width), bf16)],
        [narrow],
        weights.scratch,
        16,
        10,
    )[0]


def beside(shape, y, x):
    return pl.BlockSpec((4, 1, 1) + shape[3:], lambda i, ids: (0, ids[1] ^ y, ids[2] ^ x, 0, 0))


def corner_body(ids, one, two, low, high):
    cut = low.shape[1]
    low[...] = (one[:, 0, 0, :cut].astype(f32) + two[:, 0, 0, :cut].astype(f32)).astype(bf16)
    high[...] = (one[:, 0, 0, cut:].astype(f32) + two[:, 0, 0, cut:].astype(f32)).astype(bf16)


def reduce_corner(ids, terms, cut):
    _, _, _, rows, width = terms[0].shape
    return call(
        corner_body,
        "reduce_corner",
        (1,),
        (ids, *terms),
        [beside(terms[0].shape, 1, 1)] * 2,
        [shaped((4, cut, width), bf16), shaped((4, rows - cut, width), bf16)],
        [WHOLE] * 2,
        [],
        8,
        2,
    )


def sides_body(ids, one_y, two_y, one_x, two_x, low, high, to_y, to_x):
    cut = low.shape[1]
    to_y[:, :cut] = (
        one_y[:, 0, 0, :cut].astype(f32) + two_y[:, 0, 0, :cut].astype(f32) + low[...].astype(f32)
    ).astype(bf16)
    to_y[:, cut:] = (one_y[:, 0, 0, cut:].astype(f32) + two_y[:, 0, 0, cut:].astype(f32)).astype(bf16)
    to_x[:, :cut] = (one_x[:, 0, 0, :cut].astype(f32) + two_x[:, 0, 0, :cut].astype(f32)).astype(bf16)
    to_x[:, cut:] = (
        one_x[:, 0, 0, cut:].astype(f32) + two_x[:, 0, 0, cut:].astype(f32) + high[...].astype(f32)
    ).astype(bf16)


def reduce_sides(ids, terms, low, high):
    shape = terms[0].shape
    return call(
        sides_body,
        "reduce_sides",
        (1,),
        (ids, *terms, *terms, low, high),
        [beside(shape, 1, 0)] * 2 + [beside(shape, 0, 1)] * 2 + [WHOLE] * 2,
        [shaped((4,) + shape[3:], bf16)] * 2,
        [WHOLE] * 2,
        [],
        10,
        3,
    )


def depth_body(ids, one, two, from_y, from_x, near, middle, far, mine):
    for k, out in enumerate((mine, near, middle, far)):
        z = ids[3] ^ k
        total = one[z, 0, 0].astype(f32) + two[z, 0, 0].astype(f32)
        total = total + from_y[z].astype(f32) + from_x[z].astype(f32)
        out[...] = total.astype(out.dtype)


def reduce_depth(ids, terms, from_y, from_x):
    shape = terms[0].shape
    return call(
        depth_body,
        "reduce_depth",
        (1,),
        (ids, *terms, from_y, from_x),
        [beside(shape, 0, 0)] * 2 + [WHOLE] * 2,
        [shaped(shape[3:], bf16)] * 3 + [shaped(shape[3:], f32)],
        [WHOLE] * 4,
        [],
        10,
        3,
    )


def pair_body(ids, one, two, out):
    out[0] = one[...]
    out[1] = two[...]


def pair_z(ids, one, two):
    return call(
        pair_body,
        "pair_z",
        (1,),
        (ids, one, two),
        [WHOLE] * 2,
        [shaped((2,) + one.shape, bf16)],
        [WHOLE],
        [],
        4,
        1,
    )[0]


def order_body(ids, pair, received, out):
    for k in range(2):
        out[ids[3] ^ (2 * k)] = pair[k]
        out[ids[3] ^ (2 * k + 1)] = received[k]


def order_z(ids, pair, received):
    return call(
        order_body,
        "order_z",
        (1,),
        (ids, pair, received),
        [WHOLE] * 2,
        [shaped((4,) + pair.shape[1:], bf16)],
        [WHOLE],
        [],
        6,
        1,
    )[0]


def exchange_z(sends):
    return [pp(send, "z", k) for send, k in zip(sends, (1, 2, 3))]


def local(
    hidden_in,
    cotangent,
    attention_keep,
    output_keep,
    feed_keep,
    qkv_weight,
    qkv_bias,
    out_weight,
    out_bias,
    first_gain,
    first_shift,
    up_weight,
    up_bias,
    down_weight,
    down_bias,
    second_gain,
    second_shift,
):
    micro, _, tokens, width = hidden_in.shape
    rows = micro * tokens
    own = qkv_weight.shape[0]
    wide = up_weight.shape[1]
    blocks = wide // width
    c, y, x = lax.axis_index("seq"), lax.axis_index("y"), lax.axis_index("x")
    ids = jnp.stack([c, y, x, lax.axis_index("z")]).astype(jnp.int32)
    bias_parts = (out_bias, first_gain, first_shift, up_bias, down_bias, second_gain, second_shift)
    pers = [part.shape[0] for part in bias_parts]
    per = qkv_bias.shape[0]

    column = lambda weight, i: weight[:, i * width : (i + 1) * width]
    bias_rows = lambda parts: jnp.concatenate(
        [jnp.pad(part.reshape(1, -1), ((0, 0), (0, width - part.shape[0]))) for part in parts]
        + [jnp.zeros((8 - len(parts), width), bf16)]
    )
    square = (own, width)
    hidden = hidden_in.reshape(rows, width)

    shard_a = jnp.concatenate([column(qkv_weight, i) for i in range(3)] + [bias_rows((qkv_bias,))])
    own_a = select_z(shard_a, [pp(shard_a, "z", k) for k in (1, 2, 3)])
    x_a, y_a = pp(own_a, "x"), pp(own_a, "y")
    shard_b = jnp.concatenate(
        [out_weight] + [column(up_weight, i) for i in range(blocks)] + [bias_rows(bias_parts)]
    )
    shard_b = after(shard_b, own_a)
    far_b = pp(shard_b, "z", 2)
    turned, keep_output, keep_feed = prepare(
        ids, after(hidden, own_a), output_keep.transpose(0, 1, 3, 2), feed_keep.transpose(0, 1, 3, 2), tokens
    )
    x_a, y_a, far_b = hold((x_a, y_a, far_b), turned)
    cut_a = shard_a.shape[0] // 2
    low_a, high_a = pp(x_a[:, :cut_a], "y"), pp(y_a[:, cut_a:], "x")
    pieces = [(0, 0, own_a), (1, 0, x_a), (2, 0, y_a), (3, 0, low_a), (3, cut_a, high_a)]
    pieces += [(number + 4, first, pp(piece, "seq")) for number, first, piece in pieces]
    pair_b = pair_z(ids, shard_b, far_b)
    near_b = pp(pair_b, "z", 1)
    plan = [(i * own, own, i, 0, 0) for i in range(3)]
    plan = divide(plan, cut_a)
    weights = Weights(pieces, plan + [(3 * own, 8, 3, 0, 0)], [square] * 3 + [(8, width)])
    weights_again = Weights(pieces, plan, [square] * 3)
    own_b = order_z(ids, pair_b, after(near_b, low_a, high_a))
    x_b, y_b = pp(own_b, "x"), pp(own_b, "y")
    queries, *near = project(ids, weights, hidden, after(turned, own_b), micro, per)
    near = (near[: 2 * PARTS[0]], near[2 * PARTS[0] :])
    far = [[pp(value, "seq") for value in values] for values in near]
    shard_c = after(down_weight, own_b)
    far_c = pp(shard_c, "z", 2)
    words = attention_keep.reshape(micro, H, tokens, -1)
    context, signed = attention(ids, 0, queries, near, far, words)
    far_c, own_b, x_b, y_b, *far[1] = hold((far_c, own_b, x_b, y_b, *far[1]), context)
    pair_c = pair_z(ids, shard_c, far_c)
    near_c = pp(pair_c, "z", 1)
    cut_b = shard_b.shape[0] // 2
    low_b, high_b = pp(x_b[:, :cut_b], "y"), pp(y_b[:, cut_b:], "x")
    context, signed = attention(ids, 1, queries, near, far, words, (context, signed))
    low_b, high_b, near_c = hold((low_b, high_b, near_c), context)
    pieces = [(0, 0, own_b), (1, 0, x_b), (2, 0, y_b)]
    pieces += [(number + 4, first, pp(piece, "seq")) for number, first, piece in pieces]
    pieces += [(3, 0, low_b), (3, cut_b, high_b), (7, 0, pp(low_b, "seq")), (7, cut_b, pp(high_b, "seq"))]
    plan = [(0, own, 0, 0, 0)] + [((i + 1) * own, own, 1, 0, i * width) for i in range(blocks)]
    plan = divide(plan, cut_b)
    weights = Weights(
        pieces, plan + [((blocks + 1) * own, 8, 2, 0, 0)], [square, (own, wide), (8, width)]
    )
    back_weights = Weights(pieces, plan, [square, (own, wide)])
    own_c = order_z(ids, pair_c, after(near_c, low_b, high_b))
    x_c, y_c = pp(own_c, "x"), pp(own_c, "y")
    context = context.reshape(rows, width)
    vectors, scaled, inverse, activated, slope = feed_up(
        ids, weights, pers, context, hidden, keep_output, tokens, wide
    )
    x_c, y_c = hold((x_c, y_c), activated)
    down_rows = down_weight.shape[0]
    cut_c = down_rows // 2
    low_c, high_c = pp(x_c[:, :cut_c], "y"), pp(y_c[:, cut_c:], "x")
    pieces = [(0, 0, own_c), (1, 0, x_c), (2, 0, y_c), (3, 0, low_c), (3, cut_c, high_c)]
    pieces += [(number + 4, first, pp(piece, "seq")) for number, first, piece in pieces]
    weights = Weights(
        pieces, divide([(0, down_rows, 0, 0, 0)], cut_c), [(down_rows, width)]
    )
    layer_out, g_second, g_inner, down_own, down_send, sums = feed_down(
        ids, weights, activated, slope, scaled, keep_feed, cotangent.reshape(rows, width), vectors, tokens
    )

    unit = lambda value: value.reshape((4, 2, 2) + value.shape[1:])
    down_core = pp(down_send, "seq")
    g_first, g_attended, g_context, more = middle(
        ids, back_weights, g_inner, g_second, scaled, inverse, keep_output, vectors, tokens
    )
    down = [unit(down_own), unit(after(down_core, g_context))]
    corner = reduce_corner(ids, down, cut_c)
    low, high = pp(corner[0], "x"), pp(corner[1], "y")
    mid_own, mid_send = middle_grads(
        ids, pers, g_inner, scaled, context, after(g_attended, *corner), vectors, sums, more
    )
    low, high = hold((low, high), mid_send)
    to_y, to_x = reduce_sides(ids, down, low, high)
    down_y, down_x = pp(to_y, "y"), pp(to_x, "x")
    mid_core = pp(after(mid_send, low, high), "seq")
    grads = attention_back(ids, 0, queries, near, far, signed, after(g_context, to_y, to_x))
    mid = [unit(mid_own), unit(after(mid_core, *grads))]
    corner = reduce_corner(ids, mid, cut_b)
    low, high = pp(corner[0], "x"), pp(corner[1], "y")
    g_q, g_near, g_far = attention_back(
        ids, 1, queries, near, far, signed, after(g_context, *corner), tuple(grads)
    )
    low, high, down_y, down_x = hold((low, high, down_y, down_x), g_q)
    far_grads = pp(after(g_far, low, high, down_y, down_x), "seq")
    to_y, to_x = reduce_sides(ids, mid, low, high)
    mid_y, mid_x = pp(to_y, "y"), pp(to_x, "x")
    *sends, down_mine = reduce_depth(ids, down, down_y, down_x)
    down_z = exchange_z(sends)
    a_own, a_send, g_keys, g_values = input_grads(
        ids, hidden, turned, g_q, g_near, after(far_grads, to_y, to_x, *sends), per
    )
    grad_in = last(ids, weights_again, g_first, g_q.reshape(rows, width), g_keys, g_values, tokens)
    mid_y, mid_x, *down_z = hold((mid_y, mid_x, *down_z), grad_in)
    core_sums = pp(after(a_send, mid_y, mid_x), "seq")
    part = [unit(a_own), unit(core_sums)]
    corner = reduce_corner(ids, part, cut_a)
    low, high = pp(corner[0], "x"), pp(corner[1], "y")
    *sends, mid_mine = reduce_depth(ids, mid, after(mid_y, *corner), mid_x)
    mid_z = exchange_z(sends)
    low, high = hold((low, high), *sends)
    grad_down = add_up([down_mine, *down_z])
    to_y, to_x = reduce_sides(ids, part, low, high)
    side_y, side_x = pp(to_y, "y"), pp(to_x, "x")
    mid = add_up([mid_mine, *hold(mid_z, to_y, to_x)])
    side_y, side_x = hold((side_y, side_x), mid)
    *sends, part_mine = reduce_depth(ids, part, side_y, side_x)
    part = add_up([part_mine, *exchange_z(sends)])

    stripe = lambda value, i: value[i * own : (i + 1) * own]
    grad_qkv = jnp.concatenate([stripe(part, i) for i in range(3)], axis=1)
    grad_up = jnp.concatenate([stripe(mid, i + 1) for i in range(blocks)], axis=1)
    vector_grads = [mid[(blocks + 1) * own + i, :length] for i, length in enumerate(pers)]
    return (
        layer_out.reshape(hidden_in.shape),
        grad_in.reshape(hidden_in.shape),
        grad_qkv,
        part[3 * own, :per],
        stripe(mid, 0),
        vector_grads[0],
        vector_grads[1],
        vector_grads[2],
        grad_up,
        vector_grads[3],
        grad_down,
        vector_grads[4],
        vector_grads[5],
        vector_grads[6],
    )


def solution(mesh):
    groups, cores = mesh.devices.shape
    split = Mesh(mesh.devices.reshape(groups // 4, 2, 2, cores), ("z", "y", "x", "seq"))
    dp = ("z", "y", "x")
    token_rows = P(None, dp, "seq", None)
    matrix = P(every, None)
    vector = P(every)
    params = (matrix, vector, matrix, vector, vector, vector, matrix, vector, matrix, vector, vector, vector)

    def layer(*arrays):
        tiled = groups == 16 and cores == 2 and arrays[5].shape[0] % 8 == 0
        return (local if tiled else plain_local)(*arrays)

    return jax.shard_map(
        layer,
        mesh=split,
        in_specs=(token_rows, token_rows, P(None, dp, None, "seq", None), token_rows, token_rows) + params,
        out_specs=(token_rows, token_rows) + params,
        check_vma=False,
    )
```

```python
import functools

import jax
import jax.numpy as jnp
from jax import lax
from jax.experimental import pallas as pl
from jax.experimental.pallas import tpu as pltpu
from jax.sharding import Mesh
from jax.sharding import PartitionSpec as P

H = 12
epsilon = 1e-12
keep_scale = 8.0 / 7.0
root_half = 0.7071067811865476
inverse_root_tau = 0.3989422804014327
every = ("z", "y", "x", "seq")
f32 = jnp.float32
bf16 = jnp.bfloat16


def unpack_keep(packed_words):
    shifts = jnp.arange(4, dtype=jnp.int32) * 3
    nibble = jnp.right_shift(packed_words[..., None], shifts) & 7
    keep_value = (nibble >= 1).astype(jnp.float32) * keep_scale
    return keep_value.reshape(packed_words.shape[:-1] + (packed_words.shape[-1] * 4,))


def normalize(values, norm_gain, norm_shift):
    centred = values - jnp.mean(values, axis=-1, keepdims=True)
    inverse = lax.rsqrt(jnp.mean(centred * centred, axis=-1, keepdims=True) + epsilon)
    scaled = centred * inverse
    return (scaled * norm_gain + norm_shift, scaled, inverse)


def norm_back(upstream, scaled, inverse, norm_gain):
    weighted = upstream * norm_gain
    centre_term = jnp.mean(weighted, axis=-1, keepdims=True)
    slope_term = jnp.mean(weighted * scaled, axis=-1, keepdims=True)
    return inverse * (weighted - centre_term - scaled * slope_term)


def gelu_slope(inner_sum):
    normal_cdf = 0.5 * (1.0 + lax.erf(inner_sum * root_half))
    density = jnp.exp(-0.5 * inner_sum * inner_sum) * inverse_root_tau
    return normal_cdf + inner_sum * density


def matmul(left_side, right_side):
    return jnp.dot(left_side, right_side, preferred_element_type=jnp.float32)


def plain_local(
    hidden_in,
    cotangent,
    attention_keep,
    output_keep,
    feed_keep,
    qkv_weight,
    qkv_bias,
    out_weight,
    out_bias,
    first_gain,
    first_shift,
    up_weight,
    up_bias,
    down_weight,
    down_bias,
    second_gain,
    second_shift,
):
    model_width = hidden_in.shape[-1]
    sequence_count = hidden_in.shape[1]
    local_tokens = hidden_in.shape[2]
    token_rows = sequence_count * local_tokens
    head_count = H
    head_size = model_width // head_count
    held_params = (
        lax.all_gather(qkv_weight, every, axis=0, tiled=True),
        lax.all_gather(qkv_bias, every, axis=0, tiled=True),
        lax.all_gather(out_weight, every, axis=0, tiled=True),
        lax.all_gather(out_bias, every, axis=0, tiled=True),
        lax.all_gather(first_gain, every, axis=0, tiled=True),
        lax.all_gather(first_shift, every, axis=0, tiled=True),
        lax.all_gather(up_weight, every, axis=0, tiled=True),
        lax.all_gather(up_bias, every, axis=0, tiled=True),
        lax.all_gather(down_weight, every, axis=0, tiled=True),
        lax.all_gather(down_bias, every, axis=0, tiled=True),
        lax.all_gather(second_gain, every, axis=0, tiled=True),
        lax.all_gather(second_shift, every, axis=0, tiled=True),
    )
    totals = None
    outputs = []
    inputs_grad = []
    for micro_step in range(hidden_in.shape[0]):
        (
            full_qkv_w,
            full_qkv_b,
            full_out_w,
            full_out_b,
            full_gain_one,
            full_shift_one,
            full_up_w,
            full_up_b,
            full_down_w,
            full_down_b,
            full_gain_two,
            full_shift_two,
        ) = held_params
        rows_in = hidden_in[micro_step].reshape(token_rows, model_width)
        qkv_float = full_qkv_b.astype(jnp.float32)
        bias_full = jnp.concatenate(
            [
                qkv_float[:model_width],
                jnp.zeros((model_width,), jnp.float32),
                qkv_float[model_width:],
            ]
        )
        projected = (matmul(rows_in, full_qkv_w) + bias_full).astype(jnp.bfloat16)
        queries = projected[:, :model_width].reshape(
            sequence_count, local_tokens, head_count, head_size
        )
        keys_local = projected[:, model_width : 2 * model_width].reshape(
            sequence_count, local_tokens, model_width
        )
        values_local = projected[:, 2 * model_width :].reshape(
            sequence_count, local_tokens, model_width
        )
        keys_all, values_all = (
            lax.all_gather(keys_local, "seq", axis=1, tiled=True),
            lax.all_gather(values_local, "seq", axis=1, tiled=True),
        )
        keys_heads = keys_all.reshape(sequence_count, -1, head_count, head_size)
        values_heads = values_all.reshape(sequence_count, -1, head_count, head_size)
        scores = (
            jnp.einsum("sqhd,skhd->shqk", queries, keys_heads, preferred_element_type=jnp.float32)
            * 0.125
        )
        row_peak = jnp.max(scores, axis=-1, keepdims=True)
        exponent = jnp.exp(scores - row_peak)
        row_total = jnp.sum(exponent, axis=-1, keepdims=True)
        log_total = row_peak + jnp.log(row_total)
        softmax_weights = exponent / row_total
        keep_attention = unpack_keep(attention_keep[micro_step])
        dropped = (softmax_weights * keep_attention).astype(jnp.bfloat16)
        context = jnp.einsum(
            "shqk,skhd->sqhd", dropped, values_heads, preferred_element_type=jnp.float32
        )
        context = context.reshape(token_rows, model_width).astype(jnp.bfloat16)
        attended = matmul(context, full_out_w) + full_out_b.astype(jnp.float32)
        keep_output = unpack_keep(output_keep[micro_step]).reshape(token_rows, model_width)
        first_sum = rows_in.astype(jnp.float32) + attended * keep_output
        gain_one = full_gain_one.astype(jnp.float32)
        normed, scaled_one, inverse_one = normalize(
            first_sum, gain_one, full_shift_one.astype(jnp.float32)
        )
        normed_low = normed.astype(jnp.bfloat16)
        inner_sum = matmul(normed_low, full_up_w) + full_up_b.astype(jnp.float32)
        activated = jax.nn.gelu(inner_sum, approximate=False).astype(jnp.bfloat16)
        outer_sum = matmul(activated, full_down_w) + full_down_b.astype(jnp.float32)
        keep_feed = unpack_keep(feed_keep[micro_step]).reshape(token_rows, model_width)
        second_sum = normed + outer_sum * keep_feed
        gain_two = full_gain_two.astype(jnp.float32)
        result, scaled_two, inverse_two = normalize(
            second_sum, gain_two, full_shift_two.astype(jnp.float32)
        )
        outputs.append(
            result.astype(jnp.bfloat16).reshape(sequence_count, local_tokens, model_width)
        )
        (
            back_qkv_w,
            back_qkv_b,
            back_out_w,
            back_out_b,
            back_gain_one,
            back_shift_one,
            back_up_w,
            back_up_b,
            back_down_w,
            back_down_b,
            back_gain_two,
            back_shift_two,
        ) = held_params
        upstream = cotangent[micro_step].reshape(token_rows, model_width).astype(jnp.float32)
        g_second = norm_back(upstream, scaled_two, inverse_two, back_gain_two.astype(jnp.float32))
        grad_gain_two = jnp.sum(upstream * scaled_two, axis=0)
        grad_shift_two = jnp.sum(upstream, axis=0)
        g_outer = (g_second * keep_feed).astype(jnp.bfloat16)
        grad_down_b = jnp.sum(g_outer.astype(jnp.float32), axis=0)
        grad_down_w = matmul(activated.T, g_outer)
        g_inner = (matmul(g_outer, back_down_w.T) * gelu_slope(inner_sum)).astype(jnp.bfloat16)
        grad_up_b = jnp.sum(g_inner.astype(jnp.float32), axis=0)
        grad_up_w = matmul(normed_low.T, g_inner)
        g_normed = g_second + matmul(g_inner, back_up_w.T)
        g_first = norm_back(g_normed, scaled_one, inverse_one, back_gain_one.astype(jnp.float32))
        grad_gain_one = jnp.sum(g_normed * scaled_one, axis=0)
        grad_shift_one = jnp.sum(g_normed, axis=0)
        g_attended = (g_first * keep_output).astype(jnp.bfloat16)
        grad_out_b = jnp.sum(g_attended.astype(jnp.float32), axis=0)
        grad_out_w = matmul(context.T, g_attended)
        g_context = matmul(g_attended, back_out_w.T).astype(jnp.bfloat16)
        g_context = g_context.reshape(sequence_count, local_tokens, head_count, head_size)
        keys_again, values_again = (
            lax.all_gather(keys_local, "seq", axis=1, tiled=True),
            lax.all_gather(values_local, "seq", axis=1, tiled=True),
        )
        keys_heads = keys_again.reshape(sequence_count, -1, head_count, head_size)
        values_heads = values_again.reshape(sequence_count, -1, head_count, head_size)
        scores_again = (
            jnp.einsum("sqhd,skhd->shqk", queries, keys_heads, preferred_element_type=jnp.float32)
            * 0.125
        )
        weights_again = jnp.exp(scores_again - log_total)
        dropped_again = (weights_again * keep_attention).astype(jnp.bfloat16)
        g_values_all = jnp.einsum(
            "shqk,sqhd->skhd", dropped_again, g_context, preferred_element_type=jnp.float32
        )
        g_dropped = jnp.einsum(
            "sqhd,skhd->shqk", g_context, values_heads, preferred_element_type=jnp.float32
        )
        g_weights = g_dropped * keep_attention
        row_delta = jnp.sum(g_weights * weights_again, axis=-1, keepdims=True)
        g_scores = (weights_again * (g_weights - row_delta)).astype(jnp.bfloat16)
        g_queries = (
            jnp.einsum("shqk,skhd->sqhd", g_scores, keys_heads, preferred_element_type=jnp.float32)
            * 0.125
        )
        g_keys_all = (
            jnp.einsum("shqk,sqhd->skhd", g_scores, queries, preferred_element_type=jnp.float32)
            * 0.125
        )
        g_keys, g_values = (
            lax.psum_scatter(
                g_keys_all.reshape(sequence_count, -1, model_width).astype(jnp.bfloat16),
                "seq",
                scatter_dimension=1,
                tiled=True,
            ).astype(jnp.float32),
            lax.psum_scatter(
                g_values_all.reshape(sequence_count, -1, model_width).astype(jnp.bfloat16),
                "seq",
                scatter_dimension=1,
                tiled=True,
            ).astype(jnp.float32),
        )
        g_projected = jnp.concatenate(
            [
                g_queries.reshape(token_rows, model_width),
                g_keys.reshape(token_rows, model_width),
                g_values.reshape(token_rows, model_width),
            ],
            axis=1,
        ).astype(jnp.bfloat16)
        g_projected_float = g_projected.astype(jnp.float32)
        grad_qkv_b = jnp.concatenate(
            [
                jnp.sum(g_projected_float[:, :model_width], axis=0),
                jnp.sum(g_projected_float[:, 2 * model_width :], axis=0),
            ]
        )
        grad_qkv_w = matmul(rows_in.T, g_projected)
        input_grad = g_first + matmul(g_projected, back_qkv_w.T)
        inputs_grad.append(
            input_grad.astype(jnp.bfloat16).reshape(sequence_count, local_tokens, model_width)
        )
        grads_now = (
            grad_qkv_w,
            grad_qkv_b,
            grad_out_w,
            grad_out_b,
            grad_gain_one,
            grad_shift_one,
            grad_up_w,
            grad_up_b,
            grad_down_w,
            grad_down_b,
            grad_gain_two,
            grad_shift_two,
        )
        if totals is None:
            totals = grads_now
        else:
            totals = tuple((before + added for before, added in zip(totals, grads_now)))
    summed = (
        lax.psum_scatter(totals[0], every, scatter_dimension=0, tiled=True),
        lax.psum_scatter(totals[1], every, scatter_dimension=0, tiled=True),
        lax.psum_scatter(totals[2], every, scatter_dimension=0, tiled=True),
        lax.psum_scatter(totals[3], every, scatter_dimension=0, tiled=True),
        lax.psum_scatter(totals[4], every, scatter_dimension=0, tiled=True),
        lax.psum_scatter(totals[5], every, scatter_dimension=0, tiled=True),
        lax.psum_scatter(totals[6], every, scatter_dimension=0, tiled=True),
        lax.psum_scatter(totals[7], every, scatter_dimension=0, tiled=True),
        lax.psum_scatter(totals[8], every, scatter_dimension=0, tiled=True),
        lax.psum_scatter(totals[9], every, scatter_dimension=0, tiled=True),
        lax.psum_scatter(totals[10], every, scatter_dimension=0, tiled=True),
        lax.psum_scatter(totals[11], every, scatter_dimension=0, tiled=True),
    )
    return (
        jnp.stack(outputs, axis=0),
        jnp.stack(inputs_grad, axis=0),
        summed[0],
        summed[1],
        summed[2],
        summed[3],
        summed[4],
        summed[5],
        summed[6],
        summed[7],
        summed[8],
        summed[9],
        summed[10],
        summed[11],
    )


ANY = pl.BlockSpec(memory_space=pl.ANY)
WHOLE = pl.BlockSpec(memory_space=pltpu.VMEM)
MIB = 2**20
PARTS = (2, 1)
GROUP = 2


def dot_t(left_side, right_side):
    return lax.dot_general(left_side, right_side, (((1,), (1,)), ((), ())), preferred_element_type=f32)


def t_dot(left_side, right_side):
    return lax.dot_general(left_side, right_side, (((0,), (0,)), ((), ())), preferred_element_type=f32)


def iota(shape, axis):
    return lax.broadcasted_iota(jnp.int32, shape, axis)


def pp(value, axis, step=1):
    size = lax.axis_size(axis)
    return lax.ppermute(value, axis, [(i, i ^ step) for i in range(size)])


def pick(value, axis, index):
    return lax.dynamic_index_in_dim(value, index, axis, keepdims=False)


def after(value, *earlier):
    return lax.optimization_barrier((value,) + earlier)[0]


def hold(values, *earlier):
    return lax.optimization_barrier(tuple(values) + earlier)[: len(values)]


def add_up(terms):
    total = terms[0].astype(f32)
    for term in terms[1:]:
        total = total + term.astype(f32)
    return total


def divide(plan, cut):
    parts = []
    for start, rows, out, row, column in plan:
        ends = [start, cut, start + rows] if start < cut < start + rows else [start, start + rows]
        for first, last in zip(ends, ends[1:]):
            parts.append((first, last - first, out, row + first - start, column))
    return parts


def whole(number, first, array):
    return (number, first, array, 0, array.shape[1])


def at_core(piece):
    number, first, array, row, rows = piece
    return (number + 4, first, pp(array, "seq"), row, rows)


class Weights:
    def __init__(self, pieces, plan, shapes):
        arrays = []
        self.spans = []
        for number, first, array, row, rows in pieces:
            place = next((i for i, held in enumerate(arrays) if held is array), len(arrays))
            if place == len(arrays):
                arrays.append(array)
            self.spans.append((number, first, place, row, rows))
        self.operands = [pltpu.with_memory_space_constraint(array, pltpu.HBM) for array in arrays]
        self.plan, self.shapes = plan, shapes
        self.specs = [pl.BlockSpec(memory_space=pltpu.HBM)] * len(arrays)
        self.scratch = [pltpu.VMEM((4, 2, 2, 2, rows, columns), bf16) for rows, columns in shapes]
        self.scratch.append(pltpu.SemaphoreType.DMA((8 * len(plan),)))

    def copies(self, ids, sources, places, sems):
        found = [[] for _ in self.shapes]
        count = 0
        for start, rows, out, row, column in self.plan:
            for number, first, place, source_row, held in self.spans:
                if first <= start and start + rows <= first + held:
                    c = ids[0] ^ (number >> 2)
                    y = ids[1] ^ ((number >> 1) & 1)
                    x = ids[2] ^ (number & 1)
                    source = sources[place]
                    src = source.at[:, pl.ds(source_row + start - first, rows), :]
                    dst = places[out].at[:, y, x, c, pl.ds(row, rows), pl.ds(column, source.shape[2])]
                    found[out].append(pltpu.make_async_copy(src, dst, sems.at[count]))
                    count += 1
        return found

    def matrix(self, places, out):
        rows, columns = self.shapes[out]
        return places[out].reshape(32 * rows, columns)


def begin(copies):
    for group in copies:
        for copy in group:
            copy.start()


def finish(group):
    for copy in group:
        copy.wait()


def spread(block, row, count, per):
    values = block[:, row, : -(-per // 128) * 128].astype(bf16)
    lanes = values.shape[1]
    select = (iota((lanes, count), 1) % per == iota((lanes, count), 0)).astype(bf16)
    wide = jnp.dot(values, select, preferred_element_type=f32)
    return jnp.sum(jnp.where(iota(wide.shape, 1) // per == iota(wide.shape, 0), wide, 0.0), axis=0, keepdims=True)


def unspread(vectors, pers, block, first=0):
    block[:, first:] = jnp.zeros((32, 8 - first, block.shape[2]), f32)
    for row, (vector, per) in enumerate(zip(vectors, pers), first):
        count = vector.shape[1]
        lanes = -(-per // 128) * 128
        shape = (32, count)
        wide = jnp.where(iota(shape, 1) // per == iota(shape, 0), vector, 0.0).astype(bf16)
        select = (iota((count, lanes), 0) % per == iota((count, lanes), 1)).astype(bf16)
        block[:, row, :lanes] = jnp.dot(wide, select, preferred_element_type=f32)


def layer_norm(values):
    centred = values - jnp.mean(values, axis=-1, keepdims=True)
    inverse = lax.rsqrt(jnp.mean(centred * centred, axis=-1, keepdims=True) + epsilon)
    return centred * inverse, inverse


def turn_matrix(tokens):
    place = iota((tokens, tokens), 0)
    quarter = tokens // 4
    return (iota((tokens, tokens), 1) == 4 * (place % quarter) + place // quarter).astype(bf16)


def call(body, name, grid, operands, specs, outs, out_specs, scratch, room, load, aliases=None):
    return pl.pallas_call(
        body,
        grid_spec=pltpu.PrefetchScalarGridSpec(
            num_scalar_prefetch=1, grid=grid, in_specs=specs, out_specs=out_specs, scratch_shapes=scratch
        ),
        out_shape=outs,
        compiler_params=pltpu.CompilerParams(vmem_limit_bytes=room * MIB),
        cost_estimate=pl.CostEstimate(flops=1024, bytes_accessed=load * MIB // 16, transcendentals=0),
        input_output_aliases=aliases or {},
        name=name,
    )(*operands)


def shaped(shape, dtype):
    return jax.ShapeDtypeStruct(shape, dtype)


def rows_spec(rows, columns):
    return pl.BlockSpec((rows, columns), lambda i, ids: (i, 0))


def fixed_spec(shape):
    return pl.BlockSpec(shape, lambda i, ids: (0,) * len(shape))


def prepare_body(ids, hidden, output_words, feed_words, turned, keep_output, keep_feed):
    tokens, width = hidden.shape
    turned[...] = jnp.dot(turn_matrix(tokens), hidden[...], preferred_element_type=f32).astype(bf16)
    quarter = width // 4
    for words, keep in ((output_words, keep_output), (feed_words, keep_feed)):
        packed = words[0, 0]
        total = jnp.zeros((tokens, width), f32)
        for i in range(4):
            bit = ((packed & (7 << (3 * i))) != 0).astype(f32).astype(bf16)
            place = (iota((quarter, width), 1) == 4 * iota((quarter, width), 0) + i).astype(bf16)
            total = total + t_dot(bit, place)
        keep[...] = total.astype(bf16)


def prepare(ids, hidden, output_words, feed_words, tokens):
    rows, width = hidden.shape
    wide = rows_spec(tokens, width)
    narrow = pl.BlockSpec((1, 1, width // 4, tokens), lambda i, ids: (i, 0, 0, 0))
    return call(
        prepare_body,
        "prepare",
        (rows // tokens,),
        (ids, hidden, output_words, feed_words),
        [wide, narrow, narrow],
        [shaped((rows, width), bf16)] * 3,
        [wide] * 3,
        [],
        12,
        6,
    )


def project_body(weights, per, ids, *refs):
    count = len(weights.operands)
    sources, (hidden, turned, queries), rest = refs[:count], refs[count : count + 3], refs[count + 3 :]
    micro, tokens, width = queries.shape
    places, sems = rest[len(rest) - 1 - len(weights.shapes) : -1], rest[-1]
    near = iter(rest[: len(rest) - 1 - len(weights.shapes)])
    copies = weights.copies(ids, sources, places, sems)
    begin(copies)
    finish(copies[3])
    block = weights.matrix(places, 3)[:, :128].astype(f32).reshape(32, 8, 128)
    bias = spread(block, 0, 2 * width, per)
    for n in range(3):
        finish(copies[n])
    for m in range(micro):
        natural, other = hidden[m * tokens : (m + 1) * tokens, :], turned[m * tokens : (m + 1) * tokens, :]
        q = jnp.dot(natural, weights.matrix(places, 0)[...], preferred_element_type=f32) + bias[:, :width]
        queries[m] = q.astype(bf16)
        k = jnp.dot(other, weights.matrix(places, 1)[...], preferred_element_type=f32).astype(bf16)
        v = jnp.dot(other, weights.matrix(places, 2)[...], preferred_element_type=f32) + bias[:, width:]
        for value in (k, v.astype(bf16)):
            rows = tokens // PARTS[m]
            for part in range(PARTS[m]):
                next(near)[...] = value[part * rows : (part + 1) * rows]


def project(ids, weights, hidden, turned, micro, per):
    rows, width = hidden.shape
    return call(
        functools.partial(project_body, weights, per),
        "project",
        (1,),
        (ids, *weights.operands, hidden, turned),
        weights.specs + [WHOLE] * 2,
        [shaped((micro, rows // micro, width), bf16)]
        + [shaped((rows // micro // PARTS[m], width), bf16) for m in range(micro) for _ in range(2 * PARTS[m])],
        [WHOLE] * (1 + 2 * sum(PARTS)),
        weights.scratch,
        16,
        10,
    )


def lane_half(shape):
    return iota(shape, len(shape) - 1) < 64


def by_head(pair):
    left, zero = lane_half(pair.shape), jnp.zeros_like(pair)
    return jnp.concatenate([jnp.where(left, pair, zero), jnp.where(left, zero, pair)], axis=0)


def join_keys(core, near, far, buffer, lanes):
    quarter = buffer.shape[0] // 8
    parts = len(near)
    for i in range(4):
        here = pl.multiple_of((2 * i + core) * quarter, quarter)
        there = pl.multiple_of((2 * i + 1 - core) * quarter, quarter)
        at = (i * parts % 4) // parts * quarter
        buffer[pl.ds(here, quarter), :] = near[i * parts // 4][at : at + quarter, lanes]
        buffer[pl.ds(there, quarter), :] = far[i * parts // 4][at : at + quarter, lanes]


def group_lanes():
    return [slice(j * 128, (j + 1) * 128) for j in range(GROUP)]


def attention_body(parts, ids, q, *refs):
    ours, words = refs[: 4 * parts], refs[4 * parts]
    context, signed, keys, values = refs[-4:]
    core = ids[0]
    tokens = q.shape[1]
    for j, lanes in enumerate(group_lanes()):
        join_keys(core, ours[:parts], ours[2 * parts : 3 * parts], keys.at[j], lanes)
        join_keys(core, ours[parts : 2 * parts], ours[3 * parts :], values.at[j], lanes)
    scores = [dot_t(by_head(q[0, :, lanes]) * 0.125, keys[j]) for j, lanes in enumerate(group_lanes())]
    for j, lanes in enumerate(group_lanes()):
        blocks = [scores[j][:, i * 128 : (i + 1) * 128] for i in range(4)]
        peak = jnp.maximum(jnp.maximum(blocks[0], blocks[1]), jnp.maximum(blocks[2], blocks[3]))
        peak = jnp.max(peak, axis=1, keepdims=True)
        blocks = [jnp.exp(block - peak) for block in blocks]
        total = jnp.sum((blocks[0] + blocks[1]) + (blocks[2] + blocks[3]), axis=1, keepdims=True)
        scale = 1.0 / total
        word = words[0, 2 * j : 2 * j + 2].reshape(2 * tokens, 128)
        dropped = []
        for i in range(4):
            weight = blocks[i] * scale
            keep = (word & (7 << (3 * i))) != 0
            weight = jnp.where(keep, weight, -weight).astype(bf16)
            signed[0, j, i] = weight
            dropped.append(jnp.maximum(weight, jnp.zeros_like(weight)))
        out = jnp.dot(jnp.concatenate(dropped, axis=1), values[j], preferred_element_type=f32) * keep_scale
        context[0, :, lanes] = jnp.where(lane_half((tokens, 128)), out[:tokens], out[tokens:]).astype(bf16)


def attention(ids, m, queries, near, far, words, earlier=()):
    micro, tokens, width = queries.shape
    pairs = width // 128
    part = pl.BlockSpec((1, tokens, 128 * GROUP), lambda p, ids: (m, 0, p))
    flat = pl.BlockSpec((tokens // PARTS[m], 128 * GROUP), lambda p, ids: (0, p))
    operands = (ids, queries, *near[m], *far[m], words)
    return call(
        functools.partial(attention_body, PARTS[m]),
        "attention",
        (pairs // GROUP,),
        operands + tuple(earlier),
        [part] + [flat] * (4 * PARTS[m])
        + [pl.BlockSpec((1, 2 * GROUP, tokens, 128), lambda p, ids: (m, p, 0, 0))]
        + [ANY] * len(earlier),
        [shaped((micro, tokens, width), bf16), shaped((micro, pairs, 4, 2 * tokens, 128), bf16)],
        [part, pl.BlockSpec((1, GROUP, 4, 2 * tokens, 128), lambda p, ids: (m, p, 0, 0, 0))],
        [pltpu.VMEM((GROUP, 2 * tokens, 128), bf16)] * 2,
        16,
        14,
        {len(operands) + i: i for i in range(len(earlier))},
    )


def attention_back_body(parts, ids, q, *refs):
    ours, signed, upstream, refs = refs[: 4 * parts], refs[4 * parts], refs[4 * parts + 1], refs[4 * parts + 2 :]
    g_q, *grads, keys, values, sums = refs
    g_near, g_far = grads[:2], grads[2:]
    core = ids[0]
    tokens = q.shape[1]
    for j, lanes in enumerate(group_lanes()):
        join_keys(core, ours[:parts], ours[2 * parts : 3 * parts], keys.at[j], lanes)
        join_keys(core, ours[parts : 2 * parts], ours[3 * parts :], values.at[j], lanes)
    aboves = [by_head(upstream[:, lanes]) for lanes in group_lanes()]
    g_droppeds = [dot_t(aboves[j], values[j]) for j in range(GROUP)]
    for j, lanes in enumerate(group_lanes()):
        weights, kept, g_weights = [], [], []
        delta = None
        for i in range(4):
            both_signs = signed[0, j, i].astype(f32)
            weight = jnp.abs(both_signs)
            g_weight = jnp.where(both_signs > 0.0, g_droppeds[j][:, i * 128 : (i + 1) * 128], 0.0)
            term = g_weight * weight
            delta = term if delta is None else delta + term
            weights.append(weight)
            g_weights.append(g_weight)
            kept.append(jnp.maximum(both_signs, 0.0).astype(bf16))
        delta = jnp.sum(delta, axis=1, keepdims=True)
        g_scores = jnp.concatenate(
            [(weights[i] * (g_weights[i] - delta)).astype(bf16) for i in range(4)], axis=1
        )
        dropped = jnp.concatenate(kept, axis=1)
        out = jnp.dot(g_scores, keys[j], preferred_element_type=f32)
        out = jnp.where(lane_half((tokens, 128)), out[:tokens], out[tokens:])
        g_q[:, lanes] = (out * (0.125 * keep_scale)).astype(bf16)
        quarter = keys.shape[1] // 8
        sums[j, 0] = t_dot(g_scores, by_head(q[0, :, lanes])) * (0.125 * keep_scale)
        sums[j, 1] = t_dot(dropped, aboves[j]) * keep_scale
        for kind in range(2):
            for i in range(4):
                here = pl.multiple_of((2 * i + core) * quarter, quarter)
                there = pl.multiple_of((2 * i + 1 - core) * quarter, quarter)
                rows = slice(i * quarter, (i + 1) * quarter)
                g_near[kind][rows, lanes] = sums[j, kind, pl.ds(here, quarter), :]
                g_far[kind][rows, lanes] = sums[j, kind, pl.ds(there, quarter), :].astype(bf16)


def attention_back(ids, m, queries, near, far, signed, upstream):
    micro, tokens, width = queries.shape
    pairs = width // 128
    part = pl.BlockSpec((1, tokens, 128 * GROUP), lambda p, ids: (m, 0, p))
    flat = pl.BlockSpec((tokens // PARTS[m], 128 * GROUP), lambda p, ids: (0, p))
    both = pl.BlockSpec((tokens, 128 * GROUP), lambda p, ids: (0, p))
    operands = (ids, queries, *near[m], *far[m], signed, upstream)
    return call(
        functools.partial(attention_back_body, PARTS[m]),
        "attention_back",
        (pairs // GROUP,),
        operands,
        [part] + [flat] * (4 * PARTS[m])
        + [pl.BlockSpec((1, GROUP, 4, 2 * tokens, 128), lambda p, ids: (m, p, 0, 0, 0))]
        + [pl.BlockSpec((tokens, 128 * GROUP), lambda p, ids: (m, p))],
        [
            shaped((tokens, width), bf16),
            shaped((tokens, width), f32),
            shaped((tokens, width), f32),
            shaped((tokens, width), bf16),
            shaped((tokens, width), bf16),
        ],
        [both] * 5,
        [pltpu.VMEM((GROUP, 2 * tokens, 128), bf16)] * 2 + [pltpu.VMEM((GROUP, 2, 2 * tokens, 128), f32)],
        24,
        20,
    )


def up_body(weights, pers, tokens, ids, *refs):
    count = len(weights.operands)
    sources = refs[:count]
    context, hidden, keep, vectors, scaled, inverse, activated, slope = refs[count : count + 8]
    places, (sems, lows) = refs[count + 8 : -2], refs[-2:]
    copies = weights.copies(ids, sources, places, sems)
    rows, width = scaled.shape
    wide = activated.shape[1]
    begin([copies[0], copies[2], copies[1]])
    finish(copies[2])
    block = weights.matrix(places, 2)[:, :128].astype(f32).reshape(32, 8, 128)
    for row, per in enumerate(pers):
        vectors[row : row + 1, : 32 * per] = spread(block, row, 32 * per, per)
    finish(copies[0])
    for m in range(rows // tokens):
        at = slice(m * tokens, (m + 1) * tokens)
        attended = jnp.dot(context[at], weights.matrix(places, 0)[...], preferred_element_type=f32)
        attended = attended + vectors[0:1, :width]
        first_sum = hidden[at].astype(f32) + attended * (keep[at].astype(f32) * keep_scale)
        normal, scale = layer_norm(first_sum)
        scaled[at] = normal
        inverse[at] = jnp.broadcast_to(scale, (tokens, 128))
        lows[at] = (normal * vectors[1:2, :width] + vectors[2:3, :width]).astype(bf16)
    finish(copies[1])
    up = weights.matrix(places, 1)
    step = 512

    def part(n, carry):
        at = pl.ds(pl.multiple_of(n * step, step), step)
        inner = jnp.dot(lows[...], up[:, at], preferred_element_type=f32) + vectors[3:4, at]
        cdf = 0.5 * (1.0 + lax.erf(inner * root_half))
        density = jnp.exp(-0.5 * inner * inner) * inverse_root_tau
        activated[:, at] = (inner * cdf).astype(bf16)
        slope[:, at] = (cdf + inner * density).astype(bf16)
        return carry

    lax.fori_loop(0, wide // step, part, 0)


def feed_up(ids, weights, pers, context, hidden, keep, tokens, wide):
    rows, width = hidden.shape
    return call(
        functools.partial(up_body, weights, pers, tokens),
        "feed_up",
        (1,),
        (ids, *weights.operands, context, hidden, keep),
        weights.specs + [WHOLE] * 3,
        [
            shaped((8, wide), f32),
            shaped((rows, width), f32),
            shaped((rows, 128), f32),
            shaped((rows, wide), bf16),
            shaped((rows, wide), bf16),
        ],
        [WHOLE] * 5,
        weights.scratch + [pltpu.VMEM((rows, width), bf16)],
        28,
        24,
    )


def hand_out(core, total, rows, own, send, first, at):
    def one(n, carry):
        here = pl.multiple_of((2 * n + core) * rows, 8)
        there = pl.multiple_of((2 * n + 1 - core) * rows, 8)
        own[first + n, at : at + rows, :] = total[pl.ds(here, rows), :].astype(bf16)
        send[first + n, at : at + rows, :] = total[pl.ds(there, rows), :].astype(bf16)
        return carry

    lax.fori_loop(0, total.shape[0] // (2 * rows), one, 0)


def down_body(weights, tokens, ids, *refs):
    count = len(weights.operands)
    sources, refs = refs[:count], refs[count:]
    activated, slope, scaled, keep, cotangent, vectors = refs[:6]
    layer_out, g_second_out, g_inner, own, send, sums = refs[6:12]
    place, sems, total, g_outers = refs[12:]
    copies = weights.copies(ids, sources, (place,), sems)
    rows, width = scaled.shape
    wide = activated.shape[1]
    begin(copies)
    sums[...] = jnp.zeros_like(sums)
    finish(copies[0])
    down = weights.matrix((place,), 0)
    gain = vectors[5:6, :width]
    for m in range(rows // tokens):
        at = slice(m * tokens, (m + 1) * tokens)
        outer = jnp.dot(activated[at], down[...], preferred_element_type=f32) + vectors[4:5, :width]
        factor = keep[at].astype(f32) * keep_scale
        normed = scaled[at] * vectors[1:2, :width] + vectors[2:3, :width]
        normal, scale = layer_norm(normed + outer * factor)
        layer_out[at] = (normal * gain + vectors[6:7, :width]).astype(bf16)
        above = cotangent[at].astype(f32)
        weighted = above * gain
        g_second = scale * (
            weighted
            - jnp.mean(weighted, axis=-1, keepdims=True)
            - normal * jnp.mean(weighted * normal, axis=-1, keepdims=True)
        )
        g_second_out[at] = g_second
        g_outer = (g_second * factor).astype(bf16)
        g_outers[at] = g_outer
        sums[0:1, :width] += jnp.sum(g_outer.astype(f32), axis=0, keepdims=True)
        sums[1:2, :width] += jnp.sum(above * normal, axis=0, keepdims=True)
        sums[2:3, :width] += jnp.sum(above, axis=0, keepdims=True)
    step = 512

    def part(n, carry):
        at = pl.ds(pl.multiple_of(n * step, step), step)
        g_in = (dot_t(g_outers[...], down[at, :]) * slope[:, at].astype(f32)).astype(bf16)
        g_inner[:, at] = g_in
        sums[3:4, at] = jnp.sum(g_in.astype(f32), axis=0, keepdims=True)
        return carry

    lax.fori_loop(0, wide // step, part, 0)

    def grads(n, carry):
        at = pl.ds(pl.multiple_of(n * width, width), width)
        total[...] = t_dot(activated[:, at], g_outers[...])
        hand_out(ids[0], total, wide // 32, own, send, n * (16 * width // wide), 0)
        return carry

    lax.fori_loop(0, wide // width, grads, 0)


def feed_down(ids, weights, activated, slope, scaled, keep, cotangent, vectors, tokens):
    rows, width = scaled.shape
    wide = activated.shape[1]
    halves = (16, wide // 32, width)
    return call(
        functools.partial(down_body, weights, tokens),
        "feed_down",
        (1,),
        (ids, *weights.operands, activated, slope, scaled, keep, cotangent, vectors),
        weights.specs + [WHOLE] * 6,
        [
            shaped((rows, width), bf16),
            shaped((rows, width), f32),
            shaped((rows, wide), bf16),
            shaped(halves, bf16),
            shaped(halves, bf16),
            shaped((8, wide), f32),
        ],
        [WHOLE] * 6,
        weights.scratch + [pltpu.VMEM((width, width), f32), pltpu.VMEM((rows, width), bf16)],
        30,
        36,
    )


def middle_body(weights, pers, tokens, ids, *refs):
    count = len(weights.operands)
    sources, refs = refs[:count], refs[count:]
    g_inner, g_second, scaled, inverse, keep, vectors, context, down_sums = refs[:8]
    g_first_out, g_context, own, send, block = refs[8:13]
    *places, sems, g_normeds, g_attendeds, sums = refs[13:]
    copies = weights.copies(ids, sources, places, sems)
    begin([copies[1], copies[0]])
    rows, width = scaled.shape
    out_w, up_w = weights.matrix(places, 0), weights.matrix(places, 1)
    finish(copies[1])
    step = 256
    for n in range(width // step):
        at = slice(n * step, (n + 1) * step)
        g_normeds[:rows, at] = g_second[:, at] + dot_t(g_inner[...], up_w[at, :])
    sums[...] = jnp.zeros_like(sums)
    for m in range(rows // tokens):
        at = slice(m * tokens, (m + 1) * tokens)
        normal = scaled[at]
        g_normed = g_normeds[at, :]
        weighted = g_normed * vectors[1:2, :width]
        g_first = inverse[at, 0:1] * (
            weighted
            - jnp.mean(weighted, axis=-1, keepdims=True)
            - normal * jnp.mean(weighted * normal, axis=-1, keepdims=True)
        )
        g_first_out[at] = g_first
        g_attended = (g_first * (keep[at].astype(f32) * keep_scale)).astype(bf16)
        g_attendeds[at] = g_attended
        sums[0:1, :] += jnp.sum(g_attended.astype(f32), axis=0, keepdims=True)
        sums[1:2, :] += jnp.sum(g_normed * normal, axis=0, keepdims=True)
        sums[2:3, :] += jnp.sum(g_normed, axis=0, keepdims=True)
    finish(copies[0])
    g_context[...] = dot_t(g_attendeds[...], out_w[...]).astype(bf16)
    g_normeds[:width] = t_dot(context[...], g_attendeds[...])
    hand_out(ids[0], g_normeds, width // 32, own, send, 0, 0)
    vector_sums = [sums[n : n + 1, :] for n in range(3)]
    vector_sums += [down_sums[3:4, :]] + [down_sums[n : n + 1, :width] for n in range(3)]
    unspread(vector_sums, pers, block)


def middle(ids, weights, pers, g_inner, g_second, scaled, inverse, keep, vectors, context, sums, tokens):
    rows, width = scaled.shape
    halves = (16, width // 32, width)
    return call(
        functools.partial(middle_body, weights, pers, tokens),
        "middle",
        (1,),
        (ids, *weights.operands, g_inner, g_second, scaled, inverse, keep, vectors, context, sums),
        weights.specs + [WHOLE] * 8,
        [
            shaped((rows, width), f32),
            shaped((rows, width), bf16),
            shaped(halves, bf16),
            shaped(halves, bf16),
            shaped((32, 8, width), f32),
        ],
        [WHOLE] * 5,
        weights.scratch
        + [pltpu.VMEM((max(rows, width), width), f32), pltpu.VMEM((rows, width), bf16), pltpu.VMEM((8, width), f32)],
        26,
        18,
    )


def grads_body(ids, g_inner, scaled, vectors, own, send, total, low_t):
    n = pl.program_id(0)
    width = scaled.shape[1]

    @pl.when(n == 0)
    def _():
        low_t[...] = (scaled[...] * vectors[1:2, :width] + vectors[2:3, :width]).T.astype(bf16)

    total[...] = jnp.dot(low_t[...], g_inner[...], preferred_element_type=f32)
    for block in range(own.shape[1] // (width // 32)):

        @pl.when(n == block)
        def _():
            hand_out(ids[0], total, width // 32, own, send, 0, block * (width // 32))


def up_grads(ids, g_inner, scaled, vectors):
    rows, width = scaled.shape
    wide = g_inner.shape[1]
    halves = (16, wide // 32, width)
    return call(
        grads_body,
        "up_grads",
        (wide // width,),
        (ids, g_inner, scaled, vectors),
        [pl.BlockSpec((rows, width), lambda i, ids: (0, i))] + [WHOLE] * 2,
        [shaped(halves, bf16), shaped(halves, bf16)],
        [WHOLE] * 2,
        [pltpu.VMEM((width, width), f32), pltpu.VMEM((width, rows), bf16)],
        24,
        20,
    )


def hand_out_rows(core, block, own, send, at):
    for n in range(16):
        own[n, at : at + 8, :] = block[2 * n + core].astype(bf16)
        send[n, at : at + 8, :] = block[2 * n + 1 - core].astype(bf16)


def inputs_body(per, ids, hidden, turned, *refs):
    micro = (len(refs) - 8) // 5
    grads, (block, own, send, g_queries, g_keys, g_values, total, bias) = refs[: 5 * micro], refs[5 * micro :]
    width = hidden.shape[1]
    sums = []
    for n, out in enumerate((g_queries, g_keys, g_values)):
        for m in range(micro):
            g_q, near, far = grads[m], grads[micro + 2 * m :][:2], grads[3 * micro + 2 * m :][:2]
            rows = slice(m * g_q.shape[0], (m + 1) * g_q.shape[0])
            if n == 0:
                out[rows] = g_q[...]
            else:
                out[rows] = (near[n - 1][...] + far[n - 1][...].astype(f32)).astype(bf16)
        if n != 1:
            sums.append(jnp.sum(out[...].astype(f32), axis=0, keepdims=True))
        left = hidden if n == 0 else turned
        for start in range(0, width, 256):
            total[start : start + 256, :] = t_dot(left[:, start : start + 256], out[...])
        hand_out(ids[0], total, width // 32, own, send, 0, n * (width // 32))
    bias[...] = block[...]
    unspread([jnp.concatenate(sums, axis=1)], [per], bias, 7)
    hand_out_rows(ids[0], bias, own, send, 3 * (width // 32))


def input_grads(ids, hidden, turned, grads, block, per):
    rows, width = hidden.shape
    halves = (16, 3 * width // 32 + 8, width)
    return call(
        functools.partial(inputs_body, per),
        "input_grads",
        (1,),
        (ids, hidden, turned, *grads, block),
        [WHOLE] * (3 + len(grads)),
        [shaped(halves, bf16)] * 2 + [shaped((rows, width), bf16)] * 3,
        [WHOLE] * 5,
        [pltpu.VMEM((width, width), f32), pltpu.VMEM((32, 8, width), f32)],
        28,
        12,
    )


def last_body(weights, ids, *refs):
    count = len(weights.operands)
    sources = refs[:count]
    g_first, g_q, g_keys, g_values, out = refs[count : count + 5]
    places, sems = refs[count + 5 : -1], refs[-1]
    copies = weights.copies(ids, sources, places, sems)

    @pl.when(pl.program_id(0) == 0)
    def _():
        begin(copies)
        for group in copies:
            finish(group)

    turn = turn_matrix(g_q.shape[0])
    total = g_first[...] + dot_t(g_q[...], weights.matrix(places, 0)[...])
    total = total + dot_t(t_dot(turn, g_keys[...]).astype(bf16), weights.matrix(places, 1)[...])
    total = total + dot_t(t_dot(turn, g_values[...]).astype(bf16), weights.matrix(places, 2)[...])
    out[...] = total.astype(bf16)


def last(ids, weights, g_first, g_q, g_keys, g_values, tokens):
    rows, width = g_first.shape
    narrow = rows_spec(tokens, width)
    return call(
        functools.partial(last_body, weights),
        "input_back",
        (rows // tokens,),
        (ids, *weights.operands, g_first, g_q, g_keys, g_values),
        weights.specs + [narrow] * 4,
        [shaped((rows, width), bf16)],
        [narrow],
        weights.scratch,
        16,
        10,
    )[0]


def beside(shape, y, x):
    return pl.BlockSpec((4, 1, 1) + shape[3:], lambda i, ids: (0, ids[1] ^ y, ids[2] ^ x, 0, 0))


def rows_of(parts, index, first, last):
    found, start = [], 0
    for part in parts:
        rows = part.shape[-2]
        low, high = max(first, start), min(last, start + rows)
        if low < high:
            found.append(part[index + (slice(low - start, high - start),)].astype(f32))
        start += rows
    return found[0] if len(found) == 1 else jnp.concatenate(found, axis=-2)


def both(parts, index, first, last):
    half = len(parts) // 2
    return rows_of(parts[:half], index, first, last) + rows_of(parts[half:], index, first, last)


def count_rows(parts):
    return sum(part.shape[3] for part in parts[: len(parts) // 2])


PLANE = (slice(None), 0, 0)


def corner_body(ids, *refs):
    *parts, low, high = refs
    half = low.shape[1]
    low[...] = both(parts, PLANE, 0, half).astype(bf16)
    high[...] = both(parts, PLANE, half, half + high.shape[1]).astype(bf16)


def reduce_corner(ids, parts, cut):
    rows, width = count_rows(parts), parts[0].shape[4]
    return call(
        corner_body,
        "reduce_corner",
        (1,),
        (ids, *parts),
        [beside(part.shape, 1, 1) for part in parts],
        [shaped((4, cut, width), bf16), shaped((4, rows - cut, width), bf16)],
        [WHOLE] * 2,
        [],
        8,
        2,
    )


def sides_body(count, ids, *refs):
    for_y, for_x, (low, high, to_y, to_x) = refs[:count], refs[count : 2 * count], refs[2 * count :]
    rows, half = to_y.shape[1], low.shape[1]
    to_y[:, :half] = (both(for_y, PLANE, 0, half) + low[...].astype(f32)).astype(bf16)
    to_y[:, half:] = both(for_y, PLANE, half, rows).astype(bf16)
    to_x[:, :half] = both(for_x, PLANE, 0, half).astype(bf16)
    to_x[:, half:] = (both(for_x, PLANE, half, rows) + high[...].astype(f32)).astype(bf16)


def reduce_sides(ids, parts, low, high):
    rows, width = count_rows(parts), parts[0].shape[4]
    return call(
        functools.partial(sides_body, len(parts)),
        "reduce_sides",
        (1,),
        (ids, *parts, *parts, low, high),
        [beside(part.shape, 1, 0) for part in parts]
        + [beside(part.shape, 0, 1) for part in parts]
        + [WHOLE] * 2,
        [shaped((4, rows, width), bf16)] * 2,
        [WHOLE] * 2,
        [],
        10,
        3,
    )


def depth_body(ids, *refs):
    *parts, from_y, from_x, near, middle, far, mine = refs
    for k, out in enumerate((mine, near, middle, far)):
        z = ids[3] ^ k
        total = both(parts, (z, 0, 0), 0, from_y.shape[1])
        total = total + from_y[z].astype(f32) + from_x[z].astype(f32)
        out[...] = total.astype(out.dtype)


def reduce_depth(ids, parts, from_y, from_x):
    shape = from_y.shape[1:]
    return call(
        depth_body,
        "reduce_depth",
        (1,),
        (ids, *parts, from_y, from_x),
        [beside(part.shape, 0, 0) for part in parts] + [WHOLE] * 2,
        [shaped(shape, bf16)] * 3 + [shaped(shape, f32)],
        [WHOLE] * 4,
        [],
        10,
        3,
    )


def pair_body(ids, one, two, out):
    out[0] = one[...]
    out[1] = two[...]


def pair_z(ids, one, two):
    return call(
        pair_body,
        "pair_z",
        (1,),
        (ids, one, two),
        [WHOLE] * 2,
        [shaped((2,) + one.shape, bf16)],
        [WHOLE],
        [],
        4,
        1,
    )[0]


def order_body(ids, pair, received, out):
    for k in range(2):
        out[ids[3] ^ (2 * k)] = pair[k]
        out[ids[3] ^ (2 * k + 1)] = received[k]


def order_z(ids, pair, received):
    return call(
        order_body,
        "order_z",
        (1,),
        (ids, pair, received),
        [WHOLE] * 2,
        [shaped((4,) + pair.shape[1:], bf16)],
        [WHOLE],
        [],
        6,
        1,
    )[0]


def four_body(ids, *refs):
    *parts, out = refs
    for k, part in enumerate(parts):
        out[ids[3] ^ k] = part[...]


def order_four(ids, *parts):
    return call(
        four_body,
        "order_four",
        (1,),
        (ids, *parts),
        [WHOLE] * 4,
        [shaped((4,) + parts[0].shape, bf16)],
        [WHOLE],
        [],
        6,
        1,
    )[0]


def halves_body(ids, pair, received, low, high):
    rows = low.shape[1]
    for k in range(2):
        for source, z in ((pair, ids[3] ^ (2 * k)), (received, ids[3] ^ (2 * k + 1))):
            low[z] = source[k, :rows]
            high[z] = source[k, rows:]


def order_halves(ids, pair, received):
    shape = (4, pair.shape[1] // 2, pair.shape[2])
    return call(
        halves_body,
        "order_halves",
        (1,),
        (ids, pair, received),
        [WHOLE] * 2,
        [shaped(shape, bf16)] * 2,
        [WHOLE] * 2,
        [],
        6,
        1,
    )


def first_body(ids, *refs):
    at_y, at_x, at_corner, (to_y, to_x) = refs[:2], refs[2:4], refs[4:6], refs[6:]
    half = to_y.shape[1] // 2
    to_y[:, :half] = both(at_y, PLANE, 0, half).astype(bf16)
    to_y[:, half:] = both(at_corner, PLANE, 0, half).astype(bf16)
    to_x[:, :half] = both(at_x, PLANE, half, 2 * half).astype(bf16)
    to_x[:, half:] = both(at_corner, PLANE, half, 2 * half).astype(bf16)


def reduce_first(ids, parts):
    shape = parts[0].shape
    return call(
        first_body,
        "reduce_first",
        (1,),
        (ids, *parts, *parts, *parts),
        [beside(shape, 1, 0)] * 2 + [beside(shape, 0, 1)] * 2 + [beside(shape, 1, 1)] * 2,
        [shaped((4,) + shape[3:], bf16)] * 2,
        [WHOLE] * 2,
        [],
        10,
        3,
    )


def second_body(ids, *refs):
    here, at_y, at_x, (from_y, from_x, send, keep) = refs[:2], refs[2:4], refs[4:6], refs[6:]
    half = from_y.shape[1] // 2
    for k, (out, at) in enumerate(((keep, 0), (send, 0), (keep, 1), (send, 1))):
        z = ids[3] ^ k
        plane = (z, 0, 0)
        quarters = (
            both(here, plane, 0, half) + from_y[z, :half].astype(f32),
            both(at_x, plane, 0, half) + from_y[z, half:].astype(f32),
            both(here, plane, half, 2 * half) + from_x[z, :half].astype(f32),
            both(at_y, plane, half, 2 * half) + from_x[z, half:].astype(f32),
        )
        for i, quarter in enumerate(quarters):
            out[at, i * half : (i + 1) * half] = quarter.astype(out.dtype)


def reduce_second(ids, parts, from_y, from_x):
    shape = parts[0].shape
    wide = (2, 2 * shape[3], shape[4])
    return call(
        second_body,
        "reduce_second",
        (1,),
        (ids, *parts, *parts, *parts, from_y, from_x),
        [beside(shape, 0, 0)] * 2 + [beside(shape, 1, 0)] * 2 + [beside(shape, 0, 1)] * 2 + [WHOLE] * 2,
        [shaped(wide, bf16), shaped(wide, f32)],
        [WHOLE] * 2,
        [],
        14,
        3,
    )


def quarter_body(ids, keep, received, send, mine):
    mine[...] = keep[0] + received[0].astype(f32)
    send[...] = (keep[1] + received[1].astype(f32)).astype(bf16)


def reduce_third(ids, keep, received):
    shape = keep.shape[1:]
    return call(
        quarter_body,
        "reduce_third",
        (1,),
        (ids, keep, received),
        [WHOLE] * 2,
        [shaped(shape, bf16), shaped(shape, f32)],
        [WHOLE] * 2,
        [],
        10,
        2,
    )


def fourth_body(ids, mine, received, to_x, to_y, own):
    half = to_x.shape[0]
    total = mine[...] + received[...].astype(f32)
    own[:half] = total[:half]
    own[half:] = total[2 * half : 3 * half]
    to_x[...] = total[half : 2 * half].astype(bf16)
    to_y[...] = total[3 * half :].astype(bf16)


def reduce_fourth(ids, mine, received):
    rows, width = mine.shape
    return call(
        fourth_body,
        "reduce_fourth",
        (1,),
        (ids, mine, received),
        [WHOLE] * 2,
        [shaped((rows // 4, width), bf16)] * 2 + [shaped((rows // 2, width), f32)],
        [WHOLE] * 3,
        [],
        8,
        2,
    )


def exchange_z(sends):
    return [pp(send, "z", k) for send, k in zip(sends, (1, 2, 3))]


def local(
    hidden_in,
    cotangent,
    attention_keep,
    output_keep,
    feed_keep,
    qkv_weight,
    qkv_bias,
    out_weight,
    out_bias,
    first_gain,
    first_shift,
    up_weight,
    up_bias,
    down_weight,
    down_bias,
    second_gain,
    second_shift,
):
    micro, _, tokens, width = hidden_in.shape
    rows = micro * tokens
    own = qkv_weight.shape[0]
    wide = up_weight.shape[1]
    blocks = wide // width
    c, y, x = lax.axis_index("seq"), lax.axis_index("y"), lax.axis_index("x")
    ids = jnp.stack([c, y, x, lax.axis_index("z")]).astype(jnp.int32)
    bias_parts = (out_bias, first_gain, first_shift, up_bias, down_bias, second_gain, second_shift)
    pers = [part.shape[0] for part in bias_parts]
    per = qkv_bias.shape[0]

    column = lambda weight, i: weight[:, i * width : (i + 1) * width]
    bias_rows = lambda parts: jnp.concatenate(
        [jnp.pad(part.reshape(1, -1), ((0, 0), (0, width - part.shape[0]))) for part in parts]
        + [jnp.zeros((8 - len(parts), width), bf16)]
    )
    square = (own, width)
    hidden = hidden_in.reshape(rows, width)

    shard_a = jnp.concatenate([column(qkv_weight, i) for i in range(3)] + [bias_rows((qkv_bias,))])
    half_c = down_weight.shape[0] // 2
    x_c, y_c = pp(down_weight[:half_c], "x"), pp(down_weight[half_c:], "y")
    shard_b = jnp.concatenate(
        [out_weight] + [column(up_weight, i) for i in range(blocks)] + [bias_rows(bias_parts)]
    )
    z_a = hold([pp(shard_a, "z", k) for k in (1, 2, 3)], x_c, y_c, shard_b)
    own_a = order_four(ids, shard_a, *z_a)
    group_c = jnp.concatenate([down_weight[:half_c], x_c, down_weight[half_c:], y_c])
    x_a, y_a = pp(own_a, "x"), pp(own_a, "y")
    shard_b = after(shard_b, own_a)
    far_b = pp(shard_b, "z", 2)
    turned, keep_output, keep_feed = prepare(
        ids, after(hidden, own_a), output_keep.transpose(0, 1, 3, 2), feed_keep.transpose(0, 1, 3, 2), tokens
    )
    x_a, y_a, far_b = hold((x_a, y_a, far_b), turned)
    cut_a = shard_a.shape[0] // 2
    low_a, high_a = pp(x_a[:, :cut_a], "y"), pp(y_a[:, cut_a:], "x")
    pieces = [whole(0, 0, own_a), whole(1, 0, x_a), whole(2, 0, y_a), whole(3, 0, low_a), whole(3, cut_a, high_a)]
    late = whole(2, 0, after(y_a, low_a))
    pieces += [at_core(piece) for piece in pieces[:2] + [late] + pieces[3:]]
    pair_b = pair_z(ids, shard_b, far_b)
    near_b = pp(pair_b, "z", 1)
    plan = [(i * own, own, i, 0, 0) for i in range(3)]
    plan = divide(plan, cut_a)
    weights = Weights(pieces, plan + [(3 * own, 8, 3, 0, 0)], [square] * 3 + [(8, width)])
    weights_again = Weights(pieces, plan, [square] * 3)
    own_b = order_z(ids, pair_b, after(near_b, low_a, high_a))
    far_c = pp(after(group_c, own_b), "z", 2)
    x_b, y_b = pp(own_b, "x"), pp(own_b, "y")
    queries, *near = project(ids, weights, hidden, after(turned, own_b), micro, per)
    near = (near[: 2 * PARTS[0]], near[2 * PARTS[0] :])
    far = [[pp(value, "seq") for value in values] for values in near]
    words = attention_keep.reshape(micro, H, tokens, -1)
    *far[0], far_c = hold((*far[0], far_c))
    pair_c = pair_z(ids, group_c, far_c)
    near_c = pp(pair_c, "z", 1)
    context, signed = attention(ids, 0, after(queries, pair_c), near, far, words)
    own_b, x_b, y_b, *far[1] = hold((own_b, x_b, y_b, *far[1]), context)
    cut_b = shard_b.shape[0] // 2
    low_b, high_b = pp(x_b[:, :cut_b], "y"), pp(y_b[:, cut_b:], "x")
    context, signed = attention(ids, 1, queries, near, far, words, (context, signed))
    low_b, high_b, near_c = hold((low_b, high_b, near_c), context)
    pieces = [whole(0, 0, own_b), whole(1, 0, x_b), whole(2, 0, after(y_b, context))]
    pieces += [at_core(piece) for piece in pieces]
    corners = [whole(3, 0, low_b), whole(3, cut_b, high_b)]
    pieces += corners + [at_core(piece) for piece in corners]
    plan = [(0, own, 0, 0, 0)] + [((i + 1) * own, own, 1, 0, i * width) for i in range(blocks)]
    plan = divide(plan, cut_b)
    weights = Weights(
        pieces, plan + [((blocks + 1) * own, 8, 2, 0, 0)], [square, (own, wide), (8, width)]
    )
    back_weights = Weights(pieces, plan, [square, (own, wide)])
    by_x, by_y = order_halves(ids, pair_c, after(near_c, low_b, high_b))
    from_y, from_x = pp(by_x, "y"), pp(by_y, "x")
    context = context.reshape(rows, width)
    vectors, scaled, inverse, activated, slope = feed_up(
        ids, weights, pers, context, hidden, keep_output, tokens, wide
    )
    from_y, from_x = hold((from_y, from_x), activated)
    down_rows = down_weight.shape[0]
    pieces = []
    for core in range(2):
        held = [by_x, from_y, by_y, from_x]
        if core == 1:
            held = [pp(array, "seq") for array in held]
        for array, numbers, first in zip(held, ((0, 1), (2, 3), (0, 2), (1, 3)), (0, 0, half_c, half_c)):
            pieces += [(4 * core + number, first, array, i * half_c, half_c) for i, number in enumerate(numbers)]
    plan = divide([(0, down_rows, 0, 0, 0)], half_c)
    weights = Weights(pieces, plan, [(down_rows, width)])
    layer_out, g_second, g_inner, down_own, down_send, sums = feed_down(
        ids, weights, activated, slope, scaled, keep_feed, cotangent.reshape(rows, width), vectors, tokens
    )

    unit = lambda value: value.reshape((4, 2, 2) + value.shape[1:])
    down_core = pp(down_send, "seq")
    mid_own, mid_send = up_grads(ids, g_inner, scaled, vectors)
    down = [unit(down_own), unit(after(down_core, mid_send))]
    to_y, to_x = reduce_first(ids, down)
    down_y, down_x = pp(to_y, "y"), pp(to_x, "x")
    mid_core = pp(after(mid_send, to_y), "seq")
    g_first, g_context, out_own, out_send, block = middle(
        ids, back_weights, pers, after(g_inner, to_y), g_second, scaled, inverse, keep_output, vectors, context, sums, tokens
    )
    out_core = pp(out_send, "seq")
    down_y, down_x, mid_core = hold((down_y, down_x, mid_core), g_context)
    mid = [unit(value) for value in (mid_own, out_own, mid_core, out_core)]
    cut_m = (count_rows(mid) + 15) // 16 * 8
    corner = reduce_corner(ids, mid, cut_m)
    low, high = pp(corner[0], "x"), pp(corner[1], "y")
    down_send, down_keep = reduce_second(ids, down, down_y, down_x)
    down_near = pp(down_send, "z", 1)
    first_q, *first_near, far_k, far_v = attention_back(
        ids, 0, queries, near, far, signed, after(g_context, down_send, *corner)
    )
    low, high = hold((low, high), first_q)
    first_far = [pp(after(value, low, high), "seq") for value in (far_k, far_v)]
    to_y, to_x = reduce_sides(ids, mid, low, high)
    mid_y, mid_x = pp(to_y, "y"), pp(to_x, "x")
    second_q, *second_near, far_k, far_v = attention_back(
        ids, 1, queries, near, far, signed, after(g_context, to_y, to_x)
    )
    first_far = hold(first_far, second_q)
    second_far = [pp(value, "seq") for value in (far_k, far_v)]
    down_near = after(down_near, second_q)
    down_send, down_mine = reduce_third(ids, down_keep, down_near)
    down_far = pp(down_send, "z", 2)
    grads = (first_q, second_q, *first_near, *second_near, *first_far, *hold(second_far, down_send))
    a_own, a_send, g_q, g_keys, g_values = input_grads(ids, hidden, turned, grads, block, per)
    mid_y, mid_x = hold((mid_y, mid_x), a_send)
    down_far = after(down_far, a_send)
    core_sums = pp(after(a_send, mid_y, mid_x, down_far), "seq")
    to_far_x, to_far_y, down_mine = reduce_fourth(ids, down_mine, down_far)
    part = [unit(a_own), unit(core_sums)]
    corner = reduce_corner(ids, part, cut_a)
    low, high = pp(corner[0], "x"), pp(corner[1], "y")
    *sends, mid_mine = reduce_depth(ids, mid, after(mid_y, *corner), mid_x)
    mid_z = exchange_z(sends)
    low, high = hold((low, high), *sends)
    to_y, to_x = reduce_sides(ids, part, low, high)
    side_y, side_x = pp(to_y, "y"), pp(to_x, "x")
    received = [pp(after(to_far_x, to_x), "x"), pp(after(to_far_y, to_y), "y")]
    grad_in = last(
        ids, weights_again, g_first, g_q, g_keys, after(g_values, to_y, to_x), tokens
    )
    mid_z = hold(mid_z, grad_in)
    mid = add_up([mid_mine, *mid_z])
    side_y, side_x, *received = hold((side_y, side_x, *received), mid, grad_in)
    *sends, part_mine = reduce_depth(ids, part, side_y, side_x)
    grad_down = add_up([down_mine, jnp.concatenate(received)])
    part = add_up([part_mine, *exchange_z(sends)])

    stripe = lambda value, i: value[i * own : (i + 1) * own]
    grad_qkv = jnp.concatenate([stripe(part, i) for i in range(3)], axis=1)
    grad_up = jnp.concatenate([stripe(mid, i) for i in range(blocks)], axis=1)
    vector_grads = [part[3 * own + i, :length] for i, length in enumerate(pers)]
    grad_out = mid[blocks * own :]
    return (
        layer_out.reshape(hidden_in.shape),
        grad_in.reshape(hidden_in.shape),
        grad_qkv,
        part[3 * own + 7, :per],
        grad_out,
        vector_grads[0],
        vector_grads[1],
        vector_grads[2],
        grad_up,
        vector_grads[3],
        grad_down,
        vector_grads[4],
        vector_grads[5],
        vector_grads[6],
    )


def solution(mesh):
    groups, cores = mesh.devices.shape
    split = Mesh(mesh.devices.reshape(groups // 4, 2, 2, cores), ("z", "y", "x", "seq"))
    dp = ("z", "y", "x")
    token_rows = P(None, dp, "seq", None)
    matrix = P(every, None)
    vector = P(every)
    params = (matrix, vector, matrix, vector, vector, vector, matrix, vector, matrix, vector, vector, vector)

    def layer(*arrays):
        tiled = groups == 16 and cores == 2 and arrays[5].shape[0] % 8 == 0
        return (local if tiled else plain_local)(*arrays)

    return jax.shard_map(
        layer,
        mesh=split,
        in_specs=(token_rows, token_rows, P(None, dp, None, "seq", None), token_rows, token_rows) + params,
        out_specs=(token_rows, token_rows) + params,
        check_vma=False,
    )
```

```python
import functools

import jax
import jax.numpy as jnp
from jax import lax
from jax.experimental import pallas as pl
from jax.experimental.pallas import tpu as pltpu
from jax.sharding import Mesh
from jax.sharding import PartitionSpec as P

H = 12
epsilon = 1e-12
keep_scale = 8.0 / 7.0
root_half = 0.7071067811865476
inverse_root_tau = 0.3989422804014327
every = ("z", "y", "x", "seq")
f32 = jnp.float32
bf16 = jnp.bfloat16


def unpack_keep(packed_words):
    shifts = jnp.arange(4, dtype=jnp.int32) * 3
    nibble = jnp.right_shift(packed_words[..., None], shifts) & 7
    keep_value = (nibble >= 1).astype(jnp.float32) * keep_scale
    return keep_value.reshape(packed_words.shape[:-1] + (packed_words.shape[-1] * 4,))


def normalize(values, norm_gain, norm_shift):
    centred = values - jnp.mean(values, axis=-1, keepdims=True)
    inverse = lax.rsqrt(jnp.mean(centred * centred, axis=-1, keepdims=True) + epsilon)
    scaled = centred * inverse
    return (scaled * norm_gain + norm_shift, scaled, inverse)


def norm_back(upstream, scaled, inverse, norm_gain):
    weighted = upstream * norm_gain
    centre_term = jnp.mean(weighted, axis=-1, keepdims=True)
    slope_term = jnp.mean(weighted * scaled, axis=-1, keepdims=True)
    return inverse * (weighted - centre_term - scaled * slope_term)


def gelu_slope(inner_sum):
    normal_cdf = 0.5 * (1.0 + lax.erf(inner_sum * root_half))
    density = jnp.exp(-0.5 * inner_sum * inner_sum) * inverse_root_tau
    return normal_cdf + inner_sum * density


def matmul(left_side, right_side):
    return jnp.dot(left_side, right_side, preferred_element_type=jnp.float32)


def plain_local(
    hidden_in,
    cotangent,
    attention_keep,
    output_keep,
    feed_keep,
    qkv_weight,
    qkv_bias,
    out_weight,
    out_bias,
    first_gain,
    first_shift,
    up_weight,
    up_bias,
    down_weight,
    down_bias,
    second_gain,
    second_shift,
):
    model_width = hidden_in.shape[-1]
    sequence_count = hidden_in.shape[1]
    local_tokens = hidden_in.shape[2]
    token_rows = sequence_count * local_tokens
    head_count = H
    head_size = model_width // head_count
    held_params = (
        lax.all_gather(qkv_weight, every, axis=0, tiled=True),
        lax.all_gather(qkv_bias, every, axis=0, tiled=True),
        lax.all_gather(out_weight, every, axis=0, tiled=True),
        lax.all_gather(out_bias, every, axis=0, tiled=True),
        lax.all_gather(first_gain, every, axis=0, tiled=True),
        lax.all_gather(first_shift, every, axis=0, tiled=True),
        lax.all_gather(up_weight, every, axis=0, tiled=True),
        lax.all_gather(up_bias, every, axis=0, tiled=True),
        lax.all_gather(down_weight, every, axis=0, tiled=True),
        lax.all_gather(down_bias, every, axis=0, tiled=True),
        lax.all_gather(second_gain, every, axis=0, tiled=True),
        lax.all_gather(second_shift, every, axis=0, tiled=True),
    )
    totals = None
    outputs = []
    inputs_grad = []
    for micro_step in range(hidden_in.shape[0]):
        (
            full_qkv_w,
            full_qkv_b,
            full_out_w,
            full_out_b,
            full_gain_one,
            full_shift_one,
            full_up_w,
            full_up_b,
            full_down_w,
            full_down_b,
            full_gain_two,
            full_shift_two,
        ) = held_params
        rows_in = hidden_in[micro_step].reshape(token_rows, model_width)
        qkv_float = full_qkv_b.astype(jnp.float32)
        bias_full = jnp.concatenate(
            [
                qkv_float[:model_width],
                jnp.zeros((model_width,), jnp.float32),
                qkv_float[model_width:],
            ]
        )
        projected = (matmul(rows_in, full_qkv_w) + bias_full).astype(jnp.bfloat16)
        queries = projected[:, :model_width].reshape(
            sequence_count, local_tokens, head_count, head_size
        )
        keys_local = projected[:, model_width : 2 * model_width].reshape(
            sequence_count, local_tokens, model_width
        )
        values_local = projected[:, 2 * model_width :].reshape(
            sequence_count, local_tokens, model_width
        )
        keys_all, values_all = (
            lax.all_gather(keys_local, "seq", axis=1, tiled=True),
            lax.all_gather(values_local, "seq", axis=1, tiled=True),
        )
        keys_heads = keys_all.reshape(sequence_count, -1, head_count, head_size)
        values_heads = values_all.reshape(sequence_count, -1, head_count, head_size)
        scores = (
            jnp.einsum("sqhd,skhd->shqk", queries, keys_heads, preferred_element_type=jnp.float32)
            * 0.125
        )
        row_peak = jnp.max(scores, axis=-1, keepdims=True)
        exponent = jnp.exp(scores - row_peak)
        row_total = jnp.sum(exponent, axis=-1, keepdims=True)
        log_total = row_peak + jnp.log(row_total)
        softmax_weights = exponent / row_total
        keep_attention = unpack_keep(attention_keep[micro_step])
        dropped = (softmax_weights * keep_attention).astype(jnp.bfloat16)
        context = jnp.einsum(
            "shqk,skhd->sqhd", dropped, values_heads, preferred_element_type=jnp.float32
        )
        context = context.reshape(token_rows, model_width).astype(jnp.bfloat16)
        attended = matmul(context, full_out_w) + full_out_b.astype(jnp.float32)
        keep_output = unpack_keep(output_keep[micro_step]).reshape(token_rows, model_width)
        first_sum = rows_in.astype(jnp.float32) + attended * keep_output
        gain_one = full_gain_one.astype(jnp.float32)
        normed, scaled_one, inverse_one = normalize(
            first_sum, gain_one, full_shift_one.astype(jnp.float32)
        )
        normed_low = normed.astype(jnp.bfloat16)
        inner_sum = matmul(normed_low, full_up_w) + full_up_b.astype(jnp.float32)
        activated = jax.nn.gelu(inner_sum, approximate=False).astype(jnp.bfloat16)
        outer_sum = matmul(activated, full_down_w) + full_down_b.astype(jnp.float32)
        keep_feed = unpack_keep(feed_keep[micro_step]).reshape(token_rows, model_width)
        second_sum = normed + outer_sum * keep_feed
        gain_two = full_gain_two.astype(jnp.float32)
        result, scaled_two, inverse_two = normalize(
            second_sum, gain_two, full_shift_two.astype(jnp.float32)
        )
        outputs.append(
            result.astype(jnp.bfloat16).reshape(sequence_count, local_tokens, model_width)
        )
        (
            back_qkv_w,
            back_qkv_b,
            back_out_w,
            back_out_b,
            back_gain_one,
            back_shift_one,
            back_up_w,
            back_up_b,
            back_down_w,
            back_down_b,
            back_gain_two,
            back_shift_two,
        ) = held_params
        upstream = cotangent[micro_step].reshape(token_rows, model_width).astype(jnp.float32)
        g_second = norm_back(upstream, scaled_two, inverse_two, back_gain_two.astype(jnp.float32))
        grad_gain_two = jnp.sum(upstream * scaled_two, axis=0)
        grad_shift_two = jnp.sum(upstream, axis=0)
        g_outer = (g_second * keep_feed).astype(jnp.bfloat16)
        grad_down_b = jnp.sum(g_outer.astype(jnp.float32), axis=0)
        grad_down_w = matmul(activated.T, g_outer)
        g_inner = (matmul(g_outer, back_down_w.T) * gelu_slope(inner_sum)).astype(jnp.bfloat16)
        grad_up_b = jnp.sum(g_inner.astype(jnp.float32), axis=0)
        grad_up_w = matmul(normed_low.T, g_inner)
        g_normed = g_second + matmul(g_inner, back_up_w.T)
        g_first = norm_back(g_normed, scaled_one, inverse_one, back_gain_one.astype(jnp.float32))
        grad_gain_one = jnp.sum(g_normed * scaled_one, axis=0)
        grad_shift_one = jnp.sum(g_normed, axis=0)
        g_attended = (g_first * keep_output).astype(jnp.bfloat16)
        grad_out_b = jnp.sum(g_attended.astype(jnp.float32), axis=0)
        grad_out_w = matmul(context.T, g_attended)
        g_context = matmul(g_attended, back_out_w.T).astype(jnp.bfloat16)
        g_context = g_context.reshape(sequence_count, local_tokens, head_count, head_size)
        keys_again, values_again = (
            lax.all_gather(keys_local, "seq", axis=1, tiled=True),
            lax.all_gather(values_local, "seq", axis=1, tiled=True),
        )
        keys_heads = keys_again.reshape(sequence_count, -1, head_count, head_size)
        values_heads = values_again.reshape(sequence_count, -1, head_count, head_size)
        scores_again = (
            jnp.einsum("sqhd,skhd->shqk", queries, keys_heads, preferred_element_type=jnp.float32)
            * 0.125
        )
        weights_again = jnp.exp(scores_again - log_total)
        dropped_again = (weights_again * keep_attention).astype(jnp.bfloat16)
        g_values_all = jnp.einsum(
            "shqk,sqhd->skhd", dropped_again, g_context, preferred_element_type=jnp.float32
        )
        g_dropped = jnp.einsum(
            "sqhd,skhd->shqk", g_context, values_heads, preferred_element_type=jnp.float32
        )
        g_weights = g_dropped * keep_attention
        row_delta = jnp.sum(g_weights * weights_again, axis=-1, keepdims=True)
        g_scores = (weights_again * (g_weights - row_delta)).astype(jnp.bfloat16)
        g_queries = (
            jnp.einsum("shqk,skhd->sqhd", g_scores, keys_heads, preferred_element_type=jnp.float32)
            * 0.125
        )
        g_keys_all = (
            jnp.einsum("shqk,sqhd->skhd", g_scores, queries, preferred_element_type=jnp.float32)
            * 0.125
        )
        g_keys, g_values = (
            lax.psum_scatter(
                g_keys_all.reshape(sequence_count, -1, model_width).astype(jnp.bfloat16),
                "seq",
                scatter_dimension=1,
                tiled=True,
            ).astype(jnp.float32),
            lax.psum_scatter(
                g_values_all.reshape(sequence_count, -1, model_width).astype(jnp.bfloat16),
                "seq",
                scatter_dimension=1,
                tiled=True,
            ).astype(jnp.float32),
        )
        g_projected = jnp.concatenate(
            [
                g_queries.reshape(token_rows, model_width),
                g_keys.reshape(token_rows, model_width),
                g_values.reshape(token_rows, model_width),
            ],
            axis=1,
        ).astype(jnp.bfloat16)
        g_projected_float = g_projected.astype(jnp.float32)
        grad_qkv_b = jnp.concatenate(
            [
                jnp.sum(g_projected_float[:, :model_width], axis=0),
                jnp.sum(g_projected_float[:, 2 * model_width :], axis=0),
            ]
        )
        grad_qkv_w = matmul(rows_in.T, g_projected)
        input_grad = g_first + matmul(g_projected, back_qkv_w.T)
        inputs_grad.append(
            input_grad.astype(jnp.bfloat16).reshape(sequence_count, local_tokens, model_width)
        )
        grads_now = (
            grad_qkv_w,
            grad_qkv_b,
            grad_out_w,
            grad_out_b,
            grad_gain_one,
            grad_shift_one,
            grad_up_w,
            grad_up_b,
            grad_down_w,
            grad_down_b,
            grad_gain_two,
            grad_shift_two,
        )
        if totals is None:
            totals = grads_now
        else:
            totals = tuple((before + added for before, added in zip(totals, grads_now)))
    summed = (
        lax.psum_scatter(totals[0], every, scatter_dimension=0, tiled=True),
        lax.psum_scatter(totals[1], every, scatter_dimension=0, tiled=True),
        lax.psum_scatter(totals[2], every, scatter_dimension=0, tiled=True),
        lax.psum_scatter(totals[3], every, scatter_dimension=0, tiled=True),
        lax.psum_scatter(totals[4], every, scatter_dimension=0, tiled=True),
        lax.psum_scatter(totals[5], every, scatter_dimension=0, tiled=True),
        lax.psum_scatter(totals[6], every, scatter_dimension=0, tiled=True),
        lax.psum_scatter(totals[7], every, scatter_dimension=0, tiled=True),
        lax.psum_scatter(totals[8], every, scatter_dimension=0, tiled=True),
        lax.psum_scatter(totals[9], every, scatter_dimension=0, tiled=True),
        lax.psum_scatter(totals[10], every, scatter_dimension=0, tiled=True),
        lax.psum_scatter(totals[11], every, scatter_dimension=0, tiled=True),
    )
    return (
        jnp.stack(outputs, axis=0),
        jnp.stack(inputs_grad, axis=0),
        summed[0],
        summed[1],
        summed[2],
        summed[3],
        summed[4],
        summed[5],
        summed[6],
        summed[7],
        summed[8],
        summed[9],
        summed[10],
        summed[11],
    )


ANY = pl.BlockSpec(memory_space=pl.ANY)
WHOLE = pl.BlockSpec(memory_space=pltpu.VMEM)
MIB = 2**20
PARTS = (2, 1)
GROUP = 2


def dot_t(left_side, right_side):
    return lax.dot_general(left_side, right_side, (((1,), (1,)), ((), ())), preferred_element_type=f32)


def t_dot(left_side, right_side):
    return lax.dot_general(left_side, right_side, (((0,), (0,)), ((), ())), preferred_element_type=f32)


def iota(shape, axis):
    return lax.broadcasted_iota(jnp.int32, shape, axis)


def pp(value, axis, step=1):
    size = lax.axis_size(axis)
    return lax.ppermute(value, axis, [(i, i ^ step) for i in range(size)])


def pick(value, axis, index):
    return lax.dynamic_index_in_dim(value, index, axis, keepdims=False)


def after(value, *earlier):
    return lax.optimization_barrier((value,) + earlier)[0]


def hold(values, *earlier):
    return lax.optimization_barrier(tuple(values) + earlier)[: len(values)]


def add_up(terms):
    total = terms[0].astype(f32)
    for term in terms[1:]:
        total = total + term.astype(f32)
    return total


def divide(plan, cut):
    parts = []
    for start, rows, out, row, column in plan:
        ends = [start, cut, start + rows] if start < cut < start + rows else [start, start + rows]
        for first, last in zip(ends, ends[1:]):
            parts.append((first, last - first, out, row + first - start, column))
    return parts


def whole(number, first, array):
    return (number, first, array, 0, array.shape[1])


def at_core(piece):
    number, first, array, row, rows = piece
    return (number + 4, first, pp(array, "seq"), row, rows)


class Weights:
    def __init__(self, pieces, plan, shapes):
        arrays = []
        self.spans = []
        for number, first, array, row, rows in pieces:
            place = next((i for i, held in enumerate(arrays) if held is array), len(arrays))
            if place == len(arrays):
                arrays.append(array)
            self.spans.append((number, first, place, row, rows))
        self.operands = [pltpu.with_memory_space_constraint(array, pltpu.HBM) for array in arrays]
        self.plan, self.shapes = plan, shapes
        self.specs = [pl.BlockSpec(memory_space=pltpu.HBM)] * len(arrays)
        self.scratch = [pltpu.VMEM((4, 2, 2, 2, rows, columns), bf16) for rows, columns in shapes]
        self.scratch.append(pltpu.SemaphoreType.DMA((8 * len(plan),)))

    def copies(self, ids, sources, places, sems):
        found = [[] for _ in self.shapes]
        count = 0
        for start, rows, out, row, column in self.plan:
            for number, first, place, source_row, held in self.spans:
                if first <= start and start + rows <= first + held:
                    c = ids[0] ^ (number >> 2)
                    y = ids[1] ^ ((number >> 1) & 1)
                    x = ids[2] ^ (number & 1)
                    source = sources[place]
                    src = source.at[:, pl.ds(source_row + start - first, rows), :]
                    dst = places[out].at[:, y, x, c, pl.ds(row, rows), pl.ds(column, source.shape[2])]
                    found[out].append(pltpu.make_async_copy(src, dst, sems.at[count]))
                    count += 1
        return found

    def matrix(self, places, out):
        rows, columns = self.shapes[out]
        return places[out].reshape(32 * rows, columns)


def begin(copies):
    for group in copies:
        for copy in group:
            copy.start()


def finish(group):
    for copy in group:
        copy.wait()


def spread(block, row, count, per):
    values = block[:, row, : -(-per // 128) * 128].astype(bf16)
    lanes = values.shape[1]
    select = (iota((lanes, count), 1) % per == iota((lanes, count), 0)).astype(bf16)
    wide = jnp.dot(values, select, preferred_element_type=f32)
    return jnp.sum(jnp.where(iota(wide.shape, 1) // per == iota(wide.shape, 0), wide, 0.0), axis=0, keepdims=True)


def unspread(vectors, pers, block, first=0):
    block[:, first:] = jnp.zeros((32, 8 - first, block.shape[2]), f32)
    for row, (vector, per) in enumerate(zip(vectors, pers), first):
        count = vector.shape[1]
        lanes = -(-per // 128) * 128
        shape = (32, count)
        wide = jnp.where(iota(shape, 1) // per == iota(shape, 0), vector, 0.0).astype(bf16)
        select = (iota((count, lanes), 0) % per == iota((count, lanes), 1)).astype(bf16)
        block[:, row, :lanes] = jnp.dot(wide, select, preferred_element_type=f32)


def layer_norm(values):
    centred = values - jnp.mean(values, axis=-1, keepdims=True)
    inverse = lax.rsqrt(jnp.mean(centred * centred, axis=-1, keepdims=True) + epsilon)
    return centred * inverse, inverse


def turn_matrix(tokens):
    place = iota((tokens, tokens), 0)
    quarter = tokens // 4
    return (iota((tokens, tokens), 1) == 4 * (place % quarter) + place // quarter).astype(bf16)


def call(body, name, grid, operands, specs, outs, out_specs, scratch, room, load, aliases=None):
    return pl.pallas_call(
        body,
        grid_spec=pltpu.PrefetchScalarGridSpec(
            num_scalar_prefetch=1, grid=grid, in_specs=specs, out_specs=out_specs, scratch_shapes=scratch
        ),
        out_shape=outs,
        compiler_params=pltpu.CompilerParams(vmem_limit_bytes=room * MIB),
        cost_estimate=pl.CostEstimate(flops=1024, bytes_accessed=load * MIB // 16, transcendentals=0),
        input_output_aliases=aliases or {},
        name=name,
    )(*operands)


def shaped(shape, dtype):
    return jax.ShapeDtypeStruct(shape, dtype)


def rows_spec(rows, columns):
    return pl.BlockSpec((rows, columns), lambda i, ids: (i, 0))


def fixed_spec(shape):
    return pl.BlockSpec(shape, lambda i, ids: (0,) * len(shape))


def prepare_body(ids, hidden, output_words, feed_words, turned, keep_output, keep_feed):
    tokens, width = hidden.shape
    turned[...] = jnp.dot(turn_matrix(tokens), hidden[...], preferred_element_type=f32).astype(bf16)
    quarter = width // 4
    for words, keep in ((output_words, keep_output), (feed_words, keep_feed)):
        packed = words[0, 0]
        total = jnp.zeros((tokens, width), f32)
        for i in range(4):
            bit = ((packed & (7 << (3 * i))) != 0).astype(f32).astype(bf16)
            place = (iota((quarter, width), 1) == 4 * iota((quarter, width), 0) + i).astype(bf16)
            total = total + t_dot(bit, place)
        keep[...] = total.astype(bf16)


def prepare(ids, hidden, output_words, feed_words, tokens):
    rows, width = hidden.shape
    wide = rows_spec(tokens, width)
    narrow = pl.BlockSpec((1, 1, width // 4, tokens), lambda i, ids: (i, 0, 0, 0))
    return call(
        prepare_body,
        "prepare",
        (rows // tokens,),
        (ids, hidden, output_words, feed_words),
        [wide, narrow, narrow],
        [shaped((rows, width), bf16)] * 3,
        [wide] * 3,
        [],
        12,
        6,
    )


def project_body(weights, per, ids, *refs):
    count = len(weights.operands)
    sources, (hidden, turned, queries), rest = refs[:count], refs[count : count + 3], refs[count + 3 :]
    micro, tokens, width = queries.shape
    places, sems = rest[len(rest) - 1 - len(weights.shapes) : -1], rest[-1]
    near = iter(rest[: len(rest) - 1 - len(weights.shapes)])
    copies = weights.copies(ids, sources, places, sems)
    begin(copies)
    finish(copies[3])
    block = weights.matrix(places, 3)[:, :128].astype(f32).reshape(32, 8, 128)
    bias = spread(block, 0, 2 * width, per)
    for n in range(3):
        finish(copies[n])
    for m in range(micro):
        natural, other = hidden[m * tokens : (m + 1) * tokens, :], turned[m * tokens : (m + 1) * tokens, :]
        q = jnp.dot(natural, weights.matrix(places, 0)[...], preferred_element_type=f32) + bias[:, :width]
        queries[m] = q.astype(bf16)
        k = jnp.dot(other, weights.matrix(places, 1)[...], preferred_element_type=f32).astype(bf16)
        v = jnp.dot(other, weights.matrix(places, 2)[...], preferred_element_type=f32) + bias[:, width:]
        for value in (k, v.astype(bf16)):
            rows = tokens // PARTS[m]
            for part in range(PARTS[m]):
                next(near)[...] = value[part * rows : (part + 1) * rows]


def project(ids, weights, hidden, turned, micro, per):
    rows, width = hidden.shape
    return call(
        functools.partial(project_body, weights, per),
        "project",
        (1,),
        (ids, *weights.operands, hidden, turned),
        weights.specs + [WHOLE] * 2,
        [shaped((micro, rows // micro, width), bf16)]
        + [shaped((rows // micro // PARTS[m], width), bf16) for m in range(micro) for _ in range(2 * PARTS[m])],
        [WHOLE] * (1 + 2 * sum(PARTS)),
        weights.scratch,
        16,
        10,
    )


def lane_half(shape):
    return iota(shape, len(shape) - 1) < 64


def by_head(pair):
    left, zero = lane_half(pair.shape), jnp.zeros_like(pair)
    return jnp.concatenate([jnp.where(left, pair, zero), jnp.where(left, zero, pair)], axis=0)


def join_keys(core, near, far, buffer, lanes):
    quarter = buffer.shape[0] // 8
    parts = len(near)
    for i in range(4):
        here = pl.multiple_of((2 * i + core) * quarter, quarter)
        there = pl.multiple_of((2 * i + 1 - core) * quarter, quarter)
        at = (i * parts % 4) // parts * quarter
        buffer[pl.ds(here, quarter), :] = near[i * parts // 4][at : at + quarter, lanes]
        buffer[pl.ds(there, quarter), :] = far[i * parts // 4][at : at + quarter, lanes]


def group_lanes():
    return [slice(j * 128, (j + 1) * 128) for j in range(GROUP)]


def attention_body(parts, ids, q, *refs):
    ours, words = refs[: 4 * parts], refs[4 * parts]
    context, signed, keys, values = refs[-4:]
    core = ids[0]
    tokens = q.shape[1]
    for j, lanes in enumerate(group_lanes()):
        join_keys(core, ours[:parts], ours[2 * parts : 3 * parts], keys.at[j], lanes)
        join_keys(core, ours[parts : 2 * parts], ours[3 * parts :], values.at[j], lanes)
    scores = [dot_t(by_head(q[0, :, lanes]) * 0.125, keys[j]) for j, lanes in enumerate(group_lanes())]
    for j, lanes in enumerate(group_lanes()):
        blocks = [scores[j][:, i * 128 : (i + 1) * 128] for i in range(4)]
        peak = jnp.maximum(jnp.maximum(blocks[0], blocks[1]), jnp.maximum(blocks[2], blocks[3]))
        peak = jnp.max(peak, axis=1, keepdims=True)
        blocks = [jnp.exp(block - peak) for block in blocks]
        total = jnp.sum((blocks[0] + blocks[1]) + (blocks[2] + blocks[3]), axis=1, keepdims=True)
        scale = 1.0 / total
        word = words[0, 2 * j : 2 * j + 2].reshape(2 * tokens, 128)
        dropped = []
        for i in range(4):
            weight = blocks[i] * scale
            keep = (word & (7 << (3 * i))) != 0
            weight = jnp.where(keep, weight, -weight).astype(bf16)
            signed[0, j, i] = weight
            dropped.append(jnp.maximum(weight, jnp.zeros_like(weight)))
        out = jnp.dot(jnp.concatenate(dropped, axis=1), values[j], preferred_element_type=f32) * keep_scale
        context[0, :, lanes] = jnp.where(lane_half((tokens, 128)), out[:tokens], out[tokens:]).astype(bf16)


def attention(ids, m, queries, near, far, words, earlier=()):
    micro, tokens, width = queries.shape
    pairs = width // 128
    part = pl.BlockSpec((1, tokens, 128 * GROUP), lambda p, ids: (m, 0, p))
    flat = pl.BlockSpec((tokens // PARTS[m], 128 * GROUP), lambda p, ids: (0, p))
    operands = (ids, queries, *near[m], *far[m], words)
    return call(
        functools.partial(attention_body, PARTS[m]),
        "attention",
        (pairs // GROUP,),
        operands + tuple(earlier),
        [part] + [flat] * (4 * PARTS[m])
        + [pl.BlockSpec((1, 2 * GROUP, tokens, 128), lambda p, ids: (m, p, 0, 0))]
        + [ANY] * len(earlier),
        [shaped((micro, tokens, width), bf16), shaped((micro, pairs, 4, 2 * tokens, 128), bf16)],
        [part, pl.BlockSpec((1, GROUP, 4, 2 * tokens, 128), lambda p, ids: (m, p, 0, 0, 0))],
        [pltpu.VMEM((GROUP, 2 * tokens, 128), bf16)] * 2,
        16,
        14,
        {len(operands) + i: i for i in range(len(earlier))},
    )


def attention_back_body(parts, ids, q, *refs):
    ours, signed, upstream, refs = refs[: 4 * parts], refs[4 * parts], refs[4 * parts + 1], refs[4 * parts + 2 :]
    g_q, *grads, keys, values, sums = refs
    g_near, g_far = grads[:2], grads[2:]
    core = ids[0]
    tokens = q.shape[1]
    for j, lanes in enumerate(group_lanes()):
        join_keys(core, ours[:parts], ours[2 * parts : 3 * parts], keys.at[j], lanes)
        join_keys(core, ours[parts : 2 * parts], ours[3 * parts :], values.at[j], lanes)
    aboves = [by_head(upstream[:, lanes]) for lanes in group_lanes()]
    g_droppeds = [dot_t(aboves[j], values[j]) for j in range(GROUP)]
    for j, lanes in enumerate(group_lanes()):
        weights, kept, g_weights = [], [], []
        delta = None
        for i in range(4):
            both_signs = signed[0, j, i].astype(f32)
            weight = jnp.abs(both_signs)
            g_weight = jnp.where(both_signs > 0.0, g_droppeds[j][:, i * 128 : (i + 1) * 128], 0.0)
            term = g_weight * weight
            delta = term if delta is None else delta + term
            weights.append(weight)
            g_weights.append(g_weight)
            kept.append(jnp.maximum(both_signs, 0.0).astype(bf16))
        delta = jnp.sum(delta, axis=1, keepdims=True)
        g_scores = jnp.concatenate(
            [(weights[i] * (g_weights[i] - delta)).astype(bf16) for i in range(4)], axis=1
        )
        dropped = jnp.concatenate(kept, axis=1)
        out = jnp.dot(g_scores, keys[j], preferred_element_type=f32)
        out = jnp.where(lane_half((tokens, 128)), out[:tokens], out[tokens:])
        g_q[:, lanes] = (out * (0.125 * keep_scale)).astype(bf16)
        quarter = keys.shape[1] // 8
        sums[j, 0] = t_dot(g_scores, by_head(q[0, :, lanes])) * (0.125 * keep_scale)
        sums[j, 1] = t_dot(dropped, aboves[j]) * keep_scale
        for kind in range(2):
            for i in range(4):
                here = pl.multiple_of((2 * i + core) * quarter, quarter)
                there = pl.multiple_of((2 * i + 1 - core) * quarter, quarter)
                rows = slice(i * quarter, (i + 1) * quarter)
                g_near[kind][rows, lanes] = sums[j, kind, pl.ds(here, quarter), :]
                g_far[kind][rows, lanes] = sums[j, kind, pl.ds(there, quarter), :].astype(bf16)


def attention_back(ids, m, queries, near, far, signed, upstream):
    micro, tokens, width = queries.shape
    pairs = width // 128
    part = pl.BlockSpec((1, tokens, 128 * GROUP), lambda p, ids: (m, 0, p))
    flat = pl.BlockSpec((tokens // PARTS[m], 128 * GROUP), lambda p, ids: (0, p))
    both = pl.BlockSpec((tokens, 128 * GROUP), lambda p, ids: (0, p))
    operands = (ids, queries, *near[m], *far[m], signed, upstream)
    return call(
        functools.partial(attention_back_body, PARTS[m]),
        "attention_back",
        (pairs // GROUP,),
        operands,
        [part] + [flat] * (4 * PARTS[m])
        + [pl.BlockSpec((1, GROUP, 4, 2 * tokens, 128), lambda p, ids: (m, p, 0, 0, 0))]
        + [pl.BlockSpec((tokens, 128 * GROUP), lambda p, ids: (m, p))],
        [
            shaped((tokens, width), bf16),
            shaped((tokens, width), f32),
            shaped((tokens, width), f32),
            shaped((tokens, width), bf16),
            shaped((tokens, width), bf16),
        ],
        [both] * 5,
        [pltpu.VMEM((GROUP, 2 * tokens, 128), bf16)] * 2 + [pltpu.VMEM((GROUP, 2, 2 * tokens, 128), f32)],
        24,
        20,
    )


def up_body(weights, pers, tokens, ids, *refs):
    count = len(weights.operands)
    sources = refs[:count]
    context, hidden, keep, vectors, scaled, inverse, activated, slope = refs[count : count + 8]
    places, (sems, lows) = refs[count + 8 : -2], refs[-2:]
    copies = weights.copies(ids, sources, places, sems)
    rows, width = scaled.shape
    wide = activated.shape[1]
    begin([copies[0], copies[2], copies[1]])
    finish(copies[2])
    block = weights.matrix(places, 2)[:, :128].astype(f32).reshape(32, 8, 128)
    for row, per in enumerate(pers):
        vectors[row : row + 1, : 32 * per] = spread(block, row, 32 * per, per)
    finish(copies[0])

    def rows_part(m, carry):
        at = pl.ds(pl.multiple_of(m * tokens, tokens), tokens)
        attended = jnp.dot(context[at], weights.matrix(places, 0)[...], preferred_element_type=f32)
        attended = attended + vectors[0:1, :width]
        first_sum = hidden[at].astype(f32) + attended * (keep[at].astype(f32) * keep_scale)
        normal, scale = layer_norm(first_sum)
        scaled[at] = normal
        inverse[at] = jnp.broadcast_to(scale, (tokens, 128))
        lows[at] = (normal * vectors[1:2, :width] + vectors[2:3, :width]).astype(bf16)
        return carry

    lax.fori_loop(0, rows // tokens, rows_part, 0)
    finish(copies[1])
    up = weights.matrix(places, 1)
    step = 512

    def part(n, carry):
        at = pl.ds(pl.multiple_of(n * step, step), step)
        inner = jnp.dot(lows[...], up[:, at], preferred_element_type=f32) + vectors[3:4, at]
        cdf = 0.5 * (1.0 + lax.erf(inner * root_half))
        density = jnp.exp(-0.5 * inner * inner) * inverse_root_tau
        activated[:, at] = (inner * cdf).astype(bf16)
        slope[:, at] = (cdf + inner * density).astype(bf16)
        return carry

    lax.fori_loop(0, wide // step, part, 0)


def feed_up(ids, weights, pers, context, hidden, keep, tokens, wide):
    rows, width = hidden.shape
    return call(
        functools.partial(up_body, weights, pers, tokens),
        "feed_up",
        (1,),
        (ids, *weights.operands, context, hidden, keep),
        weights.specs + [WHOLE] * 3,
        [
            shaped((8, wide), f32),
            shaped((rows, width), f32),
            shaped((rows, 128), f32),
            shaped((rows, wide), bf16),
            shaped((rows, wide), bf16),
        ],
        [WHOLE] * 5,
        weights.scratch + [pltpu.VMEM((rows, width), bf16)],
        28,
        24,
    )


def hand_out(core, total, rows, own, send, first, at):
    def one(n, carry):
        here = pl.multiple_of((2 * n + core) * rows, 8)
        there = pl.multiple_of((2 * n + 1 - core) * rows, 8)
        own[first + n, at : at + rows, :] = total[pl.ds(here, rows), :].astype(bf16)
        send[first + n, at : at + rows, :] = total[pl.ds(there, rows), :].astype(bf16)
        return carry

    lax.fori_loop(0, total.shape[0] // (2 * rows), one, 0)


def down_body(weights, tokens, ids, *refs):
    count = len(weights.operands)
    sources, refs = refs[:count], refs[count:]
    activated, slope, scaled, keep, cotangent, vectors = refs[:6]
    layer_out, g_second_out, g_inner, own, send, sums = refs[6:12]
    place, sems, total, g_outers = refs[12:]
    copies = weights.copies(ids, sources, (place,), sems)
    rows, width = scaled.shape
    wide = activated.shape[1]
    begin(copies)
    sums[...] = jnp.zeros_like(sums)
    finish(copies[0])
    down = weights.matrix((place,), 0)
    gain = vectors[5:6, :width]

    def rows_part(m, carry):
        at = pl.ds(pl.multiple_of(m * tokens, tokens), tokens)
        outer = jnp.dot(activated[at], down[...], preferred_element_type=f32) + vectors[4:5, :width]
        factor = keep[at].astype(f32) * keep_scale
        normed = scaled[at] * vectors[1:2, :width] + vectors[2:3, :width]
        normal, scale = layer_norm(normed + outer * factor)
        layer_out[at] = (normal * gain + vectors[6:7, :width]).astype(bf16)
        above = cotangent[at].astype(f32)
        weighted = above * gain
        g_second = scale * (
            weighted
            - jnp.mean(weighted, axis=-1, keepdims=True)
            - normal * jnp.mean(weighted * normal, axis=-1, keepdims=True)
        )
        g_second_out[at] = g_second
        g_outer = (g_second * factor).astype(bf16)
        g_outers[at] = g_outer
        sums[0:1, :width] += jnp.sum(g_outer.astype(f32), axis=0, keepdims=True)
        sums[1:2, :width] += jnp.sum(above * normal, axis=0, keepdims=True)
        sums[2:3, :width] += jnp.sum(above, axis=0, keepdims=True)
        return carry

    lax.fori_loop(0, rows // tokens, rows_part, 0)
    step = 512

    def part(n, carry):
        at = pl.ds(pl.multiple_of(n * step, step), step)
        g_in = (dot_t(g_outers[...], down[at, :]) * slope[:, at].astype(f32)).astype(bf16)
        g_inner[:, at] = g_in
        sums[3:4, at] = jnp.sum(g_in.astype(f32), axis=0, keepdims=True)
        return carry

    lax.fori_loop(0, wide // step, part, 0)

    def grads(n, carry):
        at = pl.ds(pl.multiple_of(n * width, width), width)
        total[...] = t_dot(activated[:, at], g_outers[...])
        hand_out(ids[0], total, wide // 32, own, send, n * (16 * width // wide), 0)
        return carry

    lax.fori_loop(0, wide // width, grads, 0)


def feed_down(ids, weights, activated, slope, scaled, keep, cotangent, vectors, tokens):
    rows, width = scaled.shape
    wide = activated.shape[1]
    halves = (16, wide // 32, width)
    return call(
        functools.partial(down_body, weights, tokens),
        "feed_down",
        (1,),
        (ids, *weights.operands, activated, slope, scaled, keep, cotangent, vectors),
        weights.specs + [WHOLE] * 6,
        [
            shaped((rows, width), bf16),
            shaped((rows, width), f32),
            shaped((rows, wide), bf16),
            shaped(halves, bf16),
            shaped(halves, bf16),
            shaped((8, wide), f32),
        ],
        [WHOLE] * 6,
        weights.scratch + [pltpu.VMEM((width, width), f32), pltpu.VMEM((rows, width), bf16)],
        30,
        36,
    )


def middle_body(weights, pers, tokens, ids, *refs):
    count = len(weights.operands)
    sources, refs = refs[:count], refs[count:]
    g_inner, g_second, scaled, inverse, keep, vectors, context, down_sums = refs[:8]
    g_first_out, g_context, own, send, block = refs[8:13]
    *places, sems, g_normeds, g_attendeds, sums = refs[13:]
    copies = weights.copies(ids, sources, places, sems)
    begin([copies[1], copies[0]])
    rows, width = scaled.shape
    out_w, up_w = weights.matrix(places, 0), weights.matrix(places, 1)
    finish(copies[1])
    step = 256

    def columns_part(n, carry):
        at = pl.ds(pl.multiple_of(n * step, step), step)
        g_normeds[:rows, at] = g_second[:, at] + dot_t(g_inner[...], up_w[at, :])
        return carry

    lax.fori_loop(0, width // step, columns_part, 0)
    sums[...] = jnp.zeros_like(sums)

    def rows_part(m, carry):
        at = pl.ds(pl.multiple_of(m * tokens, tokens), tokens)
        normal = scaled[at]
        g_normed = g_normeds[at, :]
        weighted = g_normed * vectors[1:2, :width]
        g_first = inverse[at, 0:1] * (
            weighted
            - jnp.mean(weighted, axis=-1, keepdims=True)
            - normal * jnp.mean(weighted * normal, axis=-1, keepdims=True)
        )
        g_first_out[at] = g_first
        g_attended = (g_first * (keep[at].astype(f32) * keep_scale)).astype(bf16)
        g_attendeds[at] = g_attended
        sums[0:1, :] += jnp.sum(g_attended.astype(f32), axis=0, keepdims=True)
        sums[1:2, :] += jnp.sum(g_normed * normal, axis=0, keepdims=True)
        sums[2:3, :] += jnp.sum(g_normed, axis=0, keepdims=True)
        return carry

    lax.fori_loop(0, rows // tokens, rows_part, 0)
    finish(copies[0])
    g_context[...] = dot_t(g_attendeds[...], out_w[...]).astype(bf16)
    g_normeds[:width] = t_dot(context[...], g_attendeds[...])
    hand_out(ids[0], g_normeds, width // 32, own, send, 0, 0)
    vector_sums = [sums[n : n + 1, :] for n in range(3)]
    vector_sums += [down_sums[3:4, :]] + [down_sums[n : n + 1, :width] for n in range(3)]
    unspread(vector_sums, pers, block)


def middle(ids, weights, pers, g_inner, g_second, scaled, inverse, keep, vectors, context, sums, tokens):
    rows, width = scaled.shape
    halves = (16, width // 32, width)
    return call(
        functools.partial(middle_body, weights, pers, tokens),
        "middle",
        (1,),
        (ids, *weights.operands, g_inner, g_second, scaled, inverse, keep, vectors, context, sums),
        weights.specs + [WHOLE] * 8,
        [
            shaped((rows, width), f32),
            shaped((rows, width), bf16),
            shaped(halves, bf16),
            shaped(halves, bf16),
            shaped((32, 8, width), f32),
        ],
        [WHOLE] * 5,
        weights.scratch
        + [pltpu.VMEM((max(rows, width), width), f32), pltpu.VMEM((rows, width), bf16), pltpu.VMEM((8, width), f32)],
        26,
        18,
    )


def grads_body(ids, g_inner, scaled, vectors, own, send, total, low_t):
    n = pl.program_id(0)
    width = scaled.shape[1]

    @pl.when(n == 0)
    def _():
        low_t[...] = (scaled[...] * vectors[1:2, :width] + vectors[2:3, :width]).T.astype(bf16)

    total[...] = jnp.dot(low_t[...], g_inner[...], preferred_element_type=f32)
    for block in range(own.shape[1] // (width // 32)):

        @pl.when(n == block)
        def _():
            hand_out(ids[0], total, width // 32, own, send, 0, block * (width // 32))


def up_grads(ids, g_inner, scaled, vectors):
    rows, width = scaled.shape
    wide = g_inner.shape[1]
    halves = (16, wide // 32, width)
    return call(
        grads_body,
        "up_grads",
        (wide // width,),
        (ids, g_inner, scaled, vectors),
        [pl.BlockSpec((rows, width), lambda i, ids: (0, i))] + [WHOLE] * 2,
        [shaped(halves, bf16), shaped(halves, bf16)],
        [WHOLE] * 2,
        [pltpu.VMEM((width, width), f32), pltpu.VMEM((width, rows), bf16)],
        24,
        20,
    )


def hand_out_rows(core, block, own, send, at):
    for n in range(16):
        own[n, at : at + 8, :] = block[2 * n + core].astype(bf16)
        send[n, at : at + 8, :] = block[2 * n + 1 - core].astype(bf16)


def inputs_body(per, ids, hidden, turned, *refs):
    micro = (len(refs) - 8) // 5
    grads, (block, own, send, g_queries, g_keys, g_values, total, bias) = refs[: 5 * micro], refs[5 * micro :]
    width = hidden.shape[1]
    sums = []
    for n, out in enumerate((g_queries, g_keys, g_values)):
        for m in range(micro):
            g_q, near, far = grads[m], grads[micro + 2 * m :][:2], grads[3 * micro + 2 * m :][:2]
            rows = slice(m * g_q.shape[0], (m + 1) * g_q.shape[0])
            if n == 0:
                out[rows] = g_q[...]
            else:
                out[rows] = (near[n - 1][...] + far[n - 1][...].astype(f32)).astype(bf16)
        if n != 1:
            sums.append(jnp.sum(out[...].astype(f32), axis=0, keepdims=True))
        left = hidden if n == 0 else turned

        def part(k, carry, left=left, out=out):
            at = pl.ds(pl.multiple_of(k * 256, 256), 256)
            total[at, :] = t_dot(left[:, at], out[...])
            return carry

        lax.fori_loop(0, width // 256, part, 0)
        hand_out(ids[0], total, width // 32, own, send, 0, n * (width // 32))
    bias[...] = block[...]
    unspread([jnp.concatenate(sums, axis=1)], [per], bias, 7)
    hand_out_rows(ids[0], bias, own, send, 3 * (width // 32))


def input_grads(ids, hidden, turned, grads, block, per):
    rows, width = hidden.shape
    halves = (16, 3 * width // 32 + 8, width)
    return call(
        functools.partial(inputs_body, per),
        "input_grads",
        (1,),
        (ids, hidden, turned, *grads, block),
        [WHOLE] * (3 + len(grads)),
        [shaped(halves, bf16)] * 2 + [shaped((rows, width), bf16)] * 3,
        [WHOLE] * 5,
        [pltpu.VMEM((width, width), f32), pltpu.VMEM((32, 8, width), f32)],
        28,
        12,
    )


def last_body(weights, ids, *refs):
    count = len(weights.operands)
    sources = refs[:count]
    g_first, g_q, g_keys, g_values, out = refs[count : count + 5]
    places, sems = refs[count + 5 : -1], refs[-1]
    copies = weights.copies(ids, sources, places, sems)

    @pl.when(pl.program_id(0) == 0)
    def _():
        begin(copies)
        for group in copies:
            finish(group)

    turn = turn_matrix(g_q.shape[0])
    total = g_first[...] + dot_t(g_q[...], weights.matrix(places, 0)[...])
    total = total + dot_t(t_dot(turn, g_keys[...]).astype(bf16), weights.matrix(places, 1)[...])
    total = total + dot_t(t_dot(turn, g_values[...]).astype(bf16), weights.matrix(places, 2)[...])
    out[...] = total.astype(bf16)


def last(ids, weights, g_first, g_q, g_keys, g_values, tokens):
    rows, width = g_first.shape
    narrow = rows_spec(tokens, width)
    return call(
        functools.partial(last_body, weights),
        "input_back",
        (rows // tokens,),
        (ids, *weights.operands, g_first, g_q, g_keys, g_values),
        weights.specs + [narrow] * 4,
        [shaped((rows, width), bf16)],
        [narrow],
        weights.scratch,
        16,
        10,
    )[0]


def beside(shape, y, x):
    return pl.BlockSpec((4, 1, 1) + shape[3:], lambda i, ids: (0, ids[1] ^ y, ids[2] ^ x, 0, 0))


def rows_of(parts, index, first, last):
    found, start = [], 0
    for part in parts:
        rows = part.shape[-2]
        low, high = max(first, start), min(last, start + rows)
        if low < high:
            found.append(part[index + (slice(low - start, high - start),)].astype(f32))
        start += rows
    return found[0] if len(found) == 1 else jnp.concatenate(found, axis=-2)


def both(parts, index, first, last):
    half = len(parts) // 2
    return rows_of(parts[:half], index, first, last) + rows_of(parts[half:], index, first, last)


def count_rows(parts):
    return sum(part.shape[3] for part in parts[: len(parts) // 2])


PLANE = (slice(None), 0, 0)


def corner_body(ids, *refs):
    *parts, low, high = refs
    half = low.shape[1]
    low[...] = both(parts, PLANE, 0, half).astype(bf16)
    high[...] = both(parts, PLANE, half, half + high.shape[1]).astype(bf16)


def reduce_corner(ids, parts, cut):
    rows, width = count_rows(parts), parts[0].shape[4]
    return call(
        corner_body,
        "reduce_corner",
        (1,),
        (ids, *parts),
        [beside(part.shape, 1, 1) for part in parts],
        [shaped((4, cut, width), bf16), shaped((4, rows - cut, width), bf16)],
        [WHOLE] * 2,
        [],
        8,
        2,
    )


def sides_body(count, ids, *refs):
    for_y, for_x, (low, high, to_y, to_x) = refs[:count], refs[count : 2 * count], refs[2 * count :]
    rows, half = to_y.shape[1], low.shape[1]
    to_y[:, :half] = (both(for_y, PLANE, 0, half) + low[...].astype(f32)).astype(bf16)
    to_y[:, half:] = both(for_y, PLANE, half, rows).astype(bf16)
    to_x[:, :half] = both(for_x, PLANE, 0, half).astype(bf16)
    to_x[:, half:] = (both(for_x, PLANE, half, rows) + high[...].astype(f32)).astype(bf16)


def reduce_sides(ids, parts, low, high):
    rows, width = count_rows(parts), parts[0].shape[4]
    return call(
        functools.partial(sides_body, len(parts)),
        "reduce_sides",
        (1,),
        (ids, *parts, *parts, low, high),
        [beside(part.shape, 1, 0) for part in parts]
        + [beside(part.shape, 0, 1) for part in parts]
        + [WHOLE] * 2,
        [shaped((4, rows, width), bf16)] * 2,
        [WHOLE] * 2,
        [],
        10,
        3,
    )


def depth_body(ids, *refs):
    *parts, from_y, from_x, near, middle, far, mine = refs
    for k, out in enumerate((mine, near, middle, far)):
        z = ids[3] ^ k
        total = both(parts, (z, 0, 0), 0, from_y.shape[1])
        total = total + from_y[z].astype(f32) + from_x[z].astype(f32)
        out[...] = total.astype(out.dtype)


def reduce_depth(ids, parts, from_y, from_x):
    shape = from_y.shape[1:]
    return call(
        depth_body,
        "reduce_depth",
        (1,),
        (ids, *parts, from_y, from_x),
        [beside(part.shape, 0, 0) for part in parts] + [WHOLE] * 2,
        [shaped(shape, bf16)] * 3 + [shaped(shape, f32)],
        [WHOLE] * 4,
        [],
        10,
        3,
    )


def pair_body(ids, one, two, out):
    out[0] = one[...]
    out[1] = two[...]


def pair_z(ids, one, two):
    return call(
        pair_body,
        "pair_z",
        (1,),
        (ids, one, two),
        [WHOLE] * 2,
        [shaped((2,) + one.shape, bf16)],
        [WHOLE],
        [],
        4,
        1,
    )[0]


def order_body(ids, pair, received, out):
    for k in range(2):
        out[ids[3] ^ (2 * k)] = pair[k]
        out[ids[3] ^ (2 * k + 1)] = received[k]


def order_z(ids, pair, received):
    return call(
        order_body,
        "order_z",
        (1,),
        (ids, pair, received),
        [WHOLE] * 2,
        [shaped((4,) + pair.shape[1:], bf16)],
        [WHOLE],
        [],
        6,
        1,
    )[0]


def four_body(ids, *refs):
    *parts, out = refs
    for k, part in enumerate(parts):
        out[ids[3] ^ k] = part[...]


def order_four(ids, *parts):
    return call(
        four_body,
        "order_four",
        (1,),
        (ids, *parts),
        [WHOLE] * 4,
        [shaped((4,) + parts[0].shape, bf16)],
        [WHOLE],
        [],
        6,
        1,
    )[0]


def halves_body(ids, pair, received, low, high):
    rows = low.shape[1]
    for k in range(2):
        for source, z in ((pair, ids[3] ^ (2 * k)), (received, ids[3] ^ (2 * k + 1))):
            low[z] = source[k, :rows]
            high[z] = source[k, rows:]


def order_halves(ids, pair, received):
    shape = (4, pair.shape[1] // 2, pair.shape[2])
    return call(
        halves_body,
        "order_halves",
        (1,),
        (ids, pair, received),
        [WHOLE] * 2,
        [shaped(shape, bf16)] * 2,
        [WHOLE] * 2,
        [],
        6,
        1,
    )


def first_body(ids, *refs):
    at_y, at_x, at_corner, (to_y, to_x) = refs[:2], refs[2:4], refs[4:6], refs[6:]
    half = to_y.shape[1] // 2
    to_y[:, :half] = both(at_y, PLANE, 0, half).astype(bf16)
    to_y[:, half:] = both(at_corner, PLANE, 0, half).astype(bf16)
    to_x[:, :half] = both(at_x, PLANE, half, 2 * half).astype(bf16)
    to_x[:, half:] = both(at_corner, PLANE, half, 2 * half).astype(bf16)


def reduce_first(ids, parts):
    shape = parts[0].shape
    return call(
        first_body,
        "reduce_first",
        (1,),
        (ids, *parts, *parts, *parts),
        [beside(shape, 1, 0)] * 2 + [beside(shape, 0, 1)] * 2 + [beside(shape, 1, 1)] * 2,
        [shaped((4,) + shape[3:], bf16)] * 2,
        [WHOLE] * 2,
        [],
        10,
        3,
    )


def second_body(ids, *refs):
    here, at_y, at_x, (from_y, from_x, send, keep) = refs[:2], refs[2:4], refs[4:6], refs[6:]
    half = from_y.shape[1] // 2
    for k, (out, at) in enumerate(((keep, 0), (send, 0), (keep, 1), (send, 1))):
        z = ids[3] ^ k
        plane = (z, 0, 0)
        quarters = (
            both(here, plane, 0, half) + from_y[z, :half].astype(f32),
            both(at_x, plane, 0, half) + from_y[z, half:].astype(f32),
            both(here, plane, half, 2 * half) + from_x[z, :half].astype(f32),
            both(at_y, plane, half, 2 * half) + from_x[z, half:].astype(f32),
        )
        for i, quarter in enumerate(quarters):
            out[at, i * half : (i + 1) * half] = quarter.astype(out.dtype)


def reduce_second(ids, parts, from_y, from_x):
    shape = parts[0].shape
    wide = (2, 2 * shape[3], shape[4])
    return call(
        second_body,
        "reduce_second",
        (1,),
        (ids, *parts, *parts, *parts, from_y, from_x),
        [beside(shape, 0, 0)] * 2 + [beside(shape, 1, 0)] * 2 + [beside(shape, 0, 1)] * 2 + [WHOLE] * 2,
        [shaped(wide, bf16), shaped(wide, f32)],
        [WHOLE] * 2,
        [],
        14,
        3,
    )


def quarter_body(ids, keep, received, send, mine):
    mine[...] = keep[0] + received[0].astype(f32)
    send[...] = (keep[1] + received[1].astype(f32)).astype(bf16)


def reduce_third(ids, keep, received):
    shape = keep.shape[1:]
    return call(
        quarter_body,
        "reduce_third",
        (1,),
        (ids, keep, received),
        [WHOLE] * 2,
        [shaped(shape, bf16), shaped(shape, f32)],
        [WHOLE] * 2,
        [],
        10,
        2,
    )


def fourth_body(ids, mine, received, to_x, to_y, own):
    half = to_x.shape[0]
    total = mine[...] + received[...].astype(f32)
    own[:half] = total[:half]
    own[half:] = total[2 * half : 3 * half]
    to_x[...] = total[half : 2 * half].astype(bf16)
    to_y[...] = total[3 * half :].astype(bf16)


def reduce_fourth(ids, mine, received):
    rows, width = mine.shape
    return call(
        fourth_body,
        "reduce_fourth",
        (1,),
        (ids, mine, received),
        [WHOLE] * 2,
        [shaped((rows // 4, width), bf16)] * 2 + [shaped((rows // 2, width), f32)],
        [WHOLE] * 3,
        [],
        8,
        2,
    )


def exchange_z(sends):
    return [pp(send, "z", k) for send, k in zip(sends, (1, 2, 3))]


def local(
    hidden_in,
    cotangent,
    attention_keep,
    output_keep,
    feed_keep,
    qkv_weight,
    qkv_bias,
    out_weight,
    out_bias,
    first_gain,
    first_shift,
    up_weight,
    up_bias,
    down_weight,
    down_bias,
    second_gain,
    second_shift,
):
    micro, _, tokens, width = hidden_in.shape
    rows = micro * tokens
    own = qkv_weight.shape[0]
    wide = up_weight.shape[1]
    blocks = wide // width
    c, y, x = lax.axis_index("seq"), lax.axis_index("y"), lax.axis_index("x")
    ids = jnp.stack([c, y, x, lax.axis_index("z")]).astype(jnp.int32)
    bias_parts = (out_bias, first_gain, first_shift, up_bias, down_bias, second_gain, second_shift)
    pers = [part.shape[0] for part in bias_parts]
    per = qkv_bias.shape[0]

    column = lambda weight, i: weight[:, i * width : (i + 1) * width]
    bias_rows = lambda parts: jnp.concatenate(
        [jnp.pad(part.reshape(1, -1), ((0, 0), (0, width - part.shape[0]))) for part in parts]
        + [jnp.zeros((8 - len(parts), width), bf16)]
    )
    square = (own, width)
    hidden = hidden_in.reshape(rows, width)

    shard_a = jnp.concatenate([column(qkv_weight, i) for i in range(3)] + [bias_rows((qkv_bias,))])
    half_c = down_weight.shape[0] // 2
    x_c, y_c = pp(down_weight[:half_c], "x"), pp(down_weight[half_c:], "y")
    shard_b = jnp.concatenate(
        [out_weight] + [column(up_weight, i) for i in range(blocks)] + [bias_rows(bias_parts)]
    )
    z_a = hold([pp(shard_a, "z", k) for k in (1, 2, 3)], x_c, y_c, shard_b)
    own_a = order_four(ids, shard_a, *z_a)
    group_c = jnp.concatenate([down_weight[:half_c], x_c, down_weight[half_c:], y_c])
    x_a, y_a = pp(own_a, "x"), pp(own_a, "y")
    shard_b = after(shard_b, own_a)
    far_b = pp(shard_b, "z", 2)
    turned, keep_output, keep_feed = prepare(
        ids, after(hidden, own_a), output_keep.transpose(0, 1, 3, 2), feed_keep.transpose(0, 1, 3, 2), tokens
    )
    x_a, y_a, far_b = hold((x_a, y_a, far_b), turned)
    cut_a = shard_a.shape[0] // 2
    low_a, high_a = pp(x_a[:, :cut_a], "y"), pp(y_a[:, cut_a:], "x")
    pieces = [whole(0, 0, own_a), whole(1, 0, x_a), whole(2, 0, y_a), whole(3, 0, low_a), whole(3, cut_a, high_a)]
    late = whole(2, 0, after(y_a, low_a))
    pieces += [at_core(piece) for piece in pieces[:2] + [late] + pieces[3:]]
    pair_b = pair_z(ids, shard_b, far_b)
    near_b = pp(pair_b, "z", 1)
    plan = [(i * own, own, i, 0, 0) for i in range(3)]
    plan = divide(plan, cut_a)
    weights = Weights(pieces, plan + [(3 * own, 8, 3, 0, 0)], [square] * 3 + [(8, width)])
    weights_again = Weights(pieces, plan, [square] * 3)
    own_b = order_z(ids, pair_b, after(near_b, low_a, high_a))
    far_c = pp(after(group_c, own_b), "z", 2)
    x_b, y_b = pp(own_b, "x"), pp(own_b, "y")
    queries, *near = project(ids, weights, hidden, after(turned, own_b), micro, per)
    near = (near[: 2 * PARTS[0]], near[2 * PARTS[0] :])
    far = [[pp(value, "seq") for value in values] for values in near]
    words = attention_keep.reshape(micro, H, tokens, -1)
    *far[0], far_c = hold((*far[0], far_c))
    pair_c = pair_z(ids, group_c, far_c)
    near_c = pp(pair_c, "z", 1)
    context, signed = attention(ids, 0, after(queries, pair_c), near, far, words)
    own_b, x_b, y_b, *far[1] = hold((own_b, x_b, y_b, *far[1]), context)
    cut_b = shard_b.shape[0] // 2
    low_b, high_b = pp(x_b[:, :cut_b], "y"), pp(y_b[:, cut_b:], "x")
    context, signed = attention(ids, 1, queries, near, far, words, (context, signed))
    low_b, high_b, near_c = hold((low_b, high_b, near_c), context)
    pieces = [whole(0, 0, own_b), whole(1, 0, x_b), whole(2, 0, after(y_b, context))]
    pieces += [at_core(piece) for piece in pieces]
    corners = [whole(3, 0, low_b), whole(3, cut_b, high_b)]
    pieces += corners + [at_core(piece) for piece in corners]
    plan = [(0, own, 0, 0, 0)] + [((i + 1) * own, own, 1, 0, i * width) for i in range(blocks)]
    plan = divide(plan, cut_b)
    weights = Weights(
        pieces, plan + [((blocks + 1) * own, 8, 2, 0, 0)], [square, (own, wide), (8, width)]
    )
    back_weights = Weights(pieces, plan, [square, (own, wide)])
    by_x, by_y = order_halves(ids, pair_c, after(near_c, low_b, high_b))
    from_y, from_x = pp(by_x, "y"), pp(by_y, "x")
    context = context.reshape(rows, width)
    vectors, scaled, inverse, activated, slope = feed_up(
        ids, weights, pers, context, hidden, keep_output, tokens, wide
    )
    from_y, from_x = hold((from_y, from_x), activated)
    down_rows = down_weight.shape[0]
    pieces = []
    for core in range(2):
        held = [by_x, from_y, by_y, from_x]
        if core == 1:
            held = [pp(array, "seq") for array in held]
        for array, numbers, first in zip(held, ((0, 1), (2, 3), (0, 2), (1, 3)), (0, 0, half_c, half_c)):
            pieces += [(4 * core + number, first, array, i * half_c, half_c) for i, number in enumerate(numbers)]
    plan = divide([(0, down_rows, 0, 0, 0)], half_c)
    weights = Weights(pieces, plan, [(down_rows, width)])
    layer_out, g_second, g_inner, down_own, down_send, sums = feed_down(
        ids, weights, activated, slope, scaled, keep_feed, cotangent.reshape(rows, width), vectors, tokens
    )

    unit = lambda value: value.reshape((4, 2, 2) + value.shape[1:])
    down_core = pp(down_send, "seq")
    mid_own, mid_send = up_grads(ids, g_inner, scaled, vectors)
    down = [unit(down_own), unit(after(down_core, mid_send))]
    to_y, to_x = reduce_first(ids, down)
    down_y, down_x = pp(to_y, "y"), pp(to_x, "x")
    mid_core = pp(after(mid_send, to_y), "seq")
    g_first, g_context, out_own, out_send, block = middle(
        ids, back_weights, pers, after(g_inner, to_y), g_second, scaled, inverse, keep_output, vectors, context, sums, tokens
    )
    out_core = pp(out_send, "seq")
    down_y, down_x, mid_core = hold((down_y, down_x, mid_core), g_context)
    mid = [unit(value) for value in (mid_own, out_own, mid_core, out_core)]
    cut_m = (count_rows(mid) + 15) // 16 * 8
    corner = reduce_corner(ids, mid, cut_m)
    low, high = pp(corner[0], "x"), pp(corner[1], "y")
    down_send, down_keep = reduce_second(ids, down, down_y, down_x)
    down_near = pp(down_send, "z", 1)
    first_q, *first_near, far_k, far_v = attention_back(
        ids, 0, queries, near, far, signed, after(g_context, down_send, *corner)
    )
    low, high = hold((low, high), first_q)
    first_far = [pp(after(value, low, high), "seq") for value in (far_k, far_v)]
    to_y, to_x = reduce_sides(ids, mid, low, high)
    mid_y, mid_x = pp(to_y, "y"), pp(to_x, "x")
    second_q, *second_near, far_k, far_v = attention_back(
        ids, 1, queries, near, far, signed, after(g_context, to_y, to_x)
    )
    first_far = hold(first_far, second_q)
    second_far = [pp(value, "seq") for value in (far_k, far_v)]
    down_near = after(down_near, second_q)
    down_send, down_mine = reduce_third(ids, down_keep, down_near)
    down_far = pp(down_send, "z", 2)
    grads = (first_q, second_q, *first_near, *second_near, *first_far, *hold(second_far, down_send))
    a_own, a_send, g_q, g_keys, g_values = input_grads(ids, hidden, turned, grads, block, per)
    mid_y, mid_x = hold((mid_y, mid_x), a_send)
    down_far = after(down_far, a_send)
    core_sums = pp(after(a_send, mid_y, mid_x, down_far), "seq")
    to_far_x, to_far_y, down_mine = reduce_fourth(ids, down_mine, down_far)
    part = [unit(a_own), unit(core_sums)]
    corner = reduce_corner(ids, part, cut_a)
    low, high = pp(corner[0], "x"), pp(corner[1], "y")
    *sends, mid_mine = reduce_depth(ids, mid, after(mid_y, *corner), mid_x)
    mid_z = exchange_z(sends)
    low, high = hold((low, high), *sends)
    to_y, to_x = reduce_sides(ids, part, low, high)
    side_y, side_x = pp(to_y, "y"), pp(to_x, "x")
    received = [pp(after(to_far_x, to_x), "x"), pp(after(to_far_y, to_y), "y")]
    grad_in = last(
        ids, weights_again, g_first, g_q, g_keys, after(g_values, to_y, to_x), tokens
    )
    mid_z = hold(mid_z, grad_in)
    mid = add_up([mid_mine, *mid_z])
    side_y, side_x, *received = hold((side_y, side_x, *received), mid, grad_in)
    *sends, part_mine = reduce_depth(ids, part, side_y, side_x)
    grad_down = add_up([down_mine, jnp.concatenate(received)])
    part = add_up([part_mine, *exchange_z(sends)])

    stripe = lambda value, i: value[i * own : (i + 1) * own]
    grad_qkv = jnp.concatenate([stripe(part, i) for i in range(3)], axis=1)
    grad_up = jnp.concatenate([stripe(mid, i) for i in range(blocks)], axis=1)
    vector_grads = [part[3 * own + i, :length] for i, length in enumerate(pers)]
    grad_out = mid[blocks * own :]
    return (
        layer_out.reshape(hidden_in.shape),
        grad_in.reshape(hidden_in.shape),
        grad_qkv,
        part[3 * own + 7, :per],
        grad_out,
        vector_grads[0],
        vector_grads[1],
        vector_grads[2],
        grad_up,
        vector_grads[3],
        grad_down,
        vector_grads[4],
        vector_grads[5],
        vector_grads[6],
    )


def solution(mesh):
    groups, cores = mesh.devices.shape
    split = Mesh(mesh.devices.reshape(groups // 4, 2, 2, cores), ("z", "y", "x", "seq"))
    dp = ("z", "y", "x")
    token_rows = P(None, dp, "seq", None)
    matrix = P(every, None)
    vector = P(every)
    params = (matrix, vector, matrix, vector, vector, vector, matrix, vector, matrix, vector, vector, vector)

    def layer(*arrays):
        tiled = groups == 16 and cores == 2 and arrays[5].shape[0] % 8 == 0
        return (local if tiled else plain_local)(*arrays)

    return jax.shard_map(
        layer,
        mesh=split,
        in_specs=(token_rows, token_rows, P(None, dp, None, "seq", None), token_rows, token_rows) + params,
        out_specs=(token_rows, token_rows) + params,
        check_vma=False,
    )
```

```python
import functools

import jax
import jax.numpy as jnp
from jax import lax
from jax.experimental import pallas as pl
from jax.experimental.pallas import tpu as pltpu
from jax.sharding import Mesh
from jax.sharding import PartitionSpec as P

H = 12
epsilon = 1e-12
keep_scale = 8.0 / 7.0
root_half = 0.7071067811865476
inverse_root_tau = 0.3989422804014327
every = ("z", "y", "x", "seq")
f32 = jnp.float32
bf16 = jnp.bfloat16


def unpack_keep(packed_words):
    shifts = jnp.arange(4, dtype=jnp.int32) * 3
    nibble = jnp.right_shift(packed_words[..., None], shifts) & 7
    keep_value = (nibble >= 1).astype(jnp.float32) * keep_scale
    return keep_value.reshape(packed_words.shape[:-1] + (packed_words.shape[-1] * 4,))


def normalize(values, norm_gain, norm_shift):
    centred = values - jnp.mean(values, axis=-1, keepdims=True)
    inverse = lax.rsqrt(jnp.mean(centred * centred, axis=-1, keepdims=True) + epsilon)
    scaled = centred * inverse
    return (scaled * norm_gain + norm_shift, scaled, inverse)


def norm_back(upstream, scaled, inverse, norm_gain):
    weighted = upstream * norm_gain
    centre_term = jnp.mean(weighted, axis=-1, keepdims=True)
    slope_term = jnp.mean(weighted * scaled, axis=-1, keepdims=True)
    return inverse * (weighted - centre_term - scaled * slope_term)


def gelu_slope(inner_sum):
    normal_cdf = 0.5 * (1.0 + lax.erf(inner_sum * root_half))
    density = jnp.exp(-0.5 * inner_sum * inner_sum) * inverse_root_tau
    return normal_cdf + inner_sum * density


def matmul(left_side, right_side):
    return jnp.dot(left_side, right_side, preferred_element_type=jnp.float32)


def plain_local(
    hidden_in,
    cotangent,
    attention_keep,
    output_keep,
    feed_keep,
    qkv_weight,
    qkv_bias,
    out_weight,
    out_bias,
    first_gain,
    first_shift,
    up_weight,
    up_bias,
    down_weight,
    down_bias,
    second_gain,
    second_shift,
):
    model_width = hidden_in.shape[-1]
    sequence_count = hidden_in.shape[1]
    local_tokens = hidden_in.shape[2]
    token_rows = sequence_count * local_tokens
    head_count = H
    head_size = model_width // head_count
    held_params = (
        lax.all_gather(qkv_weight, every, axis=0, tiled=True),
        lax.all_gather(qkv_bias, every, axis=0, tiled=True),
        lax.all_gather(out_weight, every, axis=0, tiled=True),
        lax.all_gather(out_bias, every, axis=0, tiled=True),
        lax.all_gather(first_gain, every, axis=0, tiled=True),
        lax.all_gather(first_shift, every, axis=0, tiled=True),
        lax.all_gather(up_weight, every, axis=0, tiled=True),
        lax.all_gather(up_bias, every, axis=0, tiled=True),
        lax.all_gather(down_weight, every, axis=0, tiled=True),
        lax.all_gather(down_bias, every, axis=0, tiled=True),
        lax.all_gather(second_gain, every, axis=0, tiled=True),
        lax.all_gather(second_shift, every, axis=0, tiled=True),
    )
    totals = None
    outputs = []
    inputs_grad = []
    for micro_step in range(hidden_in.shape[0]):
        (
            full_qkv_w,
            full_qkv_b,
            full_out_w,
            full_out_b,
            full_gain_one,
            full_shift_one,
            full_up_w,
            full_up_b,
            full_down_w,
            full_down_b,
            full_gain_two,
            full_shift_two,
        ) = held_params
        rows_in = hidden_in[micro_step].reshape(token_rows, model_width)
        qkv_float = full_qkv_b.astype(jnp.float32)
        bias_full = jnp.concatenate(
            [
                qkv_float[:model_width],
                jnp.zeros((model_width,), jnp.float32),
                qkv_float[model_width:],
            ]
        )
        projected = (matmul(rows_in, full_qkv_w) + bias_full).astype(jnp.bfloat16)
        queries = projected[:, :model_width].reshape(
            sequence_count, local_tokens, head_count, head_size
        )
        keys_local = projected[:, model_width : 2 * model_width].reshape(
            sequence_count, local_tokens, model_width
        )
        values_local = projected[:, 2 * model_width :].reshape(
            sequence_count, local_tokens, model_width
        )
        keys_all, values_all = (
            lax.all_gather(keys_local, "seq", axis=1, tiled=True),
            lax.all_gather(values_local, "seq", axis=1, tiled=True),
        )
        keys_heads = keys_all.reshape(sequence_count, -1, head_count, head_size)
        values_heads = values_all.reshape(sequence_count, -1, head_count, head_size)
        scores = (
            jnp.einsum("sqhd,skhd->shqk", queries, keys_heads, preferred_element_type=jnp.float32)
            * 0.125
        )
        row_peak = jnp.max(scores, axis=-1, keepdims=True)
        exponent = jnp.exp(scores - row_peak)
        row_total = jnp.sum(exponent, axis=-1, keepdims=True)
        log_total = row_peak + jnp.log(row_total)
        softmax_weights = exponent / row_total
        keep_attention = unpack_keep(attention_keep[micro_step])
        dropped = (softmax_weights * keep_attention).astype(jnp.bfloat16)
        context = jnp.einsum(
            "shqk,skhd->sqhd", dropped, values_heads, preferred_element_type=jnp.float32
        )
        context = context.reshape(token_rows, model_width).astype(jnp.bfloat16)
        attended = matmul(context, full_out_w) + full_out_b.astype(jnp.float32)
        keep_output = unpack_keep(output_keep[micro_step]).reshape(token_rows, model_width)
        first_sum = rows_in.astype(jnp.float32) + attended * keep_output
        gain_one = full_gain_one.astype(jnp.float32)
        normed, scaled_one, inverse_one = normalize(
            first_sum, gain_one, full_shift_one.astype(jnp.float32)
        )
        normed_low = normed.astype(jnp.bfloat16)
        inner_sum = matmul(normed_low, full_up_w) + full_up_b.astype(jnp.float32)
        activated = jax.nn.gelu(inner_sum, approximate=False).astype(jnp.bfloat16)
        outer_sum = matmul(activated, full_down_w) + full_down_b.astype(jnp.float32)
        keep_feed = unpack_keep(feed_keep[micro_step]).reshape(token_rows, model_width)
        second_sum = normed + outer_sum * keep_feed
        gain_two = full_gain_two.astype(jnp.float32)
        result, scaled_two, inverse_two = normalize(
            second_sum, gain_two, full_shift_two.astype(jnp.float32)
        )
        outputs.append(
            result.astype(jnp.bfloat16).reshape(sequence_count, local_tokens, model_width)
        )
        (
            back_qkv_w,
            back_qkv_b,
            back_out_w,
            back_out_b,
            back_gain_one,
            back_shift_one,
            back_up_w,
            back_up_b,
            back_down_w,
            back_down_b,
            back_gain_two,
            back_shift_two,
        ) = held_params
        upstream = cotangent[micro_step].reshape(token_rows, model_width).astype(jnp.float32)
        g_second = norm_back(upstream, scaled_two, inverse_two, back_gain_two.astype(jnp.float32))
        grad_gain_two = jnp.sum(upstream * scaled_two, axis=0)
        grad_shift_two = jnp.sum(upstream, axis=0)
        g_outer = (g_second * keep_feed).astype(jnp.bfloat16)
        grad_down_b = jnp.sum(g_outer.astype(jnp.float32), axis=0)
        grad_down_w = matmul(activated.T, g_outer)
        g_inner = (matmul(g_outer, back_down_w.T) * gelu_slope(inner_sum)).astype(jnp.bfloat16)
        grad_up_b = jnp.sum(g_inner.astype(jnp.float32), axis=0)
        grad_up_w = matmul(normed_low.T, g_inner)
        g_normed = g_second + matmul(g_inner, back_up_w.T)
        g_first = norm_back(g_normed, scaled_one, inverse_one, back_gain_one.astype(jnp.float32))
        grad_gain_one = jnp.sum(g_normed * scaled_one, axis=0)
        grad_shift_one = jnp.sum(g_normed, axis=0)
        g_attended = (g_first * keep_output).astype(jnp.bfloat16)
        grad_out_b = jnp.sum(g_attended.astype(jnp.float32), axis=0)
        grad_out_w = matmul(context.T, g_attended)
        g_context = matmul(g_attended, back_out_w.T).astype(jnp.bfloat16)
        g_context = g_context.reshape(sequence_count, local_tokens, head_count, head_size)
        keys_again, values_again = (
            lax.all_gather(keys_local, "seq", axis=1, tiled=True),
            lax.all_gather(values_local, "seq", axis=1, tiled=True),
        )
        keys_heads = keys_again.reshape(sequence_count, -1, head_count, head_size)
        values_heads = values_again.reshape(sequence_count, -1, head_count, head_size)
        scores_again = (
            jnp.einsum("sqhd,skhd->shqk", queries, keys_heads, preferred_element_type=jnp.float32)
            * 0.125
        )
        weights_again = jnp.exp(scores_again - log_total)
        dropped_again = (weights_again * keep_attention).astype(jnp.bfloat16)
        g_values_all = jnp.einsum(
            "shqk,sqhd->skhd", dropped_again, g_context, preferred_element_type=jnp.float32
        )
        g_dropped = jnp.einsum(
            "sqhd,skhd->shqk", g_context, values_heads, preferred_element_type=jnp.float32
        )
        g_weights = g_dropped * keep_attention
        row_delta = jnp.sum(g_weights * weights_again, axis=-1, keepdims=True)
        g_scores = (weights_again * (g_weights - row_delta)).astype(jnp.bfloat16)
        g_queries = (
            jnp.einsum("shqk,skhd->sqhd", g_scores, keys_heads, preferred_element_type=jnp.float32)
            * 0.125
        )
        g_keys_all = (
            jnp.einsum("shqk,sqhd->skhd", g_scores, queries, preferred_element_type=jnp.float32)
            * 0.125
        )
        g_keys, g_values = (
            lax.psum_scatter(
                g_keys_all.reshape(sequence_count, -1, model_width).astype(jnp.bfloat16),
                "seq",
                scatter_dimension=1,
                tiled=True,
            ).astype(jnp.float32),
            lax.psum_scatter(
                g_values_all.reshape(sequence_count, -1, model_width).astype(jnp.bfloat16),
                "seq",
                scatter_dimension=1,
                tiled=True,
            ).astype(jnp.float32),
        )
        g_projected = jnp.concatenate(
            [
                g_queries.reshape(token_rows, model_width),
                g_keys.reshape(token_rows, model_width),
                g_values.reshape(token_rows, model_width),
            ],
            axis=1,
        ).astype(jnp.bfloat16)
        g_projected_float = g_projected.astype(jnp.float32)
        grad_qkv_b = jnp.concatenate(
            [
                jnp.sum(g_projected_float[:, :model_width], axis=0),
                jnp.sum(g_projected_float[:, 2 * model_width :], axis=0),
            ]
        )
        grad_qkv_w = matmul(rows_in.T, g_projected)
        input_grad = g_first + matmul(g_projected, back_qkv_w.T)
        inputs_grad.append(
            input_grad.astype(jnp.bfloat16).reshape(sequence_count, local_tokens, model_width)
        )
        grads_now = (
            grad_qkv_w,
            grad_qkv_b,
            grad_out_w,
            grad_out_b,
            grad_gain_one,
            grad_shift_one,
            grad_up_w,
            grad_up_b,
            grad_down_w,
            grad_down_b,
            grad_gain_two,
            grad_shift_two,
        )
        if totals is None:
            totals = grads_now
        else:
            totals = tuple((before + added for before, added in zip(totals, grads_now)))
    summed = (
        lax.psum_scatter(totals[0], every, scatter_dimension=0, tiled=True),
        lax.psum_scatter(totals[1], every, scatter_dimension=0, tiled=True),
        lax.psum_scatter(totals[2], every, scatter_dimension=0, tiled=True),
        lax.psum_scatter(totals[3], every, scatter_dimension=0, tiled=True),
        lax.psum_scatter(totals[4], every, scatter_dimension=0, tiled=True),
        lax.psum_scatter(totals[5], every, scatter_dimension=0, tiled=True),
        lax.psum_scatter(totals[6], every, scatter_dimension=0, tiled=True),
        lax.psum_scatter(totals[7], every, scatter_dimension=0, tiled=True),
        lax.psum_scatter(totals[8], every, scatter_dimension=0, tiled=True),
        lax.psum_scatter(totals[9], every, scatter_dimension=0, tiled=True),
        lax.psum_scatter(totals[10], every, scatter_dimension=0, tiled=True),
        lax.psum_scatter(totals[11], every, scatter_dimension=0, tiled=True),
    )
    return (
        jnp.stack(outputs, axis=0),
        jnp.stack(inputs_grad, axis=0),
        summed[0],
        summed[1],
        summed[2],
        summed[3],
        summed[4],
        summed[5],
        summed[6],
        summed[7],
        summed[8],
        summed[9],
        summed[10],
        summed[11],
    )


ANY = pl.BlockSpec(memory_space=pl.ANY)
WHOLE = pl.BlockSpec(memory_space=pltpu.VMEM)
MIB = 2**20
PARTS = (2, 1)
GROUP = 2


def dot_t(left_side, right_side):
    return lax.dot_general(left_side, right_side, (((1,), (1,)), ((), ())), preferred_element_type=f32)


def t_dot(left_side, right_side):
    return lax.dot_general(left_side, right_side, (((0,), (0,)), ((), ())), preferred_element_type=f32)


def iota(shape, axis):
    return lax.broadcasted_iota(jnp.int32, shape, axis)


def pp(value, axis, step=1):
    size = lax.axis_size(axis)
    return lax.ppermute(value, axis, [(i, i ^ step) for i in range(size)])


def pick(value, axis, index):
    return lax.dynamic_index_in_dim(value, index, axis, keepdims=False)


def after(value, *earlier):
    return lax.optimization_barrier((value,) + earlier)[0]


def hold(values, *earlier):
    return lax.optimization_barrier(tuple(values) + earlier)[: len(values)]


def add_up(terms):
    total = terms[0].astype(f32)
    for term in terms[1:]:
        total = total + term.astype(f32)
    return total


def divide(plan, cut):
    parts = []
    for start, rows, out, row, column in plan:
        ends = [start, cut, start + rows] if start < cut < start + rows else [start, start + rows]
        for first, last in zip(ends, ends[1:]):
            parts.append((first, last - first, out, row + first - start, column))
    return parts


def whole(number, first, array):
    return (number, first, array, 0, array.shape[1])


def at_core(piece):
    number, first, array, row, rows = piece
    return (number + 4, first, pp(array, "seq"), row, rows)


class Weights:
    def __init__(self, pieces, plan, shapes):
        arrays = []
        self.spans = []
        for number, first, array, row, rows in pieces:
            place = next((i for i, held in enumerate(arrays) if held is array), len(arrays))
            if place == len(arrays):
                arrays.append(array)
            self.spans.append((number, first, place, row, rows))
        self.operands = [pltpu.with_memory_space_constraint(array, pltpu.HBM) for array in arrays]
        self.plan, self.shapes = plan, shapes
        self.specs = [pl.BlockSpec(memory_space=pltpu.HBM)] * len(arrays)
        self.scratch = [pltpu.VMEM((4, 2, 2, 2, rows, columns), bf16) for rows, columns in shapes]
        self.scratch.append(pltpu.SemaphoreType.DMA((8 * len(plan),)))

    def copies(self, ids, sources, places, sems):
        found = [[] for _ in self.shapes]
        count = 0
        for start, rows, out, row, column in self.plan:
            for number, first, place, source_row, held in self.spans:
                if first <= start and start + rows <= first + held:
                    c = ids[0] ^ (number >> 2)
                    y = ids[1] ^ ((number >> 1) & 1)
                    x = ids[2] ^ (number & 1)
                    source = sources[place]
                    src = source.at[:, pl.ds(source_row + start - first, rows), :]
                    dst = places[out].at[:, y, x, c, pl.ds(row, rows), pl.ds(column, source.shape[2])]
                    found[out].append(pltpu.make_async_copy(src, dst, sems.at[count]))
                    count += 1
        return found

    def matrix(self, places, out):
        rows, columns = self.shapes[out]
        return places[out].reshape(32 * rows, columns)


def begin(copies):
    for group in copies:
        for copy in group:
            copy.start()


def finish(group):
    for copy in group:
        copy.wait()


def spread(block, row, count, per):
    values = block[:, row, : -(-per // 128) * 128].astype(bf16)
    lanes = values.shape[1]
    select = (iota((lanes, count), 1) % per == iota((lanes, count), 0)).astype(bf16)
    wide = jnp.dot(values, select, preferred_element_type=f32)
    return jnp.sum(jnp.where(iota(wide.shape, 1) // per == iota(wide.shape, 0), wide, 0.0), axis=0, keepdims=True)


def unspread(vectors, pers, block, first=0):
    block[:, first:] = jnp.zeros((32, 8 - first, block.shape[2]), f32)
    for row, (vector, per) in enumerate(zip(vectors, pers), first):
        count = vector.shape[1]
        lanes = -(-per // 128) * 128
        shape = (32, count)
        wide = jnp.where(iota(shape, 1) // per == iota(shape, 0), vector, 0.0).astype(bf16)
        select = (iota((count, lanes), 0) % per == iota((count, lanes), 1)).astype(bf16)
        block[:, row, :lanes] = jnp.dot(wide, select, preferred_element_type=f32)


def layer_norm(values):
    centred = values - jnp.mean(values, axis=-1, keepdims=True)
    inverse = lax.rsqrt(jnp.mean(centred * centred, axis=-1, keepdims=True) + epsilon)
    return centred * inverse, inverse


def turn_matrix(tokens):
    place = iota((tokens, tokens), 0)
    quarter = tokens // 4
    return (iota((tokens, tokens), 1) == 4 * (place % quarter) + place // quarter).astype(bf16)


def call(body, name, grid, operands, specs, outs, out_specs, scratch, room, load, aliases=None):
    return pl.pallas_call(
        body,
        grid_spec=pltpu.PrefetchScalarGridSpec(
            num_scalar_prefetch=1, grid=grid, in_specs=specs, out_specs=out_specs, scratch_shapes=scratch
        ),
        out_shape=outs,
        compiler_params=pltpu.CompilerParams(vmem_limit_bytes=room * MIB),
        cost_estimate=pl.CostEstimate(flops=1024, bytes_accessed=load * MIB // 16, transcendentals=0),
        input_output_aliases=aliases or {},
        name=name,
    )(*operands)


def shaped(shape, dtype):
    return jax.ShapeDtypeStruct(shape, dtype)


def rows_spec(rows, columns):
    return pl.BlockSpec((rows, columns), lambda i, ids: (i, 0))


def fixed_spec(shape):
    return pl.BlockSpec(shape, lambda i, ids: (0,) * len(shape))


def prepare_body(ids, hidden, output_words, feed_words, turned, keep_output, keep_feed):
    tokens, width = hidden.shape
    turned[...] = jnp.dot(turn_matrix(tokens), hidden[...], preferred_element_type=f32).astype(bf16)
    quarter = width // 4
    for words, keep in ((output_words, keep_output), (feed_words, keep_feed)):
        packed = words[0, 0]
        total = jnp.zeros((tokens, width), f32)
        for i in range(4):
            bit = ((packed & (7 << (3 * i))) != 0).astype(f32).astype(bf16)
            place = (iota((quarter, width), 1) == 4 * iota((quarter, width), 0) + i).astype(bf16)
            total = total + t_dot(bit, place)
        keep[...] = total.astype(bf16)


def prepare(ids, hidden, output_words, feed_words, tokens):
    rows, width = hidden.shape
    wide = rows_spec(tokens, width)
    narrow = pl.BlockSpec((1, 1, width // 4, tokens), lambda i, ids: (i, 0, 0, 0))
    return call(
        prepare_body,
        "prepare",
        (rows // tokens,),
        (ids, hidden, output_words, feed_words),
        [wide, narrow, narrow],
        [shaped((rows, width), bf16)] * 3,
        [wide] * 3,
        [],
        12,
        6,
    )


def project_body(weights, per, ids, *refs):
    count = len(weights.operands)
    sources, (hidden, turned, queries), rest = refs[:count], refs[count : count + 3], refs[count + 3 :]
    micro, tokens, width = queries.shape
    places, sems = rest[len(rest) - 1 - len(weights.shapes) : -1], rest[-1]
    near = iter(rest[: len(rest) - 1 - len(weights.shapes)])
    copies = weights.copies(ids, sources, places, sems)
    begin(copies)
    finish(copies[3])
    block = weights.matrix(places, 3)[:, :128].astype(f32).reshape(32, 8, 128)
    bias = spread(block, 0, 2 * width, per)
    for n in range(3):
        finish(copies[n])
    for m in range(micro):
        natural, other = hidden[m * tokens : (m + 1) * tokens, :], turned[m * tokens : (m + 1) * tokens, :]
        q = jnp.dot(natural, weights.matrix(places, 0)[...], preferred_element_type=f32) + bias[:, :width]
        queries[m] = q.astype(bf16)
        k = jnp.dot(other, weights.matrix(places, 1)[...], preferred_element_type=f32).astype(bf16)
        v = jnp.dot(other, weights.matrix(places, 2)[...], preferred_element_type=f32) + bias[:, width:]
        for value in (k, v.astype(bf16)):
            rows = tokens // PARTS[m]
            for part in range(PARTS[m]):
                next(near)[...] = value[part * rows : (part + 1) * rows]


def project(ids, weights, hidden, turned, micro, per):
    rows, width = hidden.shape
    return call(
        functools.partial(project_body, weights, per),
        "project",
        (1,),
        (ids, *weights.operands, hidden, turned),
        weights.specs + [WHOLE] * 2,
        [shaped((micro, rows // micro, width), bf16)]
        + [shaped((rows // micro // PARTS[m], width), bf16) for m in range(micro) for _ in range(2 * PARTS[m])],
        [WHOLE] * (1 + 2 * sum(PARTS)),
        weights.scratch,
        16,
        10,
    )


def lane_half(shape):
    return iota(shape, len(shape) - 1) < 64


def by_head(pair):
    left, zero = lane_half(pair.shape), jnp.zeros_like(pair)
    return jnp.concatenate([jnp.where(left, pair, zero), jnp.where(left, zero, pair)], axis=0)


def join_keys(core, near, far, buffer, lanes):
    quarter = buffer.shape[0] // 8
    parts = len(near)
    for i in range(4):
        here = pl.multiple_of((2 * i + core) * quarter, quarter)
        there = pl.multiple_of((2 * i + 1 - core) * quarter, quarter)
        at = (i * parts % 4) // parts * quarter
        buffer[pl.ds(here, quarter), :] = near[i * parts // 4][at : at + quarter, lanes]
        buffer[pl.ds(there, quarter), :] = far[i * parts // 4][at : at + quarter, lanes]


def group_lanes():
    return [slice(j * 128, (j + 1) * 128) for j in range(GROUP)]


def attention_body(parts, ids, q, *refs):
    ours, words = refs[: 4 * parts], refs[4 * parts]
    context, signed, keys, values = refs[-4:]
    core = ids[0]
    tokens = q.shape[1]
    for j, lanes in enumerate(group_lanes()):
        join_keys(core, ours[:parts], ours[2 * parts : 3 * parts], keys.at[j], lanes)
        join_keys(core, ours[parts : 2 * parts], ours[3 * parts :], values.at[j], lanes)
    scores = [dot_t(by_head(q[0, :, lanes]) * 0.125, keys[j]) for j, lanes in enumerate(group_lanes())]
    for j, lanes in enumerate(group_lanes()):
        blocks = [scores[j][:, i * 128 : (i + 1) * 128] for i in range(4)]
        peak = jnp.maximum(jnp.maximum(blocks[0], blocks[1]), jnp.maximum(blocks[2], blocks[3]))
        peak = jnp.max(peak, axis=1, keepdims=True)
        blocks = [jnp.exp(block - peak) for block in blocks]
        total = jnp.sum((blocks[0] + blocks[1]) + (blocks[2] + blocks[3]), axis=1, keepdims=True)
        scale = 1.0 / total
        word = words[0, 2 * j : 2 * j + 2].reshape(2 * tokens, 128)
        dropped = []
        for i in range(4):
            weight = blocks[i] * scale
            keep = (word & (7 << (3 * i))) != 0
            weight = jnp.where(keep, weight, -weight).astype(bf16)
            signed[0, j, i] = weight
            dropped.append(jnp.maximum(weight, jnp.zeros_like(weight)))
        out = jnp.dot(jnp.concatenate(dropped, axis=1), values[j], preferred_element_type=f32) * keep_scale
        context[0, :, lanes] = jnp.where(lane_half((tokens, 128)), out[:tokens], out[tokens:]).astype(bf16)


def attention(ids, m, queries, near, far, words, earlier=()):
    micro, tokens, width = queries.shape
    pairs = width // 128
    part = pl.BlockSpec((1, tokens, 128 * GROUP), lambda p, ids: (m, 0, p))
    flat = pl.BlockSpec((tokens // PARTS[m], 128 * GROUP), lambda p, ids: (0, p))
    operands = (ids, queries, *near[m], *far[m], words)
    return call(
        functools.partial(attention_body, PARTS[m]),
        "attention",
        (pairs // GROUP,),
        operands + tuple(earlier),
        [part] + [flat] * (4 * PARTS[m])
        + [pl.BlockSpec((1, 2 * GROUP, tokens, 128), lambda p, ids: (m, p, 0, 0))]
        + [ANY] * len(earlier),
        [shaped((micro, tokens, width), bf16), shaped((micro, pairs, 4, 2 * tokens, 128), bf16)],
        [part, pl.BlockSpec((1, GROUP, 4, 2 * tokens, 128), lambda p, ids: (m, p, 0, 0, 0))],
        [pltpu.VMEM((GROUP, 2 * tokens, 128), bf16)] * 2,
        16,
        14,
        {len(operands) + i: i for i in range(len(earlier))},
    )


def attention_back_body(parts, ids, q, *refs):
    ours, signed, upstream, refs = refs[: 4 * parts], refs[4 * parts], refs[4 * parts + 1], refs[4 * parts + 2 :]
    g_q, *grads, keys, values, sums = refs
    g_near, g_far = grads[:2], grads[2:]
    core = ids[0]
    tokens = q.shape[1]
    for j, lanes in enumerate(group_lanes()):
        join_keys(core, ours[:parts], ours[2 * parts : 3 * parts], keys.at[j], lanes)
        join_keys(core, ours[parts : 2 * parts], ours[3 * parts :], values.at[j], lanes)
    aboves = [by_head(upstream[:, lanes]) for lanes in group_lanes()]
    g_droppeds = [dot_t(aboves[j], values[j]) for j in range(GROUP)]
    for j, lanes in enumerate(group_lanes()):
        weights, kept, g_weights = [], [], []
        delta = None
        for i in range(4):
            both_signs = signed[0, j, i].astype(f32)
            weight = jnp.abs(both_signs)
            g_weight = jnp.where(both_signs > 0.0, g_droppeds[j][:, i * 128 : (i + 1) * 128], 0.0)
            term = g_weight * weight
            delta = term if delta is None else delta + term
            weights.append(weight)
            g_weights.append(g_weight)
            kept.append(jnp.maximum(both_signs, 0.0).astype(bf16))
        delta = jnp.sum(delta, axis=1, keepdims=True)
        g_scores = jnp.concatenate(
            [(weights[i] * (g_weights[i] - delta)).astype(bf16) for i in range(4)], axis=1
        )
        dropped = jnp.concatenate(kept, axis=1)
        out = jnp.dot(g_scores, keys[j], preferred_element_type=f32)
        out = jnp.where(lane_half((tokens, 128)), out[:tokens], out[tokens:])
        g_q[:, lanes] = (out * (0.125 * keep_scale)).astype(bf16)
        quarter = keys.shape[1] // 8
        sums[j, 0] = t_dot(g_scores, by_head(q[0, :, lanes])) * (0.125 * keep_scale)
        sums[j, 1] = t_dot(dropped, aboves[j]) * keep_scale
        for kind in range(2):
            for i in range(4):
                here = pl.multiple_of((2 * i + core) * quarter, quarter)
                there = pl.multiple_of((2 * i + 1 - core) * quarter, quarter)
                rows = slice(i * quarter, (i + 1) * quarter)
                g_near[kind][rows, lanes] = sums[j, kind, pl.ds(here, quarter), :]
                g_far[kind][rows, lanes] = sums[j, kind, pl.ds(there, quarter), :].astype(bf16)


def attention_back(ids, m, queries, near, far, signed, upstream):
    micro, tokens, width = queries.shape
    pairs = width // 128
    part = pl.BlockSpec((1, tokens, 128 * GROUP), lambda p, ids: (m, 0, p))
    flat = pl.BlockSpec((tokens // PARTS[m], 128 * GROUP), lambda p, ids: (0, p))
    both = pl.BlockSpec((tokens, 128 * GROUP), lambda p, ids: (0, p))
    operands = (ids, queries, *near[m], *far[m], signed, upstream)
    return call(
        functools.partial(attention_back_body, PARTS[m]),
        "attention_back",
        (pairs // GROUP,),
        operands,
        [part] + [flat] * (4 * PARTS[m])
        + [pl.BlockSpec((1, GROUP, 4, 2 * tokens, 128), lambda p, ids: (m, p, 0, 0, 0))]
        + [pl.BlockSpec((tokens, 128 * GROUP), lambda p, ids: (m, p))],
        [
            shaped((tokens, width), bf16),
            shaped((tokens, width), f32),
            shaped((tokens, width), f32),
            shaped((tokens, width), bf16),
            shaped((tokens, width), bf16),
        ],
        [both] * 5,
        [pltpu.VMEM((GROUP, 2 * tokens, 128), bf16)] * 2 + [pltpu.VMEM((GROUP, 2, 2 * tokens, 128), f32)],
        24,
        20,
    )


def up_body(weights, pers, tokens, ids, *refs):
    count = len(weights.operands)
    sources = refs[:count]
    context, hidden, keep, vectors, scaled, inverse, activated, slope = refs[count : count + 8]
    places, (sems, lows) = refs[count + 8 : -2], refs[-2:]
    copies = weights.copies(ids, sources, places, sems)
    rows, width = scaled.shape
    wide = activated.shape[1]
    begin([copies[0], copies[2], copies[1]])
    finish(copies[2])
    block = weights.matrix(places, 2)[:, :128].astype(f32).reshape(32, 8, 128)
    for row, per in enumerate(pers):
        vectors[row : row + 1, : 32 * per] = spread(block, row, 32 * per, per)
    finish(copies[0])

    def rows_part(m, carry):
        at = pl.ds(pl.multiple_of(m * tokens, tokens), tokens)
        attended = jnp.dot(context[at], weights.matrix(places, 0)[...], preferred_element_type=f32)
        attended = attended + vectors[0:1, :width]
        first_sum = hidden[at].astype(f32) + attended * (keep[at].astype(f32) * keep_scale)
        normal, scale = layer_norm(first_sum)
        scaled[at] = normal
        inverse[at] = jnp.broadcast_to(scale, (tokens, 128))
        lows[at] = (normal * vectors[1:2, :width] + vectors[2:3, :width]).astype(bf16)
        return carry

    lax.fori_loop(0, rows // tokens, rows_part, 0)
    finish(copies[1])
    up = weights.matrix(places, 1)
    step = 512

    def part(n, carry):
        at = pl.ds(pl.multiple_of(n * step, step), step)
        inner = jnp.dot(lows[...], up[:, at], preferred_element_type=f32) + vectors[3:4, at]
        cdf = 0.5 * (1.0 + lax.erf(inner * root_half))
        density = jnp.exp(-0.5 * inner * inner) * inverse_root_tau
        activated[:, at] = (inner * cdf).astype(bf16)
        slope[:, at] = (cdf + inner * density).astype(bf16)
        return carry

    lax.fori_loop(0, wide // step, part, 0)


def feed_up(ids, weights, pers, context, hidden, keep, tokens, wide):
    rows, width = hidden.shape
    return call(
        functools.partial(up_body, weights, pers, tokens),
        "feed_up",
        (1,),
        (ids, *weights.operands, context, hidden, keep),
        weights.specs + [WHOLE] * 3,
        [
            shaped((8, wide), f32),
            shaped((rows, width), f32),
            shaped((rows, 128), f32),
            shaped((rows, wide), bf16),
            shaped((rows, wide), bf16),
        ],
        [WHOLE] * 5,
        weights.scratch + [pltpu.VMEM((rows, width), bf16)],
        28,
        24,
    )


def hand_out(core, total, rows, own, send, first, at):
    def one(n, carry):
        here = pl.multiple_of((2 * n + core) * rows, 8)
        there = pl.multiple_of((2 * n + 1 - core) * rows, 8)
        own[first + n, at : at + rows, :] = total[pl.ds(here, rows), :].astype(bf16)
        send[first + n, at : at + rows, :] = total[pl.ds(there, rows), :].astype(bf16)
        return carry

    lax.fori_loop(0, total.shape[0] // (2 * rows), one, 0)


def down_body(weights, tokens, ids, *refs):
    count = len(weights.operands)
    sources, refs = refs[:count], refs[count:]
    activated, slope, scaled, keep, cotangent, vectors = refs[:6]
    layer_out, g_second_out, g_inner, own, send, sums = refs[6:12]
    place, sems, total, g_outers = refs[12:]
    copies = weights.copies(ids, sources, (place,), sems)
    rows, width = scaled.shape
    wide = activated.shape[1]
    begin(copies)
    sums[...] = jnp.zeros_like(sums)
    finish(copies[0])
    down = weights.matrix((place,), 0)
    gain = vectors[5:6, :width]

    def rows_part(m, carry):
        at = pl.ds(pl.multiple_of(m * tokens, tokens), tokens)
        outer = jnp.dot(activated[at], down[...], preferred_element_type=f32) + vectors[4:5, :width]
        factor = keep[at].astype(f32) * keep_scale
        normed = scaled[at] * vectors[1:2, :width] + vectors[2:3, :width]
        normal, scale = layer_norm(normed + outer * factor)
        layer_out[at] = (normal * gain + vectors[6:7, :width]).astype(bf16)
        above = cotangent[at].astype(f32)
        weighted = above * gain
        g_second = scale * (
            weighted
            - jnp.mean(weighted, axis=-1, keepdims=True)
            - normal * jnp.mean(weighted * normal, axis=-1, keepdims=True)
        )
        g_second_out[at] = g_second
        g_outer = (g_second * factor).astype(bf16)
        g_outers[at] = g_outer
        sums[0:1, :width] += jnp.sum(g_outer.astype(f32), axis=0, keepdims=True)
        sums[1:2, :width] += jnp.sum(above * normal, axis=0, keepdims=True)
        sums[2:3, :width] += jnp.sum(above, axis=0, keepdims=True)
        return carry

    lax.fori_loop(0, rows // tokens, rows_part, 0)
    step = 512

    def part(n, carry):
        at = pl.ds(pl.multiple_of(n * step, step), step)
        g_in = (dot_t(g_outers[...], down[at, :]) * slope[:, at].astype(f32)).astype(bf16)
        g_inner[:, at] = g_in
        sums[3:4, at] = jnp.sum(g_in.astype(f32), axis=0, keepdims=True)
        return carry

    lax.fori_loop(0, wide // step, part, 0)

    def grads(n, carry):
        at = pl.ds(pl.multiple_of(n * width, width), width)
        total[...] = t_dot(activated[:, at], g_outers[...])
        hand_out(ids[0], total, wide // 32, own, send, n * (16 * width // wide), 0)
        return carry

    lax.fori_loop(0, wide // width, grads, 0)


def feed_down(ids, weights, activated, slope, scaled, keep, cotangent, vectors, tokens):
    rows, width = scaled.shape
    wide = activated.shape[1]
    halves = (16, wide // 32, width)
    return call(
        functools.partial(down_body, weights, tokens),
        "feed_down",
        (1,),
        (ids, *weights.operands, activated, slope, scaled, keep, cotangent, vectors),
        weights.specs + [WHOLE] * 6,
        [
            shaped((rows, width), bf16),
            shaped((rows, width), f32),
            shaped((rows, wide), bf16),
            shaped(halves, bf16),
            shaped(halves, bf16),
            shaped((8, wide), f32),
        ],
        [WHOLE] * 6,
        weights.scratch + [pltpu.VMEM((width, width), f32), pltpu.VMEM((rows, width), bf16)],
        30,
        36,
    )


def middle_body(weights, pers, tokens, ids, *refs):
    count = len(weights.operands)
    sources, refs = refs[:count], refs[count:]
    g_inner, g_second, scaled, inverse, keep, vectors, context, down_sums = refs[:8]
    g_first_out, g_context, own, send, block = refs[8:13]
    *places, sems, g_normeds, g_attendeds, sums = refs[13:]
    copies = weights.copies(ids, sources, places, sems)
    begin([copies[1], copies[0]])
    rows, width = scaled.shape
    out_w, up_w = weights.matrix(places, 0), weights.matrix(places, 1)
    finish(copies[1])
    step = 256

    def columns_part(n, carry):
        at = pl.ds(pl.multiple_of(n * step, step), step)
        g_normeds[:rows, at] = g_second[:, at] + dot_t(g_inner[...], up_w[at, :])
        return carry

    lax.fori_loop(0, width // step, columns_part, 0)
    sums[...] = jnp.zeros_like(sums)

    def rows_part(m, carry):
        at = pl.ds(pl.multiple_of(m * tokens, tokens), tokens)
        normal = scaled[at]
        g_normed = g_normeds[at, :]
        weighted = g_normed * vectors[1:2, :width]
        g_first = inverse[at, 0:1] * (
            weighted
            - jnp.mean(weighted, axis=-1, keepdims=True)
            - normal * jnp.mean(weighted * normal, axis=-1, keepdims=True)
        )
        g_first_out[at] = g_first
        g_attended = (g_first * (keep[at].astype(f32) * keep_scale)).astype(bf16)
        g_attendeds[at] = g_attended
        sums[0:1, :] += jnp.sum(g_attended.astype(f32), axis=0, keepdims=True)
        sums[1:2, :] += jnp.sum(g_normed * normal, axis=0, keepdims=True)
        sums[2:3, :] += jnp.sum(g_normed, axis=0, keepdims=True)
        return carry

    lax.fori_loop(0, rows // tokens, rows_part, 0)
    finish(copies[0])
    g_context[...] = dot_t(g_attendeds[...], out_w[...]).astype(bf16)
    g_normeds[:width] = t_dot(context[...], g_attendeds[...])
    hand_out(ids[0], g_normeds, width // 32, own, send, 0, 0)
    vector_sums = [sums[n : n + 1, :] for n in range(3)]
    vector_sums += [down_sums[3:4, :]] + [down_sums[n : n + 1, :width] for n in range(3)]
    unspread(vector_sums, pers, block)


def middle(ids, weights, pers, g_inner, g_second, scaled, inverse, keep, vectors, context, sums, tokens):
    rows, width = scaled.shape
    halves = (16, width // 32, width)
    return call(
        functools.partial(middle_body, weights, pers, tokens),
        "middle",
        (1,),
        (ids, *weights.operands, g_inner, g_second, scaled, inverse, keep, vectors, context, sums),
        weights.specs + [WHOLE] * 8,
        [
            shaped((rows, width), f32),
            shaped((rows, width), bf16),
            shaped(halves, bf16),
            shaped(halves, bf16),
            shaped((32, 8, width), f32),
        ],
        [WHOLE] * 5,
        weights.scratch
        + [pltpu.VMEM((max(rows, width), width), f32), pltpu.VMEM((rows, width), bf16), pltpu.VMEM((8, width), f32)],
        26,
        18,
    )


def grads_body(ids, g_inner, scaled, vectors, own, send, total, low_t):
    n = pl.program_id(0)
    width = scaled.shape[1]

    @pl.when(n == 0)
    def _():
        low_t[...] = (scaled[...] * vectors[1:2, :width] + vectors[2:3, :width]).T.astype(bf16)

    total[...] = jnp.dot(low_t[...], g_inner[...], preferred_element_type=f32)
    for block in range(own.shape[1] // (width // 32)):

        @pl.when(n == block)
        def _():
            hand_out(ids[0], total, width // 32, own, send, 0, block * (width // 32))


def up_grads(ids, g_inner, scaled, vectors):
    rows, width = scaled.shape
    wide = g_inner.shape[1]
    halves = (16, wide // 32, width)
    return call(
        grads_body,
        "up_grads",
        (wide // width,),
        (ids, g_inner, scaled, vectors),
        [pl.BlockSpec((rows, width), lambda i, ids: (0, i))] + [WHOLE] * 2,
        [shaped(halves, bf16), shaped(halves, bf16)],
        [WHOLE] * 2,
        [pltpu.VMEM((width, width), f32), pltpu.VMEM((width, rows), bf16)],
        24,
        20,
    )


def hand_out_rows(core, block, own, send, at):
    for n in range(16):
        own[n, at : at + 8, :] = block[2 * n + core].astype(bf16)
        send[n, at : at + 8, :] = block[2 * n + 1 - core].astype(bf16)


def inputs_body(per, ids, hidden, turned, *refs):
    micro = (len(refs) - 8) // 5
    grads, (block, own, send, g_queries, g_keys, g_values, total, bias) = refs[: 5 * micro], refs[5 * micro :]
    width = hidden.shape[1]
    sums = []
    for n, out in enumerate((g_queries, g_keys, g_values)):
        for m in range(micro):
            g_q, near, far = grads[m], grads[micro + 2 * m :][:2], grads[3 * micro + 2 * m :][:2]
            rows = slice(m * g_q.shape[0], (m + 1) * g_q.shape[0])
            if n == 0:
                out[rows] = g_q[...]
            else:
                out[rows] = (near[n - 1][...] + far[n - 1][...].astype(f32)).astype(bf16)
        if n != 1:
            sums.append(jnp.sum(out[...].astype(f32), axis=0, keepdims=True))
        left = hidden if n == 0 else turned
        for start in range(0, width, 256):
            total[start : start + 256, :] = t_dot(left[:, start : start + 256], out[...])
        hand_out(ids[0], total, width // 32, own, send, 0, n * (width // 32))
    bias[...] = block[...]
    unspread([jnp.concatenate(sums, axis=1)], [per], bias, 7)
    hand_out_rows(ids[0], bias, own, send, 3 * (width // 32))


def input_grads(ids, hidden, turned, grads, block, per):
    rows, width = hidden.shape
    halves = (16, 3 * width // 32 + 8, width)
    return call(
        functools.partial(inputs_body, per),
        "input_grads",
        (1,),
        (ids, hidden, turned, *grads, block),
        [WHOLE] * (3 + len(grads)),
        [shaped(halves, bf16)] * 2 + [shaped((rows, width), bf16)] * 3,
        [WHOLE] * 5,
        [pltpu.VMEM((width, width), f32), pltpu.VMEM((32, 8, width), f32)],
        28,
        12,
    )


def last_body(weights, ids, *refs):
    count = len(weights.operands)
    sources = refs[:count]
    g_first, g_q, g_keys, g_values, out = refs[count : count + 5]
    places, sems = refs[count + 5 : -1], refs[-1]
    copies = weights.copies(ids, sources, places, sems)

    @pl.when(pl.program_id(0) == 0)
    def _():
        begin(copies)
        for group in copies:
            finish(group)

    turn = turn_matrix(g_q.shape[0])
    total = g_first[...] + dot_t(g_q[...], weights.matrix(places, 0)[...])
    total = total + dot_t(t_dot(turn, g_keys[...]).astype(bf16), weights.matrix(places, 1)[...])
    total = total + dot_t(t_dot(turn, g_values[...]).astype(bf16), weights.matrix(places, 2)[...])
    out[...] = total.astype(bf16)


def last(ids, weights, g_first, g_q, g_keys, g_values, tokens):
    rows, width = g_first.shape
    narrow = rows_spec(tokens, width)
    return call(
        functools.partial(last_body, weights),
        "input_back",
        (rows // tokens,),
        (ids, *weights.operands, g_first, g_q, g_keys, g_values),
        weights.specs + [narrow] * 4,
        [shaped((rows, width), bf16)],
        [narrow],
        weights.scratch,
        16,
        10,
    )[0]


def beside(shape, y, x):
    return pl.BlockSpec((4, 1, 1) + shape[3:], lambda i, ids: (0, ids[1] ^ y, ids[2] ^ x, 0, 0))


def rows_of(parts, index, first, last):
    found, start = [], 0
    for part in parts:
        rows = part.shape[-2]
        low, high = max(first, start), min(last, start + rows)
        if low < high:
            found.append(part[index + (slice(low - start, high - start),)].astype(f32))
        start += rows
    return found[0] if len(found) == 1 else jnp.concatenate(found, axis=-2)


def both(parts, index, first, last):
    half = len(parts) // 2
    return rows_of(parts[:half], index, first, last) + rows_of(parts[half:], index, first, last)


def count_rows(parts):
    return sum(part.shape[3] for part in parts[: len(parts) // 2])


PLANE = (slice(None), 0, 0)


def corner_body(ids, *refs):
    *parts, low, high = refs
    half = low.shape[1]
    low[...] = both(parts, PLANE, 0, half).astype(bf16)
    high[...] = both(parts, PLANE, half, half + high.shape[1]).astype(bf16)


def reduce_corner(ids, parts, cut):
    rows, width = count_rows(parts), parts[0].shape[4]
    return call(
        corner_body,
        "reduce_corner",
        (1,),
        (ids, *parts),
        [beside(part.shape, 1, 1) for part in parts],
        [shaped((4, cut, width), bf16), shaped((4, rows - cut, width), bf16)],
        [WHOLE] * 2,
        [],
        8,
        2,
    )


def sides_body(count, ids, *refs):
    for_y, for_x, (low, high, to_y, to_x) = refs[:count], refs[count : 2 * count], refs[2 * count :]
    rows, half = to_y.shape[1], low.shape[1]
    to_y[:, :half] = (both(for_y, PLANE, 0, half) + low[...].astype(f32)).astype(bf16)
    to_y[:, half:] = both(for_y, PLANE, half, rows).astype(bf16)
    to_x[:, :half] = both(for_x, PLANE, 0, half).astype(bf16)
    to_x[:, half:] = (both(for_x, PLANE, half, rows) + high[...].astype(f32)).astype(bf16)


def reduce_sides(ids, parts, low, high):
    rows, width = count_rows(parts), parts[0].shape[4]
    return call(
        functools.partial(sides_body, len(parts)),
        "reduce_sides",
        (1,),
        (ids, *parts, *parts, low, high),
        [beside(part.shape, 1, 0) for part in parts]
        + [beside(part.shape, 0, 1) for part in parts]
        + [WHOLE] * 2,
        [shaped((4, rows, width), bf16)] * 2,
        [WHOLE] * 2,
        [],
        10,
        3,
    )


def depth_body(ids, *refs):
    *parts, from_y, from_x, near, middle, far, mine = refs
    for k, out in enumerate((mine, near, middle, far)):
        z = ids[3] ^ k
        total = both(parts, (z, 0, 0), 0, from_y.shape[1])
        total = total + from_y[z].astype(f32) + from_x[z].astype(f32)
        out[...] = total.astype(out.dtype)


def reduce_depth(ids, parts, from_y, from_x):
    shape = from_y.shape[1:]
    return call(
        depth_body,
        "reduce_depth",
        (1,),
        (ids, *parts, from_y, from_x),
        [beside(part.shape, 0, 0) for part in parts] + [WHOLE] * 2,
        [shaped(shape, bf16)] * 3 + [shaped(shape, f32)],
        [WHOLE] * 4,
        [],
        10,
        3,
    )


def pair_body(ids, one, two, out):
    out[0] = one[...]
    out[1] = two[...]


def pair_z(ids, one, two):
    return call(
        pair_body,
        "pair_z",
        (1,),
        (ids, one, two),
        [WHOLE] * 2,
        [shaped((2,) + one.shape, bf16)],
        [WHOLE],
        [],
        4,
        1,
    )[0]


def order_body(ids, pair, received, out):
    for k in range(2):
        out[ids[3] ^ (2 * k)] = pair[k]
        out[ids[3] ^ (2 * k + 1)] = received[k]


def order_z(ids, pair, received):
    return call(
        order_body,
        "order_z",
        (1,),
        (ids, pair, received),
        [WHOLE] * 2,
        [shaped((4,) + pair.shape[1:], bf16)],
        [WHOLE],
        [],
        6,
        1,
    )[0]


def four_body(ids, *refs):
    *parts, out = refs
    for k, part in enumerate(parts):
        out[ids[3] ^ k] = part[...]


def order_four(ids, *parts):
    return call(
        four_body,
        "order_four",
        (1,),
        (ids, *parts),
        [WHOLE] * 4,
        [shaped((4,) + parts[0].shape, bf16)],
        [WHOLE],
        [],
        6,
        1,
    )[0]


def halves_body(ids, pair, received, low, high):
    rows = low.shape[1]
    for k in range(2):
        for source, z in ((pair, ids[3] ^ (2 * k)), (received, ids[3] ^ (2 * k + 1))):
            low[z] = source[k, :rows]
            high[z] = source[k, rows:]


def order_halves(ids, pair, received):
    shape = (4, pair.shape[1] // 2, pair.shape[2])
    return call(
        halves_body,
        "order_halves",
        (1,),
        (ids, pair, received),
        [WHOLE] * 2,
        [shaped(shape, bf16)] * 2,
        [WHOLE] * 2,
        [],
        6,
        1,
    )


def first_body(ids, *refs):
    at_y, at_x, at_corner, (to_y, to_x) = refs[:2], refs[2:4], refs[4:6], refs[6:]
    half = to_y.shape[1] // 2
    to_y[:, :half] = both(at_y, PLANE, 0, half).astype(bf16)
    to_y[:, half:] = both(at_corner, PLANE, 0, half).astype(bf16)
    to_x[:, :half] = both(at_x, PLANE, half, 2 * half).astype(bf16)
    to_x[:, half:] = both(at_corner, PLANE, half, 2 * half).astype(bf16)


def reduce_first(ids, parts):
    shape = parts[0].shape
    return call(
        first_body,
        "reduce_first",
        (1,),
        (ids, *parts, *parts, *parts),
        [beside(shape, 1, 0)] * 2 + [beside(shape, 0, 1)] * 2 + [beside(shape, 1, 1)] * 2,
        [shaped((4,) + shape[3:], bf16)] * 2,
        [WHOLE] * 2,
        [],
        10,
        3,
    )


def second_body(ids, *refs):
    here, at_y, at_x, (from_y, from_x, *outs) = refs[:2], refs[2:4], refs[4:6], refs[6:]
    half = from_y.shape[1] // 2
    by_next, keep_next, by_far, keep_far = outs
    for k, upper, lower in (
        (0, (keep_next, 0), (keep_far, 0)),
        (1, (by_next, 0), (keep_far, 1)),
        (2, (keep_next, 1), (by_far, 0)),
        (3, (by_next, 1), (by_far, 1)),
    ):
        z = ids[3] ^ k
        plane = (z, 0, 0)
        quarters = (
            both(here, plane, 0, half) + from_y[z, :half].astype(f32),
            both(at_x, plane, 0, half) + from_y[z, half:].astype(f32),
            both(here, plane, half, 2 * half) + from_x[z, :half].astype(f32),
            both(at_y, plane, half, 2 * half) + from_x[z, half:].astype(f32),
        )
        for i, quarter in enumerate(quarters):
            out, at = upper if i < 2 else lower
            out[at, i % 2 * half : (i % 2 + 1) * half] = quarter.astype(out.dtype)


def reduce_second(ids, parts, from_y, from_x):
    shape = parts[0].shape
    wide = (2,) + shape[3:]
    return call(
        second_body,
        "reduce_second",
        (1,),
        (ids, *parts, *parts, *parts, from_y, from_x),
        [beside(shape, 0, 0)] * 2 + [beside(shape, 1, 0)] * 2 + [beside(shape, 0, 1)] * 2 + [WHOLE] * 2,
        [shaped(wide, bf16), shaped(wide, f32)] * 2,
        [WHOLE] * 4,
        [],
        14,
        3,
    )


def third_body(ids, keep_next, keep_far, next_in, far_in, next_mine, far_mine, to_far, to_next):
    next_mine[...] = keep_next[0] + next_in[0].astype(f32)
    to_far[...] = (keep_next[1] + next_in[1].astype(f32)).astype(bf16)
    far_mine[...] = keep_far[0] + far_in[0].astype(f32)
    to_next[...] = (keep_far[1] + far_in[1].astype(f32)).astype(bf16)


def reduce_third(ids, keep_next, keep_far, next_in, far_in):
    shape = keep_next.shape[1:]
    return call(
        third_body,
        "reduce_third",
        (1,),
        (ids, keep_next, keep_far, next_in, far_in),
        [WHOLE] * 4,
        [shaped(shape, f32)] * 2 + [shaped(shape, bf16)] * 2,
        [WHOLE] * 4,
        [],
        10,
        2,
    )


def fourth_body(ids, upper, lower, from_far, from_next, to_x, to_y, own):
    half = to_x.shape[0]
    first = upper[...] + from_far[...].astype(f32)
    second = lower[...] + from_next[...].astype(f32)
    own[:half] = first[:half]
    own[half:] = second[:half]
    to_x[...] = first[half:].astype(bf16)
    to_y[...] = second[half:].astype(bf16)


def reduce_fourth(ids, upper, lower, from_far, from_next):
    rows, width = upper.shape
    return call(
        fourth_body,
        "reduce_fourth",
        (1,),
        (ids, upper, lower, from_far, from_next),
        [WHOLE] * 4,
        [shaped((rows // 2, width), bf16)] * 2 + [shaped((rows, width), f32)],
        [WHOLE] * 3,
        [],
        8,
        2,
    )


def exchange_z(sends):
    return [pp(send, "z", k) for send, k in zip(sends, (1, 2, 3))]


def local(
    hidden_in,
    cotangent,
    attention_keep,
    output_keep,
    feed_keep,
    qkv_weight,
    qkv_bias,
    out_weight,
    out_bias,
    first_gain,
    first_shift,
    up_weight,
    up_bias,
    down_weight,
    down_bias,
    second_gain,
    second_shift,
):
    micro, _, tokens, width = hidden_in.shape
    rows = micro * tokens
    own = qkv_weight.shape[0]
    wide = up_weight.shape[1]
    blocks = wide // width
    c, y, x = lax.axis_index("seq"), lax.axis_index("y"), lax.axis_index("x")
    ids = jnp.stack([c, y, x, lax.axis_index("z")]).astype(jnp.int32)
    bias_parts = (out_bias, first_gain, first_shift, up_bias, down_bias, second_gain, second_shift)
    pers = [part.shape[0] for part in bias_parts]
    per = qkv_bias.shape[0]

    column = lambda weight, i: weight[:, i * width : (i + 1) * width]
    bias_rows = lambda parts: jnp.concatenate(
        [jnp.pad(part.reshape(1, -1), ((0, 0), (0, width - part.shape[0]))) for part in parts]
        + [jnp.zeros((8 - len(parts), width), bf16)]
    )
    square = (own, width)
    hidden = hidden_in.reshape(rows, width)

    shard_a = jnp.concatenate([column(qkv_weight, i) for i in range(3)] + [bias_rows((qkv_bias,))])
    half_c = down_weight.shape[0] // 2
    x_c, y_c = pp(down_weight[:half_c], "x"), pp(down_weight[half_c:], "y")
    shard_b = jnp.concatenate(
        [out_weight] + [column(up_weight, i) for i in range(blocks)] + [bias_rows(bias_parts)]
    )
    z_a = hold([pp(shard_a, "z", k) for k in (1, 2, 3)], x_c, y_c, shard_b)
    own_a = order_four(ids, shard_a, *z_a)
    group_c = jnp.concatenate([down_weight[:half_c], x_c, down_weight[half_c:], y_c])
    x_a, y_a = pp(own_a, "x"), pp(own_a, "y")
    shard_b = after(shard_b, own_a)
    far_b = pp(shard_b, "z", 2)
    turned, keep_output, keep_feed = prepare(
        ids, after(hidden, own_a), output_keep.transpose(0, 1, 3, 2), feed_keep.transpose(0, 1, 3, 2), tokens
    )
    x_a, y_a, far_b = hold((x_a, y_a, far_b), turned)
    cut_a = shard_a.shape[0] // 2
    low_a, high_a = pp(x_a[:, :cut_a], "y"), pp(y_a[:, cut_a:], "x")
    pieces = [whole(0, 0, own_a), whole(1, 0, x_a), whole(2, 0, y_a), whole(3, 0, low_a), whole(3, cut_a, high_a)]
    late = whole(2, 0, after(y_a, low_a))
    pieces += [at_core(piece) for piece in pieces[:2] + [late] + pieces[3:]]
    pair_b = pair_z(ids, shard_b, far_b)
    near_b = pp(pair_b, "z", 1)
    plan = [(i * own, own, i, 0, 0) for i in range(3)]
    plan = divide(plan, cut_a)
    weights = Weights(pieces, plan + [(3 * own, 8, 3, 0, 0)], [square] * 3 + [(8, width)])
    weights_again = Weights(pieces, plan, [square] * 3)
    own_b = order_z(ids, pair_b, after(near_b, low_a, high_a))
    far_c = pp(after(group_c, own_b), "z", 2)
    x_b, y_b = pp(own_b, "x"), pp(own_b, "y")
    queries, *near = project(ids, weights, hidden, after(turned, own_b), micro, per)
    near = (near[: 2 * PARTS[0]], near[2 * PARTS[0] :])
    far = [[pp(value, "seq") for value in values] for values in near]
    words = attention_keep.reshape(micro, H, tokens, -1)
    *far[0], far_c = hold((*far[0], far_c))
    pair_c = pair_z(ids, group_c, far_c)
    near_c = pp(pair_c, "z", 1)
    context, signed = attention(ids, 0, after(queries, pair_c), near, far, words)
    own_b, x_b, y_b, *far[1] = hold((own_b, x_b, y_b, *far[1]), context)
    cut_b = shard_b.shape[0] // 2
    low_b, high_b = pp(x_b[:, :cut_b], "y"), pp(y_b[:, cut_b:], "x")
    context, signed = attention(ids, 1, queries, near, far, words, (context, signed))
    low_b, high_b, near_c = hold((low_b, high_b, near_c), context)
    pieces = [whole(0, 0, own_b), whole(1, 0, x_b), whole(2, 0, after(y_b, context))]
    pieces += [at_core(piece) for piece in pieces]
    corners = [whole(3, 0, low_b), whole(3, cut_b, high_b)]
    pieces += corners + [at_core(piece) for piece in corners]
    plan = [(0, own, 0, 0, 0)] + [((i + 1) * own, own, 1, 0, i * width) for i in range(blocks)]
    plan = divide(plan, cut_b)
    weights = Weights(
        pieces, plan + [((blocks + 1) * own, 8, 2, 0, 0)], [square, (own, wide), (8, width)]
    )
    back_weights = Weights(pieces, plan, [square, (own, wide)])
    by_x, by_y = order_halves(ids, pair_c, after(near_c, low_b, high_b))
    from_y, from_x = pp(by_x, "y"), pp(by_y, "x")
    context = context.reshape(rows, width)
    vectors, scaled, inverse, activated, slope = feed_up(
        ids, weights, pers, context, hidden, keep_output, tokens, wide
    )
    from_y, from_x = hold((from_y, from_x), activated)
    down_rows = down_weight.shape[0]
    pieces = []
    for core in range(2):
        held = [by_x, from_y, by_y, from_x]
        if core == 1:
            held = [pp(array, "seq") for array in held]
        for array, numbers, first in zip(held, ((0, 1), (2, 3), (0, 2), (1, 3)), (0, 0, half_c, half_c)):
            pieces += [(4 * core + number, first, array, i * half_c, half_c) for i, number in enumerate(numbers)]
    plan = divide([(0, down_rows, 0, 0, 0)], half_c)
    weights = Weights(pieces, plan, [(down_rows, width)])
    layer_out, g_second, g_inner, down_own, down_send, sums = feed_down(
        ids, weights, activated, slope, scaled, keep_feed, cotangent.reshape(rows, width), vectors, tokens
    )

    unit = lambda value: value.reshape((4, 2, 2) + value.shape[1:])
    down_core = pp(down_send, "seq")
    mid_own, mid_send = up_grads(ids, g_inner, scaled, vectors)
    down = [unit(down_own), unit(after(down_core, mid_send))]
    to_y, to_x = reduce_first(ids, down)
    down_y, down_x = pp(to_y, "y"), pp(to_x, "x")
    mid_core = pp(after(mid_send, to_y), "seq")
    g_first, g_context, out_own, out_send, block = middle(
        ids, back_weights, pers, after(g_inner, to_y), g_second, scaled, inverse, keep_output, vectors, context, sums, tokens
    )
    out_core = pp(out_send, "seq")
    down_y, down_x, mid_core = hold((down_y, down_x, mid_core), g_context)
    mid = [unit(value) for value in (mid_own, out_own, mid_core, out_core)]
    cut_m = (count_rows(mid) + 15) // 16 * 8
    corner = reduce_corner(ids, mid, cut_m)
    low, high = pp(corner[0], "x"), pp(corner[1], "y")
    to_next, keep_next, to_far, keep_far = reduce_second(ids, down, down_y, down_x)
    next_in, far_in = pp(to_next, "z", 1), pp(to_far, "z", 2)
    first_q, *first_near, far_k, far_v = attention_back(
        ids, 0, queries, near, far, signed, after(g_context, to_next, *corner)
    )
    low, high = hold((low, high), first_q)
    first_far = [pp(after(value, low, high), "seq") for value in (far_k, far_v)]
    to_y, to_x = reduce_sides(ids, mid, low, high)
    mid_y, mid_x = pp(to_y, "y"), pp(to_x, "x")
    second_q, *second_near, far_k, far_v = attention_back(
        ids, 1, queries, near, far, signed, after(g_context, to_y, to_x)
    )
    first_far = hold(first_far, second_q)
    second_far = [pp(value, "seq") for value in (far_k, far_v)]
    next_in, far_in = hold((next_in, far_in), second_q)
    upper, lower, to_far, to_next = reduce_third(ids, keep_next, keep_far, next_in, far_in)
    far_in, next_in = pp(to_far, "z", 2), pp(to_next, "z", 1)
    grads = (first_q, second_q, *first_near, *second_near, *first_far, *hold(second_far, to_far))
    a_own, a_send, g_q, g_keys, g_values = input_grads(ids, hidden, turned, grads, block, per)
    mid_y, mid_x = hold((mid_y, mid_x), a_send)
    far_in, next_in = hold((far_in, next_in), a_send)
    core_sums = pp(after(a_send, mid_y, mid_x, far_in, next_in), "seq")
    to_far_x, to_far_y, down_mine = reduce_fourth(ids, upper, lower, far_in, next_in)
    part = [unit(a_own), unit(core_sums)]
    corner = reduce_corner(ids, part, cut_a)
    low, high = pp(corner[0], "x"), pp(corner[1], "y")
    *sends, mid_mine = reduce_depth(ids, mid, after(mid_y, *corner), mid_x)
    mid_z = exchange_z(sends)
    low, high = hold((low, high), *sends)
    to_y, to_x = reduce_sides(ids, part, low, high)
    side_y, side_x = pp(to_y, "y"), pp(to_x, "x")
    received = [pp(after(to_far_x, to_x), "x"), pp(after(to_far_y, to_y), "y")]
    grad_in = last(
        ids, weights_again, g_first, g_q, g_keys, after(g_values, to_y, to_x), tokens
    )
    mid_z = hold(mid_z, grad_in)
    mid = add_up([mid_mine, *mid_z])
    side_y, side_x, *received = hold((side_y, side_x, *received), mid, grad_in)
    *sends, part_mine = reduce_depth(ids, part, side_y, side_x)
    grad_down = add_up([down_mine, jnp.concatenate(received)])
    part = add_up([part_mine, *exchange_z(sends)])

    stripe = lambda value, i: value[i * own : (i + 1) * own]
    grad_qkv = jnp.concatenate([stripe(part, i) for i in range(3)], axis=1)
    grad_up = jnp.concatenate([stripe(mid, i) for i in range(blocks)], axis=1)
    vector_grads = [part[3 * own + i, :length] for i, length in enumerate(pers)]
    grad_out = mid[blocks * own :]
    return (
        layer_out.reshape(hidden_in.shape),
        grad_in.reshape(hidden_in.shape),
        grad_qkv,
        part[3 * own + 7, :per],
        grad_out,
        vector_grads[0],
        vector_grads[1],
        vector_grads[2],
        grad_up,
        vector_grads[3],
        grad_down,
        vector_grads[4],
        vector_grads[5],
        vector_grads[6],
    )


def solution(mesh):
    groups, cores = mesh.devices.shape
    split = Mesh(mesh.devices.reshape(groups // 4, 2, 2, cores), ("z", "y", "x", "seq"))
    dp = ("z", "y", "x")
    token_rows = P(None, dp, "seq", None)
    matrix = P(every, None)
    vector = P(every)
    params = (matrix, vector, matrix, vector, vector, vector, matrix, vector, matrix, vector, vector, vector)

    def layer(*arrays):
        tiled = groups == 16 and cores == 2 and arrays[5].shape[0] % 8 == 0
        return (local if tiled else plain_local)(*arrays)

    return jax.shard_map(
        layer,
        mesh=split,
        in_specs=(token_rows, token_rows, P(None, dp, None, "seq", None), token_rows, token_rows) + params,
        out_specs=(token_rows, token_rows) + params,
        check_vma=False,
    )
```

```python
import functools

import jax
import jax.numpy as jnp
from jax import lax
from jax.experimental import pallas as pl
from jax.experimental.pallas import tpu as pltpu
from jax.sharding import Mesh
from jax.sharding import PartitionSpec as P

H = 12
epsilon = 1e-12
keep_scale = 8.0 / 7.0
root_half = 0.7071067811865476
inverse_root_tau = 0.3989422804014327
every = ("z", "y", "x", "seq")
f32 = jnp.float32
bf16 = jnp.bfloat16


def unpack_keep(packed_words):
    shifts = jnp.arange(4, dtype=jnp.int32) * 3
    nibble = jnp.right_shift(packed_words[..., None], shifts) & 7
    keep_value = (nibble >= 1).astype(jnp.float32) * keep_scale
    return keep_value.reshape(packed_words.shape[:-1] + (packed_words.shape[-1] * 4,))


def normalize(values, norm_gain, norm_shift):
    centred = values - jnp.mean(values, axis=-1, keepdims=True)
    inverse = lax.rsqrt(jnp.mean(centred * centred, axis=-1, keepdims=True) + epsilon)
    scaled = centred * inverse
    return (scaled * norm_gain + norm_shift, scaled, inverse)


def norm_back(upstream, scaled, inverse, norm_gain):
    weighted = upstream * norm_gain
    centre_term = jnp.mean(weighted, axis=-1, keepdims=True)
    slope_term = jnp.mean(weighted * scaled, axis=-1, keepdims=True)
    return inverse * (weighted - centre_term - scaled * slope_term)


def gelu_slope(inner_sum):
    normal_cdf = 0.5 * (1.0 + lax.erf(inner_sum * root_half))
    density = jnp.exp(-0.5 * inner_sum * inner_sum) * inverse_root_tau
    return normal_cdf + inner_sum * density


def matmul(left_side, right_side):
    return jnp.dot(left_side, right_side, preferred_element_type=jnp.float32)


def plain_local(
    hidden_in,
    cotangent,
    attention_keep,
    output_keep,
    feed_keep,
    qkv_weight,
    qkv_bias,
    out_weight,
    out_bias,
    first_gain,
    first_shift,
    up_weight,
    up_bias,
    down_weight,
    down_bias,
    second_gain,
    second_shift,
):
    model_width = hidden_in.shape[-1]
    sequence_count = hidden_in.shape[1]
    local_tokens = hidden_in.shape[2]
    token_rows = sequence_count * local_tokens
    head_count = H
    head_size = model_width // head_count
    held_params = (
        lax.all_gather(qkv_weight, every, axis=0, tiled=True),
        lax.all_gather(qkv_bias, every, axis=0, tiled=True),
        lax.all_gather(out_weight, every, axis=0, tiled=True),
        lax.all_gather(out_bias, every, axis=0, tiled=True),
        lax.all_gather(first_gain, every, axis=0, tiled=True),
        lax.all_gather(first_shift, every, axis=0, tiled=True),
        lax.all_gather(up_weight, every, axis=0, tiled=True),
        lax.all_gather(up_bias, every, axis=0, tiled=True),
        lax.all_gather(down_weight, every, axis=0, tiled=True),
        lax.all_gather(down_bias, every, axis=0, tiled=True),
        lax.all_gather(second_gain, every, axis=0, tiled=True),
        lax.all_gather(second_shift, every, axis=0, tiled=True),
    )
    totals = None
    outputs = []
    inputs_grad = []
    for micro_step in range(hidden_in.shape[0]):
        (
            full_qkv_w,
            full_qkv_b,
            full_out_w,
            full_out_b,
            full_gain_one,
            full_shift_one,
            full_up_w,
            full_up_b,
            full_down_w,
            full_down_b,
            full_gain_two,
            full_shift_two,
        ) = held_params
        rows_in = hidden_in[micro_step].reshape(token_rows, model_width)
        qkv_float = full_qkv_b.astype(jnp.float32)
        bias_full = jnp.concatenate(
            [
                qkv_float[:model_width],
                jnp.zeros((model_width,), jnp.float32),
                qkv_float[model_width:],
            ]
        )
        projected = (matmul(rows_in, full_qkv_w) + bias_full).astype(jnp.bfloat16)
        queries = projected[:, :model_width].reshape(
            sequence_count, local_tokens, head_count, head_size
        )
        keys_local = projected[:, model_width : 2 * model_width].reshape(
            sequence_count, local_tokens, model_width
        )
        values_local = projected[:, 2 * model_width :].reshape(
            sequence_count, local_tokens, model_width
        )
        keys_all, values_all = (
            lax.all_gather(keys_local, "seq", axis=1, tiled=True),
            lax.all_gather(values_local, "seq", axis=1, tiled=True),
        )
        keys_heads = keys_all.reshape(sequence_count, -1, head_count, head_size)
        values_heads = values_all.reshape(sequence_count, -1, head_count, head_size)
        scores = (
            jnp.einsum("sqhd,skhd->shqk", queries, keys_heads, preferred_element_type=jnp.float32)
            * 0.125
        )
        row_peak = jnp.max(scores, axis=-1, keepdims=True)
        exponent = jnp.exp(scores - row_peak)
        row_total = jnp.sum(exponent, axis=-1, keepdims=True)
        log_total = row_peak + jnp.log(row_total)
        softmax_weights = exponent / row_total
        keep_attention = unpack_keep(attention_keep[micro_step])
        dropped = (softmax_weights * keep_attention).astype(jnp.bfloat16)
        context = jnp.einsum(
            "shqk,skhd->sqhd", dropped, values_heads, preferred_element_type=jnp.float32
        )
        context = context.reshape(token_rows, model_width).astype(jnp.bfloat16)
        attended = matmul(context, full_out_w) + full_out_b.astype(jnp.float32)
        keep_output = unpack_keep(output_keep[micro_step]).reshape(token_rows, model_width)
        first_sum = rows_in.astype(jnp.float32) + attended * keep_output
        gain_one = full_gain_one.astype(jnp.float32)
        normed, scaled_one, inverse_one = normalize(
            first_sum, gain_one, full_shift_one.astype(jnp.float32)
        )
        normed_low = normed.astype(jnp.bfloat16)
        inner_sum = matmul(normed_low, full_up_w) + full_up_b.astype(jnp.float32)
        activated = jax.nn.gelu(inner_sum, approximate=False).astype(jnp.bfloat16)
        outer_sum = matmul(activated, full_down_w) + full_down_b.astype(jnp.float32)
        keep_feed = unpack_keep(feed_keep[micro_step]).reshape(token_rows, model_width)
        second_sum = normed + outer_sum * keep_feed
        gain_two = full_gain_two.astype(jnp.float32)
        result, scaled_two, inverse_two = normalize(
            second_sum, gain_two, full_shift_two.astype(jnp.float32)
        )
        outputs.append(
            result.astype(jnp.bfloat16).reshape(sequence_count, local_tokens, model_width)
        )
        (
            back_qkv_w,
            back_qkv_b,
            back_out_w,
            back_out_b,
            back_gain_one,
            back_shift_one,
            back_up_w,
            back_up_b,
            back_down_w,
            back_down_b,
            back_gain_two,
            back_shift_two,
        ) = held_params
        upstream = cotangent[micro_step].reshape(token_rows, model_width).astype(jnp.float32)
        g_second = norm_back(upstream, scaled_two, inverse_two, back_gain_two.astype(jnp.float32))
        grad_gain_two = jnp.sum(upstream * scaled_two, axis=0)
        grad_shift_two = jnp.sum(upstream, axis=0)
        g_outer = (g_second * keep_feed).astype(jnp.bfloat16)
        grad_down_b = jnp.sum(g_outer.astype(jnp.float32), axis=0)
        grad_down_w = matmul(activated.T, g_outer)
        g_inner = (matmul(g_outer, back_down_w.T) * gelu_slope(inner_sum)).astype(jnp.bfloat16)
        grad_up_b = jnp.sum(g_inner.astype(jnp.float32), axis=0)
        grad_up_w = matmul(normed_low.T, g_inner)
        g_normed = g_second + matmul(g_inner, back_up_w.T)
        g_first = norm_back(g_normed, scaled_one, inverse_one, back_gain_one.astype(jnp.float32))
        grad_gain_one = jnp.sum(g_normed * scaled_one, axis=0)
        grad_shift_one = jnp.sum(g_normed, axis=0)
        g_attended = (g_first * keep_output).astype(jnp.bfloat16)
        grad_out_b = jnp.sum(g_attended.astype(jnp.float32), axis=0)
        grad_out_w = matmul(context.T, g_attended)
        g_context = matmul(g_attended, back_out_w.T).astype(jnp.bfloat16)
        g_context = g_context.reshape(sequence_count, local_tokens, head_count, head_size)
        keys_again, values_again = (
            lax.all_gather(keys_local, "seq", axis=1, tiled=True),
            lax.all_gather(values_local, "seq", axis=1, tiled=True),
        )
        keys_heads = keys_again.reshape(sequence_count, -1, head_count, head_size)
        values_heads = values_again.reshape(sequence_count, -1, head_count, head_size)
        scores_again = (
            jnp.einsum("sqhd,skhd->shqk", queries, keys_heads, preferred_element_type=jnp.float32)
            * 0.125
        )
        weights_again = jnp.exp(scores_again - log_total)
        dropped_again = (weights_again * keep_attention).astype(jnp.bfloat16)
        g_values_all = jnp.einsum(
            "shqk,sqhd->skhd", dropped_again, g_context, preferred_element_type=jnp.float32
        )
        g_dropped = jnp.einsum(
            "sqhd,skhd->shqk", g_context, values_heads, preferred_element_type=jnp.float32
        )
        g_weights = g_dropped * keep_attention
        row_delta = jnp.sum(g_weights * weights_again, axis=-1, keepdims=True)
        g_scores = (weights_again * (g_weights - row_delta)).astype(jnp.bfloat16)
        g_queries = (
            jnp.einsum("shqk,skhd->sqhd", g_scores, keys_heads, preferred_element_type=jnp.float32)
            * 0.125
        )
        g_keys_all = (
            jnp.einsum("shqk,sqhd->skhd", g_scores, queries, preferred_element_type=jnp.float32)
            * 0.125
        )
        g_keys, g_values = (
            lax.psum_scatter(
                g_keys_all.reshape(sequence_count, -1, model_width).astype(jnp.bfloat16),
                "seq",
                scatter_dimension=1,
                tiled=True,
            ).astype(jnp.float32),
            lax.psum_scatter(
                g_values_all.reshape(sequence_count, -1, model_width).astype(jnp.bfloat16),
                "seq",
                scatter_dimension=1,
                tiled=True,
            ).astype(jnp.float32),
        )
        g_projected = jnp.concatenate(
            [
                g_queries.reshape(token_rows, model_width),
                g_keys.reshape(token_rows, model_width),
                g_values.reshape(token_rows, model_width),
            ],
            axis=1,
        ).astype(jnp.bfloat16)
        g_projected_float = g_projected.astype(jnp.float32)
        grad_qkv_b = jnp.concatenate(
            [
                jnp.sum(g_projected_float[:, :model_width], axis=0),
                jnp.sum(g_projected_float[:, 2 * model_width :], axis=0),
            ]
        )
        grad_qkv_w = matmul(rows_in.T, g_projected)
        input_grad = g_first + matmul(g_projected, back_qkv_w.T)
        inputs_grad.append(
            input_grad.astype(jnp.bfloat16).reshape(sequence_count, local_tokens, model_width)
        )
        grads_now = (
            grad_qkv_w,
            grad_qkv_b,
            grad_out_w,
            grad_out_b,
            grad_gain_one,
            grad_shift_one,
            grad_up_w,
            grad_up_b,
            grad_down_w,
            grad_down_b,
            grad_gain_two,
            grad_shift_two,
        )
        if totals is None:
            totals = grads_now
        else:
            totals = tuple((before + added for before, added in zip(totals, grads_now)))
    summed = (
        lax.psum_scatter(totals[0], every, scatter_dimension=0, tiled=True),
        lax.psum_scatter(totals[1], every, scatter_dimension=0, tiled=True),
        lax.psum_scatter(totals[2], every, scatter_dimension=0, tiled=True),
        lax.psum_scatter(totals[3], every, scatter_dimension=0, tiled=True),
        lax.psum_scatter(totals[4], every, scatter_dimension=0, tiled=True),
        lax.psum_scatter(totals[5], every, scatter_dimension=0, tiled=True),
        lax.psum_scatter(totals[6], every, scatter_dimension=0, tiled=True),
        lax.psum_scatter(totals[7], every, scatter_dimension=0, tiled=True),
        lax.psum_scatter(totals[8], every, scatter_dimension=0, tiled=True),
        lax.psum_scatter(totals[9], every, scatter_dimension=0, tiled=True),
        lax.psum_scatter(totals[10], every, scatter_dimension=0, tiled=True),
        lax.psum_scatter(totals[11], every, scatter_dimension=0, tiled=True),
    )
    return (
        jnp.stack(outputs, axis=0),
        jnp.stack(inputs_grad, axis=0),
        summed[0],
        summed[1],
        summed[2],
        summed[3],
        summed[4],
        summed[5],
        summed[6],
        summed[7],
        summed[8],
        summed[9],
        summed[10],
        summed[11],
    )


ANY = pl.BlockSpec(memory_space=pl.ANY)
WHOLE = pl.BlockSpec(memory_space=pltpu.VMEM)
MIB = 2**20
PARTS = (2, 1)
GROUP = 2


def dot_t(left_side, right_side):
    return lax.dot_general(left_side, right_side, (((1,), (1,)), ((), ())), preferred_element_type=f32)


def t_dot(left_side, right_side):
    return lax.dot_general(left_side, right_side, (((0,), (0,)), ((), ())), preferred_element_type=f32)


def iota(shape, axis):
    return lax.broadcasted_iota(jnp.int32, shape, axis)


def pp(value, axis, step=1):
    size = lax.axis_size(axis)
    return lax.ppermute(value, axis, [(i, i ^ step) for i in range(size)])


def pick(value, axis, index):
    return lax.dynamic_index_in_dim(value, index, axis, keepdims=False)


def after(value, *earlier):
    return lax.optimization_barrier((value,) + earlier)[0]


def hold(values, *earlier):
    return lax.optimization_barrier(tuple(values) + earlier)[: len(values)]


def add_up(terms):
    total = terms[0].astype(f32)
    for term in terms[1:]:
        total = total + term.astype(f32)
    return total


def divide(plan, cut):
    parts = []
    for start, rows, out, row, column in plan:
        ends = [start, cut, start + rows] if start < cut < start + rows else [start, start + rows]
        for first, last in zip(ends, ends[1:]):
            parts.append((first, last - first, out, row + first - start, column))
    return parts


def whole(number, first, array):
    return (number, first, array, 0, array.shape[1])


def at_core(piece):
    number, first, array, row, rows = piece
    return (number + 4, first, pp(array, "seq"), row, rows)


class Weights:
    def __init__(self, pieces, plan, shapes, free=()):
        arrays = []
        self.spans = []
        for number, first, array, row, rows in pieces:
            place = next((i for i, held in enumerate(arrays) if held is array), len(arrays))
            if place == len(arrays):
                arrays.append(array)
            self.spans.append((number, first, place, row, rows))
        loose = [any(array is other for other in free) for array in arrays]
        self.operands = [
            array if found else pltpu.with_memory_space_constraint(array, pltpu.HBM)
            for array, found in zip(arrays, loose)
        ]
        self.plan, self.shapes = plan, shapes
        self.specs = [ANY if found else pl.BlockSpec(memory_space=pltpu.HBM) for found in loose]
        self.scratch = [pltpu.VMEM((4, 2, 2, 2, rows, columns), bf16) for rows, columns in shapes]
        self.scratch.append(pltpu.SemaphoreType.DMA((8 * len(plan),)))

    def copies(self, ids, sources, places, sems):
        found = [[] for _ in self.shapes]
        count = 0
        for start, rows, out, row, column in self.plan:
            for number, first, place, source_row, held in self.spans:
                if first <= start and start + rows <= first + held:
                    c = ids[0] ^ (number >> 2)
                    y = ids[1] ^ ((number >> 1) & 1)
                    x = ids[2] ^ (number & 1)
                    source = sources[place]
                    src = source.at[:, pl.ds(source_row + start - first, rows), :]
                    dst = places[out].at[:, y, x, c, pl.ds(row, rows), pl.ds(column, source.shape[2])]
                    found[out].append(pltpu.make_async_copy(src, dst, sems.at[count]))
                    count += 1
        return found

    def matrix(self, places, out):
        rows, columns = self.shapes[out]
        return places[out].reshape(32 * rows, columns)


def begin(copies):
    for group in copies:
        for copy in group:
            copy.start()


def finish(group):
    for copy in group:
        copy.wait()


def spread(block, row, count, per):
    values = block[:, row, : -(-per // 128) * 128].astype(bf16)
    lanes = values.shape[1]
    select = (iota((lanes, count), 1) % per == iota((lanes, count), 0)).astype(bf16)
    wide = jnp.dot(values, select, preferred_element_type=f32)
    return jnp.sum(jnp.where(iota(wide.shape, 1) // per == iota(wide.shape, 0), wide, 0.0), axis=0, keepdims=True)


def unspread(vectors, pers, block, first=0):
    block[:, first:] = jnp.zeros((32, 8 - first, block.shape[2]), f32)
    for row, (vector, per) in enumerate(zip(vectors, pers), first):
        count = vector.shape[1]
        lanes = -(-per // 128) * 128
        shape = (32, count)
        wide = jnp.where(iota(shape, 1) // per == iota(shape, 0), vector, 0.0).astype(bf16)
        select = (iota((count, lanes), 0) % per == iota((count, lanes), 1)).astype(bf16)
        block[:, row, :lanes] = jnp.dot(wide, select, preferred_element_type=f32)


def layer_norm(values):
    centred = values - jnp.mean(values, axis=-1, keepdims=True)
    inverse = lax.rsqrt(jnp.mean(centred * centred, axis=-1, keepdims=True) + epsilon)
    return centred * inverse, inverse


def turn_matrix(tokens):
    place = iota((tokens, tokens), 0)
    quarter = tokens // 4
    return (iota((tokens, tokens), 1) == 4 * (place % quarter) + place // quarter).astype(bf16)


def call(body, name, grid, operands, specs, outs, out_specs, scratch, room, load, aliases=None):
    return pl.pallas_call(
        body,
        grid_spec=pltpu.PrefetchScalarGridSpec(
            num_scalar_prefetch=1, grid=grid, in_specs=specs, out_specs=out_specs, scratch_shapes=scratch
        ),
        out_shape=outs,
        compiler_params=pltpu.CompilerParams(vmem_limit_bytes=room * MIB),
        cost_estimate=pl.CostEstimate(flops=1024, bytes_accessed=load * MIB // 16, transcendentals=0),
        input_output_aliases=aliases or {},
        name=name,
    )(*operands)


def shaped(shape, dtype):
    return jax.ShapeDtypeStruct(shape, dtype)


def rows_spec(rows, columns):
    return pl.BlockSpec((rows, columns), lambda i, ids: (i, 0))


def fixed_spec(shape):
    return pl.BlockSpec(shape, lambda i, ids: (0,) * len(shape))


def prepare_body(ids, hidden, output_words, feed_words, turned, keep_output, keep_feed):
    tokens, width = hidden.shape
    turned[...] = jnp.dot(turn_matrix(tokens), hidden[...], preferred_element_type=f32).astype(bf16)
    quarter = width // 4
    for words, keep in ((output_words, keep_output), (feed_words, keep_feed)):
        packed = words[0, 0]
        total = jnp.zeros((tokens, width), f32)
        for i in range(4):
            bit = ((packed & (7 << (3 * i))) != 0).astype(f32).astype(bf16)
            place = (iota((quarter, width), 1) == 4 * iota((quarter, width), 0) + i).astype(bf16)
            total = total + t_dot(bit, place)
        keep[...] = total.astype(bf16)


def prepare(ids, hidden, output_words, feed_words, tokens):
    rows, width = hidden.shape
    wide = rows_spec(tokens, width)
    narrow = pl.BlockSpec((1, 1, width // 4, tokens), lambda i, ids: (i, 0, 0, 0))
    return call(
        prepare_body,
        "prepare",
        (rows // tokens,),
        (ids, hidden, output_words, feed_words),
        [wide, narrow, narrow],
        [shaped((rows, width), bf16)] * 3,
        [wide] * 3,
        [],
        12,
        6,
    )


def project_body(weights, per, ids, *refs):
    count = len(weights.operands)
    sources, (hidden, turned, queries), rest = refs[:count], refs[count : count + 3], refs[count + 3 :]
    micro, tokens, width = queries.shape
    places, sems = rest[len(rest) - 1 - len(weights.shapes) : -1], rest[-1]
    near = iter(rest[: len(rest) - 1 - len(weights.shapes)])
    copies = weights.copies(ids, sources, places, sems)
    begin(copies)
    finish(copies[3])
    block = weights.matrix(places, 3)[:, :128].astype(f32).reshape(32, 8, 128)
    bias = spread(block, 0, 2 * width, per)
    for n in range(3):
        finish(copies[n])
    for m in range(micro):
        natural, other = hidden[m * tokens : (m + 1) * tokens, :], turned[m * tokens : (m + 1) * tokens, :]
        q = jnp.dot(natural, weights.matrix(places, 0)[...], preferred_element_type=f32) + bias[:, :width]
        queries[m] = q.astype(bf16)
        k = jnp.dot(other, weights.matrix(places, 1)[...], preferred_element_type=f32).astype(bf16)
        v = jnp.dot(other, weights.matrix(places, 2)[...], preferred_element_type=f32) + bias[:, width:]
        for value in (k, v.astype(bf16)):
            rows = tokens // PARTS[m]
            for part in range(PARTS[m]):
                next(near)[...] = value[part * rows : (part + 1) * rows]


def project(ids, weights, hidden, turned, micro, per):
    rows, width = hidden.shape
    return call(
        functools.partial(project_body, weights, per),
        "project",
        (1,),
        (ids, *weights.operands, hidden, turned),
        weights.specs + [WHOLE] * 2,
        [shaped((micro, rows // micro, width), bf16)]
        + [shaped((rows // micro // PARTS[m], width), bf16) for m in range(micro) for _ in range(2 * PARTS[m])],
        [WHOLE] * (1 + 2 * sum(PARTS)),
        weights.scratch,
        16,
        10,
    )


def lane_half(shape):
    return iota(shape, len(shape) - 1) < 64


def by_head(pair):
    left, zero = lane_half(pair.shape), jnp.zeros_like(pair)
    return jnp.concatenate([jnp.where(left, pair, zero), jnp.where(left, zero, pair)], axis=0)


def join_keys(core, near, far, buffer, lanes):
    quarter = buffer.shape[0] // 8
    parts = len(near)
    for i in range(4):
        here = pl.multiple_of((2 * i + core) * quarter, quarter)
        there = pl.multiple_of((2 * i + 1 - core) * quarter, quarter)
        at = (i * parts % 4) // parts * quarter
        buffer[pl.ds(here, quarter), :] = near[i * parts // 4][at : at + quarter, lanes]
        buffer[pl.ds(there, quarter), :] = far[i * parts // 4][at : at + quarter, lanes]


def group_lanes():
    return [slice(j * 128, (j + 1) * 128) for j in range(GROUP)]


def attention_body(parts, ids, q, *refs):
    ours, words = refs[: 4 * parts], refs[4 * parts]
    context, signed, keys, values = refs[-4:]
    core = ids[0]
    tokens = q.shape[1]
    for j, lanes in enumerate(group_lanes()):
        join_keys(core, ours[:parts], ours[2 * parts : 3 * parts], keys.at[j], lanes)
        join_keys(core, ours[parts : 2 * parts], ours[3 * parts :], values.at[j], lanes)
    scores = [dot_t(by_head(q[0, :, lanes]) * 0.125, keys[j]) for j, lanes in enumerate(group_lanes())]
    for j, lanes in enumerate(group_lanes()):
        blocks = [scores[j][:, i * 128 : (i + 1) * 128] for i in range(4)]
        peak = jnp.maximum(jnp.maximum(blocks[0], blocks[1]), jnp.maximum(blocks[2], blocks[3]))
        peak = jnp.max(peak, axis=1, keepdims=True)
        blocks = [jnp.exp(block - peak) for block in blocks]
        total = jnp.sum((blocks[0] + blocks[1]) + (blocks[2] + blocks[3]), axis=1, keepdims=True)
        scale = 1.0 / total
        word = words[0, 2 * j : 2 * j + 2].reshape(2 * tokens, 128)
        dropped = []
        for i in range(4):
            weight = blocks[i] * scale
            keep = (word & (7 << (3 * i))) != 0
            weight = jnp.where(keep, weight, -weight).astype(bf16)
            signed[0, j, i] = weight
            dropped.append(jnp.maximum(weight, jnp.zeros_like(weight)))
        out = jnp.dot(jnp.concatenate(dropped, axis=1), values[j], preferred_element_type=f32) * keep_scale
        context[0, :, lanes] = jnp.where(lane_half((tokens, 128)), out[:tokens], out[tokens:]).astype(bf16)


def attention(ids, m, queries, near, far, words, earlier=()):
    micro, tokens, width = queries.shape
    pairs = width // 128
    part = pl.BlockSpec((1, tokens, 128 * GROUP), lambda p, ids: (m, 0, p))
    flat = pl.BlockSpec((tokens // PARTS[m], 128 * GROUP), lambda p, ids: (0, p))
    operands = (ids, queries, *near[m], *far[m], words)
    return call(
        functools.partial(attention_body, PARTS[m]),
        "attention",
        (pairs // GROUP,),
        operands + tuple(earlier),
        [part] + [flat] * (4 * PARTS[m])
        + [pl.BlockSpec((1, 2 * GROUP, tokens, 128), lambda p, ids: (m, p, 0, 0))]
        + [ANY] * len(earlier),
        [shaped((micro, tokens, width), bf16), shaped((micro, pairs, 4, 2 * tokens, 128), bf16)],
        [part, pl.BlockSpec((1, GROUP, 4, 2 * tokens, 128), lambda p, ids: (m, p, 0, 0, 0))],
        [pltpu.VMEM((GROUP, 2 * tokens, 128), bf16)] * 2,
        16,
        14,
        {len(operands) + i: i for i in range(len(earlier))},
    )


def attention_back_body(parts, ids, q, *refs):
    ours, signed, upstream, refs = refs[: 4 * parts], refs[4 * parts], refs[4 * parts + 1], refs[4 * parts + 2 :]
    g_q, *grads, keys, values, sums = refs
    g_near, g_far = grads[:2], grads[2:]
    core = ids[0]
    tokens = q.shape[1]
    for j, lanes in enumerate(group_lanes()):
        join_keys(core, ours[:parts], ours[2 * parts : 3 * parts], keys.at[j], lanes)
        join_keys(core, ours[parts : 2 * parts], ours[3 * parts :], values.at[j], lanes)
    aboves = [by_head(upstream[:, lanes]) for lanes in group_lanes()]
    g_droppeds = [dot_t(aboves[j], values[j]) for j in range(GROUP)]
    for j, lanes in enumerate(group_lanes()):
        weights, kept, g_weights = [], [], []
        delta = None
        for i in range(4):
            both_signs = signed[0, j, i].astype(f32)
            weight = jnp.abs(both_signs)
            g_weight = jnp.where(both_signs > 0.0, g_droppeds[j][:, i * 128 : (i + 1) * 128], 0.0)
            term = g_weight * weight
            delta = term if delta is None else delta + term
            weights.append(weight)
            g_weights.append(g_weight)
            kept.append(jnp.maximum(both_signs, 0.0).astype(bf16))
        delta = jnp.sum(delta, axis=1, keepdims=True)
        g_scores = jnp.concatenate(
            [(weights[i] * (g_weights[i] - delta)).astype(bf16) for i in range(4)], axis=1
        )
        dropped = jnp.concatenate(kept, axis=1)
        out = jnp.dot(g_scores, keys[j], preferred_element_type=f32)
        out = jnp.where(lane_half((tokens, 128)), out[:tokens], out[tokens:])
        g_q[:, lanes] = (out * (0.125 * keep_scale)).astype(bf16)
        quarter = keys.shape[1] // 8
        sums[j, 0] = t_dot(g_scores, by_head(q[0, :, lanes])) * (0.125 * keep_scale)
        sums[j, 1] = t_dot(dropped, aboves[j]) * keep_scale
        for kind in range(2):
            for i in range(4):
                here = pl.multiple_of((2 * i + core) * quarter, quarter)
                there = pl.multiple_of((2 * i + 1 - core) * quarter, quarter)
                rows = slice(i * quarter, (i + 1) * quarter)
                g_near[kind][rows, lanes] = sums[j, kind, pl.ds(here, quarter), :]
                g_far[kind][rows, lanes] = sums[j, kind, pl.ds(there, quarter), :].astype(bf16)


def attention_back(ids, m, queries, near, far, signed, upstream):
    micro, tokens, width = queries.shape
    pairs = width // 128
    part = pl.BlockSpec((1, tokens, 128 * GROUP), lambda p, ids: (m, 0, p))
    flat = pl.BlockSpec((tokens // PARTS[m], 128 * GROUP), lambda p, ids: (0, p))
    both = pl.BlockSpec((tokens, 128 * GROUP), lambda p, ids: (0, p))
    operands = (ids, queries, *near[m], *far[m], signed, upstream)
    return call(
        functools.partial(attention_back_body, PARTS[m]),
        "attention_back",
        (pairs // GROUP,),
        operands,
        [part] + [flat] * (4 * PARTS[m])
        + [pl.BlockSpec((1, GROUP, 4, 2 * tokens, 128), lambda p, ids: (m, p, 0, 0, 0))]
        + [pl.BlockSpec((tokens, 128 * GROUP), lambda p, ids: (m, p))],
        [
            shaped((tokens, width), bf16),
            shaped((tokens, width), f32),
            shaped((tokens, width), f32),
            shaped((tokens, width), bf16),
            shaped((tokens, width), bf16),
        ],
        [both] * 5,
        [pltpu.VMEM((GROUP, 2 * tokens, 128), bf16)] * 2 + [pltpu.VMEM((GROUP, 2, 2 * tokens, 128), f32)],
        24,
        20,
    )


def up_body(weights, pers, tokens, ids, *refs):
    count = len(weights.operands)
    sources = refs[:count]
    context, hidden, keep, vectors, scaled, inverse, activated, slope = refs[count : count + 8]
    places, (sems, lows) = refs[count + 8 : -2], refs[-2:]
    copies = weights.copies(ids, sources, places, sems)
    rows, width = scaled.shape
    wide = activated.shape[1]
    begin([copies[0], copies[2], copies[1]])
    finish(copies[2])
    block = weights.matrix(places, 2)[:, :128].astype(f32).reshape(32, 8, 128)
    for row, per in enumerate(pers):
        vectors[row : row + 1, : 32 * per] = spread(block, row, 32 * per, per)
    finish(copies[0])

    def rows_part(m, carry):
        at = pl.ds(pl.multiple_of(m * tokens, tokens), tokens)
        attended = jnp.dot(context[at], weights.matrix(places, 0)[...], preferred_element_type=f32)
        attended = attended + vectors[0:1, :width]
        first_sum = hidden[at].astype(f32) + attended * (keep[at].astype(f32) * keep_scale)
        normal, scale = layer_norm(first_sum)
        scaled[at] = normal
        inverse[at] = jnp.broadcast_to(scale, (tokens, 128))
        lows[at] = (normal * vectors[1:2, :width] + vectors[2:3, :width]).astype(bf16)
        return carry

    lax.fori_loop(0, rows // tokens, rows_part, 0)
    finish(copies[1])
    up = weights.matrix(places, 1)
    step = 512

    def part(n, carry):
        at = pl.ds(pl.multiple_of(n * step, step), step)
        inner = jnp.dot(lows[...], up[:, at], preferred_element_type=f32) + vectors[3:4, at]
        cdf = 0.5 * (1.0 + lax.erf(inner * root_half))
        density = jnp.exp(-0.5 * inner * inner) * inverse_root_tau
        activated[:, at] = (inner * cdf).astype(bf16)
        slope[:, at] = (cdf + inner * density).astype(bf16)
        return carry

    lax.fori_loop(0, wide // step, part, 0)


def feed_up(ids, weights, pers, context, hidden, keep, tokens, wide):
    rows, width = hidden.shape
    return call(
        functools.partial(up_body, weights, pers, tokens),
        "feed_up",
        (1,),
        (ids, *weights.operands, context, hidden, keep),
        weights.specs + [WHOLE] * 3,
        [
            shaped((8, wide), f32),
            shaped((rows, width), f32),
            shaped((rows, 128), f32),
            shaped((rows, wide), bf16),
            shaped((rows, wide), bf16),
        ],
        [WHOLE] * 5,
        weights.scratch + [pltpu.VMEM((rows, width), bf16)],
        16,
        24,
    )


def hand_out(core, total, rows, own, send, first, at):
    def one(n, carry):
        here = pl.multiple_of((2 * n + core) * rows, 8)
        there = pl.multiple_of((2 * n + 1 - core) * rows, 8)
        own[first + n, at : at + rows, :] = total[pl.ds(here, rows), :].astype(bf16)
        send[first + n, at : at + rows, :] = total[pl.ds(there, rows), :].astype(bf16)
        return carry

    lax.fori_loop(0, total.shape[0] // (2 * rows), one, 0)


def down_body(weights, tokens, ids, *refs):
    count = len(weights.operands)
    sources, refs = refs[:count], refs[count:]
    activated, slope, scaled, keep, cotangent, vectors = refs[:6]
    layer_out, g_second_out, g_inner, own, send, sums = refs[6:12]
    place, sems, total, g_outers = refs[12:]
    copies = weights.copies(ids, sources, (place,), sems)
    rows, width = scaled.shape
    wide = activated.shape[1]
    begin(copies)
    sums[...] = jnp.zeros_like(sums)
    finish(copies[0])
    down = weights.matrix((place,), 0)
    gain = vectors[5:6, :width]

    def rows_part(m, carry):
        at = pl.ds(pl.multiple_of(m * tokens, tokens), tokens)
        outer = jnp.dot(activated[at], down[...], preferred_element_type=f32) + vectors[4:5, :width]
        factor = keep[at].astype(f32) * keep_scale
        normed = scaled[at] * vectors[1:2, :width] + vectors[2:3, :width]
        normal, scale = layer_norm(normed + outer * factor)
        layer_out[at] = (normal * gain + vectors[6:7, :width]).astype(bf16)
        above = cotangent[at].astype(f32)
        weighted = above * gain
        g_second = scale * (
            weighted
            - jnp.mean(weighted, axis=-1, keepdims=True)
            - normal * jnp.mean(weighted * normal, axis=-1, keepdims=True)
        )
        g_second_out[at] = g_second
        g_outer = (g_second * factor).astype(bf16)
        g_outers[at] = g_outer
        sums[0:1, :width] += jnp.sum(g_outer.astype(f32), axis=0, keepdims=True)
        sums[1:2, :width] += jnp.sum(above * normal, axis=0, keepdims=True)
        sums[2:3, :width] += jnp.sum(above, axis=0, keepdims=True)
        return carry

    lax.fori_loop(0, rows // tokens, rows_part, 0)
    step = 512

    def part(n, carry):
        at = pl.ds(pl.multiple_of(n * step, step), step)
        g_in = (dot_t(g_outers[...], down[at, :]) * slope[:, at].astype(f32)).astype(bf16)
        g_inner[:, at] = g_in
        sums[3:4, at] = jnp.sum(g_in.astype(f32), axis=0, keepdims=True)
        return carry

    lax.fori_loop(0, wide // step, part, 0)

    def grads(n, carry):
        at = pl.ds(pl.multiple_of(n * width, width), width)
        total[...] = t_dot(activated[:, at], g_outers[...])
        hand_out(ids[0], total, wide // 32, own, send, n * (16 * width // wide), 0)
        return carry

    lax.fori_loop(0, wide // width, grads, 0)


def feed_down(ids, weights, activated, slope, scaled, keep, cotangent, vectors, tokens):
    rows, width = scaled.shape
    wide = activated.shape[1]
    halves = (16, wide // 32, width)
    return call(
        functools.partial(down_body, weights, tokens),
        "feed_down",
        (1,),
        (ids, *weights.operands, activated, slope, scaled, keep, cotangent, vectors),
        weights.specs + [WHOLE] * 6,
        [
            shaped((rows, width), bf16),
            shaped((rows, width), f32),
            shaped((rows, wide), bf16),
            shaped(halves, bf16),
            shaped(halves, bf16),
            shaped((8, wide), f32),
        ],
        [WHOLE] * 6,
        weights.scratch + [pltpu.VMEM((width, width), f32), pltpu.VMEM((rows, width), bf16)],
        16,
        36,
    )


def middle_body(weights, pers, tokens, ids, *refs):
    count = len(weights.operands)
    sources, refs = refs[:count], refs[count:]
    g_inner, g_second, scaled, inverse, keep, vectors, context, down_sums = refs[:8]
    g_first_out, g_context, own, send, block = refs[8:13]
    *places, sems, g_normeds, g_attendeds, sums = refs[13:]
    copies = weights.copies(ids, sources, places, sems)
    begin([copies[1], copies[0]])
    rows, width = scaled.shape
    out_w, up_w = weights.matrix(places, 0), weights.matrix(places, 1)
    finish(copies[1])
    step = 256

    def columns_part(n, carry):
        at = pl.ds(pl.multiple_of(n * step, step), step)
        g_normeds[:rows, at] = g_second[:, at] + dot_t(g_inner[...], up_w[at, :])
        return carry

    lax.fori_loop(0, width // step, columns_part, 0)
    sums[...] = jnp.zeros_like(sums)

    def rows_part(m, carry):
        at = pl.ds(pl.multiple_of(m * tokens, tokens), tokens)
        normal = scaled[at]
        g_normed = g_normeds[at, :]
        weighted = g_normed * vectors[1:2, :width]
        g_first = inverse[at, 0:1] * (
            weighted
            - jnp.mean(weighted, axis=-1, keepdims=True)
            - normal * jnp.mean(weighted * normal, axis=-1, keepdims=True)
        )
        g_first_out[at] = g_first
        g_attended = (g_first * (keep[at].astype(f32) * keep_scale)).astype(bf16)
        g_attendeds[at] = g_attended
        sums[0:1, :] += jnp.sum(g_attended.astype(f32), axis=0, keepdims=True)
        sums[1:2, :] += jnp.sum(g_normed * normal, axis=0, keepdims=True)
        sums[2:3, :] += jnp.sum(g_normed, axis=0, keepdims=True)
        return carry

    lax.fori_loop(0, rows // tokens, rows_part, 0)
    finish(copies[0])
    g_context[...] = dot_t(g_attendeds[...], out_w[...]).astype(bf16)
    g_normeds[:width] = t_dot(context[...], g_attendeds[...])
    hand_out(ids[0], g_normeds, width // 32, own, send, 0, 0)
    vector_sums = [sums[n : n + 1, :] for n in range(3)]
    vector_sums += [down_sums[3:4, :]] + [down_sums[n : n + 1, :width] for n in range(3)]
    unspread(vector_sums, pers, block)


def middle(ids, weights, pers, g_inner, g_second, scaled, inverse, keep, vectors, context, sums, tokens):
    rows, width = scaled.shape
    halves = (16, width // 32, width)
    return call(
        functools.partial(middle_body, weights, pers, tokens),
        "middle",
        (1,),
        (ids, *weights.operands, g_inner, g_second, scaled, inverse, keep, vectors, context, sums),
        weights.specs + [WHOLE] * 8,
        [
            shaped((rows, width), f32),
            shaped((rows, width), bf16),
            shaped(halves, bf16),
            shaped(halves, bf16),
            shaped((32, 8, width), f32),
        ],
        [WHOLE] * 5,
        weights.scratch
        + [pltpu.VMEM((max(rows, width), width), f32), pltpu.VMEM((rows, width), bf16), pltpu.VMEM((8, width), f32)],
        16,
        18,
    )


def grads_body(ids, g_inner, scaled, vectors, own, send, total, low_t):
    n = pl.program_id(0)
    width = scaled.shape[1]

    @pl.when(n == 0)
    def _():
        low_t[...] = (scaled[...] * vectors[1:2, :width] + vectors[2:3, :width]).T.astype(bf16)

    total[...] = jnp.dot(low_t[...], g_inner[...], preferred_element_type=f32)
    for block in range(own.shape[1] // (width // 32)):

        @pl.when(n == block)
        def _():
            hand_out(ids[0], total, width // 32, own, send, 0, block * (width // 32))


def up_grads(ids, g_inner, scaled, vectors):
    rows, width = scaled.shape
    wide = g_inner.shape[1]
    halves = (16, wide // 32, width)
    return call(
        grads_body,
        "up_grads",
        (wide // width,),
        (ids, g_inner, scaled, vectors),
        [pl.BlockSpec((rows, width), lambda i, ids: (0, i))] + [WHOLE] * 2,
        [shaped(halves, bf16), shaped(halves, bf16)],
        [WHOLE] * 2,
        [pltpu.VMEM((width, width), f32), pltpu.VMEM((width, rows), bf16)],
        14,
        20,
    )


def hand_out_rows(core, block, own, send, at):
    for n in range(16):
        own[n, at : at + 8, :] = block[2 * n + core].astype(bf16)
        send[n, at : at + 8, :] = block[2 * n + 1 - core].astype(bf16)


def inputs_body(per, ids, hidden, turned, *refs):
    micro = (len(refs) - 8) // 5
    grads, (block, own, send, g_queries, g_keys, g_values, total, bias) = refs[: 5 * micro], refs[5 * micro :]
    width = hidden.shape[1]
    sums = []
    for n, out in enumerate((g_queries, g_keys, g_values)):
        for m in range(micro):
            g_q, near, far = grads[m], grads[micro + 2 * m :][:2], grads[3 * micro + 2 * m :][:2]
            rows = slice(m * g_q.shape[0], (m + 1) * g_q.shape[0])
            if n == 0:
                out[rows] = g_q[...]
            else:
                out[rows] = (near[n - 1][...] + far[n - 1][...].astype(f32)).astype(bf16)
        if n != 1:
            sums.append(jnp.sum(out[...].astype(f32), axis=0, keepdims=True))
        left = hidden if n == 0 else turned
        for start in range(0, width, 256):
            total[start : start + 256, :] = t_dot(left[:, start : start + 256], out[...])
        hand_out(ids[0], total, width // 32, own, send, 0, n * (width // 32))
    bias[...] = block[...]
    unspread([jnp.concatenate(sums, axis=1)], [per], bias, 7)
    hand_out_rows(ids[0], bias, own, send, 3 * (width // 32))


def input_grads(ids, hidden, turned, grads, block, per):
    rows, width = hidden.shape
    halves = (16, 3 * width // 32 + 8, width)
    return call(
        functools.partial(inputs_body, per),
        "input_grads",
        (1,),
        (ids, hidden, turned, *grads, block),
        [WHOLE] * (3 + len(grads)),
        [shaped(halves, bf16)] * 2 + [shaped((rows, width), bf16)] * 3,
        [WHOLE] * 5,
        [pltpu.VMEM((width, width), f32), pltpu.VMEM((32, 8, width), f32)],
        14,
        12,
    )


def last_body(weights, ids, *refs):
    count = len(weights.operands)
    sources = refs[:count]
    g_first, g_q, g_keys, g_values, out = refs[count : count + 5]
    places, sems = refs[count + 5 : -1], refs[-1]
    copies = weights.copies(ids, sources, places, sems)

    @pl.when(pl.program_id(0) == 0)
    def _():
        begin(copies)
        for group in copies:
            finish(group)

    turn = turn_matrix(g_q.shape[0])
    total = g_first[...] + dot_t(g_q[...], weights.matrix(places, 0)[...])
    total = total + dot_t(t_dot(turn, g_keys[...]).astype(bf16), weights.matrix(places, 1)[...])
    total = total + dot_t(t_dot(turn, g_values[...]).astype(bf16), weights.matrix(places, 2)[...])
    out[...] = total.astype(bf16)


def last(ids, weights, g_first, g_q, g_keys, g_values, tokens):
    rows, width = g_first.shape
    narrow = rows_spec(tokens, width)
    return call(
        functools.partial(last_body, weights),
        "input_back",
        (rows // tokens,),
        (ids, *weights.operands, g_first, g_q, g_keys, g_values),
        weights.specs + [narrow] * 4,
        [shaped((rows, width), bf16)],
        [narrow],
        weights.scratch,
        16,
        10,
    )[0]


def beside(shape, y, x):
    return pl.BlockSpec((4, 1, 1) + shape[3:], lambda i, ids: (0, ids[1] ^ y, ids[2] ^ x, 0, 0))


def rows_of(parts, index, first, last):
    found, start = [], 0
    for part in parts:
        rows = part.shape[-2]
        low, high = max(first, start), min(last, start + rows)
        if low < high:
            found.append(part[index + (slice(low - start, high - start),)].astype(f32))
        start += rows
    return found[0] if len(found) == 1 else jnp.concatenate(found, axis=-2)


def both(parts, index, first, last):
    half = len(parts) // 2
    return rows_of(parts[:half], index, first, last) + rows_of(parts[half:], index, first, last)


def count_rows(parts):
    return sum(part.shape[3] for part in parts[: len(parts) // 2])


PLANE = (slice(None), 0, 0)


def corner_body(ids, *refs):
    *parts, low, high = refs
    half = low.shape[1]
    low[...] = both(parts, PLANE, 0, half).astype(bf16)
    high[...] = both(parts, PLANE, half, half + high.shape[1]).astype(bf16)


def reduce_corner(ids, parts, cut):
    rows, width = count_rows(parts), parts[0].shape[4]
    return call(
        corner_body,
        "reduce_corner",
        (1,),
        (ids, *parts),
        [beside(part.shape, 1, 1) for part in parts],
        [shaped((4, cut, width), bf16), shaped((4, rows - cut, width), bf16)],
        [WHOLE] * 2,
        [],
        8,
        2,
    )


def sides_body(count, ids, *refs):
    for_y, for_x, (low, high, to_y, to_x) = refs[:count], refs[count : 2 * count], refs[2 * count :]
    rows, half = to_y.shape[1], low.shape[1]
    to_y[:, :half] = (both(for_y, PLANE, 0, half) + low[...].astype(f32)).astype(bf16)
    to_y[:, half:] = both(for_y, PLANE, half, rows).astype(bf16)
    to_x[:, :half] = both(for_x, PLANE, 0, half).astype(bf16)
    to_x[:, half:] = (both(for_x, PLANE, half, rows) + high[...].astype(f32)).astype(bf16)


def reduce_sides(ids, parts, low, high):
    rows, width = count_rows(parts), parts[0].shape[4]
    return call(
        functools.partial(sides_body, len(parts)),
        "reduce_sides",
        (1,),
        (ids, *parts, *parts, low, high),
        [beside(part.shape, 1, 0) for part in parts]
        + [beside(part.shape, 0, 1) for part in parts]
        + [WHOLE] * 2,
        [shaped((4, rows, width), bf16)] * 2,
        [WHOLE] * 2,
        [],
        10,
        3,
    )


def depth_body(ids, *refs):
    *parts, from_y, from_x, near, middle, far, mine = refs
    for k, out in enumerate((mine, near, middle, far)):
        z = ids[3] ^ k
        total = both(parts, (z, 0, 0), 0, from_y.shape[1])
        total = total + from_y[z].astype(f32) + from_x[z].astype(f32)
        out[...] = total.astype(out.dtype)


def reduce_depth(ids, parts, from_y, from_x):
    shape = from_y.shape[1:]
    return call(
        depth_body,
        "reduce_depth",
        (1,),
        (ids, *parts, from_y, from_x),
        [beside(part.shape, 0, 0) for part in parts] + [WHOLE] * 2,
        [shaped(shape, bf16)] * 3 + [shaped(shape, f32)],
        [WHOLE] * 4,
        [],
        10,
        3,
    )


def pair_body(ids, one, two, out):
    out[0] = one[...]
    out[1] = two[...]


def pair_z(ids, one, two):
    return call(
        pair_body,
        "pair_z",
        (1,),
        (ids, one, two),
        [WHOLE] * 2,
        [shaped((2,) + one.shape, bf16)],
        [WHOLE],
        [],
        4,
        1,
    )[0]


def order_body(ids, pair, received, out):
    for k in range(2):
        out[ids[3] ^ (2 * k)] = pair[k]
        out[ids[3] ^ (2 * k + 1)] = received[k]


def order_z(ids, pair, received):
    return call(
        order_body,
        "order_z",
        (1,),
        (ids, pair, received),
        [WHOLE] * 2,
        [shaped((4,) + pair.shape[1:], bf16)],
        [WHOLE],
        [],
        6,
        1,
    )[0]


def four_body(ids, *refs):
    *parts, out = refs
    for k, part in enumerate(parts):
        out[ids[3] ^ k] = part[...]


def order_four(ids, *parts):
    return call(
        four_body,
        "order_four",
        (1,),
        (ids, *parts),
        [WHOLE] * 4,
        [shaped((4,) + parts[0].shape, bf16)],
        [WHOLE],
        [],
        6,
        1,
    )[0]


def halves_body(ids, pair, received, low, high):
    rows = low.shape[1]
    for k in range(2):
        for source, z in ((pair, ids[3] ^ (2 * k)), (received, ids[3] ^ (2 * k + 1))):
            low[z] = source[k, :rows]
            high[z] = source[k, rows:]


def order_halves(ids, pair, received):
    shape = (4, pair.shape[1] // 2, pair.shape[2])
    return call(
        halves_body,
        "order_halves",
        (1,),
        (ids, pair, received),
        [WHOLE] * 2,
        [shaped(shape, bf16)] * 2,
        [WHOLE] * 2,
        [],
        6,
        1,
    )


def first_body(ids, *refs):
    at_y, at_x, at_corner, (to_y, to_x) = refs[:2], refs[2:4], refs[4:6], refs[6:]
    half = to_y.shape[1] // 2
    to_y[:, :half] = both(at_y, PLANE, 0, half).astype(bf16)
    to_y[:, half:] = both(at_corner, PLANE, 0, half).astype(bf16)
    to_x[:, :half] = both(at_x, PLANE, half, 2 * half).astype(bf16)
    to_x[:, half:] = both(at_corner, PLANE, half, 2 * half).astype(bf16)


def reduce_first(ids, parts):
    shape = parts[0].shape
    return call(
        first_body,
        "reduce_first",
        (1,),
        (ids, *parts, *parts, *parts),
        [beside(shape, 1, 0)] * 2 + [beside(shape, 0, 1)] * 2 + [beside(shape, 1, 1)] * 2,
        [shaped((4,) + shape[3:], bf16)] * 2,
        [WHOLE] * 2,
        [],
        10,
        3,
    )


def second_body(ids, *refs):
    here, at_y, at_x, (from_y, from_x, *outs) = refs[:2], refs[2:4], refs[4:6], refs[6:]
    half = from_y.shape[1] // 2
    by_next, keep_next, by_far, keep_far = outs
    for k, upper, lower in (
        (0, (keep_next, 0), (keep_far, 0)),
        (1, (by_next, 0), (keep_far, 1)),
        (2, (keep_next, 1), (by_far, 0)),
        (3, (by_next, 1), (by_far, 1)),
    ):
        z = ids[3] ^ k
        plane = (z, 0, 0)
        quarters = (
            both(here, plane, 0, half) + from_y[z, :half].astype(f32),
            both(at_x, plane, 0, half) + from_y[z, half:].astype(f32),
            both(here, plane, half, 2 * half) + from_x[z, :half].astype(f32),
            both(at_y, plane, half, 2 * half) + from_x[z, half:].astype(f32),
        )
        for i, quarter in enumerate(quarters):
            out, at = upper if i < 2 else lower
            out[at, i % 2 * half : (i % 2 + 1) * half] = quarter.astype(out.dtype)


def reduce_second(ids, parts, from_y, from_x):
    shape = parts[0].shape
    wide = (2,) + shape[3:]
    return call(
        second_body,
        "reduce_second",
        (1,),
        (ids, *parts, *parts, *parts, from_y, from_x),
        [beside(shape, 0, 0)] * 2 + [beside(shape, 1, 0)] * 2 + [beside(shape, 0, 1)] * 2 + [WHOLE] * 2,
        [shaped(wide, bf16), shaped(wide, f32)] * 2,
        [WHOLE] * 4,
        [],
        14,
        3,
    )


def third_body(ids, keep_next, keep_far, next_in, far_in, next_mine, far_mine, to_far, to_next):
    next_mine[...] = keep_next[0] + next_in[0].astype(f32)
    to_far[...] = (keep_next[1] + next_in[1].astype(f32)).astype(bf16)
    far_mine[...] = keep_far[0] + far_in[0].astype(f32)
    to_next[...] = (keep_far[1] + far_in[1].astype(f32)).astype(bf16)


def reduce_third(ids, keep_next, keep_far, next_in, far_in):
    shape = keep_next.shape[1:]
    return call(
        third_body,
        "reduce_third",
        (1,),
        (ids, keep_next, keep_far, next_in, far_in),
        [WHOLE] * 4,
        [shaped(shape, f32)] * 2 + [shaped(shape, bf16)] * 2,
        [WHOLE] * 4,
        [],
        10,
        2,
    )


def fourth_body(ids, upper, lower, from_far, from_next, to_x, to_y, own):
    half = to_x.shape[0]
    first = upper[...] + from_far[...].astype(f32)
    second = lower[...] + from_next[...].astype(f32)
    own[:half] = first[:half]
    own[half:] = second[:half]
    to_x[...] = first[half:].astype(bf16)
    to_y[...] = second[half:].astype(bf16)


def reduce_fourth(ids, upper, lower, from_far, from_next):
    rows, width = upper.shape
    return call(
        fourth_body,
        "reduce_fourth",
        (1,),
        (ids, upper, lower, from_far, from_next),
        [WHOLE] * 4,
        [shaped((rows // 2, width), bf16)] * 2 + [shaped((rows, width), f32)],
        [WHOLE] * 3,
        [],
        8,
        2,
    )


def exchange_z(sends):
    return [pp(send, "z", k) for send, k in zip(sends, (1, 2, 3))]


def local(
    hidden_in,
    cotangent,
    attention_keep,
    output_keep,
    feed_keep,
    qkv_weight,
    qkv_bias,
    out_weight,
    out_bias,
    first_gain,
    first_shift,
    up_weight,
    up_bias,
    down_weight,
    down_bias,
    second_gain,
    second_shift,
):
    micro, _, tokens, width = hidden_in.shape
    rows = micro * tokens
    own = qkv_weight.shape[0]
    wide = up_weight.shape[1]
    blocks = wide // width
    c, y, x = lax.axis_index("seq"), lax.axis_index("y"), lax.axis_index("x")
    ids = jnp.stack([c, y, x, lax.axis_index("z")]).astype(jnp.int32)
    bias_parts = (out_bias, first_gain, first_shift, up_bias, down_bias, second_gain, second_shift)
    pers = [part.shape[0] for part in bias_parts]
    per = qkv_bias.shape[0]

    column = lambda weight, i: weight[:, i * width : (i + 1) * width]
    bias_rows = lambda parts: jnp.concatenate(
        [jnp.pad(part.reshape(1, -1), ((0, 0), (0, width - part.shape[0]))) for part in parts]
        + [jnp.zeros((8 - len(parts), width), bf16)]
    )
    square = (own, width)
    hidden = hidden_in.reshape(rows, width)

    shard_a = jnp.concatenate([column(qkv_weight, i) for i in range(3)] + [bias_rows((qkv_bias,))])
    half_c = down_weight.shape[0] // 2
    x_c, y_c = pp(down_weight[:half_c], "x"), pp(down_weight[half_c:], "y")
    shard_b = jnp.concatenate(
        [out_weight] + [column(up_weight, i) for i in range(blocks)] + [bias_rows(bias_parts)]
    )
    z_a = hold([pp(shard_a, "z", k) for k in (1, 2, 3)], x_c, y_c, shard_b)
    own_a = order_four(ids, shard_a, *z_a)
    group_c = jnp.concatenate([down_weight[:half_c], x_c, down_weight[half_c:], y_c])
    x_a, y_a = pp(own_a, "x"), pp(own_a, "y")
    shard_b = after(shard_b, own_a)
    far_b = pp(shard_b, "z", 2)
    turned, keep_output, keep_feed = prepare(
        ids, after(hidden, own_a), output_keep.transpose(0, 1, 3, 2), feed_keep.transpose(0, 1, 3, 2), tokens
    )
    x_a, y_a, far_b = hold((x_a, y_a, far_b), turned)
    cut_a = shard_a.shape[0] // 2
    low_a, high_a = pp(x_a[:, :cut_a], "y"), pp(y_a[:, cut_a:], "x")
    pieces = [whole(0, 0, own_a), whole(1, 0, x_a), whole(2, 0, y_a), whole(3, 0, low_a), whole(3, cut_a, high_a)]
    late = whole(2, 0, after(y_a, low_a))
    pieces += [at_core(piece) for piece in pieces[:2] + [late] + pieces[3:]]
    pair_b = pair_z(ids, shard_b, far_b)
    near_b = pp(pair_b, "z", 1)
    plan = [(i * own, own, i, 0, 0) for i in range(3)]
    plan = divide(plan, cut_a)
    loose = [piece[2] for piece in pieces]
    weights = Weights(pieces, plan + [(3 * own, 8, 3, 0, 0)], [square] * 3 + [(8, width)], loose)
    weights_again = Weights(pieces, plan, [square] * 3)
    own_b = order_z(ids, pair_b, after(near_b, low_a, high_a))
    far_c = pp(after(group_c, own_b), "z", 2)
    x_b, y_b = pp(own_b, "x"), pp(own_b, "y")
    queries, *near = project(ids, weights, hidden, after(turned, own_b), micro, per)
    near = (near[: 2 * PARTS[0]], near[2 * PARTS[0] :])
    far = [[pp(value, "seq") for value in values] for values in near]
    words = attention_keep.reshape(micro, H, tokens, -1)
    *far[0], far_c = hold((*far[0], far_c))
    pair_c = pair_z(ids, group_c, far_c)
    near_c = pp(pair_c, "z", 1)
    context, signed = attention(ids, 0, after(queries, pair_c), near, far, words)
    own_b, x_b, y_b, *far[1] = hold((own_b, x_b, y_b, *far[1]), context)
    cut_b = shard_b.shape[0] // 2
    low_b, high_b = pp(x_b[:, :cut_b], "y"), pp(y_b[:, cut_b:], "x")
    context, signed = attention(ids, 1, queries, near, far, words, (context, signed))
    low_b, high_b, near_c = hold((low_b, high_b, near_c), context)
    pieces = [whole(0, 0, own_b), whole(1, 0, x_b), whole(2, 0, after(y_b, context))]
    pieces += [at_core(piece) for piece in pieces]
    corners = [whole(3, 0, low_b), whole(3, cut_b, high_b)]
    pieces += corners + [at_core(piece) for piece in corners]
    plan = [(0, own, 0, 0, 0)] + [((i + 1) * own, own, 1, 0, i * width) for i in range(blocks)]
    plan = divide(plan, cut_b)
    weights = Weights(
        pieces,
        plan + [((blocks + 1) * own, 8, 2, 0, 0)],
        [square, (own, wide), (8, width)],
        [piece[2] for piece in pieces],
    )
    back_weights = Weights(pieces, plan, [square, (own, wide)])
    by_x, by_y = order_halves(ids, pair_c, after(near_c, low_b, high_b))
    from_y, from_x = pp(by_x, "y"), pp(by_y, "x")
    context = context.reshape(rows, width)
    vectors, scaled, inverse, activated, slope = feed_up(
        ids, weights, pers, context, hidden, keep_output, tokens, wide
    )
    from_y, from_x = hold((from_y, from_x), activated)
    down_rows = down_weight.shape[0]
    pieces = []
    for core in range(2):
        held = [by_x, from_y, by_y, from_x]
        if core == 1:
            held = [pp(array, "seq") for array in held]
        for array, numbers, first in zip(held, ((0, 1), (2, 3), (0, 2), (1, 3)), (0, 0, half_c, half_c)):
            pieces += [(4 * core + number, first, array, i * half_c, half_c) for i, number in enumerate(numbers)]
    plan = divide([(0, down_rows, 0, 0, 0)], half_c)
    weights = Weights(pieces, plan, [(down_rows, width)], [piece[2] for piece in pieces])
    layer_out, g_second, g_inner, down_own, down_send, sums = feed_down(
        ids, weights, activated, slope, scaled, keep_feed, cotangent.reshape(rows, width), vectors, tokens
    )

    unit = lambda value: value.reshape((4, 2, 2) + value.shape[1:])
    down_core = pp(down_send, "seq")
    mid_own, mid_send = up_grads(ids, g_inner, scaled, vectors)
    down = [unit(down_own), unit(after(down_core, mid_send))]
    to_y, to_x = reduce_first(ids, down)
    down_y, down_x = pp(to_y, "y"), pp(to_x, "x")
    mid_core = pp(after(mid_send, to_y), "seq")
    g_first, g_context, out_own, out_send, block = middle(
        ids, back_weights, pers, after(g_inner, to_y), g_second, scaled, inverse, keep_output, vectors, context, sums, tokens
    )
    out_core = pp(out_send, "seq")
    down_y, down_x, mid_core = hold((down_y, down_x, mid_core), g_context)
    mid = [unit(value) for value in (mid_own, out_own, mid_core, out_core)]
    cut_m = (count_rows(mid) + 15) // 16 * 8
    corner = reduce_corner(ids, mid, cut_m)
    low, high = pp(corner[0], "x"), pp(corner[1], "y")
    to_next, keep_next, to_far, keep_far = reduce_second(ids, down, down_y, down_x)
    next_in, far_in = pp(to_next, "z", 1), pp(to_far, "z", 2)
    first_q, *first_near, far_k, far_v = attention_back(
        ids, 0, queries, near, far, signed, after(g_context, to_next, *corner)
    )
    low, high = hold((low, high), first_q)
    first_far = [pp(after(value, low, high), "seq") for value in (far_k, far_v)]
    to_y, to_x = reduce_sides(ids, mid, low, high)
    mid_y, mid_x = pp(to_y, "y"), pp(to_x, "x")
    second_q, *second_near, far_k, far_v = attention_back(
        ids, 1, queries, near, far, signed, after(g_context, to_y, to_x)
    )
    first_far = hold(first_far, second_q)
    second_far = [pp(value, "seq") for value in (far_k, far_v)]
    next_in, far_in = hold((next_in, far_in), second_q)
    upper, lower, to_far, to_next = reduce_third(ids, keep_next, keep_far, next_in, far_in)
    far_in, next_in = pp(to_far, "z", 2), pp(to_next, "z", 1)
    grads = (first_q, second_q, *first_near, *second_near, *first_far, *hold(second_far, to_far))
    a_own, a_send, g_q, g_keys, g_values = input_grads(ids, hidden, turned, grads, block, per)
    mid_y, mid_x = hold((mid_y, mid_x), a_send)
    far_in, next_in = hold((far_in, next_in), a_send)
    core_sums = pp(after(a_send, mid_y, mid_x, far_in, next_in), "seq")
    to_far_x, to_far_y, down_mine = reduce_fourth(ids, upper, lower, far_in, next_in)
    part = [unit(a_own), unit(core_sums)]
    corner = reduce_corner(ids, part, cut_a)
    low, high = pp(corner[0], "x"), pp(corner[1], "y")
    *sends, mid_mine = reduce_depth(ids, mid, after(mid_y, *corner), mid_x)
    mid_z = exchange_z(sends)
    low, high = hold((low, high), *sends)
    to_y, to_x = reduce_sides(ids, part, low, high)
    side_y, side_x = pp(to_y, "y"), pp(to_x, "x")
    received = [pp(after(to_far_x, to_x), "x"), pp(after(to_far_y, to_y), "y")]
    grad_in = last(
        ids, weights_again, g_first, g_q, g_keys, after(g_values, to_y, to_x), tokens
    )
    mid_z = hold(mid_z, grad_in)
    mid = add_up([mid_mine, *mid_z])
    side_y, side_x, *received = hold((side_y, side_x, *received), mid, grad_in)
    *sends, part_mine = reduce_depth(ids, part, side_y, side_x)
    grad_down = add_up([down_mine, jnp.concatenate(received)])
    part = add_up([part_mine, *exchange_z(sends)])

    stripe = lambda value, i: value[i * own : (i + 1) * own]
    grad_qkv = jnp.concatenate([stripe(part, i) for i in range(3)], axis=1)
    grad_up = jnp.concatenate([stripe(mid, i) for i in range(blocks)], axis=1)
    vector_grads = [part[3 * own + i, :length] for i, length in enumerate(pers)]
    grad_out = mid[blocks * own :]
    return (
        layer_out.reshape(hidden_in.shape),
        grad_in.reshape(hidden_in.shape),
        grad_qkv,
        part[3 * own + 7, :per],
        grad_out,
        vector_grads[0],
        vector_grads[1],
        vector_grads[2],
        grad_up,
        vector_grads[3],
        grad_down,
        vector_grads[4],
        vector_grads[5],
        vector_grads[6],
    )


def solution(mesh):
    groups, cores = mesh.devices.shape
    split = Mesh(mesh.devices.reshape(groups // 4, 2, 2, cores), ("z", "y", "x", "seq"))
    dp = ("z", "y", "x")
    token_rows = P(None, dp, "seq", None)
    matrix = P(every, None)
    vector = P(every)
    params = (matrix, vector, matrix, vector, vector, vector, matrix, vector, matrix, vector, vector, vector)

    def layer(*arrays):
        tiled = groups == 16 and cores == 2 and arrays[5].shape[0] % 8 == 0
        return (local if tiled else plain_local)(*arrays)

    return jax.shard_map(
        layer,
        mesh=split,
        in_specs=(token_rows, token_rows, P(None, dp, None, "seq", None), token_rows, token_rows) + params,
        out_specs=(token_rows, token_rows) + params,
        check_vma=False,
    )
```

```python
import functools

import jax
import jax.numpy as jnp
from jax import lax
from jax.experimental import pallas as pl
from jax.experimental.pallas import tpu as pltpu
from jax.sharding import Mesh
from jax.sharding import PartitionSpec as P

H = 12
epsilon = 1e-12
keep_scale = 8.0 / 7.0
root_half = 0.7071067811865476
inverse_root_tau = 0.3989422804014327
every = ("z", "y", "x", "seq")
f32 = jnp.float32
bf16 = jnp.bfloat16


def unpack_keep(packed_words):
    shifts = jnp.arange(4, dtype=jnp.int32) * 3
    nibble = jnp.right_shift(packed_words[..., None], shifts) & 7
    keep_value = (nibble >= 1).astype(jnp.float32) * keep_scale
    return keep_value.reshape(packed_words.shape[:-1] + (packed_words.shape[-1] * 4,))


def normalize(values, norm_gain, norm_shift):
    centred = values - jnp.mean(values, axis=-1, keepdims=True)
    inverse = lax.rsqrt(jnp.mean(centred * centred, axis=-1, keepdims=True) + epsilon)
    scaled = centred * inverse
    return (scaled * norm_gain + norm_shift, scaled, inverse)


def norm_back(upstream, scaled, inverse, norm_gain):
    weighted = upstream * norm_gain
    centre_term = jnp.mean(weighted, axis=-1, keepdims=True)
    slope_term = jnp.mean(weighted * scaled, axis=-1, keepdims=True)
    return inverse * (weighted - centre_term - scaled * slope_term)


def gelu_slope(inner_sum):
    normal_cdf = 0.5 * (1.0 + lax.erf(inner_sum * root_half))
    density = jnp.exp(-0.5 * inner_sum * inner_sum) * inverse_root_tau
    return normal_cdf + inner_sum * density


def matmul(left_side, right_side):
    return jnp.dot(left_side, right_side, preferred_element_type=jnp.float32)


def plain_local(
    hidden_in,
    cotangent,
    attention_keep,
    output_keep,
    feed_keep,
    qkv_weight,
    qkv_bias,
    out_weight,
    out_bias,
    first_gain,
    first_shift,
    up_weight,
    up_bias,
    down_weight,
    down_bias,
    second_gain,
    second_shift,
):
    model_width = hidden_in.shape[-1]
    sequence_count = hidden_in.shape[1]
    local_tokens = hidden_in.shape[2]
    token_rows = sequence_count * local_tokens
    head_count = H
    head_size = model_width // head_count
    held_params = (
        lax.all_gather(qkv_weight, every, axis=0, tiled=True),
        lax.all_gather(qkv_bias, every, axis=0, tiled=True),
        lax.all_gather(out_weight, every, axis=0, tiled=True),
        lax.all_gather(out_bias, every, axis=0, tiled=True),
        lax.all_gather(first_gain, every, axis=0, tiled=True),
        lax.all_gather(first_shift, every, axis=0, tiled=True),
        lax.all_gather(up_weight, every, axis=0, tiled=True),
        lax.all_gather(up_bias, every, axis=0, tiled=True),
        lax.all_gather(down_weight, every, axis=0, tiled=True),
        lax.all_gather(down_bias, every, axis=0, tiled=True),
        lax.all_gather(second_gain, every, axis=0, tiled=True),
        lax.all_gather(second_shift, every, axis=0, tiled=True),
    )
    totals = None
    outputs = []
    inputs_grad = []
    for micro_step in range(hidden_in.shape[0]):
        (
            full_qkv_w,
            full_qkv_b,
            full_out_w,
            full_out_b,
            full_gain_one,
            full_shift_one,
            full_up_w,
            full_up_b,
            full_down_w,
            full_down_b,
            full_gain_two,
            full_shift_two,
        ) = held_params
        rows_in = hidden_in[micro_step].reshape(token_rows, model_width)
        qkv_float = full_qkv_b.astype(jnp.float32)
        bias_full = jnp.concatenate(
            [
                qkv_float[:model_width],
                jnp.zeros((model_width,), jnp.float32),
                qkv_float[model_width:],
            ]
        )
        projected = (matmul(rows_in, full_qkv_w) + bias_full).astype(jnp.bfloat16)
        queries = projected[:, :model_width].reshape(
            sequence_count, local_tokens, head_count, head_size
        )
        keys_local = projected[:, model_width : 2 * model_width].reshape(
            sequence_count, local_tokens, model_width
        )
        values_local = projected[:, 2 * model_width :].reshape(
            sequence_count, local_tokens, model_width
        )
        keys_all, values_all = (
            lax.all_gather(keys_local, "seq", axis=1, tiled=True),
            lax.all_gather(values_local, "seq", axis=1, tiled=True),
        )
        keys_heads = keys_all.reshape(sequence_count, -1, head_count, head_size)
        values_heads = values_all.reshape(sequence_count, -1, head_count, head_size)
        scores = (
            jnp.einsum("sqhd,skhd->shqk", queries, keys_heads, preferred_element_type=jnp.float32)
            * 0.125
        )
        row_peak = jnp.max(scores, axis=-1, keepdims=True)
        exponent = jnp.exp(scores - row_peak)
        row_total = jnp.sum(exponent, axis=-1, keepdims=True)
        log_total = row_peak + jnp.log(row_total)
        softmax_weights = exponent / row_total
        keep_attention = unpack_keep(attention_keep[micro_step])
        dropped = (softmax_weights * keep_attention).astype(jnp.bfloat16)
        context = jnp.einsum(
            "shqk,skhd->sqhd", dropped, values_heads, preferred_element_type=jnp.float32
        )
        context = context.reshape(token_rows, model_width).astype(jnp.bfloat16)
        attended = matmul(context, full_out_w) + full_out_b.astype(jnp.float32)
        keep_output = unpack_keep(output_keep[micro_step]).reshape(token_rows, model_width)
        first_sum = rows_in.astype(jnp.float32) + attended * keep_output
        gain_one = full_gain_one.astype(jnp.float32)
        normed, scaled_one, inverse_one = normalize(
            first_sum, gain_one, full_shift_one.astype(jnp.float32)
        )
        normed_low = normed.astype(jnp.bfloat16)
        inner_sum = matmul(normed_low, full_up_w) + full_up_b.astype(jnp.float32)
        activated = jax.nn.gelu(inner_sum, approximate=False).astype(jnp.bfloat16)
        outer_sum = matmul(activated, full_down_w) + full_down_b.astype(jnp.float32)
        keep_feed = unpack_keep(feed_keep[micro_step]).reshape(token_rows, model_width)
        second_sum = normed + outer_sum * keep_feed
        gain_two = full_gain_two.astype(jnp.float32)
        result, scaled_two, inverse_two = normalize(
            second_sum, gain_two, full_shift_two.astype(jnp.float32)
        )
        outputs.append(
            result.astype(jnp.bfloat16).reshape(sequence_count, local_tokens, model_width)
        )
        (
            back_qkv_w,
            back_qkv_b,
            back_out_w,
            back_out_b,
            back_gain_one,
            back_shift_one,
            back_up_w,
            back_up_b,
            back_down_w,
            back_down_b,
            back_gain_two,
            back_shift_two,
        ) = held_params
        upstream = cotangent[micro_step].reshape(token_rows, model_width).astype(jnp.float32)
        g_second = norm_back(upstream, scaled_two, inverse_two, back_gain_two.astype(jnp.float32))
        grad_gain_two = jnp.sum(upstream * scaled_two, axis=0)
        grad_shift_two = jnp.sum(upstream, axis=0)
        g_outer = (g_second * keep_feed).astype(jnp.bfloat16)
        grad_down_b = jnp.sum(g_outer.astype(jnp.float32), axis=0)
        grad_down_w = matmul(activated.T, g_outer)
        g_inner = (matmul(g_outer, back_down_w.T) * gelu_slope(inner_sum)).astype(jnp.bfloat16)
        grad_up_b = jnp.sum(g_inner.astype(jnp.float32), axis=0)
        grad_up_w = matmul(normed_low.T, g_inner)
        g_normed = g_second + matmul(g_inner, back_up_w.T)
        g_first = norm_back(g_normed, scaled_one, inverse_one, back_gain_one.astype(jnp.float32))
        grad_gain_one = jnp.sum(g_normed * scaled_one, axis=0)
        grad_shift_one = jnp.sum(g_normed, axis=0)
        g_attended = (g_first * keep_output).astype(jnp.bfloat16)
        grad_out_b = jnp.sum(g_attended.astype(jnp.float32), axis=0)
        grad_out_w = matmul(context.T, g_attended)
        g_context = matmul(g_attended, back_out_w.T).astype(jnp.bfloat16)
        g_context = g_context.reshape(sequence_count, local_tokens, head_count, head_size)
        keys_again, values_again = (
            lax.all_gather(keys_local, "seq", axis=1, tiled=True),
            lax.all_gather(values_local, "seq", axis=1, tiled=True),
        )
        keys_heads = keys_again.reshape(sequence_count, -1, head_count, head_size)
        values_heads = values_again.reshape(sequence_count, -1, head_count, head_size)
        scores_again = (
            jnp.einsum("sqhd,skhd->shqk", queries, keys_heads, preferred_element_type=jnp.float32)
            * 0.125
        )
        weights_again = jnp.exp(scores_again - log_total)
        dropped_again = (weights_again * keep_attention).astype(jnp.bfloat16)
        g_values_all = jnp.einsum(
            "shqk,sqhd->skhd", dropped_again, g_context, preferred_element_type=jnp.float32
        )
        g_dropped = jnp.einsum(
            "sqhd,skhd->shqk", g_context, values_heads, preferred_element_type=jnp.float32
        )
        g_weights = g_dropped * keep_attention
        row_delta = jnp.sum(g_weights * weights_again, axis=-1, keepdims=True)
        g_scores = (weights_again * (g_weights - row_delta)).astype(jnp.bfloat16)
        g_queries = (
            jnp.einsum("shqk,skhd->sqhd", g_scores, keys_heads, preferred_element_type=jnp.float32)
            * 0.125
        )
        g_keys_all = (
            jnp.einsum("shqk,sqhd->skhd", g_scores, queries, preferred_element_type=jnp.float32)
            * 0.125
        )
        g_keys, g_values = (
            lax.psum_scatter(
                g_keys_all.reshape(sequence_count, -1, model_width).astype(jnp.bfloat16),
                "seq",
                scatter_dimension=1,
                tiled=True,
            ).astype(jnp.float32),
            lax.psum_scatter(
                g_values_all.reshape(sequence_count, -1, model_width).astype(jnp.bfloat16),
                "seq",
                scatter_dimension=1,
                tiled=True,
            ).astype(jnp.float32),
        )
        g_projected = jnp.concatenate(
            [
                g_queries.reshape(token_rows, model_width),
                g_keys.reshape(token_rows, model_width),
                g_values.reshape(token_rows, model_width),
            ],
            axis=1,
        ).astype(jnp.bfloat16)
        g_projected_float = g_projected.astype(jnp.float32)
        grad_qkv_b = jnp.concatenate(
            [
                jnp.sum(g_projected_float[:, :model_width], axis=0),
                jnp.sum(g_projected_float[:, 2 * model_width :], axis=0),
            ]
        )
        grad_qkv_w = matmul(rows_in.T, g_projected)
        input_grad = g_first + matmul(g_projected, back_qkv_w.T)
        inputs_grad.append(
            input_grad.astype(jnp.bfloat16).reshape(sequence_count, local_tokens, model_width)
        )
        grads_now = (
            grad_qkv_w,
            grad_qkv_b,
            grad_out_w,
            grad_out_b,
            grad_gain_one,
            grad_shift_one,
            grad_up_w,
            grad_up_b,
            grad_down_w,
            grad_down_b,
            grad_gain_two,
            grad_shift_two,
        )
        if totals is None:
            totals = grads_now
        else:
            totals = tuple((before + added for before, added in zip(totals, grads_now)))
    summed = (
        lax.psum_scatter(totals[0], every, scatter_dimension=0, tiled=True),
        lax.psum_scatter(totals[1], every, scatter_dimension=0, tiled=True),
        lax.psum_scatter(totals[2], every, scatter_dimension=0, tiled=True),
        lax.psum_scatter(totals[3], every, scatter_dimension=0, tiled=True),
        lax.psum_scatter(totals[4], every, scatter_dimension=0, tiled=True),
        lax.psum_scatter(totals[5], every, scatter_dimension=0, tiled=True),
        lax.psum_scatter(totals[6], every, scatter_dimension=0, tiled=True),
        lax.psum_scatter(totals[7], every, scatter_dimension=0, tiled=True),
        lax.psum_scatter(totals[8], every, scatter_dimension=0, tiled=True),
        lax.psum_scatter(totals[9], every, scatter_dimension=0, tiled=True),
        lax.psum_scatter(totals[10], every, scatter_dimension=0, tiled=True),
        lax.psum_scatter(totals[11], every, scatter_dimension=0, tiled=True),
    )
    return (
        jnp.stack(outputs, axis=0),
        jnp.stack(inputs_grad, axis=0),
        summed[0],
        summed[1],
        summed[2],
        summed[3],
        summed[4],
        summed[5],
        summed[6],
        summed[7],
        summed[8],
        summed[9],
        summed[10],
        summed[11],
    )


ANY = pl.BlockSpec(memory_space=pl.ANY)
WHOLE = pl.BlockSpec(memory_space=pltpu.VMEM)
MIB = 2**20
PARTS = (2, 1)
GROUP = 2


def dot_t(left_side, right_side):
    return lax.dot_general(left_side, right_side, (((1,), (1,)), ((), ())), preferred_element_type=f32)


def t_dot(left_side, right_side):
    return lax.dot_general(left_side, right_side, (((0,), (0,)), ((), ())), preferred_element_type=f32)


def iota(shape, axis):
    return lax.broadcasted_iota(jnp.int32, shape, axis)


def pp(value, axis, step=1):
    size = lax.axis_size(axis)
    return lax.ppermute(value, axis, [(i, i ^ step) for i in range(size)])


def pick(value, axis, index):
    return lax.dynamic_index_in_dim(value, index, axis, keepdims=False)


def after(value, *earlier):
    return lax.optimization_barrier((value,) + earlier)[0]


def hold(values, *earlier):
    return lax.optimization_barrier(tuple(values) + earlier)[: len(values)]


def add_up(terms):
    total = terms[0].astype(f32)
    for term in terms[1:]:
        total = total + term.astype(f32)
    return total


def divide(plan, cut):
    parts = []
    for start, rows, out, row, column in plan:
        ends = [start, cut, start + rows] if start < cut < start + rows else [start, start + rows]
        for first, last in zip(ends, ends[1:]):
            parts.append((first, last - first, out, row + first - start, column))
    return parts


def whole(number, first, array):
    return (number, first, array, 0, array.shape[1])


def at_core(piece):
    number, first, array, row, rows = piece
    return (number + 4, first, pp(array, "seq"), row, rows)


class Weights:
    def __init__(self, pieces, plan, shapes, free=()):
        arrays = []
        self.spans = []
        for number, first, array, row, rows in pieces:
            place = next((i for i, held in enumerate(arrays) if held is array), len(arrays))
            if place == len(arrays):
                arrays.append(array)
            self.spans.append((number, first, place, row, rows))
        loose = [any(array is other for other in free) for array in arrays]
        self.operands = [
            array if found else pltpu.with_memory_space_constraint(array, pltpu.HBM)
            for array, found in zip(arrays, loose)
        ]
        self.plan, self.shapes = plan, shapes
        self.specs = [ANY if found else pl.BlockSpec(memory_space=pltpu.HBM) for found in loose]
        self.scratch = [pltpu.VMEM((4, 2, 2, 2, rows, columns), bf16) for rows, columns in shapes]
        self.scratch.append(pltpu.SemaphoreType.DMA((8 * len(plan),)))

    def copies(self, ids, sources, places, sems):
        found = [[] for _ in self.shapes]
        count = 0
        for start, rows, out, row, column in self.plan:
            for number, first, place, source_row, held in self.spans:
                if first <= start and start + rows <= first + held:
                    c = ids[0] ^ (number >> 2)
                    y = ids[1] ^ ((number >> 1) & 1)
                    x = ids[2] ^ (number & 1)
                    source = sources[place]
                    src = source.at[:, pl.ds(source_row + start - first, rows), :]
                    dst = places[out].at[:, y, x, c, pl.ds(row, rows), pl.ds(column, source.shape[2])]
                    found[out].append(pltpu.make_async_copy(src, dst, sems.at[count]))
                    count += 1
        return found

    def matrix(self, places, out):
        rows, columns = self.shapes[out]
        return places[out].reshape(32 * rows, columns)


def begin(copies):
    for group in copies:
        for copy in group:
            copy.start()


def finish(group):
    for copy in group:
        copy.wait()


def spread(block, row, count, per):
    values = block[:, row, : -(-per // 128) * 128].astype(bf16)
    lanes = values.shape[1]
    select = (iota((lanes, count), 1) % per == iota((lanes, count), 0)).astype(bf16)
    wide = jnp.dot(values, select, preferred_element_type=f32)
    return jnp.sum(jnp.where(iota(wide.shape, 1) // per == iota(wide.shape, 0), wide, 0.0), axis=0, keepdims=True)


def unspread(vectors, pers, block, first=0):
    block[:, first:] = jnp.zeros((32, 8 - first, block.shape[2]), f32)
    for row, (vector, per) in enumerate(zip(vectors, pers), first):
        count = vector.shape[1]
        lanes = -(-per // 128) * 128
        shape = (32, count)
        wide = jnp.where(iota(shape, 1) // per == iota(shape, 0), vector, 0.0).astype(bf16)
        select = (iota((count, lanes), 0) % per == iota((count, lanes), 1)).astype(bf16)
        block[:, row, :lanes] = jnp.dot(wide, select, preferred_element_type=f32)


def layer_norm(values):
    centred = values - jnp.mean(values, axis=-1, keepdims=True)
    inverse = lax.rsqrt(jnp.mean(centred * centred, axis=-1, keepdims=True) + epsilon)
    return centred * inverse, inverse


def turn_matrix(tokens):
    place = iota((tokens, tokens), 0)
    quarter = tokens // 4
    return (iota((tokens, tokens), 1) == 4 * (place % quarter) + place // quarter).astype(bf16)


def call(body, name, grid, operands, specs, outs, out_specs, scratch, room, load, aliases=None):
    return pl.pallas_call(
        body,
        grid_spec=pltpu.PrefetchScalarGridSpec(
            num_scalar_prefetch=1, grid=grid, in_specs=specs, out_specs=out_specs, scratch_shapes=scratch
        ),
        out_shape=outs,
        compiler_params=pltpu.CompilerParams(vmem_limit_bytes=room * MIB),
        cost_estimate=pl.CostEstimate(flops=1024, bytes_accessed=load * MIB // 16, transcendentals=0),
        input_output_aliases=aliases or {},
        name=name,
    )(*operands)


def shaped(shape, dtype):
    return jax.ShapeDtypeStruct(shape, dtype)


def rows_spec(rows, columns):
    return pl.BlockSpec((rows, columns), lambda i, ids: (i, 0))


def fixed_spec(shape):
    return pl.BlockSpec(shape, lambda i, ids: (0,) * len(shape))


def prepare_body(ids, hidden, output_words, feed_words, turned, keep_output, keep_feed):
    tokens, width = hidden.shape
    turned[...] = jnp.dot(turn_matrix(tokens), hidden[...], preferred_element_type=f32).astype(bf16)
    quarter = width // 4
    for words, keep in ((output_words, keep_output), (feed_words, keep_feed)):
        packed = words[0, 0]
        total = jnp.zeros((tokens, width), f32)
        for i in range(4):
            bit = ((packed & (7 << (3 * i))) != 0).astype(f32).astype(bf16)
            place = (iota((quarter, width), 1) == 4 * iota((quarter, width), 0) + i).astype(bf16)
            total = total + t_dot(bit, place)
        keep[...] = total.astype(bf16)


def prepare(ids, hidden, output_words, feed_words, tokens):
    rows, width = hidden.shape
    wide = rows_spec(tokens, width)
    narrow = pl.BlockSpec((1, 1, width // 4, tokens), lambda i, ids: (i, 0, 0, 0))
    return call(
        prepare_body,
        "prepare",
        (rows // tokens,),
        (ids, hidden, output_words, feed_words),
        [wide, narrow, narrow],
        [shaped((rows, width), bf16)] * 3,
        [wide] * 3,
        [],
        12,
        6,
    )


def project_body(weights, per, ids, *refs):
    count = len(weights.operands)
    sources, (hidden, turned, queries), rest = refs[:count], refs[count : count + 3], refs[count + 3 :]
    micro, tokens, width = queries.shape
    places, sems = rest[len(rest) - 1 - len(weights.shapes) : -1], rest[-1]
    near = iter(rest[: len(rest) - 1 - len(weights.shapes)])
    copies = weights.copies(ids, sources, places, sems)
    begin(copies)
    finish(copies[3])
    block = weights.matrix(places, 3)[:, :128].astype(f32).reshape(32, 8, 128)
    bias = spread(block, 0, 2 * width, per)
    for n in range(3):
        finish(copies[n])
    for m in range(micro):
        natural, other = hidden[m * tokens : (m + 1) * tokens, :], turned[m * tokens : (m + 1) * tokens, :]
        q = jnp.dot(natural, weights.matrix(places, 0)[...], preferred_element_type=f32) + bias[:, :width]
        queries[m] = q.astype(bf16)
        k = jnp.dot(other, weights.matrix(places, 1)[...], preferred_element_type=f32).astype(bf16)
        v = jnp.dot(other, weights.matrix(places, 2)[...], preferred_element_type=f32) + bias[:, width:]
        for value in (k, v.astype(bf16)):
            rows = tokens // PARTS[m]
            for part in range(PARTS[m]):
                next(near)[...] = value[part * rows : (part + 1) * rows]


def project(ids, weights, hidden, turned, micro, per):
    rows, width = hidden.shape
    return call(
        functools.partial(project_body, weights, per),
        "project",
        (1,),
        (ids, *weights.operands, hidden, turned),
        weights.specs + [WHOLE] * 2,
        [shaped((micro, rows // micro, width), bf16)]
        + [shaped((rows // micro // PARTS[m], width), bf16) for m in range(micro) for _ in range(2 * PARTS[m])],
        [WHOLE] * (1 + 2 * sum(PARTS)),
        weights.scratch,
        16,
        10,
    )


def lane_half(shape):
    return iota(shape, len(shape) - 1) < 64


def by_head(pair):
    left, zero = lane_half(pair.shape), jnp.zeros_like(pair)
    return jnp.concatenate([jnp.where(left, pair, zero), jnp.where(left, zero, pair)], axis=0)


def join_keys(core, near, far, buffer, lanes):
    quarter = buffer.shape[0] // 8
    parts = len(near)
    for i in range(4):
        here = pl.multiple_of((2 * i + core) * quarter, quarter)
        there = pl.multiple_of((2 * i + 1 - core) * quarter, quarter)
        at = (i * parts % 4) // parts * quarter
        buffer[pl.ds(here, quarter), :] = near[i * parts // 4][at : at + quarter, lanes]
        buffer[pl.ds(there, quarter), :] = far[i * parts // 4][at : at + quarter, lanes]


def group_lanes():
    return [slice(j * 128, (j + 1) * 128) for j in range(GROUP)]


def attention_body(parts, ids, q, *refs):
    ours, words = refs[: 4 * parts], refs[4 * parts]
    context, signed, keys, values = refs[-4:]
    core = ids[0]
    tokens = q.shape[1]
    for j, lanes in enumerate(group_lanes()):
        join_keys(core, ours[:parts], ours[2 * parts : 3 * parts], keys.at[j], lanes)
        join_keys(core, ours[parts : 2 * parts], ours[3 * parts :], values.at[j], lanes)
    scores = [dot_t(by_head(q[0, :, lanes]) * 0.125, keys[j]) for j, lanes in enumerate(group_lanes())]
    for j, lanes in enumerate(group_lanes()):
        blocks = [scores[j][:, i * 128 : (i + 1) * 128] for i in range(4)]
        peak = jnp.maximum(jnp.maximum(blocks[0], blocks[1]), jnp.maximum(blocks[2], blocks[3]))
        peak = jnp.max(peak, axis=1, keepdims=True)
        blocks = [jnp.exp(block - peak) for block in blocks]
        total = jnp.sum((blocks[0] + blocks[1]) + (blocks[2] + blocks[3]), axis=1, keepdims=True)
        scale = 1.0 / total
        word = words[0, 2 * j : 2 * j + 2].reshape(2 * tokens, 128)
        dropped = []
        for i in range(4):
            weight = blocks[i] * scale
            keep = (word & (7 << (3 * i))) != 0
            weight = jnp.where(keep, weight, -weight).astype(bf16)
            signed[0, j, i] = weight
            dropped.append(jnp.maximum(weight, jnp.zeros_like(weight)))
        out = jnp.dot(jnp.concatenate(dropped, axis=1), values[j], preferred_element_type=f32) * keep_scale
        context[0, :, lanes] = jnp.where(lane_half((tokens, 128)), out[:tokens], out[tokens:]).astype(bf16)


def attention(ids, m, queries, near, far, words, earlier=()):
    micro, tokens, width = queries.shape
    pairs = width // 128
    part = pl.BlockSpec((1, tokens, 128 * GROUP), lambda p, ids: (m, 0, p))
    flat = pl.BlockSpec((tokens // PARTS[m], 128 * GROUP), lambda p, ids: (0, p))
    operands = (ids, queries, *near[m], *far[m], words)
    return call(
        functools.partial(attention_body, PARTS[m]),
        "attention",
        (pairs // GROUP,),
        operands + tuple(earlier),
        [part] + [flat] * (4 * PARTS[m])
        + [pl.BlockSpec((1, 2 * GROUP, tokens, 128), lambda p, ids: (m, p, 0, 0))]
        + [ANY] * len(earlier),
        [shaped((micro, tokens, width), bf16), shaped((micro, pairs, 4, 2 * tokens, 128), bf16)],
        [part, pl.BlockSpec((1, GROUP, 4, 2 * tokens, 128), lambda p, ids: (m, p, 0, 0, 0))],
        [pltpu.VMEM((GROUP, 2 * tokens, 128), bf16)] * 2,
        16,
        14,
        {len(operands) + i: i for i in range(len(earlier))},
    )


def attention_back_body(parts, ids, q, *refs):
    ours, signed, upstream, refs = refs[: 4 * parts], refs[4 * parts], refs[4 * parts + 1], refs[4 * parts + 2 :]
    g_q, *grads, keys, values, sums = refs
    g_near, g_far = grads[:2], grads[2:]
    core = ids[0]
    tokens = q.shape[1]
    for j, lanes in enumerate(group_lanes()):
        join_keys(core, ours[:parts], ours[2 * parts : 3 * parts], keys.at[j], lanes)
        join_keys(core, ours[parts : 2 * parts], ours[3 * parts :], values.at[j], lanes)
    aboves = [by_head(upstream[:, lanes]) for lanes in group_lanes()]
    g_droppeds = [dot_t(aboves[j], values[j]) for j in range(GROUP)]
    for j, lanes in enumerate(group_lanes()):
        weights, kept, g_weights = [], [], []
        delta = None
        for i in range(4):
            both_signs = signed[0, j, i].astype(f32)
            weight = jnp.abs(both_signs)
            g_weight = jnp.where(both_signs > 0.0, g_droppeds[j][:, i * 128 : (i + 1) * 128], 0.0)
            term = g_weight * weight
            delta = term if delta is None else delta + term
            weights.append(weight)
            g_weights.append(g_weight)
            kept.append(jnp.maximum(both_signs, 0.0).astype(bf16))
        delta = jnp.sum(delta, axis=1, keepdims=True)
        g_scores = jnp.concatenate(
            [(weights[i] * (g_weights[i] - delta)).astype(bf16) for i in range(4)], axis=1
        )
        dropped = jnp.concatenate(kept, axis=1)
        out = jnp.dot(g_scores, keys[j], preferred_element_type=f32)
        out = jnp.where(lane_half((tokens, 128)), out[:tokens], out[tokens:])
        g_q[:, lanes] = (out * (0.125 * keep_scale)).astype(bf16)
        quarter = keys.shape[1] // 8
        sums[j, 0] = t_dot(g_scores, by_head(q[0, :, lanes])) * (0.125 * keep_scale)
        sums[j, 1] = t_dot(dropped, aboves[j]) * keep_scale
        for kind in range(2):
            for i in range(4):
                here = pl.multiple_of((2 * i + core) * quarter, quarter)
                there = pl.multiple_of((2 * i + 1 - core) * quarter, quarter)
                rows = slice(i * quarter, (i + 1) * quarter)
                g_near[kind][rows, lanes] = sums[j, kind, pl.ds(here, quarter), :]
                g_far[kind][rows, lanes] = sums[j, kind, pl.ds(there, quarter), :].astype(bf16)


def attention_back(ids, m, queries, near, far, signed, upstream):
    micro, tokens, width = queries.shape
    pairs = width // 128
    part = pl.BlockSpec((1, tokens, 128 * GROUP), lambda p, ids: (m, 0, p))
    flat = pl.BlockSpec((tokens // PARTS[m], 128 * GROUP), lambda p, ids: (0, p))
    both = pl.BlockSpec((tokens, 128 * GROUP), lambda p, ids: (0, p))
    operands = (ids, queries, *near[m], *far[m], signed, upstream)
    return call(
        functools.partial(attention_back_body, PARTS[m]),
        "attention_back",
        (pairs // GROUP,),
        operands,
        [part] + [flat] * (4 * PARTS[m])
        + [pl.BlockSpec((1, GROUP, 4, 2 * tokens, 128), lambda p, ids: (m, p, 0, 0, 0))]
        + [pl.BlockSpec((tokens, 128 * GROUP), lambda p, ids: (m, p))],
        [
            shaped((tokens, width), bf16),
            shaped((tokens, width), f32),
            shaped((tokens, width), f32),
            shaped((tokens, width), bf16),
            shaped((tokens, width), bf16),
        ],
        [both] * 5,
        [pltpu.VMEM((GROUP, 2 * tokens, 128), bf16)] * 2 + [pltpu.VMEM((GROUP, 2, 2 * tokens, 128), f32)],
        24,
        20,
    )


def up_body(weights, pers, tokens, ids, *refs):
    count = len(weights.operands)
    sources = refs[:count]
    context, hidden, keep, vectors, scaled, inverse, activated, slope = refs[count : count + 8]
    places, (sems, lows) = refs[count + 8 : -2], refs[-2:]
    copies = weights.copies(ids, sources, places, sems)
    rows, width = scaled.shape
    wide = activated.shape[1]
    begin([copies[0], copies[2], copies[1]])
    finish(copies[2])
    block = weights.matrix(places, 2)[:, :128].astype(f32).reshape(32, 8, 128)
    for row, per in enumerate(pers):
        vectors[row : row + 1, : 32 * per] = spread(block, row, 32 * per, per)
    finish(copies[0])

    def rows_part(m, carry):
        at = pl.ds(pl.multiple_of(m * tokens, tokens), tokens)
        attended = jnp.dot(context[at], weights.matrix(places, 0)[...], preferred_element_type=f32)
        attended = attended + vectors[0:1, :width]
        first_sum = hidden[at].astype(f32) + attended * (keep[at].astype(f32) * keep_scale)
        normal, scale = layer_norm(first_sum)
        scaled[at] = normal
        inverse[at] = jnp.broadcast_to(scale, (tokens, 128))
        lows[at] = (normal * vectors[1:2, :width] + vectors[2:3, :width]).astype(bf16)
        return carry

    lax.fori_loop(0, rows // tokens, rows_part, 0)
    finish(copies[1])
    up = weights.matrix(places, 1)
    step = 512

    def part(n, carry):
        at = pl.ds(pl.multiple_of(n * step, step), step)
        inner = jnp.dot(lows[...], up[:, at], preferred_element_type=f32) + vectors[3:4, at]
        cdf = 0.5 * (1.0 + lax.erf(inner * root_half))
        density = jnp.exp(-0.5 * inner * inner) * inverse_root_tau
        activated[:, at] = (inner * cdf).astype(bf16)
        slope[:, at] = (cdf + inner * density).astype(bf16)
        return carry

    lax.fori_loop(0, wide // step, part, 0)


def feed_up(ids, weights, pers, context, hidden, keep, tokens, wide):
    rows, width = hidden.shape
    return call(
        functools.partial(up_body, weights, pers, tokens),
        "feed_up",
        (1,),
        (ids, *weights.operands, context, hidden, keep),
        weights.specs + [WHOLE] * 3,
        [
            shaped((8, wide), f32),
            shaped((rows, width), f32),
            shaped((rows, 128), f32),
            shaped((rows, wide), bf16),
            shaped((rows, wide), bf16),
        ],
        [WHOLE] * 5,
        weights.scratch + [pltpu.VMEM((rows, width), bf16)],
        16,
        24,
    )


def hand_out(core, total, rows, own, send, first, at):
    def one(n, carry):
        here = pl.multiple_of((2 * n + core) * rows, 8)
        there = pl.multiple_of((2 * n + 1 - core) * rows, 8)
        own[first + n, at : at + rows, :] = total[pl.ds(here, rows), :].astype(bf16)
        send[first + n, at : at + rows, :] = total[pl.ds(there, rows), :].astype(bf16)
        return carry

    lax.fori_loop(0, total.shape[0] // (2 * rows), one, 0)


def down_body(weights, tokens, ids, *refs):
    count = len(weights.operands)
    sources, refs = refs[:count], refs[count:]
    activated, slope, scaled, keep, cotangent, vectors = refs[:6]
    layer_out, g_second_out, g_inner, own, send, sums = refs[6:12]
    place, sems, total, g_outers = refs[12:]
    copies = weights.copies(ids, sources, (place,), sems)
    rows, width = scaled.shape
    wide = activated.shape[1]
    begin(copies)
    sums[...] = jnp.zeros_like(sums)
    finish(copies[0])
    down = weights.matrix((place,), 0)
    gain = vectors[5:6, :width]

    def rows_part(m, carry):
        at = pl.ds(pl.multiple_of(m * tokens, tokens), tokens)
        outer = jnp.dot(activated[at], down[...], preferred_element_type=f32) + vectors[4:5, :width]
        factor = keep[at].astype(f32) * keep_scale
        normed = scaled[at] * vectors[1:2, :width] + vectors[2:3, :width]
        normal, scale = layer_norm(normed + outer * factor)
        layer_out[at] = (normal * gain + vectors[6:7, :width]).astype(bf16)
        above = cotangent[at].astype(f32)
        weighted = above * gain
        g_second = scale * (
            weighted
            - jnp.mean(weighted, axis=-1, keepdims=True)
            - normal * jnp.mean(weighted * normal, axis=-1, keepdims=True)
        )
        g_second_out[at] = g_second
        g_outer = (g_second * factor).astype(bf16)
        g_outers[at] = g_outer
        sums[0:1, :width] += jnp.sum(g_outer.astype(f32), axis=0, keepdims=True)
        sums[1:2, :width] += jnp.sum(above * normal, axis=0, keepdims=True)
        sums[2:3, :width] += jnp.sum(above, axis=0, keepdims=True)
        return carry

    lax.fori_loop(0, rows // tokens, rows_part, 0)
    step = 512

    def part(n, carry):
        at = pl.ds(pl.multiple_of(n * step, step), step)
        g_in = (dot_t(g_outers[...], down[at, :]) * slope[:, at].astype(f32)).astype(bf16)
        g_inner[:, at] = g_in
        sums[3:4, at] = jnp.sum(g_in.astype(f32), axis=0, keepdims=True)
        return carry

    lax.fori_loop(0, wide // step, part, 0)

    def grads(n, carry):
        at = pl.ds(pl.multiple_of(n * width, width), width)
        total[...] = t_dot(activated[:, at], g_outers[...])
        hand_out(ids[0], total, wide // 32, own, send, n * (16 * width // wide), 0)
        return carry

    lax.fori_loop(0, wide // width, grads, 0)


def feed_down(ids, weights, activated, slope, scaled, keep, cotangent, vectors, tokens):
    rows, width = scaled.shape
    wide = activated.shape[1]
    halves = (16, wide // 32, width)
    return call(
        functools.partial(down_body, weights, tokens),
        "feed_down",
        (1,),
        (ids, *weights.operands, activated, slope, scaled, keep, cotangent, vectors),
        weights.specs + [WHOLE] * 6,
        [
            shaped((rows, width), bf16),
            shaped((rows, width), f32),
            shaped((rows, wide), bf16),
            shaped(halves, bf16),
            shaped(halves, bf16),
            shaped((8, wide), f32),
        ],
        [WHOLE] * 6,
        weights.scratch + [pltpu.VMEM((width, width), f32), pltpu.VMEM((rows, width), bf16)],
        16,
        36,
    )


def middle_body(weights, pers, tokens, ids, *refs):
    count = len(weights.operands)
    sources, refs = refs[:count], refs[count:]
    g_inner, g_second, scaled, inverse, keep, vectors, context, down_sums = refs[:8]
    g_first_out, g_context, own, send, block = refs[8:13]
    *places, sems, g_normeds, g_attendeds, sums = refs[13:]
    copies = weights.copies(ids, sources, places, sems)
    begin([copies[1], copies[0]])
    rows, width = scaled.shape
    out_w, up_w = weights.matrix(places, 0), weights.matrix(places, 1)
    finish(copies[1])
    step = 256

    def columns_part(n, carry):
        at = pl.ds(pl.multiple_of(n * step, step), step)
        g_normeds[:rows, at] = g_second[:, at] + dot_t(g_inner[...], up_w[at, :])
        return carry

    lax.fori_loop(0, width // step, columns_part, 0)
    sums[...] = jnp.zeros_like(sums)

    def rows_part(m, carry):
        at = pl.ds(pl.multiple_of(m * tokens, tokens), tokens)
        normal = scaled[at]
        g_normed = g_normeds[at, :]
        weighted = g_normed * vectors[1:2, :width]
        g_first = inverse[at, 0:1] * (
            weighted
            - jnp.mean(weighted, axis=-1, keepdims=True)
            - normal * jnp.mean(weighted * normal, axis=-1, keepdims=True)
        )
        g_first_out[at] = g_first
        g_attended = (g_first * (keep[at].astype(f32) * keep_scale)).astype(bf16)
        g_attendeds[at] = g_attended
        sums[0:1, :] += jnp.sum(g_attended.astype(f32), axis=0, keepdims=True)
        sums[1:2, :] += jnp.sum(g_normed * normal, axis=0, keepdims=True)
        sums[2:3, :] += jnp.sum(g_normed, axis=0, keepdims=True)
        return carry

    lax.fori_loop(0, rows // tokens, rows_part, 0)
    finish(copies[0])
    g_context[...] = dot_t(g_attendeds[...], out_w[...]).astype(bf16)
    g_normeds[:width] = t_dot(context[...], g_attendeds[...])
    hand_out(ids[0], g_normeds, width // 32, own, send, 0, 0)
    vector_sums = [sums[n : n + 1, :] for n in range(3)]
    vector_sums += [down_sums[3:4, :]] + [down_sums[n : n + 1, :width] for n in range(3)]
    unspread(vector_sums, pers, block)


def middle(ids, weights, pers, g_inner, g_second, scaled, inverse, keep, vectors, context, sums, tokens):
    rows, width = scaled.shape
    halves = (16, width // 32, width)
    return call(
        functools.partial(middle_body, weights, pers, tokens),
        "middle",
        (1,),
        (ids, *weights.operands, g_inner, g_second, scaled, inverse, keep, vectors, context, sums),
        weights.specs + [WHOLE] * 8,
        [
            shaped((rows, width), f32),
            shaped((rows, width), bf16),
            shaped(halves, bf16),
            shaped(halves, bf16),
            shaped((32, 8, width), f32),
        ],
        [WHOLE] * 5,
        weights.scratch
        + [pltpu.VMEM((max(rows, width), width), f32), pltpu.VMEM((rows, width), bf16), pltpu.VMEM((8, width), f32)],
        16,
        18,
    )


def grads_body(ids, g_inner, scaled, vectors, own, send, total, low_t):
    n = pl.program_id(0)
    width = scaled.shape[1]

    @pl.when(n == 0)
    def _():
        low_t[...] = (scaled[...] * vectors[1:2, :width] + vectors[2:3, :width]).T.astype(bf16)

    total[...] = jnp.dot(low_t[...], g_inner[...], preferred_element_type=f32)
    for block in range(own.shape[1] // (width // 32)):

        @pl.when(n == block)
        def _():
            hand_out(ids[0], total, width // 32, own, send, 0, block * (width // 32))


def up_grads(ids, g_inner, scaled, vectors):
    rows, width = scaled.shape
    wide = g_inner.shape[1]
    halves = (16, wide // 32, width)
    return call(
        grads_body,
        "up_grads",
        (wide // width,),
        (ids, g_inner, scaled, vectors),
        [pl.BlockSpec((rows, width), lambda i, ids: (0, i))] + [WHOLE] * 2,
        [shaped(halves, bf16), shaped(halves, bf16)],
        [WHOLE] * 2,
        [pltpu.VMEM((width, width), f32), pltpu.VMEM((width, rows), bf16)],
        14,
        20,
    )


def hand_out_rows(core, block, own, send, at):
    for n in range(16):
        own[n, at : at + 8, :] = block[2 * n + core].astype(bf16)
        send[n, at : at + 8, :] = block[2 * n + 1 - core].astype(bf16)


def inputs_body(per, ids, hidden, turned, *refs):
    micro = (len(refs) - 8) // 5
    grads, (block, own, send, g_queries, g_keys, g_values, total, bias) = refs[: 5 * micro], refs[5 * micro :]
    width = hidden.shape[1]
    sums = []
    for n, out in enumerate((g_queries, g_keys, g_values)):
        for m in range(micro):
            g_q, near, far = grads[m], grads[micro + 2 * m :][:2], grads[3 * micro + 2 * m :][:2]
            rows = slice(m * g_q.shape[0], (m + 1) * g_q.shape[0])
            if n == 0:
                out[rows] = g_q[...]
            else:
                out[rows] = (near[n - 1][...] + far[n - 1][...].astype(f32)).astype(bf16)
        if n != 1:
            sums.append(jnp.sum(out[...].astype(f32), axis=0, keepdims=True))
        left = hidden if n == 0 else turned
        for start in range(0, width, 256):
            total[start : start + 256, :] = t_dot(left[:, start : start + 256], out[...])
        hand_out(ids[0], total, width // 32, own, send, 0, n * (width // 32))
    bias[...] = block[...]
    unspread([jnp.concatenate(sums, axis=1)], [per], bias, 7)
    hand_out_rows(ids[0], bias, own, send, 3 * (width // 32))


def input_grads(ids, hidden, turned, grads, block, per):
    rows, width = hidden.shape
    halves = (16, 3 * width // 32 + 8, width)
    return call(
        functools.partial(inputs_body, per),
        "input_grads",
        (1,),
        (ids, hidden, turned, *grads, block),
        [WHOLE] * (3 + len(grads)),
        [shaped(halves, bf16)] * 2 + [shaped((rows, width), bf16)] * 3,
        [WHOLE] * 5,
        [pltpu.VMEM((width, width), f32), pltpu.VMEM((32, 8, width), f32)],
        14,
        12,
    )


def last_body(weights, ids, *refs):
    count = len(weights.operands)
    sources = refs[:count]
    g_first, g_q, g_keys, g_values, out = refs[count : count + 5]
    places, sems = refs[count + 5 : -1], refs[-1]
    copies = weights.copies(ids, sources, places, sems)

    @pl.when(pl.program_id(0) == 0)
    def _():
        begin(copies)
        for group in copies:
            finish(group)

    turn = turn_matrix(g_q.shape[0])
    total = g_first[...] + dot_t(g_q[...], weights.matrix(places, 0)[...])
    total = total + dot_t(t_dot(turn, g_keys[...]).astype(bf16), weights.matrix(places, 1)[...])
    total = total + dot_t(t_dot(turn, g_values[...]).astype(bf16), weights.matrix(places, 2)[...])
    out[...] = total.astype(bf16)


def last(ids, weights, g_first, g_q, g_keys, g_values, tokens):
    rows, width = g_first.shape
    narrow = rows_spec(tokens, width)
    return call(
        functools.partial(last_body, weights),
        "input_back",
        (rows // tokens,),
        (ids, *weights.operands, g_first, g_q, g_keys, g_values),
        weights.specs + [narrow] * 4,
        [shaped((rows, width), bf16)],
        [narrow],
        weights.scratch,
        16,
        10,
    )[0]


def beside(shape, y, x):
    return pl.BlockSpec((4, 1, 1) + shape[3:], lambda i, ids: (0, ids[1] ^ y, ids[2] ^ x, 0, 0))


def rows_of(parts, index, first, last):
    found, start = [], 0
    for part in parts:
        rows = part.shape[-2]
        low, high = max(first, start), min(last, start + rows)
        if low < high:
            found.append(part[index + (slice(low - start, high - start),)].astype(f32))
        start += rows
    return found[0] if len(found) == 1 else jnp.concatenate(found, axis=-2)


def both(parts, index, first, last):
    half = len(parts) // 2
    return rows_of(parts[:half], index, first, last) + rows_of(parts[half:], index, first, last)


def count_rows(parts):
    return sum(part.shape[3] for part in parts[: len(parts) // 2])


PLANE = (slice(None), 0, 0)


def corner_body(ids, *refs):
    *parts, low, high = refs
    half = low.shape[1]
    low[...] = both(parts, PLANE, 0, half).astype(bf16)
    high[...] = both(parts, PLANE, half, half + high.shape[1]).astype(bf16)


def reduce_corner(ids, parts, cut):
    rows, width = count_rows(parts), parts[0].shape[4]
    return call(
        corner_body,
        "reduce_corner",
        (1,),
        (ids, *parts),
        [beside(part.shape, 1, 1) for part in parts],
        [shaped((4, cut, width), bf16), shaped((4, rows - cut, width), bf16)],
        [WHOLE] * 2,
        [],
        8,
        2,
    )


def sides_body(count, ids, *refs):
    for_y, for_x, (low, high, to_y, to_x) = refs[:count], refs[count : 2 * count], refs[2 * count :]
    rows, half = to_y.shape[1], low.shape[1]
    to_y[:, :half] = (both(for_y, PLANE, 0, half) + low[...].astype(f32)).astype(bf16)
    to_y[:, half:] = both(for_y, PLANE, half, rows).astype(bf16)
    to_x[:, :half] = both(for_x, PLANE, 0, half).astype(bf16)
    to_x[:, half:] = (both(for_x, PLANE, half, rows) + high[...].astype(f32)).astype(bf16)


def reduce_sides(ids, parts, low, high):
    rows, width = count_rows(parts), parts[0].shape[4]
    return call(
        functools.partial(sides_body, len(parts)),
        "reduce_sides",
        (1,),
        (ids, *parts, *parts, low, high),
        [beside(part.shape, 1, 0) for part in parts]
        + [beside(part.shape, 0, 1) for part in parts]
        + [WHOLE] * 2,
        [shaped((4, rows, width), bf16)] * 2,
        [WHOLE] * 2,
        [],
        10,
        3,
    )


def depth_body(ids, *refs):
    *parts, from_y, from_x, near, middle, far, mine = refs
    for k, out in enumerate((mine, near, middle, far)):
        z = ids[3] ^ k
        total = both(parts, (z, 0, 0), 0, from_y.shape[1])
        total = total + from_y[z].astype(f32) + from_x[z].astype(f32)
        out[...] = total.astype(out.dtype)


def reduce_depth(ids, parts, from_y, from_x):
    shape = from_y.shape[1:]
    return call(
        depth_body,
        "reduce_depth",
        (1,),
        (ids, *parts, from_y, from_x),
        [beside(part.shape, 0, 0) for part in parts] + [WHOLE] * 2,
        [shaped(shape, bf16)] * 3 + [shaped(shape, f32)],
        [WHOLE] * 4,
        [],
        10,
        3,
    )


def pair_body(ids, one, two, out):
    out[0] = one[...]
    out[1] = two[...]


def pair_z(ids, one, two):
    return call(
        pair_body,
        "pair_z",
        (1,),
        (ids, one, two),
        [WHOLE] * 2,
        [shaped((2,) + one.shape, bf16)],
        [WHOLE],
        [],
        4,
        1,
    )[0]


def order_body(ids, pair, received, out):
    for k in range(2):
        out[ids[3] ^ (2 * k)] = pair[k]
        out[ids[3] ^ (2 * k + 1)] = received[k]


def order_z(ids, pair, received):
    return call(
        order_body,
        "order_z",
        (1,),
        (ids, pair, received),
        [WHOLE] * 2,
        [shaped((4,) + pair.shape[1:], bf16)],
        [WHOLE],
        [],
        6,
        1,
    )[0]


def four_body(ids, *refs):
    *parts, out = refs
    for k, part in enumerate(parts):
        out[ids[3] ^ k] = part[...]


def order_four(ids, *parts):
    return call(
        four_body,
        "order_four",
        (1,),
        (ids, *parts),
        [WHOLE] * 4,
        [shaped((4,) + parts[0].shape, bf16)],
        [WHOLE],
        [],
        6,
        1,
    )[0]


def halves_body(ids, pair, received, low, high):
    rows = low.shape[1]
    for k in range(2):
        for source, z in ((pair, ids[3] ^ (2 * k)), (received, ids[3] ^ (2 * k + 1))):
            low[z] = source[k, :rows]
            high[z] = source[k, rows:]


def order_halves(ids, pair, received):
    shape = (4, pair.shape[1] // 2, pair.shape[2])
    return call(
        halves_body,
        "order_halves",
        (1,),
        (ids, pair, received),
        [WHOLE] * 2,
        [shaped(shape, bf16)] * 2,
        [WHOLE] * 2,
        [],
        6,
        1,
    )


def first_body(ids, *refs):
    at_y, at_x, at_corner, (to_y, to_x) = refs[:2], refs[2:4], refs[4:6], refs[6:]
    half = to_y.shape[1] // 2
    to_y[:, :half] = both(at_y, PLANE, 0, half).astype(bf16)
    to_y[:, half:] = both(at_corner, PLANE, 0, half).astype(bf16)
    to_x[:, :half] = both(at_x, PLANE, half, 2 * half).astype(bf16)
    to_x[:, half:] = both(at_corner, PLANE, half, 2 * half).astype(bf16)


def reduce_first(ids, parts):
    shape = parts[0].shape
    return call(
        first_body,
        "reduce_first",
        (1,),
        (ids, *parts, *parts, *parts),
        [beside(shape, 1, 0)] * 2 + [beside(shape, 0, 1)] * 2 + [beside(shape, 1, 1)] * 2,
        [shaped((4,) + shape[3:], bf16)] * 2,
        [WHOLE] * 2,
        [],
        10,
        3,
    )


def second_body(ids, *refs):
    here, at_y, at_x, (from_y, from_x, *outs) = refs[:2], refs[2:4], refs[4:6], refs[6:]
    half = from_y.shape[1] // 2
    by_next, keep_next, by_far, keep_far = outs
    for k, upper, lower in (
        (0, (keep_next, 0), (keep_far, 0)),
        (1, (by_next, 0), (keep_far, 1)),
        (2, (keep_next, 1), (by_far, 0)),
        (3, (by_next, 1), (by_far, 1)),
    ):
        z = ids[3] ^ k
        plane = (z, 0, 0)
        quarters = (
            both(here, plane, 0, half) + from_y[z, :half].astype(f32),
            both(at_x, plane, 0, half) + from_y[z, half:].astype(f32),
            both(here, plane, half, 2 * half) + from_x[z, :half].astype(f32),
            both(at_y, plane, half, 2 * half) + from_x[z, half:].astype(f32),
        )
        for i, quarter in enumerate(quarters):
            out, at = upper if i < 2 else lower
            out[at, i % 2 * half : (i % 2 + 1) * half] = quarter.astype(out.dtype)


def reduce_second(ids, parts, from_y, from_x):
    shape = parts[0].shape
    wide = (2,) + shape[3:]
    return call(
        second_body,
        "reduce_second",
        (1,),
        (ids, *parts, *parts, *parts, from_y, from_x),
        [beside(shape, 0, 0)] * 2 + [beside(shape, 1, 0)] * 2 + [beside(shape, 0, 1)] * 2 + [WHOLE] * 2,
        [shaped(wide, bf16), shaped(wide, f32)] * 2,
        [WHOLE] * 4,
        [],
        14,
        3,
    )


def third_body(ids, keep_next, keep_far, next_in, far_in, next_mine, far_mine, to_far, to_next):
    next_mine[...] = keep_next[0] + next_in[0].astype(f32)
    to_far[...] = (keep_next[1] + next_in[1].astype(f32)).astype(bf16)
    far_mine[...] = keep_far[0] + far_in[0].astype(f32)
    to_next[...] = (keep_far[1] + far_in[1].astype(f32)).astype(bf16)


def reduce_third(ids, keep_next, keep_far, next_in, far_in):
    shape = keep_next.shape[1:]
    return call(
        third_body,
        "reduce_third",
        (1,),
        (ids, keep_next, keep_far, next_in, far_in),
        [WHOLE] * 4,
        [shaped(shape, f32)] * 2 + [shaped(shape, bf16)] * 2,
        [WHOLE] * 4,
        [],
        10,
        2,
    )


def fourth_body(ids, upper, lower, from_far, from_next, to_x, to_y, own):
    half = to_x.shape[0]
    first = upper[...] + from_far[...].astype(f32)
    second = lower[...] + from_next[...].astype(f32)
    own[:half] = first[:half]
    own[half:] = second[:half]
    to_x[...] = first[half:].astype(bf16)
    to_y[...] = second[half:].astype(bf16)


def reduce_fourth(ids, upper, lower, from_far, from_next):
    rows, width = upper.shape
    return call(
        fourth_body,
        "reduce_fourth",
        (1,),
        (ids, upper, lower, from_far, from_next),
        [WHOLE] * 4,
        [shaped((rows // 2, width), bf16)] * 2 + [shaped((rows, width), f32)],
        [WHOLE] * 3,
        [],
        8,
        2,
    )


def exchange_z(sends):
    return [pp(send, "z", k) for send, k in zip(sends, (1, 2, 3))]


def local(
    hidden_in,
    cotangent,
    attention_keep,
    output_keep,
    feed_keep,
    qkv_weight,
    qkv_bias,
    out_weight,
    out_bias,
    first_gain,
    first_shift,
    up_weight,
    up_bias,
    down_weight,
    down_bias,
    second_gain,
    second_shift,
):
    micro, _, tokens, width = hidden_in.shape
    rows = micro * tokens
    own = qkv_weight.shape[0]
    wide = up_weight.shape[1]
    blocks = wide // width
    c, y, x = lax.axis_index("seq"), lax.axis_index("y"), lax.axis_index("x")
    ids = jnp.stack([c, y, x, lax.axis_index("z")]).astype(jnp.int32)
    bias_parts = (out_bias, first_gain, first_shift, up_bias, down_bias, second_gain, second_shift)
    pers = [part.shape[0] for part in bias_parts]
    per = qkv_bias.shape[0]

    column = lambda weight, i: weight[:, i * width : (i + 1) * width]
    bias_rows = lambda parts: jnp.concatenate(
        [jnp.pad(part.reshape(1, -1), ((0, 0), (0, width - part.shape[0]))) for part in parts]
        + [jnp.zeros((8 - len(parts), width), bf16)]
    )
    square = (own, width)
    hidden = hidden_in.reshape(rows, width)

    shard_a = jnp.concatenate([column(qkv_weight, i) for i in range(3)] + [bias_rows((qkv_bias,))])
    half_c = down_weight.shape[0] // 2
    x_c, y_c = pp(down_weight[:half_c], "x"), pp(down_weight[half_c:], "y")
    shard_b = jnp.concatenate(
        [out_weight] + [column(up_weight, i) for i in range(blocks)] + [bias_rows(bias_parts)]
    )
    z_a = hold([pp(shard_a, "z", k) for k in (1, 2, 3)], x_c, y_c, shard_b)
    own_a = order_four(ids, shard_a, *z_a)
    group_c = jnp.concatenate([down_weight[:half_c], x_c, down_weight[half_c:], y_c])
    x_a, y_a = pp(own_a, "x"), pp(own_a, "y")
    shard_b = after(shard_b, own_a)
    far_b = pp(shard_b, "z", 2)
    turned, keep_output, keep_feed = prepare(
        ids, after(hidden, own_a), output_keep.transpose(0, 1, 3, 2), feed_keep.transpose(0, 1, 3, 2), tokens
    )
    x_a, y_a, far_b = hold((x_a, y_a, far_b), turned)
    cut_a = shard_a.shape[0] // 2
    low_a, high_a = pp(x_a[:, :cut_a], "y"), pp(y_a[:, cut_a:], "x")
    pieces = [whole(0, 0, own_a), whole(1, 0, x_a), whole(2, 0, y_a), whole(3, 0, low_a), whole(3, cut_a, high_a)]
    late = whole(2, 0, after(y_a, low_a))
    pieces += [at_core(piece) for piece in pieces[:2] + [late] + pieces[3:]]
    pair_b = pair_z(ids, shard_b, far_b)
    near_b = pp(pair_b, "z", 1)
    plan = [(i * own, own, i, 0, 0) for i in range(3)]
    plan = divide(plan, cut_a)
    loose = [piece[2] for piece in pieces]
    weights = Weights(pieces, plan + [(3 * own, 8, 3, 0, 0)], [square] * 3 + [(8, width)], loose)
    weights_again = Weights(pieces, plan, [square] * 3)
    own_b = order_z(ids, pair_b, after(near_b, low_a, high_a))
    far_c = pp(after(group_c, own_b), "z", 2)
    x_b, y_b = pp(own_b, "x"), pp(own_b, "y")
    queries, *near = project(ids, weights, hidden, after(turned, own_b), micro, per)
    near = (near[: 2 * PARTS[0]], near[2 * PARTS[0] :])
    far = [[pp(value, "seq") for value in values] for values in near]
    words = attention_keep.reshape(micro, H, tokens, -1)
    *far[0], far_c = hold((*far[0], far_c))
    pair_c = pair_z(ids, group_c, far_c)
    near_c = pp(pair_c, "z", 1)
    context, signed = attention(ids, 0, after(queries, pair_c), near, far, words)
    own_b, x_b, y_b, *far[1] = hold((own_b, x_b, y_b, *far[1]), context)
    cut_b = shard_b.shape[0] // 2
    low_b, high_b = pp(x_b[:, :cut_b], "y"), pp(y_b[:, cut_b:], "x")
    context, signed = attention(ids, 1, queries, near, far, words, (context, signed))
    low_b, high_b, near_c = hold((low_b, high_b, near_c), context)
    pieces = [whole(0, 0, own_b), whole(1, 0, x_b), whole(2, 0, after(y_b, context))]
    pieces += [at_core(piece) for piece in pieces]
    corners = [whole(3, 0, low_b), whole(3, cut_b, high_b)]
    pieces += corners + [at_core(piece) for piece in corners]
    plan = [(0, own, 0, 0, 0)] + [((i + 1) * own, own, 1, 0, i * width) for i in range(blocks)]
    plan = divide(plan, cut_b)
    weights = Weights(
        pieces,
        plan + [((blocks + 1) * own, 8, 2, 0, 0)],
        [square, (own, wide), (8, width)],
        [piece[2] for piece in pieces],
    )
    back_weights = Weights(pieces, plan, [square, (own, wide)])
    by_x, by_y = order_halves(ids, pair_c, after(near_c, low_b, high_b))
    from_y, from_x = pp(by_x, "y"), pp(by_y, "x")
    context = context.reshape(rows, width)
    vectors, scaled, inverse, activated, slope = feed_up(
        ids, weights, pers, context, hidden, keep_output, tokens, wide
    )
    from_y, from_x = hold((from_y, from_x), activated)
    down_rows = down_weight.shape[0]
    pieces = []
    for core in range(2):
        held = [by_x, from_y, by_y, from_x]
        if core == 1:
            held = [pp(array, "seq") for array in held]
        for array, numbers, first in zip(held, ((0, 1), (2, 3), (0, 2), (1, 3)), (0, 0, half_c, half_c)):
            pieces += [(4 * core + number, first, array, i * half_c, half_c) for i, number in enumerate(numbers)]
    plan = divide([(0, down_rows, 0, 0, 0)], half_c)
    weights = Weights(pieces, plan, [(down_rows, width)], [piece[2] for piece in pieces])
    layer_out, g_second, g_inner, down_own, down_send, sums = feed_down(
        ids, weights, activated, slope, scaled, keep_feed, cotangent.reshape(rows, width), vectors, tokens
    )

    unit = lambda value: value.reshape((4, 2, 2) + value.shape[1:])
    down_core = pp(down_send, "seq")
    mid_own, mid_send = up_grads(ids, g_inner, scaled, vectors)
    down = [unit(down_own), unit(after(down_core, mid_send))]
    to_y, to_x = reduce_first(ids, down)
    down_y, down_x = pp(to_y, "y"), pp(to_x, "x")
    mid_core = pp(after(mid_send, to_y), "seq")
    g_first, g_context, out_own, out_send, block = middle(
        ids, back_weights, pers, after(g_inner, to_y), g_second, scaled, inverse, keep_output, vectors, context, sums, tokens
    )
    out_core = pp(out_send, "seq")
    down_y, down_x, mid_core = hold((down_y, down_x, mid_core), g_context)
    mid = [unit(value) for value in (mid_own, out_own, mid_core, out_core)]
    cut_m = (count_rows(mid) + 15) // 16 * 8
    corner = reduce_corner(ids, mid, cut_m)
    low, high = pp(corner[0], "x"), pp(corner[1], "y")
    to_next, keep_next, to_far, keep_far = reduce_second(ids, down, down_y, down_x)
    next_in, far_in = pp(to_next, "z", 1), pp(to_far, "z", 2)
    first_q, *first_near, far_k, far_v = attention_back(
        ids, 0, queries, near, far, signed, after(g_context, to_next, *corner)
    )
    low, high = hold((low, high), first_q)
    first_far = [pp(after(value, low, high), "seq") for value in (far_k, far_v)]
    to_y, to_x = reduce_sides(ids, mid, low, high)
    mid_y, mid_x = pp(to_y, "y"), pp(to_x, "x")
    second_q, *second_near, far_k, far_v = attention_back(
        ids, 1, queries, near, far, signed, after(g_context, to_y, to_x)
    )
    first_far = hold(first_far, second_q)
    second_far = [pp(value, "seq") for value in (far_k, far_v)]
    next_in, far_in = hold((next_in, far_in), second_q)
    upper, lower, to_far, to_next = reduce_third(ids, keep_next, keep_far, next_in, far_in)
    far_in, next_in = pp(to_far, "z", 2), pp(to_next, "z", 1)
    grads = (first_q, second_q, *first_near, *second_near, *first_far, *hold(second_far, to_far))
    a_own, a_send, g_q, g_keys, g_values = input_grads(ids, hidden, turned, grads, block, per)
    mid_y, mid_x = hold((mid_y, mid_x), a_send)
    far_in, next_in = hold((far_in, next_in), a_send)
    core_sums = pp(after(a_send, mid_y, mid_x, far_in, next_in), "seq")
    part = [unit(a_own), unit(core_sums)]
    corner = reduce_corner(ids, part, cut_a)
    low, high = pp(corner[0], "x"), pp(corner[1], "y")
    *sends, mid_mine = reduce_depth(ids, mid, after(mid_y, *corner), mid_x)
    mid_z = exchange_z(sends)
    low, high = hold((low, high), *sends)
    to_y, to_x = reduce_sides(ids, part, low, high)
    side_y, side_x = pp(to_y, "y"), pp(to_x, "x")
    to_far_x, to_far_y, down_mine = reduce_fourth(ids, upper, lower, after(far_in, to_y, to_x), next_in)
    received = [pp(to_far_x, "x"), pp(to_far_y, "y")]
    grad_in = last(
        ids, weights_again, g_first, g_q, g_keys, after(g_values, to_y, to_x), tokens
    )
    mid_z = hold(mid_z, grad_in)
    mid = add_up([mid_mine, *mid_z])
    side_y, side_x, *received = hold((side_y, side_x, *received), mid, grad_in)
    *sends, part_mine = reduce_depth(ids, part, side_y, side_x)
    grad_down = add_up([down_mine, jnp.concatenate(received)])
    part = add_up([part_mine, *exchange_z(sends)])

    stripe = lambda value, i: value[i * own : (i + 1) * own]
    grad_qkv = jnp.concatenate([stripe(part, i) for i in range(3)], axis=1)
    grad_up = jnp.concatenate([stripe(mid, i) for i in range(blocks)], axis=1)
    vector_grads = [part[3 * own + i, :length] for i, length in enumerate(pers)]
    grad_out = mid[blocks * own :]
    return (
        layer_out.reshape(hidden_in.shape),
        grad_in.reshape(hidden_in.shape),
        grad_qkv,
        part[3 * own + 7, :per],
        grad_out,
        vector_grads[0],
        vector_grads[1],
        vector_grads[2],
        grad_up,
        vector_grads[3],
        grad_down,
        vector_grads[4],
        vector_grads[5],
        vector_grads[6],
    )


def solution(mesh):
    groups, cores = mesh.devices.shape
    split = Mesh(mesh.devices.reshape(groups // 4, 2, 2, cores), ("z", "y", "x", "seq"))
    dp = ("z", "y", "x")
    token_rows = P(None, dp, "seq", None)
    matrix = P(every, None)
    vector = P(every)
    params = (matrix, vector, matrix, vector, vector, vector, matrix, vector, matrix, vector, vector, vector)

    def layer(*arrays):
        tiled = groups == 16 and cores == 2 and arrays[5].shape[0] % 8 == 0
        return (local if tiled else plain_local)(*arrays)

    return jax.shard_map(
        layer,
        mesh=split,
        in_specs=(token_rows, token_rows, P(None, dp, None, "seq", None), token_rows, token_rows) + params,
        out_specs=(token_rows, token_rows) + params,
        check_vma=False,
    )
```
